32 devices in a mesh: dp: 8 (over z, y), tp: 4 (over x, core).
Axes of the slice: x: 2, y: 2, z: 4, core: 2. Of those that a mesh axis runs over, the one named last changes fastest.
Arguments:
- tokens: bfloat16 [128, 256, 512], P('dp'), may hold values from -6 to 6
- frame_counts: int32 [128], P('dp'), may hold values from 128 to 256, as said below
- rate_groups: int32 [128], P('dp'), may hold values from 0 to 1
- conv_weight: bfloat16 [7, 512], replicated, may hold values from -2 to 2
- conv_bias: bfloat16 [512], replicated, may hold values from -3 to 3
- norm_scale: bfloat16 [2, 512], replicated, may hold values from 0.5 to 1.5
- norm_shift: bfloat16 [2, 512], replicated, may hold values from -2 to 2
- weight_in: bfloat16 [512, 1536], P(None, 'tp'), may hold values from -0.25 to 0.25
- bias_in: bfloat16 [1536], P('tp'), may hold values from -2 to 2
- weight_out: bfloat16 [1536, 512], P('tp'), may hold values from -0.21875 to 0.21875
- bias_out: bfloat16 [512], replicated, may hold values from -2 to 2
- layer_scale: bfloat16 [512], replicated, may hold values from 0.5 to 1.5
- cotangent: bfloat16 [128, 256, 512], P('dp'), may hold values from -6 to 6
Outputs:
- block_out: bfloat16 [128, 256, 512], P('dp')
- grad_tokens: float32 [128, 256, 512], P('dp')
- grad_conv_weight: float32 [7, 512], replicated
- grad_conv_bias: float32 [512], replicated
- grad_norm_scale: float32 [2, 512], replicated
- grad_norm_shift: float32 [2, 512], replicated
- grad_weight_in: float32 [512, 1536], P(None, 'tp')
- grad_bias_in: float32 [1536], P('tp')
- grad_weight_out: float32 [1536, 512], P('tp')
- grad_bias_out: float32 [512], replicated
- grad_layer_scale: float32 [512], replicated
The draws below stay inside these ranges and needn't reach their ends.
Inputs may be any that keep to these rules, and one draw needn't show every extreme that they name: `frame_counts`: an item of group 0 has at most 256 live frames, one of group 1 at most 240; both bounds are reached, and so is the least.
All inputs are finite; a program needn't handle non-finite values.
Results may differ from the reference program's by a relative error of at most 0.0061.
Values may be sent and summed in bfloat16 or wider, within the bound.
No kernel may reach another device: no remote copies, remote signals or barrier semaphores. Data moves between devices by JAX's collectives and lax.ppermute only.
A program may use at most 192 MiB of HBM per device.

```python
import math
import jax
import jax.numpy as jnp
from jax import lax

D = 512
FF = 1536
KS = 7
RATES = 2
FRAMES = 256
ITEMS = 128


def item_table(key):
    order_key = jax.random.fold_in(key, 21)
    length_key = jax.random.fold_in(key, 22)
    order = jax.random.permutation(order_key, ITEMS).astype(jnp.int32)
    groups = (order % RATES).astype(jnp.int32)
    limits = jnp.where(groups == 0, FRAMES, FRAMES - FRAMES // 16).astype(jnp.int32)
    counts = jax.random.randint(length_key, (ITEMS,), FRAMES // 2, limits + 1).astype(jnp.int32)
    counts = jnp.where(order == 0, FRAMES, counts)
    counts = jnp.where(order == 1, FRAMES - FRAMES // 16, counts)
    counts = jnp.where(order == 2, FRAMES // 2, counts).astype(jnp.int32)
    return (groups, counts)


def draw_frame_counts(key, part):
    return item_table(key)[1]


def draw_rate_groups(key, part):
    return item_table(key)[0]


def shard_levels(own_key, dims, cuts, low, high):
    factor_of = 1.0
    for axis_at, shards_of in cuts:
        steps = jax.random.uniform(jax.random.fold_in(jax.random.fold_in(own_key, 6), axis_at), (shards_of,), jnp.float32, low / len(cuts), high / len(cuts))
        factor_of = factor_of * jnp.repeat(jnp.exp(steps), dims[axis_at] // shards_of).reshape((-1,) + (1,) * (len(dims) - 1 - axis_at))
    return factor_of


def scatter_about(key, dims, spread, most, cuts=(), kind=jnp.bfloat16):
    values = jax.random.normal(key, dims, jnp.float32) * spread
    if len(cuts) > 0:
        values = shard_levels(key, dims, cuts, -0.22, 0.18) * values
    return jnp.clip(values, min=-most, max=most).astype(kind)


def setup_inputs(seed: int = 0) -> dict:
    key_of = jax.random.split(jax.random.key(seed), 14)
    tokens = scatter_about(key_of[0], (ITEMS, FRAMES, D), 1.0, 6.0, ((0, 8),))
    frame_counts = draw_frame_counts(jax.random.fold_in(key_of[13], 71), 0)
    rate_groups = draw_rate_groups(jax.random.fold_in(key_of[13], 71), 0)
    conv_weight = scatter_about(key_of[3], (KS, D), KS ** -0.5, 2.0)
    conv_bias = scatter_about(key_of[4], (D,), 0.5, 3.0)
    norm_scale = jnp.clip(1.0 + 0.1 * jax.random.normal(key_of[5], (RATES, D), jnp.float32), 0.5, 1.5).astype(jnp.bfloat16)
    norm_shift = scatter_about(key_of[6], (RATES, D), 0.3, 2.0)
    weight_in = scatter_about(key_of[7], (D, FF), D ** -0.5, 0.25, ((1, 4),))
    bias_in = scatter_about(key_of[8], (FF,), 0.3, 2.0, ((0, 4),))
    weight_out = scatter_about(key_of[9], (FF, D), (FF // 2) ** -0.5, 0.21875, ((0, 4),))
    bias_out = scatter_about(key_of[10], (D,), 0.3, 2.0)
    layer_scale = jnp.clip(jax.random.uniform(key_of[11], (D,), jnp.float32, 0.5, 1.5), 0.5, 1.5).astype(jnp.bfloat16)
    cotangent = scatter_about(key_of[12], (ITEMS, FRAMES, D), 1.0, 6.0, ((0, 8),))
    return dict(tokens=tokens, frame_counts=frame_counts, rate_groups=rate_groups, conv_weight=conv_weight, conv_bias=conv_bias, norm_scale=norm_scale, norm_shift=norm_shift, weight_in=weight_in, bias_in=bias_in, weight_out=weight_out, bias_out=bias_out, layer_scale=layer_scale, cotangent=cotangent)


EPS = 1e-06
HIGH = lax.Precision.HIGHEST

@jax.custom_vjp
def low(v):
    return lax.optimization_barrier(v.astype(jnp.bfloat16)).astype(jnp.float32)

@jax.custom_vjp
def low_back(v):
    return v

def low_keep(v):
    return (low(v), None)

def low_pass(kept, grad):
    return (grad,)

def back_keep(v):
    return (v, None)

def back_low(kept, grad):
    return (low(grad),)
low.defvjp(low_keep, low_pass)
low_back.defvjp(back_keep, back_low)

def block_forward(tokens, weights, frame_mask, one_hot):
    conv_weight, conv_bias, norm_scale, norm_shift, weight_in, bias_in, weight_out, bias_out, layer_scale = weights
    half_width = KS // 2
    masked = tokens * frame_mask[..., None]
    padded = jnp.pad(masked, ((0, 0), (half_width, half_width), (0, 0)))
    conv = conv_bias + conv_weight[0] * padded[:, 0:FRAMES]
    for tap_index in range(1, KS):
        conv = conv + conv_weight[tap_index] * padded[:, tap_index:tap_index + FRAMES]
    row_mean = lax.optimization_barrier(jnp.mean(conv, axis=-1, keepdims=True))
    centered = conv - row_mean
    variance = lax.optimization_barrier(jnp.mean(centered * centered, axis=-1, keepdims=True))
    normed = centered * lax.rsqrt(variance + EPS)
    scale_rows = jnp.dot(one_hot, norm_scale, precision=HIGH)
    shift_rows = jnp.dot(one_hot, norm_shift, precision=HIGH)
    adapted = low(normed * scale_rows[:, None, :] + shift_rows[:, None, :])
    pre_act = low_back(jnp.einsum('bfd,dh->bfh', adapted, weight_in, precision=HIGH)) + bias_in
    activation = low(jax.nn.gelu(pre_act, approximate=False))
    summed = low_back(jnp.einsum('bfh,hd->bfd', activation, weight_out, precision=HIGH))
    branch = summed + bias_out
    return (masked + layer_scale * branch) * frame_mask[..., None]

def reference(tokens, frame_counts, rate_groups, conv_weight, conv_bias, norm_scale, norm_shift, weight_in, bias_in, weight_out, bias_out, layer_scale, cotangent):
    frame_mask = (jnp.arange(FRAMES)[None, :] < frame_counts[:, None]).astype(jnp.float32)
    one_hot = (rate_groups[:, None] == jnp.arange(RATES)[None, :]).astype(jnp.float32)
    params = tuple((p.astype(jnp.float32) for p in (conv_weight, conv_bias, norm_scale, norm_shift, weight_in, bias_in, weight_out, bias_out, layer_scale)))
    block_items = math.gcd(ITEMS, 16)
    blocks = ITEMS // block_items

    def split(array):
        return array.reshape((blocks, block_items) + array.shape[1:])

    def one_block(totals, inputs):
        tok_block, mask_block, hot_block, cot_block = inputs

        def apply(tok, *weights):
            return block_forward(tok, weights, mask_block, hot_block)
        result, pull = jax.vjp(apply, tok_block, *params)
        grads = pull(cot_block)
        totals = tuple((t + g for t, g in zip(totals, grads[1:])))
        return (totals, (result.astype(jnp.bfloat16), grads[0]))
    start_totals = tuple((jnp.zeros_like(p) for p in params))
    totals, (outputs, tok_grads) = lax.scan(one_block, start_totals, (split(tokens.astype(jnp.float32)), split(frame_mask), split(one_hot), split(cotangent.astype(jnp.float32))))
    return (outputs.reshape(ITEMS, FRAMES, D), tok_grads.reshape(ITEMS, FRAMES, D), totals[0], totals[1], totals[2], totals[3], totals[4], totals[5], totals[6], totals[7], totals[8])
```

```python
import functools
import jax
import jax.numpy as jnp
from jax import lax
from jax.experimental import pallas as pl
from jax.experimental.pallas import tpu as pltpu
from jax.sharding import PartitionSpec as P

EPS = 1e-06
BF, F32 = jnp.bfloat16, jnp.float32
TILE = 256
VMEM_LIMIT = 60 * 1024 * 1024
PAD = 8


def fold(x):
    return jnp.sum(x.reshape(x.shape[0] // 8, 8, x.shape[1]), axis=0)


def gelu_parts(pre):
    cdf = 0.5 + 0.5 * lax.erf(pre * 0.7071067811865476)
    density = jnp.exp(-0.5 * pre * pre) * 0.3989422804014327
    return pre * cdf, cdf + pre * density


def pick(table, group):
    rows = table[...].astype(F32)
    value = rows[0:1]
    for r in range(1, rows.shape[0]):
        value = jnp.where(group == r, rows[r:r + 1], value)
    return value


def dot(a, b):
    return jnp.dot(a, b, preferred_element_type=F32)


def dot_t(a, b):
    return lax.dot_general(a, b, (((1,), (1,)), ((), ())), preferred_element_type=F32)


def dot_rows(a, b):
    return lax.dot_general(a, b, (((0,), (0,)), ((), ())), preferred_element_type=F32)


def conv_norm_kernel(n, taps, chunk, meta, tok, cot, cw, cb, ns, nsh, gamma,
                     adapted, normed, inv, low, gbo, pad):
    j = pl.program_id(0)
    frames = tok.shape[1]
    width = tok.shape[2]
    half = taps // 2
    count = meta[n + j]
    group = meta[2 * n + j]
    off = meta[3 * n + j]

    @pl.when(j == 0)
    def _():
        gbo[...] = jnp.zeros_like(gbo)
        pad[0:PAD, :] = jnp.zeros((PAD, width), F32)
        pad[PAD + frames:, :] = jnp.zeros((pad.shape[0] - PAD - frames, width), F32)

    rows = lax.broadcasted_iota(jnp.int32, (frames, 1), 0)
    pad[PAD:PAD + frames, :] = jnp.where(rows < count, tok[0].astype(F32), 0.0)
    scale = pick(ns, group)
    shift = pick(nsh, group)
    gam = gamma[...].astype(F32)
    bias = cb[...].astype(F32)
    w = cw[...].astype(F32)

    def step(i, acc):
        r0 = pl.multiple_of(i * chunk, chunk)
        live = (lax.broadcasted_iota(jnp.int32, (chunk, 1), 0) + r0) < count
        slab = pad[pl.ds(r0, chunk + 2 * PAD), :]
        conv = bias + w[0:1] * slab[PAD - half:PAD - half + chunk]
        for k in range(1, taps):
            s = PAD - half + k
            conv = conv + w[k:k + 1] * slab[s:s + chunk]
        mean = jnp.mean(conv, axis=-1, keepdims=True)
        cent = conv - mean
        var = jnp.mean(cent * cent, axis=-1, keepdims=True)
        istd = lax.rsqrt(var + EPS)
        nrm = cent * istd
        dst = pl.ds(pl.multiple_of(off + r0, 16), chunk)
        adapted[dst, :] = (nrm * scale + shift).astype(BF)
        normed[dst, :] = nrm.astype(BF)
        inv[dst, :] = jnp.broadcast_to(istd, (chunk, 128))
        bg = jnp.where(live, cot[0, pl.ds(r0, chunk), :].astype(F32), 0.0) * gam
        low[dst, :] = bg.astype(BF)
        return acc + fold(bg)

    gbo[...] += lax.fori_loop(0, pl.cdiv(count, chunk), step, jnp.zeros((8, width), F32))

    @pl.when(j == n - 1)
    def _():
        end = pl.ds(pl.multiple_of(meta[4 * n], 16), TILE)
        adapted[end, :] = jnp.zeros((TILE, width), BF)
        low[end, :] = jnp.zeros((TILE, width), BF)


def conv_norm(meta, tok, cot, cw, cb, ns, nsh, gamma, n, chunk=32):
    items, frames, width = tok.shape
    taps = cw.shape[0]
    rows = n * frames + TILE
    def whole(shape):
        return pl.BlockSpec(shape, lambda j, m: (0,) * len(shape))
    item = pl.BlockSpec((1, frames, width), lambda j, m: (m[j], 0, 0))
    return pl.pallas_call(
        functools.partial(conv_norm_kernel, n, taps, chunk),
        grid_spec=pltpu.PrefetchScalarGridSpec(
            num_scalar_prefetch=1, grid=(n,),
            in_specs=[item, item, whole(cw.shape), whole(cb.shape), whole(ns.shape), whole(nsh.shape), whole(gamma.shape)],
            out_specs=[whole((rows, width)), whole((rows, width)), whole((rows, 128)), whole((rows, width)), whole((8, width))],
            scratch_shapes=[pltpu.VMEM((frames + 2 * PAD, width), F32)]),
        out_shape=[jax.ShapeDtypeStruct((rows, width), BF), jax.ShapeDtypeStruct((rows, width), BF),
                   jax.ShapeDtypeStruct((rows, 128), F32), jax.ShapeDtypeStruct((rows, width), BF),
                   jax.ShapeDtypeStruct((8, width), F32)],
        compiler_params=pltpu.CompilerParams(dimension_semantics=("arbitrary",), vmem_limit_bytes=VMEM_LIMIT),
    )(meta, tok, cot, cw, cb, ns, nsh, gamma)


def hidden_kernel(n, meta, ad, low, wib_a, wib_b, wo_a, wo_b, act, pre_low, keep, send, gbi, win, wout, dwo, dwi):
    t = pl.program_id(0)
    width, h = wib_a.shape[0] - 16, wib_a.shape[1]

    @pl.when(t == 0)
    def _():
        win[:, :h] = wib_a[...]
        win[:, h:] = wib_b[...]
        wout[:h, :] = wo_a[...]
        wout[h:, :] = wo_b[...]
        dwo[...] = jnp.zeros_like(dwo)
        dwi[...] = jnp.zeros_like(dwi)
        gbi[...] = jnp.zeros_like(gbi)

    @pl.when(t < meta[4 * n + 1])
    def _():
        a, b = ad[...], low[...]
        activation, slope = gelu_parts(dot(a, win[:width, :]) + win[width:width + 1, :].astype(F32))
        grad = dot_t(b, wout[...]) * slope
        lo = activation.astype(BF)
        act[...] = lo
        dwo[...] += dot_rows(lo, b)
        gbi[...] += fold(grad)
        g = grad.astype(BF)
        pre_low[...] = g
        dwi[...] += dot_rows(a, g)

    @pl.when(t == pl.num_programs(0) - 1)
    def _():
        for side, dst in ((0, keep), (1, send)):
            for q in range(width // 128):
                dst[q * h:(q + 1) * h, :] = dwo[side * h:(side + 1) * h, q * 128:(q + 1) * 128]
            base = width // 128 * h
            for q in range(h // 128):
                lane = side * h + q * 128
                dst[base + q * width:base + (q + 1) * width, :] = dwi[:, lane:lane + 128]


def hidden(meta, ad, low, wib_a, wib_b, wo_a, wo_b, n, tile=TILE):
    rows, width = ad.shape
    h = wib_a.shape[1]
    tiles = (rows - TILE) // tile
    packed = 2 * width * h // 128
    def whole(shape):
        return pl.BlockSpec(shape, lambda t, m: (0,) * len(shape))
    def tiled(cols):
        return pl.BlockSpec((tile, cols), lambda t, m: (jnp.minimum(t, m[4 * n + 1] - 1), 0))
    return pl.pallas_call(
        functools.partial(hidden_kernel, n),
        grid_spec=pltpu.PrefetchScalarGridSpec(
            num_scalar_prefetch=1, grid=(tiles,),
            in_specs=[tiled(width), tiled(width), whole(wib_a.shape), whole(wib_a.shape), whole(wo_a.shape), whole(wo_a.shape)],
            out_specs=[tiled(2 * h), tiled(2 * h), whole((packed, 128)), whole((packed, 128)), whole((8, 2 * h))],
            scratch_shapes=[pltpu.VMEM((width + 16, 2 * h), BF), pltpu.VMEM((2 * h, width), BF),
                            pltpu.VMEM((2 * h, width), F32), pltpu.VMEM((width, 2 * h), F32)]),
        out_shape=[jax.ShapeDtypeStruct((rows, 2 * h), BF), jax.ShapeDtypeStruct((rows, 2 * h), BF),
                   jax.ShapeDtypeStruct((packed, 128), F32), jax.ShapeDtypeStruct((packed, 128), F32),
                   jax.ShapeDtypeStruct((8, 2 * h), F32)],
        compiler_params=pltpu.CompilerParams(dimension_semantics=("arbitrary",), vmem_limit_bytes=VMEM_LIMIT),
    )(meta, ad, low, wib_a, wib_b, wo_a, wo_b)


def mix_kernel(n, meta, ad, low, act_own, pre_own, wia, wib, woa, wob, wic, wid, woc, wod, bout, branch, ag,
               wi1, wo1, wi2, wo2):
    t = pl.program_id(0)
    width, h = wia.shape[0] - 16, wia.shape[1]

    @pl.when(t == 0)
    def _():
        for dst, a, b in ((wi1, wia, wib), (wi2, wic, wid)):
            dst[:, :h] = a[...]
            dst[:, h:] = b[...]
        for dst, a, b in ((wo1, woa, wob), (wo2, woc, wod)):
            dst[:h, :] = a[...]
            dst[h:, :] = b[...]

    @pl.when(t < meta[4 * n + 1])
    def _():
        a, b = ad[...], low[...]
        activation, slope = gelu_parts(dot(a, wi2[:width, :]) + wi2[width:width + 1, :].astype(F32))
        grad = dot_t(b, wo2[...]) * slope
        branch[...] = (dot(act_own[...], wo1[...]) + dot(activation.astype(BF), wo2[...])) + bout[...].astype(F32)
        ag[...] = dot_t(pre_own[...], wi1[:width, :]) + dot_t(grad.astype(BF), wi2[:width, :])


def mix(meta, ad, low, act_own, pre_own, w8, bout, n, tile=TILE):
    rows, width = ad.shape
    h2 = act_own.shape[1]
    tiles = (rows - TILE) // tile
    def whole(shape):
        return pl.BlockSpec(shape, lambda t, m: (0,) * len(shape))
    def tiled(cols):
        return pl.BlockSpec((tile, cols), lambda t, m: (jnp.minimum(t, m[4 * n + 1] - 1), 0))
    return pl.pallas_call(
        functools.partial(mix_kernel, n),
        grid_spec=pltpu.PrefetchScalarGridSpec(
            num_scalar_prefetch=1, grid=(tiles,),
            in_specs=[tiled(width), tiled(width), tiled(h2), tiled(h2)] + [whole(w.shape) for w in w8] + [whole((1, width))],
            out_specs=[tiled(width), tiled(width)],
            scratch_shapes=[pltpu.VMEM((width + 16, h2), BF), pltpu.VMEM((h2, width), BF)] * 2),
        out_shape=[jax.ShapeDtypeStruct((rows, width), F32), jax.ShapeDtypeStruct((rows, width), F32)],
        compiler_params=pltpu.CompilerParams(dimension_semantics=("arbitrary",), vmem_limit_bytes=VMEM_LIMIT),
    )(meta, ad, low, act_own, pre_own, *w8, bout)


def finish_kernel(n, taps, chunk, meta, tok, cot, branch, ag, normed, inv, cw, ns, gamma,
                  out, gtok, sums, cgp):
    j = pl.program_id(0)
    frames, width = tok.shape[1], tok.shape[2]
    half = taps // 2
    count = meta[n + j]
    group = meta[2 * n + j]
    off = meta[3 * n + j]
    rates = ns.shape[0]

    @pl.when(j == 0)
    def _():
        sums[...] = jnp.zeros_like(sums)
        cgp[...] = jnp.zeros_like(cgp)

    scale = pick(ns, group)
    gam = gamma[...].astype(F32)
    w = cw[...].astype(F32)
    zero = jnp.zeros((8, width), F32)
    steps = pl.cdiv(count, chunk)

    def step(i, accs):
        a_cb, a_ls, a_sc, a_sh = accs
        r0 = pl.multiple_of(i * chunk, chunk)
        live = (lax.broadcasted_iota(jnp.int32, (chunk, 1), 0) + r0) < count
        src = pl.ds(pl.multiple_of(off + r0, 16), chunk)
        br = jnp.where(live, branch[src, :], 0.0)
        tk = tok[0, pl.ds(r0, chunk), :].astype(F32)
        back = jnp.where(live, cot[0, pl.ds(r0, chunk), :].astype(F32), 0.0)
        out[0, pl.ds(r0, chunk), :] = jnp.where(live, tk + gam * br, 0.0).astype(BF)
        g = jnp.where(live, ag[src, :], 0.0)
        nr = normed[src, :].astype(F32)
        gn = g * nr
        ng = g * scale
        m1 = jnp.mean(ng, axis=-1, keepdims=True)
        m2 = jnp.mean(ng * nr, axis=-1, keepdims=True)
        cg = inv[src, 0:1] * (ng - m1 - nr * m2)
        cgp[pl.ds(pl.multiple_of(PAD + r0, 8), chunk), :] = cg
        return a_cb + fold(cg), a_ls + fold(back * br), a_sc + fold(gn), a_sh + fold(g)

    a_cb, a_ls, a_sc, a_sh = lax.fori_loop(0, steps, step, (zero,) * 4)
    sums[taps] += a_cb
    sums[taps + 1] += a_ls
    sums[taps + 2 + group] += a_sc
    sums[taps + 2 + rates + group] += a_sh
    def clear(i, _):
        r0 = pl.multiple_of(i * chunk, chunk)
        out[0, pl.ds(r0, chunk), :] = jnp.zeros((chunk, width), BF)
        gtok[0, pl.ds(r0, chunk), :] = jnp.zeros((chunk, width), gtok.dtype)
        cgp[pl.ds(pl.multiple_of(PAD + r0, 8), chunk), :] = jnp.zeros((chunk, width), F32)
        return 0
    lax.fori_loop(steps, frames // chunk, clear, 0)

    for q in range(width // 128):
        lanes = slice(q * 128, q * 128 + 128)
        wq = w[:, lanes]

        def conv_step(i, accs):
            r0 = pl.multiple_of(i * chunk, chunk)
            live = (lax.broadcasted_iota(jnp.int32, (chunk, 1), 0) + r0) < count
            slab = cgp[pl.ds(r0, chunk + 2 * PAD), lanes]
            tk = jnp.where(live, tok[0, pl.ds(r0, chunk), lanes].astype(F32), 0.0)
            total = cot[0, pl.ds(r0, chunk), lanes].astype(F32)
            new = []
            for k in range(taps):
                s = PAD + half - k
                sh = slab[s:s + chunk]
                total = total + wq[k:k + 1] * sh
                new.append(accs[k] + fold(tk * sh))
            gtok[0, pl.ds(r0, chunk), lanes] = jnp.where(live, total, 0.0).astype(gtok.dtype)
            return tuple(new)

        accs = lax.fori_loop(0, steps, conv_step, (jnp.zeros((8, 128), F32),) * taps)
        for k in range(taps):
            sums[k, :, lanes] += accs[k]


def finish(meta, tok, cot, branch, ag, normed, inv, cw, ns, gamma, n, chunk=32, gt_dtype=BF):
    items, frames, width = tok.shape
    taps = cw.shape[0]
    rates = ns.shape[0]
    n_sums = taps + 2 + 2 * rates
    rows = branch.shape[0]
    def whole(shape):
        return pl.BlockSpec(shape, lambda j, m: (0,) * len(shape))
    item = pl.BlockSpec((1, frames, width), lambda j, m: (m[j], 0, 0))
    own = pl.BlockSpec((1, frames, width), lambda j, m: (j, 0, 0))
    return pl.pallas_call(
        functools.partial(finish_kernel, n, taps, chunk),
        grid_spec=pltpu.PrefetchScalarGridSpec(
            num_scalar_prefetch=1, grid=(n,),
            in_specs=[item, item, whole((rows, width)), whole((rows, width)), whole((rows, width)), whole((rows, 128)),
                      whole(cw.shape), whole(ns.shape), whole(gamma.shape)],
            out_specs=[own, own, whole((n_sums, 8, width))],
            scratch_shapes=[pltpu.VMEM((frames + 2 * PAD, width), F32)]),
        out_shape=[jax.ShapeDtypeStruct((n, frames, width), BF), jax.ShapeDtypeStruct((n, frames, width), gt_dtype),
                   jax.ShapeDtypeStruct((n_sums, 8, width), F32)],
        compiler_params=pltpu.CompilerParams(dimension_semantics=("arbitrary",), vmem_limit_bytes=VMEM_LIMIT),
    )(meta, tok, cot, branch, ag, normed, inv, cw, ns, gamma)


def swap(x, step):
    size = lax.axis_size("tp")
    return lax.ppermute(x, "tp", [(i, i ^ step) for i in range(size)])


def exchange(x):
    return lax.all_to_all(x, "dp", 0, 0)


def per_device(tokens, frame_counts, rate_groups, conv_weight, conv_bias, norm_scale, norm_shift,
               weight_in, bias_in, weight_out, bias_out, layer_scale, cotangent):
    items, frames, width = tokens.shape
    taps, rates = conv_weight.shape[0], norm_scale.shape[0]
    quarter = weight_in.shape[1]
    n = items // 2
    dp = lax.axis_size("dp")
    core = lax.axis_index("tp") % 2

    wib = jnp.concatenate([weight_in, jnp.broadcast_to(bias_in[None], (16, quarter))], axis=0)
    wib_b, wo_b = swap(wib, 1), swap(weight_out, 1)
    wib_c, wo_c = swap(wib, 2), swap(weight_out, 2)
    wib_d, wo_d = swap(wib_c, 1), swap(wo_c, 1)

    own = core * n + jnp.arange(n, dtype=jnp.int32)
    counts = lax.dynamic_slice(frame_counts, (core * n,), (n,))
    groups = lax.dynamic_slice(rate_groups, (core * n,), (n,))
    sizes = (counts + 15) // 16 * 16
    ends = jnp.cumsum(sizes)
    total = ends[n - 1:]
    meta = jnp.concatenate([own, counts, groups, ends - sizes, total, (total + TILE - 1) // TILE]).astype(jnp.int32)

    row = lambda v: v[None, :]
    adapted, normed, inv, low, gbo = conv_norm(
        meta, tokens, cotangent, conv_weight, row(conv_bias), norm_scale, norm_shift, row(layer_scale), n)
    act, pre_low, keep, send, gbi = hidden(meta, adapted, low, wib, wib_b, weight_out, wo_b, n)
    grads = (keep + swap(send, 1)).astype(BF)
    shard = exchange(grads.reshape(dp, grads.shape[0] // dp, 128))

    branch, ag = mix(meta, adapted, low, act, pre_low,
                     (wib, wib_b, weight_out, wo_b, wib_c, wib_d, wo_c, wo_d), row(bias_out), n)
    out, gtok, sums = finish(meta, tokens, cotangent, branch, ag, normed, inv, conv_weight, norm_scale,
                             row(layer_scale), n)

    out_b, gtok_b = swap(out, 1), swap(gtok, 1)
    first = core == 0

    def join(a, b):
        return jnp.where(first, jnp.concatenate([a, b]), jnp.concatenate([b, a]))

    block_out = join(out, out_b)
    grad_tokens = join(gtok, gtok_b).astype(F32)

    small = jnp.concatenate([jnp.sum(sums, axis=1), jnp.sum(gbo, axis=0, keepdims=True)], axis=0)
    gb = jnp.sum(gbi, axis=0)
    gb_keep, gb_send = gb[:quarter], gb[quarter:]
    fill = jnp.zeros((width - quarter,), F32)
    small_send = jnp.concatenate([small, row(jnp.concatenate([gb_send, fill]))], axis=0)
    small_keep = jnp.concatenate([small, row(jnp.concatenate([gb_keep, fill]))], axis=0)
    small = small_keep + swap(small_send, 1)
    count = small.shape[0]
    small = jnp.pad(small, ((0, -count % 4), (0, 0))).reshape(-1, 128)
    high = lax.reduce_precision(small, 8, 7)
    part = jnp.concatenate([high.astype(BF), (small - high).astype(BF)], axis=0)

    mine = jnp.sum(shard.astype(F32), axis=0).astype(BF)
    message = jnp.concatenate([mine, part], axis=0)
    message = exchange(jnp.broadcast_to(message[None], (dp,) + message.shape))
    m = mine.shape[0]
    full = message[:, :m].reshape(dp * m, 128).astype(F32)
    both = jnp.sum(message[:, m:].astype(F32), axis=0)
    k = both.shape[0] // 2
    small = (both[:k] + both[k:]).reshape(-1, width)
    wq, hq = width // 128, quarter // 128
    cut = wq * quarter
    grad_weight_out = full[:cut].reshape(wq, quarter, 128).transpose(1, 0, 2).reshape(quarter, width)
    grad_weight_in = full[cut:].reshape(hq, width, 128).transpose(1, 0, 2).reshape(width, quarter)
    return (
        block_out,
        grad_tokens,
        small[:taps],
        small[taps],
        small[taps + 2:taps + 2 + rates],
        small[taps + 2 + rates:taps + 2 + 2 * rates],
        grad_weight_in,
        small[taps + 3 + 2 * rates, :quarter],
        grad_weight_out,
        small[taps + 2 + 2 * rates],
        small[taps + 1],
    )


def solution(mesh):
    items, copied = P("dp", None, None), P()
    in_specs = (items, P("dp"), P("dp"), copied, copied, copied, copied, P(None, "tp"), P("tp"), P("tp", None), copied, copied, items)
    out_specs = (items, items, copied, copied, copied, copied, P(None, "tp"), P("tp"), P("tp", None), copied, copied)
    return jax.shard_map(per_device, mesh=mesh, in_specs=in_specs, out_specs=out_specs, check_vma=False)
```

```python
import functools

import jax
import jax.numpy as jnp
from jax import lax
from jax.experimental import pallas as pl
from jax.experimental.pallas import tpu as pltpu
from jax.sharding import PartitionSpec as P

EPS = 1e-06
BF, F32 = jnp.bfloat16, jnp.float32
TILE = 256
LANES = 128
PAD = 8
CHUNK = 64
VMEM_LIMIT = 60 * 1024 * 1024


def params():
    return pltpu.CompilerParams(dimension_semantics=("arbitrary",), vmem_limit_bytes=VMEM_LIMIT)


def struct(shape, dtype):
    return jax.ShapeDtypeStruct(shape, dtype)


def whole(shape):
    return pl.BlockSpec(shape, lambda *_: (0,) * len(shape))


def any_spec():
    return pl.BlockSpec(memory_space=pl.ANY)


def lane(q):
    return slice(q * LANES, (q + 1) * LANES)


def fold(x):
    return jnp.sum(x.reshape(x.shape[0] // 8, 8, x.shape[1]), axis=0)


def pick(table, group):
    rows = table[...].astype(F32)
    value = rows[0:1]
    for r in range(1, rows.shape[0]):
        value = jnp.where(group == r, rows[r:r + 1], value)
    return value


def as_row(ref):
    return ref[...].astype(F32).reshape(1, -1)


def gelu_parts(pre):
    cdf = 0.5 + 0.5 * lax.erf(pre * 0.7071067811865476)
    density = jnp.exp(-0.5 * pre * pre) * 0.3989422804014327
    return pre * cdf, cdf + pre * density


def dot(a, b):
    return jnp.dot(a, b, preferred_element_type=F32)


def dot_t(a, b):
    return lax.dot_general(a, b, (((1,), (1,)), ((), ())), preferred_element_type=F32)


def dot_rows(a, b):
    return lax.dot_general(a, b, (((0,), (0,)), ((), ())), preferred_element_type=F32)


def place_items(n, core, counts, offs):
    end = jnp.int32(0)
    for j in range(n):
        offs[j] = end
        end = end + (counts[core[0] * n + j] + 15) // 16 * 16
    offs[n] = end
    offs[n + 1] = (end + TILE - 1) // TILE


def pack_kernel(wi, bi, wo, out):
    width, h = wi.shape
    hq, wq = h // LANES, width // LANES
    for q in range(hq):
        out[q * width:(q + 1) * width, :] = wi[:, lane(q)]
    base = hq * width
    for q in range(wq):
        out[base + q * h:base + (q + 1) * h, :] = wo[:, lane(q)]
    base += wq * h
    bias = bi[...].astype(F32).reshape(1, h)
    rows = [bias[:, lane(q)] for q in range(hq)] + [jnp.zeros((1, LANES), F32)] * (16 - hq)
    out[base:base + 16, :] = jnp.concatenate(rows, axis=0).astype(BF)


def pack(wi, bi, wo):
    rows = 2 * wi.size // LANES + 16
    return pl.pallas_call(pack_kernel, out_shape=struct((rows, LANES), BF),
                          compiler_params=pltpu.CompilerParams(vmem_limit_bytes=VMEM_LIMIT))(wi, bi, wo)


def weight_copies(buf, side, win, wout, bias, sems):
    width, h = win.shape[0], win.shape[1] // 2
    hq, wq = h // LANES, width // LANES
    copies = []
    for q in range(hq):
        at = side * h + q * LANES
        copies.append((buf.at[pl.ds(q * width, width), :], win.at[:, pl.ds(at, LANES)]))
    base = hq * width
    for q in range(wq):
        copies.append((buf.at[pl.ds(base + q * h, h), :], wout.at[pl.ds(side * h, h), pl.ds(q * LANES, LANES)]))
    copies.append((buf.at[pl.ds(base + wq * h, 16), :], bias.at[side]))
    return [pltpu.make_async_copy(src, dst, sems.at[side, i]) for i, (src, dst) in enumerate(copies)]


def spread_bias(bias, row):
    hq = row.shape[1] // LANES // 2
    for side in range(2):
        for q in range(hq):
            at = side * hq + q
            row[:, lane(at)] = bias[side, q:q + 1, :].astype(F32)


def front_kernel(n, core, counts, groups, tok, cot, cw, cb, ns, nsh, gamma, buf_a, buf_b,
                 ad_o, nrm_o, low_o, inv_o, act_o, pre_o, keep, send, gbo, gbi,
                 offs, pad, ad, nrm, low, inv, win, wout, bias, bias_row, dwo, dwi, sems):
    s = pl.program_id(0)
    frames, width = tok.shape[1], tok.shape[2]
    taps = cw.shape[0]
    half = taps // 2
    wq = width // LANES
    h = win.shape[1] // 2
    copies = weight_copies(buf_a, 0, win, wout, bias, sems) + weight_copies(buf_b, 1, win, wout, bias, sems)

    @pl.when(s == 0)
    def _():
        for c in copies:
            c.start()
        place_items(n, core, counts, offs)
        gbo[...] = jnp.zeros_like(gbo)
        pad[...] = jnp.zeros_like(pad)

    @pl.when(s < n)
    def _():
        item = core[0] * n + s
        count = counts[item]
        group = groups[item]
        off = offs[s]
        rows = lax.broadcasted_iota(jnp.int32, (frames, 1), 0)
        for q in range(wq):
            pad[q, PAD:PAD + frames, :] = jnp.where(rows < count, tok[0, :, lane(q)].astype(F32), 0.0)
        scale, shift = pick(ns, group), pick(nsh, group)
        gam, conv_bias = as_row(gamma), as_row(cb)
        w = cw[...].astype(F32)

        def step(i, acc):
            r0 = pl.multiple_of(i * CHUNK, CHUNK)
            live = (lax.broadcasted_iota(jnp.int32, (CHUNK, 1), 0) + r0) < count
            convs = []
            for q in range(wq):
                conv = conv_bias[:, lane(q)]
                for k in range(taps):
                    conv = conv + w[k:k + 1, lane(q)] * pad[q, pl.ds(r0 + (PAD - half + k), CHUNK), :]
                convs.append(conv)
            mean = jnp.sum(sum(convs[1:], convs[0]), axis=-1, keepdims=True) * (1.0 / width)
            cents = [c - mean for c in convs]
            sq = [c * c for c in cents]
            var = jnp.sum(sum(sq[1:], sq[0]), axis=-1, keepdims=True) * (1.0 / width)
            istd = lax.rsqrt(var + EPS)
            dst = pl.ds(pl.multiple_of(off + r0, 16), CHUNK)
            inv[dst, :] = jnp.broadcast_to(istd, (CHUNK, LANES))
            new = []
            for q in range(wq):
                normed = cents[q] * istd
                ad[dst, lane(q)] = (normed * scale[:, lane(q)] + shift[:, lane(q)]).astype(BF)
                nrm[dst, lane(q)] = normed.astype(BF)
                back = jnp.where(live, cot[0, pl.ds(r0, CHUNK), lane(q)].astype(F32), 0.0) * gam[:, lane(q)]
                low[dst, lane(q)] = back.astype(BF)
                new.append(acc[q] + fold(back))
            return tuple(new)

        accs = lax.fori_loop(0, pl.cdiv(count, CHUNK), step, (jnp.zeros((8, LANES), F32),) * wq)
        for q in range(wq):
            gbo[:, lane(q)] += accs[q]

    @pl.when(s == n)
    def _():
        end = pl.ds(pl.multiple_of(offs[n], 16), TILE)
        ad[end, :] = jnp.zeros((TILE, width), BF)
        low[end, :] = jnp.zeros((TILE, width), BF)
        for c in copies:
            c.wait()
        spread_bias(bias, bias_row)
        dwo[...] = jnp.zeros_like(dwo)
        dwi[...] = jnp.zeros_like(dwi)
        gbi[...] = jnp.zeros_like(gbi)

    @pl.when((s >= n) & (s - n < offs[n + 1]))
    def _():
        at = pl.ds(pl.multiple_of((s - n) * TILE, TILE), TILE)
        a, b = ad[at, :], low[at, :]
        ad_o[...] = a
        low_o[...] = b
        nrm_o[...] = nrm[at, :]
        inv_o[...] = inv[at, :]
        activation, slope = gelu_parts(dot(a, win[...]) + bias_row[...])
        grad = dot_t(b, wout[...]) * slope
        lo = activation.astype(BF)
        act_o[...] = lo
        dwo[...] += dot_rows(lo, b)
        gbi[...] += fold(grad)
        g = grad.astype(BF)
        pre_o[...] = g
        dwi[...] += dot_rows(a, g)

    @pl.when(s == pl.num_programs(0) - 1)
    def _():
        for side, dst in ((0, keep), (1, send)):
            for q in range(wq):
                dst[q * h:(q + 1) * h, :] = dwo[side * h:(side + 1) * h, lane(q)].astype(dst.dtype)
            base = wq * h
            for q in range(h // LANES):
                dst[base + q * width:base + (q + 1) * width, :] = dwi[:, lane(side * (h // LANES) + q)].astype(dst.dtype)


def front(core, counts, groups, tok, cot, cw, cb, ns, nsh, gamma, buf_a, buf_b, h):
    items, frames, width = tok.shape
    n = items // 2
    tiles = n * frames // TILE
    rows = n * frames + TILE
    packed = 2 * width * h // LANES
    wq, hq = width // LANES, h // LANES
    item = pl.BlockSpec((1, frames, width), lambda s, c, *_: (c[0] * n + jnp.minimum(s, n - 1), 0, 0))

    def tiled(cols):
        return pl.BlockSpec((TILE, cols), lambda s, *_: (jnp.maximum(s - n, 0), 0))

    return pl.pallas_call(
        functools.partial(front_kernel, n),
        grid_spec=pltpu.PrefetchScalarGridSpec(
            num_scalar_prefetch=3, grid=(n + tiles,),
            in_specs=[item, item] + [whole(v.shape) for v in (cw, cb, ns, nsh, gamma)] + [any_spec()] * 2,
            out_specs=[tiled(width), tiled(width), tiled(width), tiled(LANES), tiled(2 * h), tiled(2 * h),
                       whole((packed, LANES)), whole((packed, LANES)), whole((8, width)), whole((8, 2 * h))],
            scratch_shapes=[pltpu.SMEM((n + 2,), jnp.int32),
                            pltpu.VMEM((wq, frames + 4 * PAD, LANES), F32),
                            pltpu.VMEM((rows, width), BF), pltpu.VMEM((rows, width), BF),
                            pltpu.VMEM((rows, width), BF), pltpu.VMEM((rows, LANES), F32),
                            pltpu.VMEM((width, 2 * h), BF), pltpu.VMEM((2 * h, width), BF),
                            pltpu.VMEM((2, 16, LANES), BF), pltpu.VMEM((1, 2 * h), F32),
                            pltpu.VMEM((2 * h, width), F32), pltpu.VMEM((width, 2 * h), F32),
                            pltpu.SemaphoreType.DMA((2, hq + wq + 1))]),
        out_shape=[struct((tiles * TILE, width), BF)] * 3 + [struct((tiles * TILE, LANES), F32)]
        + [struct((tiles * TILE, 2 * h), BF)] * 2
        + [struct((packed, LANES), F32), struct((packed, LANES), BF), struct((8, width), F32), struct((8, 2 * h), F32)],
        compiler_params=params(),
    )(core, counts, groups, tok, cot, cw, cb, ns, nsh, gamma, buf_a, buf_b)


def back_kernel(n, tiles, core, counts, groups, tok, cot, ad_i, nrm_i, low_i, inv_i, act_i, pre_i, gbo, gbi,
                cw, ns, gamma, bout, buf_a, buf_b, buf_c, buf_d,
                out, gtok, out_t, gtok_t, small_keep, small_send,
                offs, win1, wout1, win2, wout2, bias, bias_row, nrm, inv, branch, ag, cgp, sums, sems):
    s = pl.program_id(0)
    frames, width = tok.shape[1], tok.shape[2]
    taps, rates = cw.shape[0], ns.shape[0]
    half = taps // 2
    wq = width // LANES
    h = win1.shape[1] // 2
    copies = (weight_copies(buf_a, 0, win1, wout1, bias, sems.at[0]) + weight_copies(buf_b, 1, win1, wout1, bias, sems.at[0]))
    copies2 = (weight_copies(buf_c, 0, win2, wout2, bias, sems.at[1]) + weight_copies(buf_d, 1, win2, wout2, bias, sems.at[1]))
    biases = (wq + h // LANES, 2 * (wq + h // LANES) + 1)

    @pl.when(s == 0)
    def _():
        for c in copies2:
            c.start()
        for i, c in enumerate(copies):
            if i not in biases:
                c.start()
        place_items(n, core, counts, offs)
        sums[...] = jnp.zeros_like(sums)
        cgp[...] = jnp.zeros_like(cgp)
        for c in copies2:
            c.wait()
        spread_bias(bias, bias_row)
        for i, c in enumerate(copies):
            if i not in biases:
                c.wait()

    @pl.when((s < tiles) & (s < offs[n + 1]))
    def _():
        at = pl.ds(pl.multiple_of(s * TILE, TILE), TILE)
        a, b = ad_i[...], low_i[...]
        nrm[at, :] = nrm_i[...]
        inv[at, :] = inv_i[...]
        activation, slope = gelu_parts(dot(a, win2[...]) + bias_row[...])
        grad = dot_t(b, wout2[...]) * slope
        branch[at, :] = (dot(act_i[...], wout1[...]) + dot(activation.astype(BF), wout2[...])) + as_row(bout)
        ag[at, :] = dot_t(pre_i[...], win1[...]) + dot_t(grad.astype(BF), win2[...])

    @pl.when(s >= tiles)
    def _():
        j = s - tiles
        item = core[0] * n + j
        count = counts[item]
        group = groups[item]
        off = offs[j]
        scale = pick(ns, group)
        gam = as_row(gamma)
        w = cw[...].astype(F32)
        zero = jnp.zeros((8, LANES), F32)
        steps = pl.cdiv(count, CHUNK)

        def step(i, accs):
            r0 = pl.multiple_of(i * CHUNK, CHUNK)
            here = pl.ds(r0, CHUNK)
            live = (lax.broadcasted_iota(jnp.int32, (CHUNK, 1), 0) + r0) < count
            src = pl.ds(pl.multiple_of(off + r0, 16), CHUNK)
            new = []
            ngs, nrs = [], []
            for q in range(wq):
                a_ls, a_sc, a_sh = accs[3 * q:3 * q + 3]
                br = jnp.where(live, branch[src, lane(q)], 0.0)
                tk = jnp.where(live, tok[0, here, lane(q)].astype(F32), 0.0)
                o = (tk + gam[:, lane(q)] * br).astype(BF)
                out[0, here, lane(q)] = o
                out_t[0, here, lane(q)] = o
                g = jnp.where(live, ag[src, lane(q)], 0.0)
                nr = nrm[src, lane(q)].astype(F32)
                new += [a_ls + fold(cot[0, here, lane(q)].astype(F32) * br), a_sc + fold(g * nr), a_sh + fold(g)]
                ngs.append(g * scale[:, lane(q)])
                nrs.append(nr)
            cross = [a * b for a, b in zip(ngs, nrs)]
            m1 = jnp.sum(sum(ngs[1:], ngs[0]), axis=-1, keepdims=True) * (1.0 / width)
            m2 = jnp.sum(sum(cross[1:], cross[0]), axis=-1, keepdims=True) * (1.0 / width)
            istd = inv[src, :]
            for q in range(wq):
                cg = istd * (ngs[q] - m1 - nrs[q] * m2)
                cgp[q, pl.ds(pl.multiple_of(r0 + PAD, 8), CHUNK), :] = jnp.where(live, cg, 0.0)
            return tuple(new)

        accs = lax.fori_loop(0, steps, step, (zero,) * (3 * wq))
        for q in range(wq):
            sums[taps + 1, :, lane(q)] += accs[3 * q]
            sums[taps + 2 + group, :, lane(q)] += accs[3 * q + 1]
            sums[taps + 2 + rates + group, :, lane(q)] += accs[3 * q + 2]

        def clear(i, _):
            r0 = pl.multiple_of(i * CHUNK, CHUNK)
            here = pl.ds(r0, CHUNK)
            out[0, here, :] = jnp.zeros((CHUNK, width), BF)
            out_t[0, here, :] = jnp.zeros((CHUNK, width), BF)
            gtok[0, here, :] = jnp.zeros((CHUNK, width), F32)
            gtok_t[0, here, :] = jnp.zeros((CHUNK, width), BF)
            for q in range(wq):
                cgp[q, pl.ds(pl.multiple_of(r0 + PAD, 8), CHUNK), :] = jnp.zeros((CHUNK, LANES), F32)
            return 0

        lax.fori_loop(steps, frames // CHUNK, clear, 0)

        for q in range(wq):
            wl = w[:, lane(q)]

            def conv_step(i, accs):
                r0 = pl.multiple_of(i * CHUNK, CHUNK)
                here = pl.ds(r0, CHUNK)
                live = (lax.broadcasted_iota(jnp.int32, (CHUNK, 1), 0) + r0) < count
                tk = jnp.where(live, tok[0, here, lane(q)].astype(F32), 0.0)
                total = cot[0, here, lane(q)].astype(F32)
                new = []
                for k in range(taps):
                    sh = cgp[q, pl.ds(r0 + (PAD + half - k), CHUNK), :]
                    total = total + wl[k:k + 1] * sh
                    new.append(accs[k] + fold(tk * sh))
                    if k == half:
                        new_bias = accs[taps] + fold(sh)
                total = jnp.where(live, total, 0.0).astype(BF)
                gtok_t[0, here, lane(q)] = total
                gtok[0, here, lane(q)] = total.astype(F32)
                return tuple(new) + (new_bias,)

            accs = lax.fori_loop(0, steps, conv_step, (zero,) * (taps + 1))
            for k in range(taps + 1):
                sums[k, :, lane(q)] += accs[k]

    @pl.when(s == pl.num_programs(0) - 1)
    def _():
        last = taps + 2 + 2 * rates
        rows = [jnp.sum(sums[i], axis=0, keepdims=True) for i in range(last)]
        rows.append(jnp.sum(gbo[...], axis=0, keepdims=True))
        gb = jnp.sum(gbi[...], axis=0, keepdims=True)
        fill = jnp.zeros((1, width - h), F32)
        spare = [jnp.zeros((1, width), F32)] * (small_keep.shape[0] - last - 2)
        for side, dst in ((0, small_keep), (1, small_send)):
            tail = [jnp.concatenate([gb[:, side * h:(side + 1) * h], fill], axis=1)]
            dst[...] = jnp.concatenate(rows + tail + spare, axis=0)


def back(core, counts, groups, tok, cot, ad, nrm, low, inv, act, pre, gbo, gbi, cw, ns, gamma, bout, bufs):
    items, frames, width = tok.shape
    n = items // 2
    h = act.shape[1] // 2
    tiles = n * frames // TILE
    rows = n * frames + TILE
    wq, hq = width // LANES, h // LANES
    taps, rates = cw.shape[0], ns.shape[0]
    n_small = -(-(taps + 4 + 2 * rates) // 8) * 8

    def at(s):
        return jnp.maximum(s - tiles, 0)

    item = pl.BlockSpec((1, frames, width), lambda s, c, *_: (c[0] * n + at(s), 0, 0))
    mine = pl.BlockSpec((1, frames, width), lambda s, *_: (at(s), 0, 0))

    def tiled(cols):
        return pl.BlockSpec((TILE, cols), lambda s, *_: (jnp.minimum(s, tiles - 1), 0))

    return pl.pallas_call(
        functools.partial(back_kernel, n, tiles),
        grid_spec=pltpu.PrefetchScalarGridSpec(
            num_scalar_prefetch=3, grid=(tiles + n,),
            in_specs=[item, item, tiled(width), tiled(width), tiled(width), tiled(LANES), tiled(2 * h), tiled(2 * h)]
            + [whole(v.shape) for v in (gbo, gbi, cw, ns, gamma, bout)] + [any_spec()] * 4,
            out_specs=[item, item, mine, mine, whole((n_small, width)), whole((n_small, width))],
            scratch_shapes=[pltpu.SMEM((n + 2,), jnp.int32),
                            pltpu.VMEM((width, 2 * h), BF), pltpu.VMEM((2 * h, width), BF),
                            pltpu.VMEM((width, 2 * h), BF), pltpu.VMEM((2 * h, width), BF),
                            pltpu.VMEM((2, 16, LANES), BF), pltpu.VMEM((1, 2 * h), F32),
                            pltpu.VMEM((rows, width), BF), pltpu.VMEM((rows, LANES), F32),
                            pltpu.VMEM((rows, width), F32), pltpu.VMEM((rows, width), F32),
                            pltpu.VMEM((wq, frames + 4 * PAD, LANES), F32),
                            pltpu.VMEM((taps + 2 + 2 * rates, 8, width), F32),
                            pltpu.SemaphoreType.DMA((2, 2, hq + wq + 1))]),
        out_shape=[struct((items, frames, width), BF), struct((items, frames, width), F32),
                   struct((n, frames, width), BF), struct((n, frames, width), BF),
                   struct((n_small, width), F32), struct((n_small, width), F32)],
        compiler_params=params(),
    )(core, counts, groups, tok, cot, ad, nrm, low, inv, act, pre, gbo, gbi, cw, ns, gamma, bout, *bufs)


def merge_kernel(core, out_b, gtok_b, out_in, gtok_in, out, gtok):
    out[...] = out_b[...]
    gtok[...] = gtok_b[...].astype(F32)


def merge(core, out_b, gtok_b, out, gtok):
    n, frames, width = out_b.shape
    mine = pl.BlockSpec((1, frames, width), lambda s, c: (s, 0, 0))
    other = pl.BlockSpec((1, frames, width), lambda s, c: ((1 - c[0]) * n + s, 0, 0))
    return pl.pallas_call(
        merge_kernel,
        grid_spec=pltpu.PrefetchScalarGridSpec(
            num_scalar_prefetch=1, grid=(n,),
            in_specs=[mine, mine, any_spec(), any_spec()], out_specs=[other, other]),
        out_shape=[struct(out.shape, out.dtype), struct(gtok.shape, gtok.dtype)],
        input_output_aliases={3: 0, 4: 1},
        compiler_params=params(),
    )(core, out_b, gtok_b, out, gtok)


def message_kernel(shard, keep, recv, out, total):
    total_rows = shard.shape[1]
    acc = shard[0].astype(F32)
    for i in range(1, shard.shape[0]):
        acc = acc + shard[i].astype(F32)
    total[:total_rows, :] = acc.astype(BF)
    small = keep[...] + recv[...]
    high = small.astype(BF)
    low = (small - high.astype(F32)).astype(BF)
    n_small = small.shape[0]
    wq = small.shape[1] // LANES
    for part, value in enumerate((high, low)):
        for q in range(wq):
            base = total_rows + (part * wq + q) * n_small
            total[base:base + n_small, :] = value[:, lane(q)]
    for i in range(out.shape[0]):
        out[i] = total[...]


def make_message(shard, keep, recv):
    dp, m, _ = shard.shape
    rows = m + 2 * keep.size // LANES
    return pl.pallas_call(
        message_kernel, out_shape=struct((dp, rows, LANES), BF),
        scratch_shapes=[pltpu.VMEM((rows, LANES), BF)],
        compiler_params=pltpu.CompilerParams(vmem_limit_bytes=VMEM_LIMIT))(shard, keep, recv)


def unpack_kernel(m, taps, rates, msg, gcw, gcb, gns, gnsh, gwi, gbi, gwo, gbo, gls, full):
    dp = msg.shape[0]
    h, width = gwo.shape
    wq, hq = width // LANES, h // LANES
    for i in range(dp):
        full[i * m:(i + 1) * m, :] = msg[i, :m, :].astype(F32)
    for q in range(wq):
        gwo[:, lane(q)] = full[q * h:(q + 1) * h, :]
    base = wq * h
    for q in range(hq):
        gwi[:, lane(q)] = full[base + q * width:base + (q + 1) * width, :]
    both = msg[0, m:, :].astype(F32)
    for i in range(1, dp):
        both = both + msg[i, m:, :].astype(F32)
    k = both.shape[0] // 2
    small = both[:k] + both[k:]
    rows = k // wq
    small = jnp.concatenate([small[q * rows:(q + 1) * rows] for q in range(wq)], axis=1)
    gcw[...] = small[:taps]
    gcb[...] = small[taps:taps + 1]
    gls[...] = small[taps + 1:taps + 2]
    gns[...] = small[taps + 2:taps + 2 + rates]
    gnsh[...] = small[taps + 2 + rates:taps + 2 + 2 * rates]
    at = taps + 2 + 2 * rates
    gbo[...] = small[at:at + 1]
    gbi[...] = small[at + 1:at + 2, :h]


def unpack(msg, m, taps, rates, width, h):
    shapes = [(taps, width), (1, width), (rates, width), (rates, width), (width, h), (1, h), (h, width), (1, width), (1, width)]
    return pl.pallas_call(
        functools.partial(unpack_kernel, m, taps, rates), out_shape=[struct(s, F32) for s in shapes],
        scratch_shapes=[pltpu.VMEM((msg.shape[0] * m, LANES), F32)],
        compiler_params=pltpu.CompilerParams(vmem_limit_bytes=VMEM_LIMIT))(msg)


def swap(x, step):
    size = lax.axis_size("tp")
    return lax.ppermute(x, "tp", [(i, i ^ step) for i in range(size)])


def exchange(x):
    return lax.all_to_all(x, "dp", 0, 0)


def per_device(tokens, frame_counts, rate_groups, conv_weight, conv_bias, norm_scale, norm_shift,
               weight_in, bias_in, weight_out, bias_out, layer_scale, cotangent):
    width, h = weight_in.shape
    taps, rates = conv_weight.shape[0], norm_scale.shape[0]
    dp = lax.axis_size("dp")
    core = (lax.axis_index("tp") % 2).astype(jnp.int32).reshape(1)

    buf_a = pack(weight_in, bias_in, weight_out)
    buf_b = swap(buf_a, 1)
    buf_c = swap(buf_a, 2)
    buf_d = swap(buf_c, 1)
    ad, nrm, low, inv, act, pre, keep, send, gbo, gbi = front(
        core, frame_counts, rate_groups, tokens, cotangent, conv_weight, conv_bias, norm_scale, norm_shift,
        layer_scale, buf_a, buf_b, h)
    grads = (keep + swap(send, 1).astype(F32)).astype(BF)
    shard = exchange(grads.reshape(dp, grads.shape[0] // dp, LANES))
    out, gtok, out_t, gtok_t, small_keep, small_send = back(
        core, frame_counts, rate_groups, tokens, cotangent, ad, nrm, low, inv, act, pre, gbo, gbi,
        conv_weight, norm_scale, layer_scale, bias_out, (buf_a, buf_b, buf_c, buf_d))
    message = exchange(make_message(shard, small_keep, swap(small_send, 1)))
    out, gtok = merge(core, swap(out_t, 1), swap(gtok_t, 1), out, gtok)
    gcw, gcb, gns, gnsh, gwi, gbi, gwo, gbo, gls = unpack(message, shard.shape[1], taps, rates, width, h)
    flat = lambda v: v.reshape(-1)
    return (out, gtok, gcw, flat(gcb), gns, gnsh, gwi, flat(gbi), gwo, flat(gbo), flat(gls))


def solution(mesh):
    items, copied = P("dp", None, None), P()
    in_specs = (items, P("dp"), P("dp"), copied, copied, copied, copied, P(None, "tp"), P("tp"), P("tp", None),
                copied, copied, items)
    out_specs = (items, items, copied, copied, copied, copied, P(None, "tp"), P("tp"), P("tp", None), copied, copied)
    return jax.shard_map(per_device, mesh=mesh, in_specs=in_specs, out_specs=out_specs, check_vma=False)
```

```python
import functools

import jax
import jax.numpy as jnp
from jax import lax
from jax.experimental import pallas as pl
from jax.experimental.pallas import tpu as pltpu
from jax.sharding import PartitionSpec as P

EPS = 1e-06
BF, F32 = jnp.bfloat16, jnp.float32
TILE = 256
LANES = 128
PAD = 8
CHUNK = 64
VMEM_LIMIT = 12 * 1024 * 1024


def params(**more):
    return pltpu.CompilerParams(vmem_limit_bytes=VMEM_LIMIT, **more)


def struct(shape, dtype):
    return jax.ShapeDtypeStruct(shape, dtype)


def whole(shape):
    return pl.BlockSpec(shape, lambda *_: (0,) * len(shape))


def hbm():
    return pl.BlockSpec(memory_space=pltpu.HBM)


def smem():
    return pl.BlockSpec(memory_space=pltpu.SMEM)


def cost(size):
    return pl.CostEstimate(flops=0, transcendentals=0, bytes_accessed=size)


def vmem():
    return pl.BlockSpec(memory_space=pltpu.VMEM)


def lane(q):
    return slice(q * LANES, (q + 1) * LANES)


def fold(x):
    return jnp.sum(x.reshape(x.shape[0] // 8, 8, x.shape[1]), axis=0)


def pick(table, group):
    rows = table[...].astype(F32)
    value = rows[0:1]
    for r in range(1, rows.shape[0]):
        value = jnp.where(group == r, rows[r:r + 1], value)
    return value


def as_row(ref):
    return ref[...].astype(F32).reshape(1, -1)


def gelu_parts(pre):
    cdf = 0.5 + 0.5 * lax.erf(pre * 0.7071067811865476)
    density = jnp.exp(-0.5 * pre * pre) * 0.3989422804014327
    return pre * cdf, cdf + pre * density


def dot(a, b):
    return jnp.dot(a, b, preferred_element_type=F32)


def dot_t(a, b):
    return lax.dot_general(a, b, (((1,), (1,)), ((), ())), preferred_element_type=F32)


def dot_rows(a, b):
    return lax.dot_general(a, b, (((0,), (0,)), ((), ())), preferred_element_type=F32)


def place_items(n, core, counts, offs):
    end = jnp.int32(0)
    for j in range(n):
        offs[j] = end
        end = end + (counts[core[0] * n + j] + 15) // 16 * 16
    offs[n] = end
    offs[n + 1] = (end + TILE - 1) // TILE


def pack_kernel(wi, bi, wo, out):
    width, h = wi.shape
    hq, wq = h // LANES, width // LANES
    for q in range(hq):
        out[q * width:(q + 1) * width, :] = wi[:, lane(q)]
    base = hq * width
    for q in range(wq):
        out[base + q * h:base + (q + 1) * h, :] = wo[:, lane(q)]
    base += wq * h
    bias = bi[...].astype(F32).reshape(1, h)
    rows = [bias[:, lane(q)] for q in range(hq)] + [jnp.zeros((1, LANES), F32)] * (16 - hq)
    out[base:base + 16, :] = jnp.concatenate(rows, axis=0).astype(BF)


def pack(wi, bi, wo):
    rows = 2 * wi.size // LANES + 16
    return pl.pallas_call(pack_kernel, out_shape=struct((rows, LANES), BF),
                          compiler_params=params())(wi, bi, wo)


def weight_copies(buf, side, win, wout, bias, sems):
    width, h = win.shape[0], win.shape[1] // 2
    hq, wq = h // LANES, width // LANES
    copies = []
    for q in range(hq):
        at = side * h + q * LANES
        copies.append((buf.at[pl.ds(q * width, width), :], win.at[:, pl.ds(at, LANES)]))
    base = hq * width
    for q in range(wq):
        copies.append((buf.at[pl.ds(base + q * h, h), :], wout.at[pl.ds(side * h, h), pl.ds(q * LANES, LANES)]))
    copies.append((buf.at[pl.ds(base + wq * h, 16), :], bias.at[side]))
    return [pltpu.make_async_copy(src, dst, sems.at[side, i]) for i, (src, dst) in enumerate(copies)]


def spread_bias(bias, row):
    hq = row.shape[1] // LANES // 2
    for side in range(2):
        for q in range(hq):
            at = side * hq + q
            row[:, lane(at)] = bias[side, q:q + 1, :].astype(F32)


def conv_norm_kernel(n, core, counts, groups, tok, cot, cw, cb, ns, nsh, gamma, ad, nrm, low, inv, gbo, offs, pad):
    s = pl.program_id(0)
    frames, width = tok.shape[1], tok.shape[2]
    taps = cw.shape[0]
    half = taps // 2
    wq = width // LANES

    @pl.when(s == 0)
    def _():
        place_items(n, core, counts, offs)
        gbo[...] = jnp.zeros_like(gbo)
        pad[...] = jnp.zeros_like(pad)

    item = core[0] * n + s
    count = counts[item]
    group = groups[item]
    off = offs[s]
    rows = lax.broadcasted_iota(jnp.int32, (frames, 1), 0)
    for q in range(wq):
        pad[q, PAD:PAD + frames, :] = jnp.where(rows < count, tok[0, :, lane(q)].astype(F32), 0.0)
    scale, shift = pick(ns, group), pick(nsh, group)
    gam, conv_bias = as_row(gamma), as_row(cb)
    w = cw[...].astype(F32)

    def step(i, acc):
        r0 = pl.multiple_of(i * CHUNK, CHUNK)
        live = (lax.broadcasted_iota(jnp.int32, (CHUNK, 1), 0) + r0) < count
        convs = []
        for q in range(wq):
            conv = conv_bias[:, lane(q)]
            for k in range(taps):
                conv = conv + w[k:k + 1, lane(q)] * pad[q, pl.ds(r0 + (PAD - half + k), CHUNK), :]
            convs.append(conv)
        mean = jnp.sum(sum(convs[1:], convs[0]), axis=-1, keepdims=True) * (1.0 / width)
        cents = [c - mean for c in convs]
        sq = [c * c for c in cents]
        var = jnp.sum(sum(sq[1:], sq[0]), axis=-1, keepdims=True) * (1.0 / width)
        istd = lax.rsqrt(var + EPS)
        dst = pl.ds(pl.multiple_of(off + r0, 16), CHUNK)
        inv[dst, :] = jnp.broadcast_to(istd, (CHUNK, LANES))
        new = []
        for q in range(wq):
            normed = cents[q] * istd
            ad[dst, lane(q)] = (normed * scale[:, lane(q)] + shift[:, lane(q)]).astype(BF)
            nrm[dst, lane(q)] = normed.astype(BF)
            back = jnp.where(live, cot[0, pl.ds(r0, CHUNK), lane(q)].astype(F32), 0.0) * gam[:, lane(q)]
            low[dst, lane(q)] = back.astype(BF)
            new.append(acc[q] + fold(back))
        return tuple(new)

    accs = lax.fori_loop(0, pl.cdiv(count, CHUNK), step, (jnp.zeros((8, LANES), F32),) * wq)
    for q in range(wq):
        gbo[:, lane(q)] += accs[q]

    @pl.when(s == n - 1)
    def _():
        end = pl.ds(pl.multiple_of(offs[n], 16), TILE)
        ad[end, :] = jnp.zeros((TILE, width), BF)
        low[end, :] = jnp.zeros((TILE, width), BF)


def conv_norm(core, counts, groups, tok, cot, cw, cb, ns, nsh, gamma):
    items, frames, width = tok.shape
    n = items // 2
    rows = n * frames + TILE
    item = pl.BlockSpec((1, frames, width), lambda s, c, *_: (c[0] * n + s, 0, 0))
    return pl.pallas_call(
        functools.partial(conv_norm_kernel, n),
        grid_spec=pltpu.PrefetchScalarGridSpec(
            num_scalar_prefetch=3, grid=(n,),
            in_specs=[item, item] + [whole(v.shape) for v in (cw, cb, ns, nsh, gamma)],
            out_specs=[vmem()] * 5,
            scratch_shapes=[pltpu.SMEM((n + 2,), jnp.int32),
                            pltpu.VMEM((width // LANES, frames + 4 * PAD, LANES), F32)]),
        out_shape=[struct((rows, width), BF)] * 3 + [struct((rows, LANES), F32), struct((8, width), F32)],
        compiler_params=params(), cost_estimate=cost(0),
    )(core, counts, groups, tok, cot, cw, cb, ns, nsh, gamma)


def hidden_kernel(n, core, counts, ad, low, buf_a, buf_b, act, pre, win, wout, keep, send, gbi,
                  offs, bias, bias_row, dwo, dwi, sems):
    width, h = win.shape[0], win.shape[1] // 2
    wq = width // LANES
    copies = weight_copies(buf_a, 0, win, wout, bias, sems) + weight_copies(buf_b, 1, win, wout, bias, sems)
    for c in copies:
        c.start()
    place_items(n, core, counts, offs)
    dwo[...] = jnp.zeros_like(dwo)
    dwi[...] = jnp.zeros_like(dwi)
    gbi[...] = jnp.zeros_like(gbi)
    for c in copies:
        c.wait()
    spread_bias(bias, bias_row)

    def tile(t, _):
        at = pl.ds(pl.multiple_of(t * TILE, TILE), TILE)
        a, b = ad[at, :], low[at, :]
        activation, slope = gelu_parts(dot(a, win[...]) + bias_row[...])
        grad = dot_t(b, wout[...]) * slope
        lo = activation.astype(BF)
        act[at, :] = lo
        dwo[...] += dot_rows(lo, b)
        gbi[...] += fold(grad)
        g = grad.astype(BF)
        pre[at, :] = g
        dwi[...] += dot_rows(a, g)
        return 0

    lax.fori_loop(0, offs[n + 1], tile, 0)
    for side, dst in ((0, keep), (1, send)):
        for q in range(wq):
            dst[q * h:(q + 1) * h, :] = dwo[side * h:(side + 1) * h, lane(q)].astype(dst.dtype)
        base = wq * h
        for q in range(h // LANES):
            dst[base + q * width:base + (q + 1) * width, :] = dwi[:, lane(side * (h // LANES) + q)].astype(dst.dtype)


def hidden(core, counts, ad, low, buf_a, buf_b, h, n):
    rows, width = ad.shape
    packed = 2 * width * h // LANES
    wq, hq = width // LANES, h // LANES
    return pl.pallas_call(
        functools.partial(hidden_kernel, n),
        in_specs=[smem(), smem(), vmem(), vmem(), hbm(), hbm()],
        out_specs=[vmem()] * 7,
        scratch_shapes=[pltpu.SMEM((n + 2,), jnp.int32),
                        pltpu.VMEM((2, 16, LANES), BF), pltpu.VMEM((1, 2 * h), F32),
                        pltpu.VMEM((2 * h, width), F32), pltpu.VMEM((width, 2 * h), F32),
                        pltpu.SemaphoreType.DMA((2, hq + wq + 1))],
        out_shape=[struct((rows, 2 * h), BF)] * 2 + [struct((width, 2 * h), BF), struct((2 * h, width), BF)]
        + [struct((packed, LANES), F32), struct((packed, LANES), BF), struct((8, 2 * h), F32)],
        compiler_params=params(), cost_estimate=cost(0),
    )(core, counts, ad, low, buf_a, buf_b)


def combine_kernel(dp, core, keep, recv, stay, leave):
    m = keep.shape[0] // dp
    for d in range(dp):
        src = pl.ds(pl.multiple_of((core[1] ^ d) * m, m), m)
        total = keep[src, :] + recv[src, :].astype(F32)
        dst = leave if d % 2 else stay
        dst[d // 2 * m:(d // 2 + 1) * m, :] = total.astype(dst.dtype)


def combine(core, keep, recv, dp):
    rows = keep.shape[0] // 2
    return pl.pallas_call(
        functools.partial(combine_kernel, dp),
        in_specs=[smem(), vmem(), vmem()], out_specs=[vmem(), vmem()],
        out_shape=[struct((rows, LANES), F32), struct((rows, LANES), BF)],
        compiler_params=params())(core, keep, recv)


def mix_kernel(n, core, counts, ad, low, act, pre, win1, wout1, bout, buf_c, buf_d, branch, ag,
               offs, win2, wout2, bias, bias_row, sems):
    copies = weight_copies(buf_c, 0, win2, wout2, bias, sems) + weight_copies(buf_d, 1, win2, wout2, bias, sems)
    for c in copies:
        c.start()
    place_items(n, core, counts, offs)
    for c in copies:
        c.wait()
    spread_bias(bias, bias_row)

    def tile(t, _):
        at = pl.ds(pl.multiple_of(t * TILE, TILE), TILE)
        a, b = ad[at, :], low[at, :]
        activation, slope = gelu_parts(dot(a, win2[...]) + bias_row[...])
        grad = dot_t(b, wout2[...]) * slope
        branch[at, :] = (dot(act[at, :], wout1[...]) + dot(activation.astype(BF), wout2[...])) + as_row(bout)
        ag[at, :] = dot_t(pre[at, :], win1[...]) + dot_t(grad.astype(BF), win2[...])
        return 0

    lax.fori_loop(0, offs[n + 1], tile, 0)


def mix(core, counts, ad, low, act, pre, win, wout, bout, buf_c, buf_d, n):
    rows, width = ad.shape
    h = act.shape[1] // 2
    wq, hq = width // LANES, h // LANES
    return pl.pallas_call(
        functools.partial(mix_kernel, n),
        in_specs=[smem(), smem()] + [vmem()] * 7 + [hbm()] * 2,
        out_specs=[vmem(), vmem()],
        scratch_shapes=[pltpu.SMEM((n + 2,), jnp.int32),
                        pltpu.VMEM((width, 2 * h), BF), pltpu.VMEM((2 * h, width), BF),
                        pltpu.VMEM((2, 16, LANES), BF), pltpu.VMEM((1, 2 * h), F32),
                        pltpu.SemaphoreType.DMA((2, hq + wq + 1))],
        out_shape=[struct((rows, width), F32)] * 2,
        compiler_params=params(), cost_estimate=cost(0),
    )(core, counts, ad, low, act, pre, win, wout, bout, buf_c, buf_d)


def finish_kernel(n, first, last_part, core, counts, groups, tok, cot, branch, ag, nrm, inv, sums_in, gbo, gbi, cw, ns,
                  gamma, out, gtok, *rest):
    results, (offs, cgp, sums) = rest[:-3], rest[-3:]
    s = pl.program_id(0) + first
    frames, width = tok.shape[1], tok.shape[2]
    taps, rates = cw.shape[0], ns.shape[0]
    half = taps // 2
    wq = width // LANES
    h = gbi.shape[1] // 2

    @pl.when(s == first)
    def _():
        place_items(n, core, counts, offs)
        sums[...] = sums_in[...] if last_part else jnp.zeros_like(sums)
        cgp[...] = jnp.zeros_like(cgp)

    item = core[0] * n + s
    count = counts[item]
    group = groups[item]
    off = offs[s]
    scale = pick(ns, group)
    gam = as_row(gamma)
    w = cw[...].astype(F32)
    zero = jnp.zeros((8, LANES), F32)
    steps = pl.cdiv(count, CHUNK)

    def step(i, accs):
        r0 = pl.multiple_of(i * CHUNK, CHUNK)
        here = pl.ds(r0, CHUNK)
        live = (lax.broadcasted_iota(jnp.int32, (CHUNK, 1), 0) + r0) < count
        src = pl.ds(pl.multiple_of(off + r0, 16), CHUNK)
        new = []
        ngs, nrs = [], []
        for q in range(wq):
            a_ls, a_sc, a_sh = accs[3 * q:3 * q + 3]
            br = jnp.where(live, branch[src, lane(q)], 0.0)
            tk = jnp.where(live, tok[0, here, lane(q)].astype(F32), 0.0)
            out[0, here, lane(q)] = (tk + gam[:, lane(q)] * br).astype(BF)
            g = jnp.where(live, ag[src, lane(q)], 0.0)
            nr = nrm[src, lane(q)].astype(F32)
            new += [a_ls + fold(cot[0, here, lane(q)].astype(F32) * br), a_sc + fold(g * nr), a_sh + fold(g)]
            ngs.append(g * scale[:, lane(q)])
            nrs.append(nr)
        cross = [a * b for a, b in zip(ngs, nrs)]
        m1 = jnp.sum(sum(ngs[1:], ngs[0]), axis=-1, keepdims=True) * (1.0 / width)
        m2 = jnp.sum(sum(cross[1:], cross[0]), axis=-1, keepdims=True) * (1.0 / width)
        istd = inv[src, :]
        for q in range(wq):
            cg = istd * (ngs[q] - m1 - nrs[q] * m2)
            cgp[q, pl.ds(pl.multiple_of(r0 + PAD, 8), CHUNK), :] = jnp.where(live, cg, 0.0)
        return tuple(new)

    accs = lax.fori_loop(0, steps, step, (zero,) * (3 * wq))
    for q in range(wq):
        sums[taps + 1, :, lane(q)] += accs[3 * q]
        sums[taps + 2 + group, :, lane(q)] += accs[3 * q + 1]
        sums[taps + 2 + rates + group, :, lane(q)] += accs[3 * q + 2]

    def clear(i, _):
        r0 = pl.multiple_of(i * CHUNK, CHUNK)
        here = pl.ds(r0, CHUNK)
        out[0, here, :] = jnp.zeros((CHUNK, width), BF)
        gtok[0, here, :] = jnp.zeros((CHUNK, width), BF)
        for q in range(wq):
            cgp[q, pl.ds(pl.multiple_of(r0 + PAD, 8), CHUNK), :] = jnp.zeros((CHUNK, LANES), F32)
        return 0

    lax.fori_loop(steps, frames // CHUNK, clear, 0)

    for q in range(wq):
        wl = w[:, lane(q)]

        def conv_step(i, accs):
            r0 = pl.multiple_of(i * CHUNK, CHUNK)
            here = pl.ds(r0, CHUNK)
            live = (lax.broadcasted_iota(jnp.int32, (CHUNK, 1), 0) + r0) < count
            tk = jnp.where(live, tok[0, here, lane(q)].astype(F32), 0.0)
            total = cot[0, here, lane(q)].astype(F32)
            new = []
            for k in range(taps):
                sh = cgp[q, pl.ds(r0 + (PAD + half - k), CHUNK), :]
                total = total + wl[k:k + 1] * sh
                new.append(accs[k] + fold(tk * sh))
                if k == half:
                    new_bias = accs[taps] + fold(sh)
            gtok[0, here, lane(q)] = jnp.where(live, total, 0.0).astype(BF)
            return tuple(new) + (new_bias,)

        accs = lax.fori_loop(0, steps, conv_step, (zero,) * (taps + 1))
        for k in range(taps + 1):
            sums[k, :, lane(q)] += accs[k]

    @pl.when(pl.program_id(0) == pl.num_programs(0) - 1)
    def _():
        if not last_part:
            results[0][...] = sums[...]
            return
        small_keep, small_send = results
        last = taps + 2 + 2 * rates
        rows = [jnp.sum(sums[i], axis=0, keepdims=True) for i in range(last)]
        rows.append(jnp.sum(gbo[...], axis=0, keepdims=True))
        gb = jnp.sum(gbi[...], axis=0, keepdims=True)
        fill = jnp.zeros((1, width - h), F32)
        spare = [jnp.zeros((1, width), F32)] * (small_keep.shape[0] - last - 2)
        for side, dst in ((0, small_keep), (1, small_send)):
            tail = [jnp.concatenate([gb[:, side * h:(side + 1) * h], fill], axis=1)]
            dst[...] = jnp.concatenate(rows + tail + spare, axis=0)


def finish(core, counts, groups, tok, cot, branch, ag, nrm, inv, sums, gbo, gbi, cw, ns, gamma, first, size):
    items, frames, width = tok.shape
    n = items // 2
    last_part = first + size == n
    wq = width // LANES
    taps, rates = cw.shape[0], ns.shape[0]
    n_small = -(-(taps + 4 + 2 * rates) // 8) * 8
    sums_shape = (taps + 2 + 2 * rates, 8, width)
    item = pl.BlockSpec((1, frames, width), lambda s, c, *_: (c[0] * n + first + s, 0, 0))
    mine = pl.BlockSpec((1, frames, width), lambda s, *_: (s, 0, 0))
    more = [(n_small, width)] * 2 if last_part else [sums_shape]
    if sums is None:
        sums = gbo
    return pl.pallas_call(
        functools.partial(finish_kernel, n, first, last_part),
        grid_spec=pltpu.PrefetchScalarGridSpec(
            num_scalar_prefetch=3, grid=(size,),
            in_specs=[item, item] + [vmem()] * 7 + [whole(v.shape) for v in (cw, ns, gamma)],
            out_specs=[mine, mine] + [vmem()] * len(more),
            scratch_shapes=[pltpu.SMEM((n + 2,), jnp.int32),
                            pltpu.VMEM((wq, frames + 4 * PAD, LANES), F32),
                            pltpu.VMEM(sums_shape, F32)]),
        out_shape=[struct((size, frames, width), BF)] * 2 + [struct(v, F32) for v in more],
        compiler_params=params(), cost_estimate=cost(40000000),
    )(core, counts, groups, tok, cot, branch, ag, nrm, inv, sums, gbo, gbi, cw, ns, gamma)


def merge_kernel(core, out_a, gtok_a, out_b, gtok_b, *rest):
    out, gtok = rest[-2:]

    @pl.when(pl.program_id(0) == 0)
    def _():
        out[...] = out_a[...]
        gtok[...] = gtok_a[...].astype(F32)

    @pl.when(pl.program_id(0) == 1)
    def _():
        out[...] = out_b[...]
        gtok[...] = gtok_b[...].astype(F32)


def merge(core, out_a, gtok_a, out_b, gtok_b, into, n, first, step=2):
    size, frames, width = out_a.shape
    blocks = size // step
    mine = pl.BlockSpec((step, frames, width), lambda side, s, c: (s * (1 - side) + (blocks - 1) * side, 0, 0))
    other = pl.BlockSpec((step, frames, width), lambda side, s, c: (s * side, 0, 0))
    dst = pl.BlockSpec((step, frames, width), lambda side, s, c: (((c[0] ^ side) * n + first) // step + s, 0, 0))
    return pl.pallas_call(
        merge_kernel,
        grid_spec=pltpu.PrefetchScalarGridSpec(
            num_scalar_prefetch=1, grid=(2, blocks),
            in_specs=[mine, mine, other, other] + [pl.BlockSpec(memory_space=pl.ANY)] * len(into), out_specs=[dst, dst]),
        out_shape=[struct((2 * n, frames, width), BF), struct((2 * n, frames, width), F32)],
        input_output_aliases={5: 0, 6: 1} if into else {},
        compiler_params=params(), cost_estimate=cost(20000000),
    )(core, out_a, gtok_a, out_b, gtok_b, *into)


def unpack_kernel(dp, taps, rates, core, mess_a, mess_b, small, gcw, gcb, gns, gnsh, gwi, gbi, gwo, gbo, gls, full):
    h, width = gwo.shape
    wq, hq = width // LANES, h // LANES
    m = full.shape[0] // dp
    half = m // 2
    for part, mess, order in ((0, mess_a, spread_order(dp, False)), (1, mess_b, spread_order(dp, True))):
        for i, d in enumerate(order):
            at = pl.multiple_of((core[1] ^ d) * m + part * half, half)
            full[pl.ds(at, half), :] = mess[i * half:(i + 1) * half, :].astype(F32)
    for q in range(wq):
        gwo[:, lane(q)] = full[q * h:(q + 1) * h, :]
    base = wq * h
    for q in range(hq):
        gwi[:, lane(q)] = full[base + q * width:base + (q + 1) * width, :]
    gcw[...] = small[:taps]
    gcb[...] = small[taps]
    gls[...] = small[taps + 1]
    gns[...] = small[taps + 2:taps + 2 + rates]
    gnsh[...] = small[taps + 2 + rates:taps + 2 + 2 * rates]
    at = taps + 2 + 2 * rates
    gbo[...] = small[at]
    gbi[...] = small[at + 1, :h]


def unpack(core, mess_a, mess_b, small, dp, taps, rates, width, h):
    shapes = [(taps, width), (width,), (rates, width), (rates, width), (width, h), (h,), (h, width), (width,), (width,)]
    return pl.pallas_call(
        functools.partial(unpack_kernel, dp, taps, rates), in_specs=[smem(), vmem(), vmem(), vmem()],
        out_shape=[struct(s, F32) for s in shapes],
        scratch_shapes=[pltpu.VMEM((2 * width * h // LANES, LANES), F32)],
        compiler_params=params())(core, mess_a, mess_b, small)


def swap(x, step):
    size = lax.axis_size("tp")
    return lax.ppermute(x, "tp", [(i, i ^ step) for i in range(size)])


def across(x, step):
    size = lax.axis_size("dp")
    return lax.ppermute(x, "dp", [(i, i ^ step) for i in range(size)])


def spread_steps(dp, second):
    far = [1 << i for i in range(dp.bit_length() - 2, 0, -1)]
    return [1] + far if second else far + [1]


def spread_order(dp, second):
    order = [0]
    for step in spread_steps(dp, second):
        order = order + [d ^ step for d in order]
    return order


def split(x):
    high = lax.reduce_precision(x, 8, 7)
    low = lax.reduce_precision(x - high, 8, 7)
    return jnp.concatenate([high, low], axis=0).astype(BF), high + low


def per_device(tokens, frame_counts, rate_groups, conv_weight, conv_bias, norm_scale, norm_shift,
               weight_in, bias_in, weight_out, bias_out, layer_scale, cotangent):
    width, h = weight_in.shape
    n = tokens.shape[0] // 2
    tokens = pltpu.with_memory_space_constraint(tokens, pltpu.HBM)
    cotangent = pltpu.with_memory_space_constraint(cotangent, pltpu.HBM)
    taps, rates = conv_weight.shape[0], norm_scale.shape[0]
    dp = lax.axis_size("dp")
    core = jnp.stack([lax.axis_index("tp") & 1, lax.axis_index("dp")]).astype(jnp.int32)

    buf_a = pack(weight_in, bias_in, weight_out)
    buf_b = swap(buf_a, 1)
    buf_c = swap(buf_a, 2)
    buf_d = swap(buf_c, 1)
    ad, nrm, low, inv, gbo = conv_norm(core, frame_counts, rate_groups, tokens, cotangent, conv_weight, conv_bias,
                                       norm_scale, norm_shift, layer_scale)
    act, pre, win, wout, keep, send, gbi = hidden(core, frame_counts, ad, low, buf_a, buf_b, h, n)
    stay, leave = combine(core, keep, swap(send, 1), dp)
    arrived = across(leave, 1)
    branch, ag = mix(core, frame_counts, ad, low, act, pre, win, wout, bias_out, buf_c, buf_d, n)
    arrived, branch = lax.optimization_barrier((arrived, branch))
    stay = (stay + arrived.astype(F32)).reshape(dp // 2, -1, LANES)
    pieces = [across(stay[d].astype(BF), 2 * d) for d in range(1, dp // 2)]

    def finish_part(sums, branch, first):
        return finish(core, frame_counts, rate_groups, tokens, cotangent, branch, ag, nrm, inv, sums,
                      gbo, gbi, conv_weight, norm_scale, layer_scale, first, n // 2)

    out_1, gtok_1, sums = finish_part(None, branch, 0)
    pieces, branch = lax.optimization_barrier((pieces, branch))
    out_2, gtok_2, small_keep, small_send = finish_part(sums, branch, n // 2)
    shard = stay[0]
    for piece in pieces:
        shard = shard + piece.astype(F32)
    shard = shard.astype(BF)
    small = small_keep + swap(small_send, 1)
    rows = small.shape[0] * width // LANES
    half = shard.shape[0] // 2
    mess_a, mess_b = shard[:half], shard[half:]
    for step_a, step_b in zip(spread_steps(dp, False), spread_steps(dp, True)):
        riding, small = split(small.reshape(rows, LANES))
        came_a = across(mess_a, step_a)
        came_b = across(jnp.concatenate([mess_b, riding], axis=0), step_b)
        k = mess_b.shape[0]
        mess_a = jnp.concatenate([mess_a, came_a], axis=0)
        mess_b = jnp.concatenate([mess_b, came_b[:k]], axis=0)
        small = small + (came_b[k:k + rows].astype(F32) + came_b[k + rows:].astype(F32))
    done = merge(core, out_1, gtok_1, swap(out_1, 1), swap(gtok_1, 1), (), n, 0)
    out, gtok = merge(core, out_2, gtok_2, swap(out_2, 1), swap(gtok_2, 1), done, n, n // 2)
    small = small.reshape(-1, width)
    gcw, gcb, gns, gnsh, gwi, gbi, gwo, gbo, gls = unpack(core, mess_a, mess_b, small, dp, taps, rates, width, h)
    return (out, gtok, gcw, gcb, gns, gnsh, gwi, gbi, gwo, gbo, gls)


def solution(mesh):
    items, copied = P("dp", None, None), P()
    in_specs = (items, P("dp"), P("dp"), copied, copied, copied, copied, P(None, "tp"), P("tp"), P("tp", None),
                copied, copied, items)
    out_specs = (items, items, copied, copied, copied, copied, P(None, "tp"), P("tp"), P("tp", None), copied, copied)
    return jax.shard_map(per_device, mesh=mesh, in_specs=in_specs, out_specs=out_specs, check_vma=False)
```

```python
import functools

import jax
import jax.numpy as jnp
from jax import lax
from jax.experimental import pallas as pl
from jax.experimental.pallas import tpu as pltpu
from jax.sharding import PartitionSpec as P

EPS = 1e-06
BF, F32 = jnp.bfloat16, jnp.float32
TILE = 256
LANES = 128
PAD = 8
CHUNK = 64
VMEM_LIMIT = 12 * 1024 * 1024


def params(**more):
    return pltpu.CompilerParams(vmem_limit_bytes=VMEM_LIMIT, **more)


def struct(shape, dtype):
    return jax.ShapeDtypeStruct(shape, dtype)


def whole(shape):
    return pl.BlockSpec(shape, lambda *_: (0,) * len(shape))


def hbm():
    return pl.BlockSpec(memory_space=pltpu.HBM)


def smem():
    return pl.BlockSpec(memory_space=pltpu.SMEM)


def cost(size):
    return pl.CostEstimate(flops=0, transcendentals=0, bytes_accessed=size)


def vmem():
    return pl.BlockSpec(memory_space=pltpu.VMEM)


def lane(q):
    return slice(q * LANES, (q + 1) * LANES)


def fold(x):
    return jnp.sum(x.reshape(x.shape[0] // 8, 8, x.shape[1]), axis=0)


def pick(table, group):
    rows = table[...].astype(F32)
    value = rows[0:1]
    for r in range(1, rows.shape[0]):
        value = jnp.where(group == r, rows[r:r + 1], value)
    return value


def as_row(ref):
    return ref[...].astype(F32).reshape(1, -1)


def gelu_parts(pre):
    cdf = 0.5 + 0.5 * lax.erf(pre * 0.7071067811865476)
    density = jnp.exp(-0.5 * pre * pre) * 0.3989422804014327
    return pre * cdf, cdf + pre * density


def dot(a, b):
    return jnp.dot(a, b, preferred_element_type=F32)


def dot_t(a, b):
    return lax.dot_general(a, b, (((1,), (1,)), ((), ())), preferred_element_type=F32)


def dot_rows(a, b):
    return lax.dot_general(a, b, (((0,), (0,)), ((), ())), preferred_element_type=F32)


def place_items(n, meta, offs):
    end = jnp.int32(0)
    for j in range(n):
        offs[j] = end
        end = end + ((meta[2 + meta[0] * n + j] + 15) & -16)
    offs[n] = end
    offs[n + 1] = (end + TILE - 1) // TILE


def pack_kernel(wi, bi, wo, out):
    width, h = wi.shape
    hq, wq = h // LANES, width // LANES
    for q in range(hq):
        out[q * width:(q + 1) * width, :] = wi[:, lane(q)]
    base = hq * width
    for q in range(wq):
        out[base + q * h:base + (q + 1) * h, :] = wo[:, lane(q)]
    base += wq * h
    bias = bi[...].astype(F32).reshape(1, h)
    rows = [bias[:, lane(q)] for q in range(hq)] + [jnp.zeros((1, LANES), F32)] * (16 - hq)
    out[base:base + 16, :] = jnp.concatenate(rows, axis=0).astype(BF)


def pack(wi, bi, wo):
    rows = 2 * wi.size // LANES + 16
    return pl.pallas_call(pack_kernel, out_shape=struct((rows, LANES), BF),
                          compiler_params=params())(wi, bi, wo)


def weight_copies(buf, side, win, wout, bias, sems):
    width, h = win.shape[0], win.shape[1] // 2
    hq, wq = h // LANES, width // LANES
    copies = []
    for q in range(hq):
        at = side * h + q * LANES
        copies.append((buf.at[pl.ds(q * width, width), :], win.at[:, pl.ds(at, LANES)]))
    base = hq * width
    for q in range(wq):
        copies.append((buf.at[pl.ds(base + q * h, h), :], wout.at[pl.ds(side * h, h), pl.ds(q * LANES, LANES)]))
    copies.append((buf.at[pl.ds(base + wq * h, 16), :], bias.at[side]))
    return [pltpu.make_async_copy(src, dst, sems.at[side, i]) for i, (src, dst) in enumerate(copies)]


def spread_bias(bias, row):
    hq = row.shape[1] // LANES // 2
    for side in range(2):
        for q in range(hq):
            at = side * hq + q
            row[:, lane(at)] = bias[side, q:q + 1, :].astype(F32)


def conv_norm_kernel(n, meta, tok, cot, cw, cb, ns, nsh, gamma, ad, nrm, low, inv, gbo, offs, pad):
    s = pl.program_id(0)
    frames, width = tok.shape[1], tok.shape[2]
    taps = cw.shape[0]
    half = taps // 2
    wq = width // LANES

    @pl.when(s == 0)
    def _():
        place_items(n, meta, offs)
        gbo[...] = jnp.zeros_like(gbo)
        pad[...] = jnp.zeros_like(pad)

    item = meta[0] * n + s
    count = meta[2 + item]
    group = meta[2 + 2 * n + item]
    off = offs[s]
    rows = lax.broadcasted_iota(jnp.int32, (frames, 1), 0)
    for q in range(wq):
        pad[q, PAD:PAD + frames, :] = jnp.where(rows < count, tok[0, :, lane(q)].astype(F32), 0.0)
    scale, shift = pick(ns, group), pick(nsh, group)
    gam, conv_bias = as_row(gamma), as_row(cb)
    w = cw[...].astype(F32)

    def step(i, acc):
        r0 = pl.multiple_of(i * CHUNK, CHUNK)
        live = (lax.broadcasted_iota(jnp.int32, (CHUNK, 1), 0) + r0) < count
        convs = []
        for q in range(wq):
            conv = conv_bias[:, lane(q)]
            for k in range(taps):
                conv = conv + w[k:k + 1, lane(q)] * pad[q, pl.ds(r0 + (PAD - half + k), CHUNK), :]
            convs.append(conv)
        mean = jnp.sum(sum(convs[1:], convs[0]), axis=-1, keepdims=True) * (1.0 / width)
        cents = [c - mean for c in convs]
        sq = [c * c for c in cents]
        var = jnp.sum(sum(sq[1:], sq[0]), axis=-1, keepdims=True) * (1.0 / width)
        istd = lax.rsqrt(var + EPS)
        dst = pl.ds(pl.multiple_of(off + r0, 16), CHUNK)
        inv[dst, :] = jnp.broadcast_to(istd, (CHUNK, LANES))
        new = []
        for q in range(wq):
            normed = cents[q] * istd
            ad[dst, lane(q)] = (normed * scale[:, lane(q)] + shift[:, lane(q)]).astype(BF)
            nrm[dst, lane(q)] = normed.astype(BF)
            back = jnp.where(live, cot[0, pl.ds(r0, CHUNK), lane(q)].astype(F32), 0.0) * gam[:, lane(q)]
            low[dst, lane(q)] = back.astype(BF)
            new.append(acc[q] + fold(back))
        return tuple(new)

    accs = lax.fori_loop(0, pl.cdiv(count, CHUNK), step, (jnp.zeros((8, LANES), F32),) * wq)
    for q in range(wq):
        gbo[:, lane(q)] += accs[q]

    @pl.when(s == n - 1)
    def _():
        end = pl.ds(pl.multiple_of(offs[n], 16), TILE)
        ad[end, :] = jnp.zeros((TILE, width), BF)
        low[end, :] = jnp.zeros((TILE, width), BF)


def conv_norm(meta, tok, cot, cw, cb, ns, nsh, gamma):
    items, frames, width = tok.shape
    n = items // 2
    rows = n * frames + TILE
    item = pl.BlockSpec((1, frames, width), lambda s, c: (c[0] * n + s, 0, 0))
    return pl.pallas_call(
        functools.partial(conv_norm_kernel, n),
        grid_spec=pltpu.PrefetchScalarGridSpec(
            num_scalar_prefetch=1, grid=(n,),
            in_specs=[item, item] + [whole(v.shape) for v in (cw, cb, ns, nsh, gamma)],
            out_specs=[vmem()] * 5,
            scratch_shapes=[pltpu.SMEM((n + 2,), jnp.int32),
                            pltpu.VMEM((width // LANES, frames + 4 * PAD, LANES), F32)]),
        out_shape=[struct((rows, width), BF)] * 3 + [struct((rows, LANES), F32), struct((8, width), F32)],
        compiler_params=params(), cost_estimate=cost(0),
    )(meta, tok, cot, cw, cb, ns, nsh, gamma)


def hidden_kernel(n, meta, ad, low, buf_a, buf_b, act, pre, win, wout, keep, send, gbi,
                  offs, bias, bias_row, dwo, dwi, sems):
    width, h = win.shape[0], win.shape[1] // 2
    wq = width // LANES
    copies = weight_copies(buf_a, 0, win, wout, bias, sems) + weight_copies(buf_b, 1, win, wout, bias, sems)
    for c in copies:
        c.start()
    place_items(n, meta, offs)
    dwo[...] = jnp.zeros_like(dwo)
    dwi[...] = jnp.zeros_like(dwi)
    gbi[...] = jnp.zeros_like(gbi)
    for c in copies:
        c.wait()
    spread_bias(bias, bias_row)

    def tile(t, _):
        at = pl.ds(pl.multiple_of(t * TILE, TILE), TILE)
        a, b = ad[at, :], low[at, :]
        activation, slope = gelu_parts(dot(a, win[...]) + bias_row[...])
        grad = dot_t(b, wout[...]) * slope
        lo = activation.astype(BF)
        act[at, :] = lo
        dwo[...] += dot_rows(lo, b)
        gbi[...] += fold(grad)
        g = grad.astype(BF)
        pre[at, :] = g
        dwi[...] += dot_rows(a, g)
        return 0

    lax.fori_loop(0, offs[n + 1], tile, 0)
    for side, dst in ((0, keep), (1, send)):
        for q in range(wq):
            dst[q * h:(q + 1) * h, :] = dwo[side * h:(side + 1) * h, lane(q)].astype(dst.dtype)
        base = wq * h
        for q in range(h // LANES):
            dst[base + q * width:base + (q + 1) * width, :] = dwi[:, lane(side * (h // LANES) + q)].astype(dst.dtype)


def hidden(meta, ad, low, buf_a, buf_b, h, n):
    rows, width = ad.shape
    packed = 2 * width * h // LANES
    wq, hq = width // LANES, h // LANES
    return pl.pallas_call(
        functools.partial(hidden_kernel, n),
        in_specs=[smem(), vmem(), vmem(), hbm(), hbm()],
        out_specs=[vmem()] * 7,
        scratch_shapes=[pltpu.SMEM((n + 2,), jnp.int32),
                        pltpu.VMEM((2, 16, LANES), BF), pltpu.VMEM((1, 2 * h), F32),
                        pltpu.VMEM((2 * h, width), F32), pltpu.VMEM((width, 2 * h), F32),
                        pltpu.SemaphoreType.DMA((2, hq + wq + 1))],
        out_shape=[struct((rows, 2 * h), BF)] * 2 + [struct((width, 2 * h), BF), struct((2 * h, width), BF)]
        + [struct((packed, LANES), F32), struct((packed, LANES), BF), struct((8, 2 * h), F32)],
        compiler_params=params(), cost_estimate=cost(0),
    )(meta, ad, low, buf_a, buf_b)


def combine_kernel(dp, meta, keep, recv, stay, leave):
    m = keep.shape[0] // dp
    for d in range(dp):
        src = pl.ds(pl.multiple_of((meta[1] ^ d) * m, m), m)
        total = keep[src, :] + recv[src, :].astype(F32)
        dst = leave if d % 2 else stay
        dst[d // 2 * m:(d // 2 + 1) * m, :] = total.astype(dst.dtype)


def combine(meta, keep, recv, dp):
    rows = keep.shape[0] // 2
    return pl.pallas_call(
        functools.partial(combine_kernel, dp),
        in_specs=[smem(), vmem(), vmem()], out_specs=[vmem(), vmem()],
        out_shape=[struct((rows, LANES), F32), struct((rows, LANES), BF)],
        compiler_params=params())(meta, keep, recv)


def mix_kernel(n, meta, ad, low, act, pre, win1, wout1, bout, buf_c, buf_d, branch, ag,
               offs, win2, wout2, bias, bias_row, sems):
    copies = weight_copies(buf_c, 0, win2, wout2, bias, sems) + weight_copies(buf_d, 1, win2, wout2, bias, sems)
    for c in copies:
        c.start()
    place_items(n, meta, offs)
    for c in copies:
        c.wait()
    spread_bias(bias, bias_row)

    def tile(t, _):
        at = pl.ds(pl.multiple_of(t * TILE, TILE), TILE)
        a, b = ad[at, :], low[at, :]
        activation, slope = gelu_parts(dot(a, win2[...]) + bias_row[...])
        grad = dot_t(b, wout2[...]) * slope
        branch[at, :] = (dot(act[at, :], wout1[...]) + dot(activation.astype(BF), wout2[...])) + as_row(bout)
        ag[at, :] = dot_t(pre[at, :], win1[...]) + dot_t(grad.astype(BF), win2[...])
        return 0

    lax.fori_loop(0, offs[n + 1], tile, 0)


def mix(meta, ad, low, act, pre, win, wout, bout, buf_c, buf_d, n):
    rows, width = ad.shape
    h = act.shape[1] // 2
    wq, hq = width // LANES, h // LANES
    return pl.pallas_call(
        functools.partial(mix_kernel, n),
        in_specs=[smem()] + [vmem()] * 6 + [whole(bout.shape)] + [hbm()] * 2,
        out_specs=[vmem(), vmem()],
        scratch_shapes=[pltpu.SMEM((n + 2,), jnp.int32),
                        pltpu.VMEM((width, 2 * h), BF), pltpu.VMEM((2 * h, width), BF),
                        pltpu.VMEM((2, 16, LANES), BF), pltpu.VMEM((1, 2 * h), F32),
                        pltpu.SemaphoreType.DMA((2, hq + wq + 1))],
        out_shape=[struct((rows, width), F32)] * 2,
        compiler_params=params(), cost_estimate=cost(0),
    )(meta, ad, low, act, pre, win, wout, bout, buf_c, buf_d)


def finish_kernel(n, first, last_part, meta, tok, cot, branch, ag, nrm, inv, sums_in, gbo, gbi, cw, ns,
                  gamma, both, *rest):
    results, (offs, cgp, sums) = rest[:-3], rest[-3:]
    s = pl.program_id(0) + first
    frames, width = tok.shape[1], tok.shape[2]
    taps, rates = cw.shape[0], ns.shape[0]
    half = taps // 2
    wq = width // LANES
    h = gbi.shape[1] // 2

    @pl.when(s == first)
    def _():
        place_items(n, meta, offs)
        sums[...] = sums_in[...] if last_part else jnp.zeros_like(sums)
        cgp[...] = jnp.zeros_like(cgp)

    item = meta[0] * n + s
    count = meta[2 + item]
    group = meta[2 + 2 * n + item]
    off = offs[s]
    scale = pick(ns, group)
    gam = as_row(gamma)
    w = cw[...].astype(F32)
    zero = jnp.zeros((8, LANES), F32)
    steps = pl.cdiv(count, CHUNK)

    def step(i, accs):
        r0 = pl.multiple_of(i * CHUNK, CHUNK)
        here = pl.ds(r0, CHUNK)
        live = (lax.broadcasted_iota(jnp.int32, (CHUNK, 1), 0) + r0) < count
        src = pl.ds(pl.multiple_of(off + r0, 16), CHUNK)
        new = []
        ngs, nrs = [], []
        for q in range(wq):
            a_ls, a_sc, a_sh = accs[3 * q:3 * q + 3]
            br = jnp.where(live, branch[src, lane(q)], 0.0)
            tk = jnp.where(live, tok[0, here, lane(q)].astype(F32), 0.0)
            both[0, 0, here, lane(q)] = (tk + gam[:, lane(q)] * br).astype(BF)
            g = jnp.where(live, ag[src, lane(q)], 0.0)
            nr = nrm[src, lane(q)].astype(F32)
            new += [a_ls + fold(cot[0, here, lane(q)].astype(F32) * br), a_sc + fold(g * nr), a_sh + fold(g)]
            ngs.append(g * scale[:, lane(q)])
            nrs.append(nr)
        cross = [a * b for a, b in zip(ngs, nrs)]
        m1 = jnp.sum(sum(ngs[1:], ngs[0]), axis=-1, keepdims=True) * (1.0 / width)
        m2 = jnp.sum(sum(cross[1:], cross[0]), axis=-1, keepdims=True) * (1.0 / width)
        istd = inv[src, :]
        for q in range(wq):
            cg = istd * (ngs[q] - m1 - nrs[q] * m2)
            cgp[q, pl.ds(pl.multiple_of(r0 + PAD, 8), CHUNK), :] = jnp.where(live, cg, 0.0)
        return tuple(new)

    accs = lax.fori_loop(0, steps, step, (zero,) * (3 * wq))
    for q in range(wq):
        sums[taps + 1, :, lane(q)] += accs[3 * q]
        sums[taps + 2 + group, :, lane(q)] += accs[3 * q + 1]
        sums[taps + 2 + rates + group, :, lane(q)] += accs[3 * q + 2]

    def clear(i, _):
        r0 = pl.multiple_of(i * CHUNK, CHUNK)
        here = pl.ds(r0, CHUNK)
        both[0, 0, here, :] = jnp.zeros((CHUNK, width), BF)
        both[1, 0, here, :] = jnp.zeros((CHUNK, width), BF)
        for q in range(wq):
            cgp[q, pl.ds(pl.multiple_of(r0 + PAD, 8), CHUNK), :] = jnp.zeros((CHUNK, LANES), F32)
        return 0

    lax.fori_loop(steps, frames // CHUNK, clear, 0)

    for q in range(wq):
        wl = w[:, lane(q)]

        def conv_step(i, accs):
            r0 = pl.multiple_of(i * CHUNK, CHUNK)
            here = pl.ds(r0, CHUNK)
            live = (lax.broadcasted_iota(jnp.int32, (CHUNK, 1), 0) + r0) < count
            tk = jnp.where(live, tok[0, here, lane(q)].astype(F32), 0.0)
            total = cot[0, here, lane(q)].astype(F32)
            new = []
            for k in range(taps):
                sh = cgp[q, pl.ds(r0 + (PAD + half - k), CHUNK), :]
                total = total + wl[k:k + 1] * sh
                new.append(accs[k] + fold(tk * sh))
                if k == half:
                    new_bias = accs[taps] + fold(sh)
            both[1, 0, here, lane(q)] = jnp.where(live, total, 0.0).astype(BF)
            return tuple(new) + (new_bias,)

        accs = lax.fori_loop(0, steps, conv_step, (zero,) * (taps + 1))
        for k in range(taps + 1):
            sums[k, :, lane(q)] += accs[k]

    @pl.when(pl.program_id(0) == pl.num_programs(0) - 1)
    def _():
        if not last_part:
            results[0][...] = sums[...]
            return
        small_keep, small_send = results
        last = taps + 2 + 2 * rates
        rows = [jnp.sum(sums[i], axis=0, keepdims=True) for i in range(last)]
        rows.append(jnp.sum(gbo[...], axis=0, keepdims=True))
        gb = jnp.sum(gbi[...], axis=0, keepdims=True)
        fill = jnp.zeros((1, width - h), F32)
        spare = [jnp.zeros((1, width), F32)] * (small_keep.shape[0] - last - 2)
        for side, dst in ((0, small_keep), (1, small_send)):
            tail = [jnp.concatenate([gb[:, side * h:(side + 1) * h], fill], axis=1)]
            dst[...] = jnp.concatenate(rows + tail + spare, axis=0)


def finish(meta, tok, cot, branch, ag, nrm, inv, sums, gbo, gbi, cw, ns, gamma, first, size):
    items, frames, width = tok.shape
    n = items // 2
    last_part = first + size == n
    wq = width // LANES
    taps, rates = cw.shape[0], ns.shape[0]
    n_small = -(-(taps + 4 + 2 * rates) // 8) * 8
    sums_shape = (taps + 2 + 2 * rates, 8, width)
    item = pl.BlockSpec((1, frames, width), lambda s, c: (c[0] * n + first + s, 0, 0))
    mine = pl.BlockSpec((2, 1, frames, width), lambda s, *_: (0, s, 0, 0))
    more = [(n_small, width)] * 2 if last_part else [sums_shape]
    if sums is None:
        sums = gbo
    return pl.pallas_call(
        functools.partial(finish_kernel, n, first, last_part),
        grid_spec=pltpu.PrefetchScalarGridSpec(
            num_scalar_prefetch=1, grid=(size,),
            in_specs=[item, item] + [vmem()] * 7 + [whole(v.shape) for v in (cw, ns, gamma)],
            out_specs=[mine] + [vmem()] * len(more),
            scratch_shapes=[pltpu.SMEM((n + 2,), jnp.int32),
                            pltpu.VMEM((wq, frames + 4 * PAD, LANES), F32),
                            pltpu.VMEM(sums_shape, F32)]),
        out_shape=[struct((2, size, frames, width), BF)] + [struct(v, F32) for v in more],
        compiler_params=params(), cost_estimate=cost(40000000),
    )(meta, tok, cot, branch, ag, nrm, inv, sums, gbo, gbi, cw, ns, gamma)


def merge_kernel(meta, mine, other, *rest):
    out, gtok = rest[-2:]
    for side, src in ((0, mine), (1, other)):
        @pl.when(pl.program_id(0) == side)
        def _():
            out[...] = src[0]
            gtok[...] = src[1].astype(F32)


def merge(meta, mine, other, into, n, first, step=2):
    _, size, frames, width = mine.shape
    blocks = size // step
    spec_a = pl.BlockSpec((2, step, frames, width), lambda side, s, c: (0, s * (1 - side) + (blocks - 1) * side, 0, 0))
    spec_b = pl.BlockSpec((2, step, frames, width), lambda side, s, c: (0, s * side, 0, 0))
    dst = pl.BlockSpec((step, frames, width), lambda side, s, c: (((c[0] ^ side) * n + first) // step + s, 0, 0))
    return pl.pallas_call(
        merge_kernel,
        grid_spec=pltpu.PrefetchScalarGridSpec(
            num_scalar_prefetch=1, grid=(2, blocks),
            in_specs=[spec_a, spec_b] + [pl.BlockSpec(memory_space=pl.ANY)] * len(into), out_specs=[dst, dst]),
        out_shape=[struct((2 * n, frames, width), BF), struct((2 * n, frames, width), F32)],
        input_output_aliases={3: 0, 4: 1} if into else {},
        compiler_params=params(), cost_estimate=cost(20000000),
    )(meta, mine, other, *into)


def put_small(small, dst, base):
    high = small.astype(BF)
    low = (small - high.astype(F32)).astype(BF)
    rows = small.shape[0]
    dst[base:base + rows, :] = high
    dst[base + rows:base + 2 * rows, :] = low


def get_small(src, base):
    rows = (src.shape[0] - base) // 2
    return src[base:base + rows, :].astype(F32) + src[base + rows:base + 2 * rows, :].astype(F32)


def message_kernel(stay, keep, recv, *refs):
    pieces, out = refs[:-1], refs[-1]
    m = pieces[0].shape[0]
    total = stay[:m, :]
    for piece in pieces:
        total = total + piece[...].astype(F32)
    out[:m, :] = total.astype(BF)
    small = keep[...] + recv[...]
    put_small(jnp.concatenate([small[:, lane(q)] for q in range(small.shape[1] // LANES)], axis=0), out, m)


def make_message(stay, keep, recv, pieces):
    rows = pieces[0].shape[0] + 2 * keep.size // LANES
    return pl.pallas_call(message_kernel, in_specs=[vmem()] * (3 + len(pieces)), out_specs=vmem(),
                          out_shape=struct((rows, LANES), BF), compiler_params=params())(stay, keep, recv, *pieces)


def relay_kernel(m, *refs):
    sources, out = refs[:-1], refs[-1]
    sums = []
    for d, src in enumerate(sources):
        out[d * m:(d + 1) * m, :] = src[:m, :]
        sums.append(get_small(src, m))
    while len(sums) > 1:
        sums = [a + b for a, b in zip(sums[::2], sums[1::2])]
    put_small(sums[0], out, len(sources) * m)


def relay(m, sources):
    rows = len(sources) * m + sources[0].shape[0] - m
    return pl.pallas_call(functools.partial(relay_kernel, m), in_specs=[vmem()] * len(sources), out_specs=vmem(),
                          out_shape=struct((rows, LANES), BF), compiler_params=params())(*sources)


def unpack_kernel(dp, taps, rates, meta, near, far, gcw, gcb, gns, gnsh, gwi, gbi, gwo, gbo, gls, full):
    h, width = gwo.shape
    wq, hq = width // LANES, h // LANES
    m = full.shape[0] // dp
    for odd, mess in ((0, near), (1, far)):
        for d in range(dp // 2):
            at = pl.multiple_of((meta[1] ^ (2 * d + odd)) * m, m)
            full[pl.ds(at, m), :] = mess[d * m:(d + 1) * m, :].astype(F32)
    for q in range(wq):
        gwo[:, lane(q)] = full[q * h:(q + 1) * h, :]
    base = wq * h
    for q in range(hq):
        gwi[:, lane(q)] = full[base + q * width:base + (q + 1) * width, :]
    small = get_small(near, dp // 2 * m) + get_small(far, dp // 2 * m)
    rows = small.shape[0] // wq
    small = jnp.concatenate([small[q * rows:(q + 1) * rows] for q in range(wq)], axis=1)
    gcw[...] = small[:taps]
    gcb[...] = small[taps]
    gls[...] = small[taps + 1]
    gns[...] = small[taps + 2:taps + 2 + rates]
    gnsh[...] = small[taps + 2 + rates:taps + 2 + 2 * rates]
    at = taps + 2 + 2 * rates
    gbo[...] = small[at]
    gbi[...] = small[at + 1, :h]


def unpack(meta, near, far, dp, taps, rates, width, h):
    shapes = [(taps, width), (width,), (rates, width), (rates, width), (width, h), (h,), (h, width), (width,), (width,)]
    return pl.pallas_call(
        functools.partial(unpack_kernel, dp, taps, rates), in_specs=[smem(), vmem(), vmem()],
        out_shape=[struct(s, F32) for s in shapes],
        scratch_shapes=[pltpu.VMEM((2 * width * h // LANES, LANES), F32)],
        compiler_params=params())(meta, near, far)


def swap(x, step):
    size = lax.axis_size("tp")
    return lax.ppermute(x, "tp", [(i, i ^ step) for i in range(size)])


def across(x, step):
    size = lax.axis_size("dp")
    return lax.ppermute(x, "dp", [(i, i ^ step) for i in range(size)])


def per_device(tokens, frame_counts, rate_groups, conv_weight, conv_bias, norm_scale, norm_shift,
               weight_in, bias_in, weight_out, bias_out, layer_scale, cotangent):
    width, h = weight_in.shape
    n = tokens.shape[0] // 2
    (tokens, cotangent, conv_weight, conv_bias, norm_scale, norm_shift, weight_in, bias_in, weight_out, bias_out,
     layer_scale) = [pltpu.with_memory_space_constraint(v, pltpu.HBM) for v in (
         tokens, cotangent, conv_weight, conv_bias, norm_scale, norm_shift, weight_in, bias_in, weight_out, bias_out,
         layer_scale)]
    taps, rates = conv_weight.shape[0], norm_scale.shape[0]
    dp = lax.axis_size("dp")
    place = jnp.stack([lax.axis_index("tp") & 1, lax.axis_index("dp")]).astype(jnp.int32)
    meta = jnp.concatenate([place, frame_counts, rate_groups])

    buf_a = pack(weight_in, bias_in, weight_out)
    buf_b = swap(buf_a, 1)
    buf_c = swap(buf_a, 2)
    buf_d = swap(buf_c, 1)
    ad, nrm, low, inv, gbo = conv_norm(meta, tokens, cotangent, conv_weight, conv_bias,
                                       norm_scale, norm_shift, layer_scale)
    act, pre, win, wout, keep, send, gbi = hidden(meta, ad, low, buf_a, buf_b, h, n)
    stay, leave = combine(meta, keep, swap(send, 1), dp)
    arrived = across(leave, 1)
    branch, ag = mix(meta, ad, low, act, pre, win, wout, bias_out, buf_c, buf_d, n)
    arrived, branch = lax.optimization_barrier((arrived, branch))
    stay = (stay + arrived.astype(F32)).reshape(dp // 2, -1, LANES)
    pieces = [across(stay[d].astype(BF), 2 * d) for d in range(1, dp // 2)]

    def finish_part(sums, branch, first):
        return finish(meta, tokens, cotangent, branch, ag, nrm, inv, sums,
                      gbo, gbi, conv_weight, norm_scale, layer_scale, first, n // 2)

    both_1, sums = finish_part(None, branch, 0)
    pieces, branch = lax.optimization_barrier((pieces, branch))
    both_2, small_keep, small_send = finish_part(sums, branch, n // 2)
    both_1, both_2 = lax.optimization_barrier((both_1, both_2))
    message = make_message(stay.reshape(-1, LANES), small_keep, swap(small_send, 1), pieces)
    near = [message] + [across(message, 2 * d) for d in range(1, dp // 2)]
    done = merge(meta, both_1, swap(both_1, 1), (), n, 0)
    near, done = lax.optimization_barrier((near, done))
    near = relay(pieces[0].shape[0], near)
    far = across(near, 1)
    out, gtok = merge(meta, both_2, swap(both_2, 1), done, n, n // 2)
    far, out, gtok = lax.optimization_barrier((far, out, gtok))
    gcw, gcb, gns, gnsh, gwi, gbi, gwo, gbo, gls = unpack(meta, near, far, dp, taps, rates, width, h)
    return (out, gtok, gcw, gcb, gns, gnsh, gwi, gbi, gwo, gbo, gls)


def solution(mesh):
    items, copied = P("dp", None, None), P()
    in_specs = (items, P("dp"), P("dp"), copied, copied, copied, copied, P(None, "tp"), P("tp"), P("tp", None),
                copied, copied, items)
    out_specs = (items, items, copied, copied, copied, copied, P(None, "tp"), P("tp"), P("tp", None), copied, copied)
    return jax.shard_map(per_device, mesh=mesh, in_specs=in_specs, out_specs=out_specs, check_vma=False)
```

```python
import functools

import jax
import jax.numpy as jnp
from jax import lax
from jax.experimental import pallas as pl
from jax.experimental.pallas import tpu as pltpu
from jax.sharding import PartitionSpec as P

EPS = 1e-06
BF, F32 = jnp.bfloat16, jnp.float32
TILE = 256
LANES = 128
PAD = 8
CHUNK = 64
VMEM_LIMIT = 12 * 1024 * 1024


def params(**more):
    return pltpu.CompilerParams(vmem_limit_bytes=VMEM_LIMIT, **more)


def struct(shape, dtype):
    return jax.ShapeDtypeStruct(shape, dtype)


def whole(shape):
    return pl.BlockSpec(shape, lambda *_: (0,) * len(shape))


def hbm():
    return pl.BlockSpec(memory_space=pltpu.HBM)


def smem():
    return pl.BlockSpec(memory_space=pltpu.SMEM)


def cost(size):
    return pl.CostEstimate(flops=0, transcendentals=0, bytes_accessed=size)


def vmem():
    return pl.BlockSpec(memory_space=pltpu.VMEM)


def lane(q):
    return slice(q * LANES, (q + 1) * LANES)


def fold(x):
    return jnp.sum(x.reshape(x.shape[0] // 8, 8, x.shape[1]), axis=0)


def pick(table, group):
    rows = table[...].astype(F32)
    value = rows[0:1]
    for r in range(1, rows.shape[0]):
        value = jnp.where(group == r, rows[r:r + 1], value)
    return value


def as_row(ref):
    return ref[...].astype(F32).reshape(1, -1)


def gelu_parts(pre):
    cdf = 0.5 + 0.5 * lax.erf(pre * 0.7071067811865476)
    density = jnp.exp(-0.5 * pre * pre) * 0.3989422804014327
    return pre * cdf, cdf + pre * density


def dot(a, b):
    return jnp.dot(a, b, preferred_element_type=F32)


def dot_t(a, b):
    return lax.dot_general(a, b, (((1,), (1,)), ((), ())), preferred_element_type=F32)


def dot_rows(a, b):
    return lax.dot_general(a, b, (((0,), (0,)), ((), ())), preferred_element_type=F32)


def place_items(n, meta, offs):
    end = jnp.int32(0)
    for j in range(n):
        offs[j] = end
        end = end + ((meta[2 + meta[0] * n + j] + 15) & -16)
    offs[n] = end
    offs[n + 1] = (end + TILE - 1) // TILE


def pack_kernel(wi, bi, wo, out):
    width, h = wi.shape
    hq, wq = h // LANES, width // LANES
    for q in range(hq):
        out[q * width:(q + 1) * width, :] = wi[:, lane(q)]
    base = hq * width
    for q in range(wq):
        out[base + q * h:base + (q + 1) * h, :] = wo[:, lane(q)]
    base += wq * h
    bias = bi[...].astype(F32).reshape(1, h)
    rows = [bias[:, lane(q)] for q in range(hq)] + [jnp.zeros((1, LANES), F32)] * (16 - hq)
    out[base:base + 16, :] = jnp.concatenate(rows, axis=0).astype(BF)


def pack(wi, bi, wo):
    rows = 2 * wi.size // LANES + 16
    return pl.pallas_call(pack_kernel, out_shape=struct((rows, LANES), BF),
                          compiler_params=params())(wi, bi, wo)


def weight_copies(buf, side, win, wout, bias, sems):
    width, h = win.shape[0], win.shape[1] // 2
    hq, wq = h // LANES, width // LANES
    copies = []
    for q in range(hq):
        at = side * h + q * LANES
        copies.append((buf.at[pl.ds(q * width, width), :], win.at[:, pl.ds(at, LANES)]))
    base = hq * width
    for q in range(wq):
        copies.append((buf.at[pl.ds(base + q * h, h), :], wout.at[pl.ds(side * h, h), pl.ds(q * LANES, LANES)]))
    copies.append((buf.at[pl.ds(base + wq * h, 16), :], bias.at[side]))
    return [pltpu.make_async_copy(src, dst, sems.at[side, i]) for i, (src, dst) in enumerate(copies)]


def spread_bias(bias, row):
    hq = row.shape[1] // LANES // 2
    for side in range(2):
        for q in range(hq):
            at = side * hq + q
            row[:, lane(at)] = bias[side, q:q + 1, :].astype(F32)


def conv_norm_kernel(n, meta, tok, cot, cw, cb, ns, nsh, gamma, ad, nrm, low, inv, gbo, offs, pad):
    s = pl.program_id(0)
    frames, width = tok.shape[1], tok.shape[2]
    taps = cw.shape[0]
    half = taps // 2
    wq = width // LANES

    @pl.when(s == 0)
    def _():
        place_items(n, meta, offs)
        gbo[...] = jnp.zeros_like(gbo)
        pad[...] = jnp.zeros_like(pad)

    item = meta[0] * n + s
    count = meta[2 + item]
    group = meta[2 + 2 * n + item]
    off = offs[s]
    rows = lax.broadcasted_iota(jnp.int32, (frames, 1), 0)
    for q in range(wq):
        pad[q, PAD:PAD + frames, :] = jnp.where(rows < count, tok[0, :, lane(q)].astype(F32), 0.0)
    scale, shift = pick(ns, group), pick(nsh, group)
    gam, conv_bias = as_row(gamma), as_row(cb)
    w = cw[...].astype(F32)

    def step(i, acc):
        r0 = pl.multiple_of(i * CHUNK, CHUNK)
        live = (lax.broadcasted_iota(jnp.int32, (CHUNK, 1), 0) + r0) < count
        convs = []
        for q in range(wq):
            conv = conv_bias[:, lane(q)]
            for k in range(taps):
                conv = conv + w[k:k + 1, lane(q)] * pad[q, pl.ds(r0 + (PAD - half + k), CHUNK), :]
            convs.append(conv)
        mean = jnp.sum(sum(convs[1:], convs[0]), axis=-1, keepdims=True) * (1.0 / width)
        cents = [c - mean for c in convs]
        sq = [c * c for c in cents]
        var = jnp.sum(sum(sq[1:], sq[0]), axis=-1, keepdims=True) * (1.0 / width)
        istd = lax.rsqrt(var + EPS)
        dst = pl.ds(pl.multiple_of(off + r0, 16), CHUNK)
        inv[dst, :] = jnp.broadcast_to(istd, (CHUNK, LANES))
        new = []
        for q in range(wq):
            normed = cents[q] * istd
            ad[dst, lane(q)] = (normed * scale[:, lane(q)] + shift[:, lane(q)]).astype(BF)
            nrm[dst, lane(q)] = normed.astype(BF)
            back = jnp.where(live, cot[0, pl.ds(r0, CHUNK), lane(q)].astype(F32), 0.0) * gam[:, lane(q)]
            low[dst, lane(q)] = back.astype(BF)
            new.append(acc[q] + fold(back))
        return tuple(new)

    accs = lax.fori_loop(0, pl.cdiv(count, CHUNK), step, (jnp.zeros((8, LANES), F32),) * wq)
    for q in range(wq):
        gbo[:, lane(q)] += accs[q]

    @pl.when(s == n - 1)
    def _():
        end = pl.ds(pl.multiple_of(offs[n], 16), TILE)
        ad[end, :] = jnp.zeros((TILE, width), BF)
        low[end, :] = jnp.zeros((TILE, width), BF)


def conv_norm(meta, tok, cot, cw, cb, ns, nsh, gamma):
    items, frames, width = tok.shape
    n = items // 2
    rows = n * frames + TILE
    item = pl.BlockSpec((1, frames, width), lambda s, c: (c[0] * n + s, 0, 0))
    return pl.pallas_call(
        functools.partial(conv_norm_kernel, n),
        grid_spec=pltpu.PrefetchScalarGridSpec(
            num_scalar_prefetch=1, grid=(n,),
            in_specs=[item, item] + [whole(v.shape) for v in (cw, cb, ns, nsh, gamma)],
            out_specs=[vmem()] * 5,
            scratch_shapes=[pltpu.SMEM((n + 2,), jnp.int32),
                            pltpu.VMEM((width // LANES, frames + 4 * PAD, LANES), F32)]),
        out_shape=[struct((rows, width), BF)] * 3 + [struct((rows, LANES), F32), struct((8, width), F32)],
        compiler_params=params(), cost_estimate=cost(0),
    )(meta, tok, cot, cw, cb, ns, nsh, gamma)


def hidden_kernel(n, meta, ad, low, buf_a, buf_b, act, pre, win, wout, keep, send, gbi,
                  offs, bias, bias_row, dwo, dwi, sems):
    width, h = win.shape[0], win.shape[1] // 2
    wq = width // LANES
    copies = weight_copies(buf_a, 0, win, wout, bias, sems) + weight_copies(buf_b, 1, win, wout, bias, sems)
    for c in copies:
        c.start()
    place_items(n, meta, offs)
    dwo[...] = jnp.zeros_like(dwo)
    dwi[...] = jnp.zeros_like(dwi)
    gbi[...] = jnp.zeros_like(gbi)
    for c in copies:
        c.wait()
    spread_bias(bias, bias_row)

    def tile(t, _):
        at = pl.ds(pl.multiple_of(t * TILE, TILE), TILE)
        a, b = ad[at, :], low[at, :]
        activation, slope = gelu_parts(dot(a, win[...]) + bias_row[...])
        grad = dot_t(b, wout[...]) * slope
        lo = activation.astype(BF)
        act[at, :] = lo
        dwo[...] += dot_rows(lo, b)
        gbi[...] += fold(grad)
        g = grad.astype(BF)
        pre[at, :] = g
        dwi[...] += dot_rows(a, g)
        return 0

    lax.fori_loop(0, offs[n + 1], tile, 0)
    for side, dst in ((0, keep), (1, send)):
        for q in range(wq):
            dst[q * h:(q + 1) * h, :] = dwo[side * h:(side + 1) * h, lane(q)].astype(dst.dtype)
        base = wq * h
        for q in range(h // LANES):
            dst[base + q * width:base + (q + 1) * width, :] = dwi[:, lane(side * (h // LANES) + q)].astype(dst.dtype)


def hidden(meta, ad, low, buf_a, buf_b, h, n):
    rows, width = ad.shape
    packed = 2 * width * h // LANES
    wq, hq = width // LANES, h // LANES
    return pl.pallas_call(
        functools.partial(hidden_kernel, n),
        in_specs=[smem(), vmem(), vmem(), hbm(), hbm()],
        out_specs=[vmem()] * 7,
        scratch_shapes=[pltpu.SMEM((n + 2,), jnp.int32),
                        pltpu.VMEM((2, 16, LANES), BF), pltpu.VMEM((1, 2 * h), F32),
                        pltpu.VMEM((2 * h, width), F32), pltpu.VMEM((width, 2 * h), F32),
                        pltpu.SemaphoreType.DMA((2, hq + wq + 1))],
        out_shape=[struct((rows, 2 * h), BF)] * 2 + [struct((width, 2 * h), BF), struct((2 * h, width), BF)]
        + [struct((packed, LANES), F32), struct((packed, LANES), BF), struct((8, 2 * h), F32)],
        compiler_params=params(), cost_estimate=cost(0),
    )(meta, ad, low, buf_a, buf_b)


def combine_kernel(dp, meta, keep, recv, stay, leave):
    m = keep.shape[0] // dp
    for d in range(dp):
        src = pl.ds(pl.multiple_of((meta[1] ^ d) * m, m), m)
        total = keep[src, :] + recv[src, :].astype(F32)
        dst = leave if d % 2 else stay
        dst[d // 2 * m:(d // 2 + 1) * m, :] = total.astype(dst.dtype)


def combine(meta, keep, recv, dp):
    rows = keep.shape[0] // 2
    return pl.pallas_call(
        functools.partial(combine_kernel, dp),
        in_specs=[smem(), vmem(), vmem()], out_specs=[vmem(), vmem()],
        out_shape=[struct((rows, LANES), F32), struct((rows, LANES), BF)],
        compiler_params=params())(meta, keep, recv)


def mix_kernel(n, meta, ad, low, act, pre, win1, wout1, bout, buf_c, buf_d, branch, ag,
               offs, win2, wout2, bias, bias_row, sems):
    copies = weight_copies(buf_c, 0, win2, wout2, bias, sems) + weight_copies(buf_d, 1, win2, wout2, bias, sems)
    for c in copies:
        c.start()
    place_items(n, meta, offs)
    for c in copies:
        c.wait()
    spread_bias(bias, bias_row)

    def tile(t, _):
        at = pl.ds(pl.multiple_of(t * TILE, TILE), TILE)
        a, b = ad[at, :], low[at, :]
        activation, slope = gelu_parts(dot(a, win2[...]) + bias_row[...])
        grad = dot_t(b, wout2[...]) * slope
        branch[at, :] = (dot(act[at, :], wout1[...]) + dot(activation.astype(BF), wout2[...])) + as_row(bout)
        ag[at, :] = dot_t(pre[at, :], win1[...]) + dot_t(grad.astype(BF), win2[...])
        return 0

    lax.fori_loop(0, offs[n + 1], tile, 0)


def mix(meta, ad, low, act, pre, win, wout, bout, buf_c, buf_d, n):
    rows, width = ad.shape
    h = act.shape[1] // 2
    wq, hq = width // LANES, h // LANES
    return pl.pallas_call(
        functools.partial(mix_kernel, n),
        in_specs=[smem()] + [vmem()] * 6 + [whole(bout.shape)] + [hbm()] * 2,
        out_specs=[vmem(), vmem()],
        scratch_shapes=[pltpu.SMEM((n + 2,), jnp.int32),
                        pltpu.VMEM((width, 2 * h), BF), pltpu.VMEM((2 * h, width), BF),
                        pltpu.VMEM((2, 16, LANES), BF), pltpu.VMEM((1, 2 * h), F32),
                        pltpu.SemaphoreType.DMA((2, hq + wq + 1))],
        out_shape=[struct((rows, width), F32)] * 2,
        compiler_params=params(), cost_estimate=cost(0),
    )(meta, ad, low, act, pre, win, wout, bout, buf_c, buf_d)


def finish_kernel(n, first, last_part, meta, tok, cot, branch, ag, nrm, inv, sums_in, gbo, gbi, cw, ns,
                  gamma, both, *rest):
    results, (offs, cgp, sums) = rest[:-3], rest[-3:]
    s = pl.program_id(0) + first
    frames, width = tok.shape[1], tok.shape[2]
    taps, rates = cw.shape[0], ns.shape[0]
    half = taps // 2
    wq = width // LANES
    h = gbi.shape[1] // 2

    @pl.when(s == first)
    def _():
        place_items(n, meta, offs)
        sums[...] = sums_in[...] if last_part else jnp.zeros_like(sums)
        cgp[...] = jnp.zeros_like(cgp)

    item = meta[0] * n + s
    count = meta[2 + item]
    group = meta[2 + 2 * n + item]
    off = offs[s]
    scale = pick(ns, group)
    gam = as_row(gamma)
    w = cw[...].astype(F32)
    zero = jnp.zeros((8, LANES), F32)
    steps = pl.cdiv(count, CHUNK)

    def step(i, accs):
        r0 = pl.multiple_of(i * CHUNK, CHUNK)
        here = pl.ds(r0, CHUNK)
        live = (lax.broadcasted_iota(jnp.int32, (CHUNK, 1), 0) + r0) < count
        src = pl.ds(pl.multiple_of(off + r0, 16), CHUNK)
        new = []
        ngs, nrs = [], []
        for q in range(wq):
            a_ls, a_sc, a_sh = accs[3 * q:3 * q + 3]
            br = jnp.where(live, branch[src, lane(q)], 0.0)
            tk = jnp.where(live, tok[0, here, lane(q)].astype(F32), 0.0)
            both[0, 0, here, lane(q)] = (tk + gam[:, lane(q)] * br).astype(BF)
            g = jnp.where(live, ag[src, lane(q)], 0.0)
            nr = nrm[src, lane(q)].astype(F32)
            new += [a_ls + fold(cot[0, here, lane(q)].astype(F32) * br), a_sc + fold(g * nr), a_sh + fold(g)]
            ngs.append(g * scale[:, lane(q)])
            nrs.append(nr)
        cross = [a * b for a, b in zip(ngs, nrs)]
        m1 = jnp.sum(sum(ngs[1:], ngs[0]), axis=-1, keepdims=True) * (1.0 / width)
        m2 = jnp.sum(sum(cross[1:], cross[0]), axis=-1, keepdims=True) * (1.0 / width)
        istd = inv[src, :]
        for q in range(wq):
            cg = istd * (ngs[q] - m1 - nrs[q] * m2)
            cgp[q, pl.ds(pl.multiple_of(r0 + PAD, 8), CHUNK), :] = jnp.where(live, cg, 0.0)
        return tuple(new)

    accs = lax.fori_loop(0, steps, step, (zero,) * (3 * wq))
    for q in range(wq):
        sums[taps + 1, :, lane(q)] += accs[3 * q]
        sums[taps + 2 + group, :, lane(q)] += accs[3 * q + 1]
        sums[taps + 2 + rates + group, :, lane(q)] += accs[3 * q + 2]

    def clear(i, _):
        r0 = pl.multiple_of(i * CHUNK, CHUNK)
        here = pl.ds(r0, CHUNK)
        both[0, 0, here, :] = jnp.zeros((CHUNK, width), BF)
        both[1, 0, here, :] = jnp.zeros((CHUNK, width), BF)
        for q in range(wq):
            cgp[q, pl.ds(pl.multiple_of(r0 + PAD, 8), CHUNK), :] = jnp.zeros((CHUNK, LANES), F32)
        return 0

    lax.fori_loop(steps, frames // CHUNK, clear, 0)

    for q in range(wq):
        wl = w[:, lane(q)]

        def conv_step(i, accs):
            r0 = pl.multiple_of(i * CHUNK, CHUNK)
            here = pl.ds(r0, CHUNK)
            live = (lax.broadcasted_iota(jnp.int32, (CHUNK, 1), 0) + r0) < count
            tk = jnp.where(live, tok[0, here, lane(q)].astype(F32), 0.0)
            total = cot[0, here, lane(q)].astype(F32)
            new = []
            for k in range(taps):
                sh = cgp[q, pl.ds(r0 + (PAD + half - k), CHUNK), :]
                total = total + wl[k:k + 1] * sh
                new.append(accs[k] + fold(tk * sh))
                if k == half:
                    new_bias = accs[taps] + fold(sh)
            both[1, 0, here, lane(q)] = jnp.where(live, total, 0.0).astype(BF)
            return tuple(new) + (new_bias,)

        accs = lax.fori_loop(0, steps, conv_step, (zero,) * (taps + 1))
        for k in range(taps + 1):
            sums[k, :, lane(q)] += accs[k]

    @pl.when(pl.program_id(0) == pl.num_programs(0) - 1)
    def _():
        if not last_part:
            results[0][...] = sums[...]
            return
        small_keep, small_send = results
        last = taps + 2 + 2 * rates
        rows = [jnp.sum(sums[i], axis=0, keepdims=True) for i in range(last)]
        rows.append(jnp.sum(gbo[...], axis=0, keepdims=True))
        gb = jnp.sum(gbi[...], axis=0, keepdims=True)
        fill = jnp.zeros((1, width - h), F32)
        spare = [jnp.zeros((1, width), F32)] * (small_keep.shape[0] - last - 2)
        for side, dst in ((0, small_keep), (1, small_send)):
            tail = [jnp.concatenate([gb[:, side * h:(side + 1) * h], fill], axis=1)]
            dst[...] = jnp.concatenate(rows + tail + spare, axis=0)


def finish(meta, tok, cot, branch, ag, nrm, inv, sums, gbo, gbi, cw, ns, gamma, first, size):
    items, frames, width = tok.shape
    n = items // 2
    last_part = first + size == n
    wq = width // LANES
    taps, rates = cw.shape[0], ns.shape[0]
    n_small = -(-(taps + 4 + 2 * rates) // 8) * 8
    sums_shape = (taps + 2 + 2 * rates, 8, width)
    item = pl.BlockSpec((1, frames, width), lambda s, c: (c[0] * n + first + s, 0, 0))
    mine = pl.BlockSpec((2, 1, frames, width), lambda s, *_: (0, s, 0, 0))
    more = [(n_small, width)] * 2 if last_part else [sums_shape]
    if sums is None:
        sums = gbo
    return pl.pallas_call(
        functools.partial(finish_kernel, n, first, last_part),
        grid_spec=pltpu.PrefetchScalarGridSpec(
            num_scalar_prefetch=1, grid=(size,),
            in_specs=[item, item] + [vmem()] * 7 + [whole(v.shape) for v in (cw, ns, gamma)],
            out_specs=[mine] + [vmem()] * len(more),
            scratch_shapes=[pltpu.SMEM((n + 2,), jnp.int32),
                            pltpu.VMEM((wq, frames + 4 * PAD, LANES), F32),
                            pltpu.VMEM(sums_shape, F32)]),
        out_shape=[struct((2, size, frames, width), BF)] + [struct(v, F32) for v in more],
        compiler_params=params(), cost_estimate=cost(40000000),
    )(meta, tok, cot, branch, ag, nrm, inv, sums, gbo, gbi, cw, ns, gamma)


def merge_kernel(meta, mine, other, *rest):
    out, gtok = rest[-2:]
    for side, src in ((0, mine), (1, other)):
        @pl.when(pl.program_id(0) == side)
        def _():
            out[...] = src[0]
            gtok[...] = src[1].astype(F32)


def merge(meta, mine, other, into, n, first, step=2):
    _, size, frames, width = mine.shape
    blocks = size // step
    spec_a = pl.BlockSpec((2, step, frames, width), lambda side, s, c: (0, s * (1 - side) + (blocks - 1) * side, 0, 0))
    spec_b = pl.BlockSpec((2, step, frames, width), lambda side, s, c: (0, s * side, 0, 0))
    dst = pl.BlockSpec((step, frames, width), lambda side, s, c: (((c[0] ^ side) * n + first) // step + s, 0, 0))
    return pl.pallas_call(
        merge_kernel,
        grid_spec=pltpu.PrefetchScalarGridSpec(
            num_scalar_prefetch=1, grid=(2, blocks),
            in_specs=[spec_a, spec_b] + [pl.BlockSpec(memory_space=pl.ANY)] * len(into), out_specs=[dst, dst]),
        out_shape=[struct((2 * n, frames, width), BF), struct((2 * n, frames, width), F32)],
        input_output_aliases={3: 0, 4: 1} if into else {},
        compiler_params=params(), cost_estimate=cost(20000000),
    )(meta, mine, other, *into)


def shard_kernel(stay, *refs):
    pieces, out = refs[:-1], refs[-1]
    total = stay[:out.shape[0], :]
    for piece in pieces:
        total = total + piece[...].astype(F32)
    out[...] = total.astype(BF)


def make_shard(stay, pieces):
    return pl.pallas_call(shard_kernel, in_specs=[vmem()] * (1 + len(pieces)), out_specs=vmem(),
                          out_shape=struct(pieces[0].shape, BF), compiler_params=params())(stay, *pieces)


def relay_kernel(*refs):
    sources, out = refs[:-1], refs[-1]
    m = sources[0].shape[0]
    for d, src in enumerate(sources):
        out[d * m:(d + 1) * m, :] = src[...]


def relay(sources):
    m = sources[0].shape[0]
    return pl.pallas_call(relay_kernel, in_specs=[vmem()] * len(sources), out_specs=vmem(),
                          out_shape=struct((len(sources) * m, LANES), BF), compiler_params=params())(*sources)


def unpack_kernel(dp, taps, rates, meta, near, far, small, gcw, gcb, gns, gnsh, gwi, gbi, gwo, gbo, gls, full):
    h, width = gwo.shape
    wq, hq = width // LANES, h // LANES
    m = full.shape[0] // dp
    for odd, mess in ((0, near), (1, far)):
        for d in range(dp // 2):
            at = pl.multiple_of((meta[1] ^ (2 * d + odd)) * m, m)
            full[pl.ds(at, m), :] = mess[d * m:(d + 1) * m, :].astype(F32)
    for q in range(wq):
        gwo[:, lane(q)] = full[q * h:(q + 1) * h, :]
    base = wq * h
    for q in range(hq):
        gwi[:, lane(q)] = full[base + q * width:base + (q + 1) * width, :]
    gcw[...] = small[:taps]
    gcb[...] = small[taps]
    gls[...] = small[taps + 1]
    gns[...] = small[taps + 2:taps + 2 + rates]
    gnsh[...] = small[taps + 2 + rates:taps + 2 + 2 * rates]
    at = taps + 2 + 2 * rates
    gbo[...] = small[at]
    gbi[...] = small[at + 1, :h]


def unpack(meta, near, far, small, dp, taps, rates, width, h):
    shapes = [(taps, width), (width,), (rates, width), (rates, width), (width, h), (h,), (h, width), (width,), (width,)]
    return pl.pallas_call(
        functools.partial(unpack_kernel, dp, taps, rates), in_specs=[smem(), vmem(), vmem(), vmem()],
        out_shape=[struct(s, F32) for s in shapes],
        scratch_shapes=[pltpu.VMEM((2 * width * h // LANES, LANES), F32)],
        compiler_params=params())(meta, near, far, small)


def swap(x, step):
    size = lax.axis_size("tp")
    return lax.ppermute(x, "tp", [(i, i ^ step) for i in range(size)])


def across(x, step):
    size = lax.axis_size("dp")
    return lax.ppermute(x, "dp", [(i, i ^ step) for i in range(size)])


def per_device(tokens, frame_counts, rate_groups, conv_weight, conv_bias, norm_scale, norm_shift,
               weight_in, bias_in, weight_out, bias_out, layer_scale, cotangent):
    width, h = weight_in.shape
    n = tokens.shape[0] // 2
    (tokens, cotangent, conv_weight, conv_bias, norm_scale, norm_shift, weight_in, bias_in, weight_out, bias_out,
     layer_scale) = [pltpu.with_memory_space_constraint(v, pltpu.HBM) for v in (
         tokens, cotangent, conv_weight, conv_bias, norm_scale, norm_shift, weight_in, bias_in, weight_out, bias_out,
         layer_scale)]
    taps, rates = conv_weight.shape[0], norm_scale.shape[0]
    dp = lax.axis_size("dp")
    place = jnp.stack([lax.axis_index("tp") & 1, lax.axis_index("dp")]).astype(jnp.int32)
    meta = jnp.concatenate([place, frame_counts, rate_groups])

    buf_a = pack(weight_in, bias_in, weight_out)
    buf_b = swap(buf_a, 1)
    buf_c = swap(buf_a, 2)
    buf_d = swap(buf_c, 1)
    ad, nrm, low, inv, gbo = conv_norm(meta, tokens, cotangent, conv_weight, conv_bias,
                                       norm_scale, norm_shift, layer_scale)
    act, pre, win, wout, keep, send, gbi = hidden(meta, ad, low, buf_a, buf_b, h, n)
    stay, leave = combine(meta, keep, swap(send, 1), dp)
    arrived = across(leave, 1)
    branch, ag = mix(meta, ad, low, act, pre, win, wout, bias_out, buf_c, buf_d, n)
    arrived, branch = lax.optimization_barrier((arrived, branch))
    stay = (stay + arrived.astype(F32)).reshape(dp // 2, -1, LANES)
    pieces = [across(stay[d].astype(BF), 2 * d) for d in range(1, dp // 2)]

    def finish_part(sums, branch, first):
        return finish(meta, tokens, cotangent, branch, ag, nrm, inv, sums,
                      gbo, gbi, conv_weight, norm_scale, layer_scale, first, n // 2)

    both_1, sums = finish_part(None, branch, 0)
    pieces, sums, branch = lax.optimization_barrier((pieces, sums, branch))
    both_2, small_keep, small_send = finish_part(sums, branch, n // 2)
    shard = make_shard(stay.reshape(-1, LANES), pieces)
    near = [shard] + [across(shard, 2 * d) for d in range(1, dp // 2)]
    near, small_send, both_1, both_2 = lax.optimization_barrier((near, small_send, both_1, both_2))
    small_got = swap(small_send, 1)
    small_got, both_1, both_2 = lax.optimization_barrier((small_got, both_1, both_2))
    near = relay(near)
    far = across(near, 1)
    small = small_keep + small_got
    for i in range(dp.bit_length() - 1):
        small = small + across(small, 1 << i)
    done = merge(meta, both_1, swap(both_1, 1), (), n, 0)
    out, gtok = merge(meta, both_2, swap(both_2, 1), done, n, n // 2)
    far, out, gtok = lax.optimization_barrier((far, out, gtok))
    gcw, gcb, gns, gnsh, gwi, gbi, gwo, gbo, gls = unpack(meta, near, far, small, dp, taps, rates, width, h)
    return (out, gtok, gcw, gcb, gns, gnsh, gwi, gbi, gwo, gbo, gls)


def solution(mesh):
    items, copied = P("dp", None, None), P()
    in_specs = (items, P("dp"), P("dp"), copied, copied, copied, copied, P(None, "tp"), P("tp"), P("tp", None),
                copied, copied, items)
    out_specs = (items, items, copied, copied, copied, copied, P(None, "tp"), P("tp"), P("tp", None), copied, copied)
    return jax.shard_map(per_device, mesh=mesh, in_specs=in_specs, out_specs=out_specs, check_vma=False)
```

```python
import functools

import jax
import jax.numpy as jnp
from jax import lax
from jax.experimental import pallas as pl
from jax.experimental.pallas import tpu as pltpu
from jax.sharding import PartitionSpec as P

EPS = 1e-06
BF, F32 = jnp.bfloat16, jnp.float32
TILE = 256
LANES = 128
PAD = 8
CHUNK = 64
VMEM_LIMIT = 12 * 1024 * 1024


def params(**more):
    return pltpu.CompilerParams(vmem_limit_bytes=VMEM_LIMIT, **more)


def struct(shape, dtype):
    return jax.ShapeDtypeStruct(shape, dtype)


def whole(shape):
    return pl.BlockSpec(shape, lambda *_: (0,) * len(shape))


def hbm():
    return pl.BlockSpec(memory_space=pltpu.HBM)


def smem():
    return pl.BlockSpec(memory_space=pltpu.SMEM)


def cost(size):
    return pl.CostEstimate(flops=0, transcendentals=0, bytes_accessed=size)


def vmem():
    return pl.BlockSpec(memory_space=pltpu.VMEM)


def lane(q):
    return slice(q * LANES, (q + 1) * LANES)


def fold(x):
    return jnp.sum(x.reshape(x.shape[0] // 8, 8, x.shape[1]), axis=0)


def pick(table, group):
    rows = table[...].astype(F32)
    value = rows[0:1]
    for r in range(1, rows.shape[0]):
        value = jnp.where(group == r, rows[r:r + 1], value)
    return value


def as_row(ref):
    return ref[...].astype(F32).reshape(1, -1)


def gelu_parts(pre):
    cdf = 0.5 + 0.5 * lax.erf(pre * 0.7071067811865476)
    density = jnp.exp(-0.5 * pre * pre) * 0.3989422804014327
    return pre * cdf, cdf + pre * density


def dot(a, b):
    return jnp.dot(a, b, preferred_element_type=F32)


def dot_t(a, b):
    return lax.dot_general(a, b, (((1,), (1,)), ((), ())), preferred_element_type=F32)


def dot_rows(a, b):
    return lax.dot_general(a, b, (((0,), (0,)), ((), ())), preferred_element_type=F32)


def place_items(n, meta, offs):
    end = jnp.int32(0)
    for j in range(n):
        offs[j] = end
        end = end + ((meta[2 + meta[0] * n + j] + 15) & -16)
    offs[n] = end
    offs[n + 1] = (end + TILE - 1) // TILE


def pack_kernel(wi, bi, wo, out):
    width, h = wi.shape
    hq, wq = h // LANES, width // LANES
    for q in range(hq):
        out[q * width:(q + 1) * width, :] = wi[:, lane(q)]
    base = hq * width
    for q in range(wq):
        out[base + q * h:base + (q + 1) * h, :] = wo[:, lane(q)]
    base += wq * h
    bias = bi[...].astype(F32).reshape(1, h)
    rows = [bias[:, lane(q)] for q in range(hq)] + [jnp.zeros((1, LANES), F32)] * (16 - hq)
    out[base:base + 16, :] = jnp.concatenate(rows, axis=0).astype(BF)


def pack(wi, bi, wo):
    rows = 2 * wi.size // LANES + 16
    return pl.pallas_call(pack_kernel, out_shape=struct((rows, LANES), BF),
                          compiler_params=params())(wi, bi, wo)


def weight_copies(buf, side, win, wout, bias, sems):
    width, h = win.shape[0], win.shape[1] // 2
    hq, wq = h // LANES, width // LANES
    copies = []
    for q in range(hq):
        at = side * h + q * LANES
        copies.append((buf.at[pl.ds(q * width, width), :], win.at[:, pl.ds(at, LANES)]))
    base = hq * width
    for q in range(wq):
        copies.append((buf.at[pl.ds(base + q * h, h), :], wout.at[pl.ds(side * h, h), pl.ds(q * LANES, LANES)]))
    copies.append((buf.at[pl.ds(base + wq * h, 16), :], bias.at[side]))
    return [pltpu.make_async_copy(src, dst, sems.at[side, i]) for i, (src, dst) in enumerate(copies)]


def spread_bias(bias, row):
    hq = row.shape[1] // LANES // 2
    for side in range(2):
        for q in range(hq):
            at = side * hq + q
            row[:, lane(at)] = bias[side, q:q + 1, :].astype(F32)


def conv_norm_kernel(n, meta, tok, cot, cw, cb, ns, nsh, gamma, ad, nrm, low, inv, gbo, offs, pad):
    s = pl.program_id(0)
    frames, width = tok.shape[1], tok.shape[2]
    taps = cw.shape[0]
    half = taps // 2
    wq = width // LANES

    @pl.when(s == 0)
    def _():
        place_items(n, meta, offs)
        gbo[...] = jnp.zeros_like(gbo)
        pad[...] = jnp.zeros_like(pad)

    item = meta[0] * n + s
    count = meta[2 + item]
    group = meta[2 + 2 * n + item]
    off = offs[s]
    rows = lax.broadcasted_iota(jnp.int32, (frames, 1), 0)
    for q in range(wq):
        pad[q, PAD:PAD + frames, :] = jnp.where(rows < count, tok[0, :, lane(q)].astype(F32), 0.0)
    scale, shift = pick(ns, group), pick(nsh, group)
    gam, conv_bias = as_row(gamma), as_row(cb)
    w = cw[...].astype(F32)

    def step(i, acc):
        r0 = pl.multiple_of(i * CHUNK, CHUNK)
        live = (lax.broadcasted_iota(jnp.int32, (CHUNK, 1), 0) + r0) < count
        convs = []
        for q in range(wq):
            conv = conv_bias[:, lane(q)]
            for k in range(taps):
                conv = conv + w[k:k + 1, lane(q)] * pad[q, pl.ds(r0 + (PAD - half + k), CHUNK), :]
            convs.append(conv)
        mean = jnp.sum(sum(convs[1:], convs[0]), axis=-1, keepdims=True) * (1.0 / width)
        cents = [c - mean for c in convs]
        sq = [c * c for c in cents]
        var = jnp.sum(sum(sq[1:], sq[0]), axis=-1, keepdims=True) * (1.0 / width)
        istd = lax.rsqrt(var + EPS)
        dst = pl.ds(pl.multiple_of(off + r0, 16), CHUNK)
        inv[dst, :] = jnp.broadcast_to(istd, (CHUNK, LANES))
        new = []
        for q in range(wq):
            normed = cents[q] * istd
            ad[dst, lane(q)] = (normed * scale[:, lane(q)] + shift[:, lane(q)]).astype(BF)
            nrm[dst, lane(q)] = normed.astype(BF)
            back = jnp.where(live, cot[0, pl.ds(r0, CHUNK), lane(q)].astype(F32), 0.0) * gam[:, lane(q)]
            low[dst, lane(q)] = back.astype(BF)
            new.append(acc[q] + fold(back))
        return tuple(new)

    accs = lax.fori_loop(0, pl.cdiv(count, CHUNK), step, (jnp.zeros((8, LANES), F32),) * wq)
    for q in range(wq):
        gbo[:, lane(q)] += accs[q]

    @pl.when(s == n - 1)
    def _():
        end = pl.ds(pl.multiple_of(offs[n], 16), TILE)
        ad[end, :] = jnp.zeros((TILE, width), BF)
        low[end, :] = jnp.zeros((TILE, width), BF)


def conv_norm(meta, tok, cot, cw, cb, ns, nsh, gamma):
    items, frames, width = tok.shape
    n = items // 2
    rows = n * frames + TILE
    item = pl.BlockSpec((1, frames, width), lambda s, c: (c[0] * n + s, 0, 0))
    return pl.pallas_call(
        functools.partial(conv_norm_kernel, n),
        grid_spec=pltpu.PrefetchScalarGridSpec(
            num_scalar_prefetch=1, grid=(n,),
            in_specs=[item, item] + [whole(v.shape) for v in (cw, cb, ns, nsh, gamma)],
            out_specs=[vmem()] * 5,
            scratch_shapes=[pltpu.SMEM((n + 2,), jnp.int32),
                            pltpu.VMEM((width // LANES, frames + 4 * PAD, LANES), F32)]),
        out_shape=[struct((rows, width), BF)] * 3 + [struct((rows, LANES), F32), struct((8, width), F32)],
        compiler_params=params(), cost_estimate=cost(0),
    )(meta, tok, cot, cw, cb, ns, nsh, gamma)


def hidden_kernel(n, meta, ad, low, buf_a, buf_b, act, pre, win, wout, keep, send, gbi,
                  offs, bias, bias_row, dwo, dwi, sems):
    width, h = win.shape[0], win.shape[1] // 2
    wq = width // LANES
    copies = weight_copies(buf_a, 0, win, wout, bias, sems) + weight_copies(buf_b, 1, win, wout, bias, sems)
    for c in copies:
        c.start()
    place_items(n, meta, offs)
    dwo[...] = jnp.zeros_like(dwo)
    dwi[...] = jnp.zeros_like(dwi)
    gbi[...] = jnp.zeros_like(gbi)
    for c in copies:
        c.wait()
    spread_bias(bias, bias_row)

    def tile(t, _):
        at = pl.ds(pl.multiple_of(t * TILE, TILE), TILE)
        a, b = ad[at, :], low[at, :]
        activation, slope = gelu_parts(dot(a, win[...]) + bias_row[...])
        grad = dot_t(b, wout[...]) * slope
        lo = activation.astype(BF)
        act[at, :] = lo
        dwo[...] += dot_rows(lo, b)
        gbi[...] += fold(grad)
        g = grad.astype(BF)
        pre[at, :] = g
        dwi[...] += dot_rows(a, g)
        return 0

    lax.fori_loop(0, offs[n + 1], tile, 0)
    for side, dst in ((0, keep), (1, send)):
        for q in range(wq):
            dst[q * h:(q + 1) * h, :] = dwo[side * h:(side + 1) * h, lane(q)].astype(dst.dtype)
        base = wq * h
        for q in range(h // LANES):
            dst[base + q * width:base + (q + 1) * width, :] = dwi[:, lane(side * (h // LANES) + q)].astype(dst.dtype)


def hidden(meta, ad, low, buf_a, buf_b, h, n):
    rows, width = ad.shape
    packed = 2 * width * h // LANES
    wq, hq = width // LANES, h // LANES
    return pl.pallas_call(
        functools.partial(hidden_kernel, n),
        in_specs=[smem(), vmem(), vmem(), hbm(), hbm()],
        out_specs=[vmem()] * 7,
        scratch_shapes=[pltpu.SMEM((n + 2,), jnp.int32),
                        pltpu.VMEM((2, 16, LANES), BF), pltpu.VMEM((1, 2 * h), F32),
                        pltpu.VMEM((2 * h, width), F32), pltpu.VMEM((width, 2 * h), F32),
                        pltpu.SemaphoreType.DMA((2, hq + wq + 1))],
        out_shape=[struct((rows, 2 * h), BF)] * 2 + [struct((width, 2 * h), BF), struct((2 * h, width), BF)]
        + [struct((packed, LANES), F32), struct((packed, LANES), BF), struct((8, 2 * h), F32)],
        compiler_params=params(), cost_estimate=cost(0),
    )(meta, ad, low, buf_a, buf_b)


def combine_kernel(dp, meta, keep, recv, stay, leave):
    m = keep.shape[0] // dp
    for d in range(dp):
        src = pl.ds(pl.multiple_of((meta[1] ^ d) * m, m), m)
        total = keep[src, :] + recv[src, :].astype(F32)
        dst = leave if d % 2 else stay
        dst[d // 2 * m:(d // 2 + 1) * m, :] = total.astype(dst.dtype)


def combine(meta, keep, recv, dp):
    rows = keep.shape[0] // 2
    return pl.pallas_call(
        functools.partial(combine_kernel, dp),
        in_specs=[smem(), vmem(), vmem()], out_specs=[vmem(), vmem()],
        out_shape=[struct((rows, LANES), F32), struct((rows, LANES), BF)],
        compiler_params=params())(meta, keep, recv)


def mix_kernel(n, meta, ad, low, act, pre, win1, wout1, bout, buf_c, buf_d, branch, ag,
               offs, win2, wout2, bias, bias_row, sems):
    copies = weight_copies(buf_c, 0, win2, wout2, bias, sems) + weight_copies(buf_d, 1, win2, wout2, bias, sems)
    for c in copies:
        c.start()
    place_items(n, meta, offs)
    for c in copies:
        c.wait()
    spread_bias(bias, bias_row)

    def tile(t, _):
        at = pl.ds(pl.multiple_of(t * TILE, TILE), TILE)
        a, b = ad[at, :], low[at, :]
        activation, slope = gelu_parts(dot(a, win2[...]) + bias_row[...])
        grad = dot_t(b, wout2[...]) * slope
        branch[at, :] = (dot(act[at, :], wout1[...]) + dot(activation.astype(BF), wout2[...])) + as_row(bout)
        ag[at, :] = dot_t(pre[at, :], win1[...]) + dot_t(grad.astype(BF), win2[...])
        return 0

    lax.fori_loop(0, offs[n + 1], tile, 0)


def mix(meta, ad, low, act, pre, win, wout, bout, buf_c, buf_d, n):
    rows, width = ad.shape
    h = act.shape[1] // 2
    wq, hq = width // LANES, h // LANES
    return pl.pallas_call(
        functools.partial(mix_kernel, n),
        in_specs=[smem()] + [vmem()] * 6 + [whole(bout.shape)] + [hbm()] * 2,
        out_specs=[vmem(), vmem()],
        scratch_shapes=[pltpu.SMEM((n + 2,), jnp.int32),
                        pltpu.VMEM((width, 2 * h), BF), pltpu.VMEM((2 * h, width), BF),
                        pltpu.VMEM((2, 16, LANES), BF), pltpu.VMEM((1, 2 * h), F32),
                        pltpu.SemaphoreType.DMA((2, hq + wq + 1))],
        out_shape=[struct((rows, width), F32)] * 2,
        compiler_params=params(), cost_estimate=cost(0),
    )(meta, ad, low, act, pre, win, wout, bout, buf_c, buf_d)


def finish_kernel(n, first, last_part, meta, tok, cot, branch, ag, nrm, inv, sums_in, gbo, gbi, cw, ns,
                  gamma, both, *rest):
    results, (offs, cgp, sums) = rest[:-3], rest[-3:]
    s = pl.program_id(0) + first
    frames, width = tok.shape[1], tok.shape[2]
    taps, rates = cw.shape[0], ns.shape[0]
    half = taps // 2
    wq = width // LANES
    h = gbi.shape[1] // 2

    @pl.when(s == first)
    def _():
        place_items(n, meta, offs)
        sums[...] = sums_in[...] if last_part else jnp.zeros_like(sums)
        cgp[...] = jnp.zeros_like(cgp)

    item = meta[0] * n + s
    count = meta[2 + item]
    group = meta[2 + 2 * n + item]
    off = offs[s]
    scale = pick(ns, group)
    gam = as_row(gamma)
    w = cw[...].astype(F32)
    zero = jnp.zeros((8, LANES), F32)
    steps = pl.cdiv(count, CHUNK)

    def step(i, accs):
        r0 = pl.multiple_of(i * CHUNK, CHUNK)
        here = pl.ds(r0, CHUNK)
        live = (lax.broadcasted_iota(jnp.int32, (CHUNK, 1), 0) + r0) < count
        src = pl.ds(pl.multiple_of(off + r0, 16), CHUNK)
        new = []
        ngs, nrs = [], []
        for q in range(wq):
            a_ls, a_sc, a_sh = accs[3 * q:3 * q + 3]
            br = jnp.where(live, branch[src, lane(q)], 0.0)
            tk = jnp.where(live, tok[0, here, lane(q)].astype(F32), 0.0)
            both[0, 0, here, lane(q)] = (tk + gam[:, lane(q)] * br).astype(BF)
            g = jnp.where(live, ag[src, lane(q)], 0.0)
            nr = nrm[src, lane(q)].astype(F32)
            new += [a_ls + fold(cot[0, here, lane(q)].astype(F32) * br), a_sc + fold(g * nr), a_sh + fold(g)]
            ngs.append(g * scale[:, lane(q)])
            nrs.append(nr)
        cross = [a * b for a, b in zip(ngs, nrs)]
        m1 = jnp.sum(sum(ngs[1:], ngs[0]), axis=-1, keepdims=True) * (1.0 / width)
        m2 = jnp.sum(sum(cross[1:], cross[0]), axis=-1, keepdims=True) * (1.0 / width)
        istd = inv[src, :]
        for q in range(wq):
            cg = istd * (ngs[q] - m1 - nrs[q] * m2)
            cgp[q, pl.ds(pl.multiple_of(r0 + PAD, 8), CHUNK), :] = jnp.where(live, cg, 0.0)
        return tuple(new)

    accs = lax.fori_loop(0, steps, step, (zero,) * (3 * wq))
    for q in range(wq):
        sums[taps + 1, :, lane(q)] += accs[3 * q]
        sums[taps + 2 + group, :, lane(q)] += accs[3 * q + 1]
        sums[taps + 2 + rates + group, :, lane(q)] += accs[3 * q + 2]

    def clear(i, _):
        r0 = pl.multiple_of(i * CHUNK, CHUNK)
        here = pl.ds(r0, CHUNK)
        both[0, 0, here, :] = jnp.zeros((CHUNK, width), BF)
        both[1, 0, here, :] = jnp.zeros((CHUNK, width), BF)
        for q in range(wq):
            cgp[q, pl.ds(pl.multiple_of(r0 + PAD, 8), CHUNK), :] = jnp.zeros((CHUNK, LANES), F32)
        return 0

    lax.fori_loop(steps, frames // CHUNK, clear, 0)

    for q in range(wq):
        wl = w[:, lane(q)]

        def conv_step(i, accs):
            r0 = pl.multiple_of(i * CHUNK, CHUNK)
            here = pl.ds(r0, CHUNK)
            live = (lax.broadcasted_iota(jnp.int32, (CHUNK, 1), 0) + r0) < count
            tk = jnp.where(live, tok[0, here, lane(q)].astype(F32), 0.0)
            total = cot[0, here, lane(q)].astype(F32)
            new = []
            for k in range(taps):
                sh = cgp[q, pl.ds(r0 + (PAD + half - k), CHUNK), :]
                total = total + wl[k:k + 1] * sh
                new.append(accs[k] + fold(tk * sh))
                if k == half:
                    new_bias = accs[taps] + fold(sh)
            both[1, 0, here, lane(q)] = jnp.where(live, total, 0.0).astype(BF)
            return tuple(new) + (new_bias,)

        accs = lax.fori_loop(0, steps, conv_step, (zero,) * (taps + 1))
        for k in range(taps + 1):
            sums[k, :, lane(q)] += accs[k]

    @pl.when(pl.program_id(0) == pl.num_programs(0) - 1)
    def _():
        if not last_part:
            results[0][...] = sums[...]
            return
        small_keep, small_send = results
        last = taps + 2 + 2 * rates
        rows = [jnp.sum(sums[i], axis=0, keepdims=True) for i in range(last)]
        rows.append(jnp.sum(gbo[...], axis=0, keepdims=True))
        gb = jnp.sum(gbi[...], axis=0, keepdims=True)
        fill = jnp.zeros((1, width - h), F32)
        spare = [jnp.zeros((1, width), F32)] * (small_keep.shape[0] - last - 2)
        for side, dst in ((0, small_keep), (1, small_send)):
            tail = [jnp.concatenate([gb[:, side * h:(side + 1) * h], fill], axis=1)]
            dst[...] = jnp.concatenate(rows + tail + spare, axis=0)


def finish(meta, tok, cot, branch, ag, nrm, inv, sums, gbo, gbi, cw, ns, gamma, first, size):
    items, frames, width = tok.shape
    n = items // 2
    last_part = first + size == n
    wq = width // LANES
    taps, rates = cw.shape[0], ns.shape[0]
    n_small = -(-(taps + 4 + 2 * rates) // 8) * 8
    sums_shape = (taps + 2 + 2 * rates, 8, width)
    item = pl.BlockSpec((1, frames, width), lambda s, c: (c[0] * n + first + s, 0, 0))
    mine = pl.BlockSpec((2, 1, frames, width), lambda s, *_: (0, s, 0, 0))
    more = [(n_small, width)] * 2 if last_part else [sums_shape]
    if sums is None:
        sums = gbo
    return pl.pallas_call(
        functools.partial(finish_kernel, n, first, last_part),
        grid_spec=pltpu.PrefetchScalarGridSpec(
            num_scalar_prefetch=1, grid=(size,),
            in_specs=[item, item] + [vmem()] * 7 + [whole(v.shape) for v in (cw, ns, gamma)],
            out_specs=[mine] + [vmem()] * len(more),
            scratch_shapes=[pltpu.SMEM((n + 2,), jnp.int32),
                            pltpu.VMEM((wq, frames + 4 * PAD, LANES), F32),
                            pltpu.VMEM(sums_shape, F32)]),
        out_shape=[struct((2, size, frames, width), BF)] + [struct(v, F32) for v in more],
        compiler_params=params(), cost_estimate=cost(40000000),
    )(meta, tok, cot, branch, ag, nrm, inv, sums, gbo, gbi, cw, ns, gamma)


def merge_kernel(meta, mine, other, *rest):
    out, gtok = rest[-2:]
    for side, src in ((0, mine), (1, other)):
        @pl.when(pl.program_id(0) == side)
        def _():
            out[...] = src[0]
            gtok[...] = src[1].astype(F32)


def merge(meta, mine, other, into, n, first, step=2):
    _, size, frames, width = mine.shape
    blocks = size // step
    spec_a = pl.BlockSpec((2, step, frames, width), lambda side, s, c: (0, s * (1 - side) + (blocks - 1) * side, 0, 0))
    spec_b = pl.BlockSpec((2, step, frames, width), lambda side, s, c: (0, s * side, 0, 0))
    dst = pl.BlockSpec((step, frames, width), lambda side, s, c: (((c[0] ^ side) * n + first) // step + s, 0, 0))
    return pl.pallas_call(
        merge_kernel,
        grid_spec=pltpu.PrefetchScalarGridSpec(
            num_scalar_prefetch=1, grid=(2, blocks),
            in_specs=[spec_a, spec_b] + [pl.BlockSpec(memory_space=pl.ANY)] * len(into), out_specs=[dst, dst]),
        out_shape=[struct((2 * n, frames, width), BF), struct((2 * n, frames, width), F32)],
        input_output_aliases={3: 0, 4: 1} if into else {},
        compiler_params=params(), cost_estimate=cost(20000000),
    )(meta, mine, other, *into)


def shard_kernel(stay, *refs):
    pieces, out = refs[:-1], refs[-1]
    total = stay[:out.shape[0], :]
    for piece in pieces:
        total = total + piece[...].astype(F32)
    out[...] = total.astype(BF)


def make_shard(stay, pieces):
    return pl.pallas_call(shard_kernel, in_specs=[vmem()] * (1 + len(pieces)), out_specs=vmem(),
                          out_shape=struct(pieces[0].shape, BF), compiler_params=params())(stay, *pieces)


def relay_kernel(*refs):
    sources, out = refs[:-1], refs[-1]
    m = sources[0].shape[0]
    for d, src in enumerate(sources):
        out[d * m:(d + 1) * m, :] = src[...]


def relay(sources):
    m = sources[0].shape[0]
    return pl.pallas_call(relay_kernel, in_specs=[vmem()] * len(sources), out_specs=vmem(),
                          out_shape=struct((len(sources) * m, LANES), BF), compiler_params=params())(*sources)


def unpack_kernel(dp, taps, rates, meta, near, far, small, gcw, gcb, gns, gnsh, gwi, gbi, gwo, gbo, gls, full):
    h, width = gwo.shape
    wq, hq = width // LANES, h // LANES
    m = full.shape[0] // dp
    for odd, mess in ((0, near), (1, far)):
        for d in range(dp // 2):
            at = pl.multiple_of((meta[1] ^ (2 * d + odd)) * m, m)
            full[pl.ds(at, m), :] = mess[d * m:(d + 1) * m, :].astype(F32)
    for q in range(wq):
        gwo[:, lane(q)] = full[q * h:(q + 1) * h, :]
    base = wq * h
    for q in range(hq):
        gwi[:, lane(q)] = full[base + q * width:base + (q + 1) * width, :]
    gcw[...] = small[:taps]
    gcb[...] = small[taps]
    gls[...] = small[taps + 1]
    gns[...] = small[taps + 2:taps + 2 + rates]
    gnsh[...] = small[taps + 2 + rates:taps + 2 + 2 * rates]
    at = taps + 2 + 2 * rates
    gbo[...] = small[at]
    gbi[...] = small[at + 1, :h]


def unpack(meta, near, far, small, dp, taps, rates, width, h):
    shapes = [(taps, width), (width,), (rates, width), (rates, width), (width, h), (h,), (h, width), (width,), (width,)]
    return pl.pallas_call(
        functools.partial(unpack_kernel, dp, taps, rates), in_specs=[smem(), vmem(), vmem(), vmem()],
        out_shape=[struct(s, F32) for s in shapes],
        scratch_shapes=[pltpu.VMEM((2 * width * h // LANES, LANES), F32)],
        compiler_params=params())(meta, near, far, small)


def swap(x, step):
    size = lax.axis_size("tp")
    return lax.ppermute(x, "tp", [(i, i ^ step) for i in range(size)])


def across(x, step):
    size = lax.axis_size("dp")
    return lax.ppermute(x, "dp", [(i, i ^ step) for i in range(size)])


def per_device(tokens, frame_counts, rate_groups, conv_weight, conv_bias, norm_scale, norm_shift,
               weight_in, bias_in, weight_out, bias_out, layer_scale, cotangent):
    width, h = weight_in.shape
    n = tokens.shape[0] // 2
    (tokens, cotangent, conv_weight, conv_bias, norm_scale, norm_shift, weight_in, bias_in, weight_out, bias_out,
     layer_scale) = [pltpu.with_memory_space_constraint(v, pltpu.HBM) for v in (
         tokens, cotangent, conv_weight, conv_bias, norm_scale, norm_shift, weight_in, bias_in, weight_out, bias_out,
         layer_scale)]
    taps, rates = conv_weight.shape[0], norm_scale.shape[0]
    dp = lax.axis_size("dp")
    place = jnp.stack([lax.axis_index("tp") & 1, lax.axis_index("dp")]).astype(jnp.int32)
    meta = jnp.concatenate([place, frame_counts, rate_groups])

    buf_a = pack(weight_in, bias_in, weight_out)
    buf_b = swap(buf_a, 1)
    buf_c = swap(buf_a, 2)
    buf_d = swap(buf_c, 1)
    ad, nrm, low, inv, gbo = conv_norm(meta, tokens, cotangent, conv_weight, conv_bias,
                                       norm_scale, norm_shift, layer_scale)
    act, pre, win, wout, keep, send, gbi = hidden(meta, ad, low, buf_a, buf_b, h, n)
    stay, leave = combine(meta, keep, swap(send, 1), dp)
    arrived = across(leave, 1)
    branch, ag = mix(meta, ad, low, act, pre, win, wout, bias_out, buf_c, buf_d, n)
    arrived, branch = lax.optimization_barrier((arrived, branch))
    stay = (stay + arrived.astype(F32)).reshape(dp // 2, -1, LANES)
    pieces = [across(stay[d].astype(BF), 2 * d) for d in range(1, dp // 2)]

    def finish_part(sums, branch, first):
        return finish(meta, tokens, cotangent, branch, ag, nrm, inv, sums,
                      gbo, gbi, conv_weight, norm_scale, layer_scale, first, n // 2)

    both_1, sums = finish_part(None, branch, 0)
    pieces, sums, branch = lax.optimization_barrier((pieces, sums, branch))
    both_2, small_keep, small_send = finish_part(sums, branch, n // 2)
    shard = make_shard(stay.reshape(-1, LANES), pieces)
    near = [shard] + [across(shard, 2 * d) for d in range(1, dp // 2)]
    near, small_send, both_1, both_2 = lax.optimization_barrier((near, small_send, both_1, both_2))
    small_got = swap(small_send, 1)
    small_got, both_1, both_2 = lax.optimization_barrier((small_got, both_1, both_2))
    near = relay(near)
    far = across(near, 1)
    small = small_keep + small_got
    steps = [1 << i for i in range(1, dp.bit_length() - 1)]
    got = across(small, steps[0])
    done = merge(meta, both_1, swap(both_1, 1), (), n, 0)
    got, done = lax.optimization_barrier((got, done))
    small = small + got
    for step in steps[1:]:
        small = small + across(small, step)
    out, gtok = merge(meta, both_2, swap(both_2, 1), done, n, n // 2)
    small, out, gtok = lax.optimization_barrier((small, out, gtok))
    small = small + across(small, 1)
    far, out, gtok = lax.optimization_barrier((far, out, gtok))
    gcw, gcb, gns, gnsh, gwi, gbi, gwo, gbo, gls = unpack(meta, near, far, small, dp, taps, rates, width, h)
    return (out, gtok, gcw, gcb, gns, gnsh, gwi, gbi, gwo, gbo, gls)


def solution(mesh):
    items, copied = P("dp", None, None), P()
    in_specs = (items, P("dp"), P("dp"), copied, copied, copied, copied, P(None, "tp"), P("tp"), P("tp", None),
                copied, copied, items)
    out_specs = (items, items, copied, copied, copied, copied, P(None, "tp"), P("tp"), P("tp", None), copied, copied)
    return jax.shard_map(per_device, mesh=mesh, in_specs=in_specs, out_specs=out_specs, check_vma=False)
```

```python
import functools

import jax
import jax.numpy as jnp
from jax import lax
from jax.experimental import pallas as pl
from jax.experimental.pallas import tpu as pltpu
from jax.sharding import PartitionSpec as P

EPS = 1e-06
BF, F32 = jnp.bfloat16, jnp.float32
TILE = 256
LANES = 128
PAD = 8
CHUNK = 64
WIDE_CHUNK = 128
VMEM_LIMIT = 12 * 1024 * 1024


def params(**more):
    return pltpu.CompilerParams(vmem_limit_bytes=VMEM_LIMIT, **more)


def struct(shape, dtype):
    return jax.ShapeDtypeStruct(shape, dtype)


def whole(shape):
    return pl.BlockSpec(shape, lambda *_: (0,) * len(shape))


def hbm():
    return pl.BlockSpec(memory_space=pltpu.HBM)


def smem():
    return pl.BlockSpec(memory_space=pltpu.SMEM)


def cost(size):
    return pl.CostEstimate(flops=0, transcendentals=0, bytes_accessed=size)


def vmem():
    return pl.BlockSpec(memory_space=pltpu.VMEM)


def lane(q):
    return slice(q * LANES, (q + 1) * LANES)


def fold(x):
    return jnp.sum(x.reshape(x.shape[0] // 8, 8, x.shape[1]), axis=0)


def pick(table, group):
    rows = table[...].astype(F32)
    value = rows[0:1]
    for r in range(1, rows.shape[0]):
        value = jnp.where(group == r, rows[r:r + 1], value)
    return value


def as_row(ref):
    return ref[...].astype(F32).reshape(1, -1)


def gelu_parts(pre):
    cdf = 0.5 + 0.5 * lax.erf(pre * 0.7071067811865476)
    density = jnp.exp(-0.5 * pre * pre) * 0.3989422804014327
    return pre * cdf, cdf + pre * density


def dot(a, b):
    return jnp.dot(a, b, preferred_element_type=F32)


def dot_t(a, b):
    return lax.dot_general(a, b, (((1,), (1,)), ((), ())), preferred_element_type=F32)


def dot_rows(a, b):
    return lax.dot_general(a, b, (((0,), (0,)), ((), ())), preferred_element_type=F32)


def place_items(n, meta, offs):
    end = jnp.int32(0)
    for j in range(n):
        offs[j] = end
        end = end + ((meta[2 + meta[0] * n + j] + 15) & -16)
    offs[n] = end
    offs[n + 1] = (end + TILE - 1) // TILE


def pack_kernel(wi, bi, wo, out):
    width, h = wi.shape
    hq, wq = h // LANES, width // LANES
    for q in range(hq):
        out[q * width:(q + 1) * width, :] = wi[:, lane(q)]
    base = hq * width
    for q in range(wq):
        out[base + q * h:base + (q + 1) * h, :] = wo[:, lane(q)]
    base += wq * h
    bias = bi[...].astype(F32).reshape(1, h)
    rows = [bias[:, lane(q)] for q in range(hq)] + [jnp.zeros((1, LANES), F32)] * (16 - hq)
    out[base:base + 16, :] = jnp.concatenate(rows, axis=0).astype(BF)


def pack(wi, bi, wo):
    rows = 2 * wi.size // LANES + 16
    return pl.pallas_call(pack_kernel, out_shape=struct((rows, LANES), BF),
                          compiler_params=params())(wi, bi, wo)


def weight_copies(buf, side, win, wout, bias, sems):
    width, h = win.shape[0], win.shape[1] // 2
    hq, wq = h // LANES, width // LANES
    copies = []
    for q in range(hq):
        at = side * h + q * LANES
        copies.append((buf.at[pl.ds(q * width, width), :], win.at[:, pl.ds(at, LANES)]))
    base = hq * width
    for q in range(wq):
        copies.append((buf.at[pl.ds(base + q * h, h), :], wout.at[pl.ds(side * h, h), pl.ds(q * LANES, LANES)]))
    copies.append((buf.at[pl.ds(base + wq * h, 16), :], bias.at[side]))
    return [pltpu.make_async_copy(src, dst, sems.at[side, i]) for i, (src, dst) in enumerate(copies)]


def spread_bias(bias, row):
    hq = row.shape[1] // LANES // 2
    for side in range(2):
        for q in range(hq):
            at = side * hq + q
            row[:, lane(at)] = bias[side, q:q + 1, :].astype(F32)


def front_kernel(n, meta, tok, cot, cw, cb, ns, nsh, gamma, buf_a, buf_b,
                 ad, nrm, low, inv, act, pre, win, wout, keep, send, gbo, gbi,
                 offs, pad, ad_s, nrm_s, low_s, inv_s, bias, bias_row, dwo, dwi, sems):
    s = pl.program_id(0)
    frames, width = tok.shape[1], tok.shape[2]
    taps = cw.shape[0]
    half = taps // 2
    wq = width // LANES
    h = win.shape[1] // 2
    copies = weight_copies(buf_a, 0, win, wout, bias, sems) + weight_copies(buf_b, 1, win, wout, bias, sems)

    @pl.when(s == 0)
    def _():
        for c in copies:
            c.start()
        place_items(n, meta, offs)
        offs[n + 2] = 0
        gbo[...] = jnp.zeros_like(gbo)
        pad[...] = jnp.zeros_like(pad)

    def flush(j):
        dst = pl.ds(pl.multiple_of(offs[j], 16), frames)
        for whole_ref, stage in ((ad, ad_s), (nrm, nrm_s), (low, low_s), (inv, inv_s)):
            whole_ref[dst, :] = stage[...]

    @pl.when(s > 0)
    def _():
        flush(s - 1)

    @pl.when(s == 1)
    def _():
        for c in copies:
            c.wait()
        spread_bias(bias, bias_row)
        dwo[...] = jnp.zeros_like(dwo)
        dwi[...] = jnp.zeros_like(dwi)
        gbi[...] = jnp.zeros_like(gbi)

    item = meta[0] * n + s
    count = meta[2 + item]
    group = meta[2 + 2 * n + item]

    def setup():
        rows = lax.broadcasted_iota(jnp.int32, (frames, LANES), 0)
        for q in range(wq):
            pad[q, PAD:PAD + frames, :] = jnp.where(rows < count, tok[0, :, lane(q)].astype(F32), 0.0)
        return pick(ns, group), pick(nsh, group), as_row(gamma), as_row(cb), cw[...].astype(F32)

    def conv_step(i, acc, consts):
        scale, shift, gam, conv_bias, w = consts
        r0 = i * CHUNK if isinstance(i, int) else pl.multiple_of(i * CHUNK, CHUNK)
        here = pl.ds(r0, CHUNK)
        live = (lax.broadcasted_iota(jnp.int32, (CHUNK, LANES), 0) + r0) < count
        convs = []
        for q in range(wq):
            conv = conv_bias[:, lane(q)]
            for k in range(taps):
                conv = conv + w[k:k + 1, lane(q)] * pad[q, pl.ds(r0 + (PAD - half + k), CHUNK), :]
            convs.append(conv)
        mean = jnp.sum(sum(convs[1:], convs[0]), axis=-1, keepdims=True) * (1.0 / width)
        cents = [c - mean for c in convs]
        sq = [c * c for c in cents]
        var = jnp.sum(sum(sq[1:], sq[0]), axis=-1, keepdims=True) * (1.0 / width)
        istd = lax.rsqrt(var + EPS)
        inv_s[here, :] = jnp.broadcast_to(istd, (CHUNK, LANES))
        new = []
        for q in range(wq):
            normed = cents[q] * istd
            ad_s[here, lane(q)] = (normed * scale[:, lane(q)] + shift[:, lane(q)]).astype(BF)
            nrm_s[here, lane(q)] = normed.astype(BF)
            back = jnp.where(live, cot[0, here, lane(q)].astype(F32), 0.0) * gam[:, lane(q)]
            low_s[here, lane(q)] = back.astype(BF)
            new.append(acc[q] + fold(back))
        return tuple(new)

    def add_gbo(accs):
        for q in range(wq):
            gbo[:, lane(q)] += accs[q]

    def tile(t, between=()):
        between = list(between)
        at = pl.ds(pl.multiple_of(t * TILE, TILE), TILE)
        a, b = ad[at, :], low[at, :]
        activation, slope = gelu_parts(dot(a, win[...]) + bias_row[...])
        if between:
            between.pop(0)()
        grad = dot_t(b, wout[...]) * slope
        lo = activation.astype(BF)
        act[at, :] = lo
        if between:
            between.pop(0)()
        dwo[...] += dot_rows(lo, b)
        gbi[...] += fold(grad)
        g = grad.astype(BF)
        pre[at, :] = g
        if between:
            between.pop(0)()
        dwi[...] += dot_rows(a, g)
        if between:
            between.pop(0)()

    done = offs[n + 2]
    ready = offs[s] >= (done + 1) * TILE
    none = (jnp.zeros((8, LANES), F32),) * wq

    @pl.when(ready)
    def _():
        consts = setup()
        state = [none]

        def part(lo_i, hi_i):
            def run():
                for i in range(lo_i, hi_i):
                    state[0] = conv_step(i, state[0], consts)
            return run

        count_c = frames // CHUNK
        cuts = [count_c * k // 4 for k in range(5)]
        tile(done, [part(cuts[k], cuts[k + 1]) for k in range(4)])
        add_gbo(state[0])
        offs[n + 2] = done + 1

    @pl.when(jnp.logical_not(ready))
    def _():
        consts = setup()
        add_gbo(lax.fori_loop(0, pl.cdiv(count, CHUNK), lambda i, acc: conv_step(i, acc, consts), none))

    @pl.when(s == n - 1)
    def _():
        flush(s)
        end = pl.ds(pl.multiple_of(offs[n], 16), TILE)
        ad[end, :] = jnp.zeros((TILE, width), BF)
        low[end, :] = jnp.zeros((TILE, width), BF)

        def rest(t, _):
            tile(t)
            return 0

        lax.fori_loop(offs[n + 2], offs[n + 1], rest, 0)
        for side, dst in ((0, keep), (1, send)):
            for q in range(wq):
                dst[q * h:(q + 1) * h, :] = dwo[side * h:(side + 1) * h, lane(q)].astype(dst.dtype)
            base = wq * h
            for q in range(h // LANES):
                dst[base + q * width:base + (q + 1) * width, :] = dwi[:, lane(side * (h // LANES) + q)].astype(dst.dtype)


def front(meta, tok, cot, cw, cb, ns, nsh, gamma, buf_a, buf_b, h):
    items, frames, width = tok.shape
    n = items // 2
    rows = n * frames + TILE
    packed = 2 * width * h // LANES
    wq, hq = width // LANES, h // LANES
    item = pl.BlockSpec((1, frames, width), lambda s, c: (c[0] * n + s, 0, 0))
    return pl.pallas_call(
        functools.partial(front_kernel, n),
        grid_spec=pltpu.PrefetchScalarGridSpec(
            num_scalar_prefetch=1, grid=(n,),
            in_specs=[item, item] + [whole(v.shape) for v in (cw, cb, ns, nsh, gamma)] + [hbm()] * 2,
            out_specs=[vmem()] * 12,
            scratch_shapes=[pltpu.SMEM((n + 3,), jnp.int32),
                            pltpu.VMEM((wq, frames + 4 * PAD, LANES), F32),
                            pltpu.VMEM((frames, width), BF), pltpu.VMEM((frames, width), BF),
                            pltpu.VMEM((frames, width), BF), pltpu.VMEM((frames, LANES), F32),
                            pltpu.VMEM((2, 16, LANES), BF), pltpu.VMEM((1, 2 * h), F32),
                            pltpu.VMEM((2 * h, width), F32), pltpu.VMEM((width, 2 * h), F32),
                            pltpu.SemaphoreType.DMA((2, hq + wq + 1))]),
        out_shape=[struct((rows, width), BF)] * 3 + [struct((rows, LANES), F32)]
        + [struct((rows, 2 * h), BF)] * 2 + [struct((width, 2 * h), BF), struct((2 * h, width), BF)]
        + [struct((packed, LANES), F32), struct((packed, LANES), BF), struct((8, width), F32), struct((8, 2 * h), F32)],
        compiler_params=params(), cost_estimate=cost(0),
    )(meta, tok, cot, cw, cb, ns, nsh, gamma, buf_a, buf_b)


def combine_kernel(dp, meta, keep, recv, stay, leave):
    m = keep.shape[0] // dp
    for d in range(dp):
        src = pl.ds(pl.multiple_of((meta[1] ^ d) * m, m), m)
        total = keep[src, :] + recv[src, :].astype(F32)
        dst = leave if d % 2 else stay
        dst[d // 2 * m:(d // 2 + 1) * m, :] = total.astype(dst.dtype)


def combine(meta, keep, recv, dp):
    rows = keep.shape[0] // 2
    return pl.pallas_call(
        functools.partial(combine_kernel, dp),
        in_specs=[smem(), vmem(), vmem()], out_specs=[vmem(), vmem()],
        out_shape=[struct((rows, LANES), F32), struct((rows, LANES), BF)],
        compiler_params=params())(meta, keep, recv)


def mix_kernel(n, meta, ad, low, act, pre, win1, wout1, bout, buf_c, buf_d, branch, ag,
               offs, win2, wout2, bias, bias_row, sems):
    copies = weight_copies(buf_c, 0, win2, wout2, bias, sems) + weight_copies(buf_d, 1, win2, wout2, bias, sems)
    for c in copies:
        c.start()
    place_items(n, meta, offs)
    for c in copies:
        c.wait()
    spread_bias(bias, bias_row)

    def tile(t, _):
        at = pl.ds(pl.multiple_of(t * TILE, TILE), TILE)
        a, b = ad[at, :], low[at, :]
        activation, slope = gelu_parts(dot(a, win2[...]) + bias_row[...])
        grad = dot_t(b, wout2[...]) * slope
        branch[at, :] = (dot(act[at, :], wout1[...]) + dot(activation.astype(BF), wout2[...])) + as_row(bout)
        ag[at, :] = dot_t(pre[at, :], win1[...]) + dot_t(grad.astype(BF), win2[...])
        return 0

    lax.fori_loop(0, offs[n + 1], tile, 0)


def mix(meta, ad, low, act, pre, win, wout, bout, buf_c, buf_d, n):
    rows, width = ad.shape
    h = act.shape[1] // 2
    wq, hq = width // LANES, h // LANES
    return pl.pallas_call(
        functools.partial(mix_kernel, n),
        in_specs=[smem()] + [vmem()] * 6 + [whole(bout.shape)] + [hbm()] * 2,
        out_specs=[vmem(), vmem()],
        scratch_shapes=[pltpu.SMEM((n + 2,), jnp.int32),
                        pltpu.VMEM((width, 2 * h), BF), pltpu.VMEM((2 * h, width), BF),
                        pltpu.VMEM((2, 16, LANES), BF), pltpu.VMEM((1, 2 * h), F32),
                        pltpu.SemaphoreType.DMA((2, hq + wq + 1))],
        out_shape=[struct((rows, width), F32)] * 2,
        compiler_params=params(), cost_estimate=cost(0),
    )(meta, ad, low, act, pre, win, wout, bout, buf_c, buf_d)


def finish_kernel(n, first, last_part, meta, tok, cot, branch, ag, nrm, inv, sums_in, gbo, gbi, cw, ns,
                  gamma, *rest):
    other = rest[0]
    (out, gtok, both), results, (offs, cgp, sums) = rest[3:6] if last_part else rest[:3], rest[6 if last_part else 3:-3], rest[-3:]
    s = pl.program_id(0) + first

    if last_part:
        @pl.when(pl.program_id(1) == 1)
        def _():
            out[...] = other[0]
            gtok[...] = other[1].astype(F32)

        @pl.when(pl.program_id(1) == 0)
        def _():
            finish_item(n, s, first, last_part, meta, tok, cot, branch, ag, nrm, inv, sums_in, gbo, gbi, cw, ns, gamma,
                        out, gtok, both, results, offs, cgp, sums)
    else:
        finish_item(n, s, first, last_part, meta, tok, cot, branch, ag, nrm, inv, sums_in, gbo, gbi, cw, ns, gamma,
                    out, gtok, both, results, offs, cgp, sums)


def finish_item(n, s, first, last_part, meta, tok, cot, branch, ag, nrm, inv, sums_in, gbo, gbi, cw, ns, gamma,
                out, gtok, both, results, offs, cgp, sums):
    frames, width = tok.shape[1], tok.shape[2]
    taps, rates = cw.shape[0], ns.shape[0]
    half = taps // 2
    wq = width // LANES
    h = gbi.shape[1] // 2

    @pl.when(s == first)
    def _():
        place_items(n, meta, offs)
        sums[...] = sums_in[...] if last_part else jnp.zeros_like(sums)
        cgp[...] = jnp.zeros_like(cgp)

    item = meta[0] * n + s
    count = meta[2 + item]
    group = meta[2 + 2 * n + item]
    off = offs[s]
    scale = pick(ns, group)
    gam = as_row(gamma)
    w = cw[...].astype(F32)
    zero = jnp.zeros((8, LANES), F32)
    steps = pl.cdiv(count, WIDE_CHUNK)

    def step(i, accs):
        r0 = pl.multiple_of(i * WIDE_CHUNK, WIDE_CHUNK)
        here = pl.ds(r0, WIDE_CHUNK)
        live = (lax.broadcasted_iota(jnp.int32, (WIDE_CHUNK, 1), 0) + r0) < count
        src = pl.ds(pl.multiple_of(off + r0, 16), WIDE_CHUNK)
        new = []
        ngs, nrs = [], []
        for q in range(wq):
            a_ls, a_sc, a_sh = accs[3 * q:3 * q + 3]
            br = jnp.where(live, branch[src, lane(q)], 0.0)
            tk = jnp.where(live, tok[0, here, lane(q)].astype(F32), 0.0)
            value = (tk + gam[:, lane(q)] * br).astype(BF)
            both[0, 0, here, lane(q)] = value
            out[0, here, lane(q)] = value
            g = jnp.where(live, ag[src, lane(q)], 0.0)
            nr = nrm[src, lane(q)].astype(F32)
            new += [a_ls + fold(cot[0, here, lane(q)].astype(F32) * br), a_sc + fold(g * nr), a_sh + fold(g)]
            ngs.append(g * scale[:, lane(q)])
            nrs.append(nr)
        cross = [a * b for a, b in zip(ngs, nrs)]
        m1 = jnp.sum(sum(ngs[1:], ngs[0]), axis=-1, keepdims=True) * (1.0 / width)
        m2 = jnp.sum(sum(cross[1:], cross[0]), axis=-1, keepdims=True) * (1.0 / width)
        istd = inv[src, :]
        for q in range(wq):
            cg = istd * (ngs[q] - m1 - nrs[q] * m2)
            cgp[q, pl.ds(pl.multiple_of(r0 + PAD, 8), WIDE_CHUNK), :] = jnp.where(live, cg, 0.0)
        return tuple(new)

    accs = lax.fori_loop(0, steps, step, (zero,) * (3 * wq))
    for q in range(wq):
        sums[taps + 1, :, lane(q)] += accs[3 * q]
        sums[taps + 2 + group, :, lane(q)] += accs[3 * q + 1]
        sums[taps + 2 + rates + group, :, lane(q)] += accs[3 * q + 2]

    def clear(i, _):
        r0 = pl.multiple_of(i * WIDE_CHUNK, WIDE_CHUNK)
        here = pl.ds(r0, WIDE_CHUNK)
        for ref in (both.at[0, 0], both.at[1, 0], out.at[0], gtok.at[0]):
            ref[here, :] = jnp.zeros((WIDE_CHUNK, width), ref.dtype)
        for q in range(wq):
            cgp[q, pl.ds(pl.multiple_of(r0 + PAD, 8), WIDE_CHUNK), :] = jnp.zeros((WIDE_CHUNK, LANES), F32)
        return 0

    lax.fori_loop(steps, frames // WIDE_CHUNK, clear, 0)

    for q in range(wq):
        wl = w[:, lane(q)]

        def conv_step(i, accs):
            r0 = pl.multiple_of(i * WIDE_CHUNK, WIDE_CHUNK)
            here = pl.ds(r0, WIDE_CHUNK)
            live = (lax.broadcasted_iota(jnp.int32, (WIDE_CHUNK, 1), 0) + r0) < count
            tk = jnp.where(live, tok[0, here, lane(q)].astype(F32), 0.0)
            total = cot[0, here, lane(q)].astype(F32)
            new = []
            for k in range(taps):
                sh = cgp[q, pl.ds(r0 + (PAD + half - k), WIDE_CHUNK), :]
                total = total + wl[k:k + 1] * sh
                new.append(accs[k] + fold(tk * sh))
                if k == half:
                    new_bias = accs[taps] + fold(sh)
            total = jnp.where(live, total, 0.0).astype(BF)
            both[1, 0, here, lane(q)] = total
            gtok[0, here, lane(q)] = total.astype(F32)
            return tuple(new) + (new_bias,)

        accs = lax.fori_loop(0, steps, conv_step, (zero,) * (taps + 1))
        for k in range(taps + 1):
            sums[k, :, lane(q)] += accs[k]

    @pl.when(pl.program_id(0) == pl.num_programs(0) - 1)
    def _():
        if not last_part:
            results[0][...] = sums[...]
            return
        small_keep, small_send = results
        last = taps + 2 + 2 * rates
        rows = [jnp.sum(sums[i], axis=0, keepdims=True) for i in range(last)]
        rows.append(jnp.sum(gbo[...], axis=0, keepdims=True))
        gb = jnp.sum(gbi[...], axis=0, keepdims=True)
        fill = jnp.zeros((1, width - h), F32)
        spare = [jnp.zeros((1, width), F32)] * (small_keep.shape[0] - last - 2)
        for side, dst in ((0, small_keep), (1, small_send)):
            tail = [jnp.concatenate([gb[:, side * h:(side + 1) * h], fill], axis=1)]
            dst[...] = jnp.concatenate(rows + tail + spare, axis=0)


def finish(meta, tok, cot, branch, ag, nrm, inv, sums, gbo, gbi, cw, ns, gamma, first, size, other=None, into=()):
    items, frames, width = tok.shape
    n = items // 2
    last_part = first + size == n
    wq = width // LANES
    taps, rates = cw.shape[0], ns.shape[0]
    n_small = -(-(taps + 4 + 2 * rates) // 8) * 8
    sums_shape = (taps + 2 + 2 * rates, 8, width)
    item = pl.BlockSpec((1, frames, width), lambda s, p, c: (c[0] * n + first + s, 0, 0))
    mine = pl.BlockSpec((2, 1, frames, width), lambda s, p, c: (0, s, 0, 0))
    dst = pl.BlockSpec((1, frames, width), lambda s, p, c: ((c[0] ^ p) * n + first * (1 - p) + s, 0, 0))
    more = [(n_small, width)] * 2 if last_part else [sums_shape]
    if sums is None:
        sums = gbo
    fixed = [meta, tok, cot, branch, ag, nrm, inv, sums, gbo, gbi, cw, ns, gamma]
    extra = [mine] + [pl.BlockSpec(memory_space=pl.ANY)] * 2 if last_part else []
    return pl.pallas_call(
        functools.partial(finish_kernel, n, first, last_part),
        grid_spec=pltpu.PrefetchScalarGridSpec(
            num_scalar_prefetch=1, grid=(size, 2 if last_part else 1),
            in_specs=[item, item] + [vmem()] * 7 + [whole(v.shape) for v in (cw, ns, gamma)] + extra,
            out_specs=[dst, dst, mine] + [vmem()] * len(more),
            scratch_shapes=[pltpu.SMEM((n + 2,), jnp.int32),
                            pltpu.VMEM((wq, frames + 4 * PAD, LANES), F32),
                            pltpu.VMEM(sums_shape, F32)]),
        out_shape=[struct((items, frames, width), BF), struct((items, frames, width), F32),
                   struct((2, size, frames, width), BF)] + [struct(v, F32) for v in more],
        input_output_aliases={14: 0, 15: 1} if last_part else {},
        compiler_params=params(), cost_estimate=cost(40000000),
    )(*fixed, *((other,) + tuple(into) if last_part else ()))


def merge_kernel(meta, other, out_in, gtok_in, out, gtok):
    out[...] = other[0]
    gtok[...] = other[1].astype(F32)


def merge(meta, other, into, n, first, step=2):
    _, size, frames, width = other.shape
    src = pl.BlockSpec((2, step, frames, width), lambda s, c: (0, s, 0, 0))
    dst = pl.BlockSpec((step, frames, width), lambda s, c: (((1 - c[0]) * n + first) // step + s, 0, 0))
    return pl.pallas_call(
        merge_kernel,
        grid_spec=pltpu.PrefetchScalarGridSpec(
            num_scalar_prefetch=1, grid=(size // step,),
            in_specs=[src] + [pl.BlockSpec(memory_space=pl.ANY)] * 2, out_specs=[dst, dst]),
        out_shape=[struct(v.shape, v.dtype) for v in into],
        input_output_aliases={2: 0, 3: 1},
        compiler_params=params(), cost_estimate=cost(20000000),
    )(meta, other, *into)


def shard_kernel(stay, *refs):
    pieces, out = refs[:-1], refs[-1]
    total = stay[:out.shape[0], :]
    for piece in pieces:
        total = total + piece[...].astype(F32)
    out[...] = total.astype(BF)


def make_shard(stay, pieces):
    return pl.pallas_call(shard_kernel, in_specs=[vmem()] * (1 + len(pieces)), out_specs=vmem(),
                          out_shape=struct(pieces[0].shape, BF), compiler_params=params())(stay, *pieces)


def relay_kernel(*refs):
    sources, out = refs[:-1], refs[-1]
    m = sources[0].shape[0]
    for d, src in enumerate(sources):
        out[d * m:(d + 1) * m, :] = src[...]


def relay(sources):
    m = sources[0].shape[0]
    return pl.pallas_call(relay_kernel, in_specs=[vmem()] * len(sources), out_specs=vmem(),
                          out_shape=struct((len(sources) * m, LANES), BF), compiler_params=params())(*sources)


def unpack_kernel(dp, taps, rates, meta, near, far, small, gcw, gcb, gns, gnsh, gwi, gbi, gwo, gbo, gls, full):
    h, width = gwo.shape
    wq, hq = width // LANES, h // LANES
    m = full.shape[0] // dp
    for odd, mess in ((0, near), (1, far)):
        for d in range(dp // 2):
            at = pl.multiple_of((meta[1] ^ (2 * d + odd)) * m, m)
            full[pl.ds(at, m), :] = mess[d * m:(d + 1) * m, :].astype(F32)
    for q in range(wq):
        gwo[:, lane(q)] = full[q * h:(q + 1) * h, :]
    base = wq * h
    for q in range(hq):
        gwi[:, lane(q)] = full[base + q * width:base + (q + 1) * width, :]
    gcw[...] = small[:taps]
    gcb[...] = small[taps]
    gls[...] = small[taps + 1]
    gns[...] = small[taps + 2:taps + 2 + rates]
    gnsh[...] = small[taps + 2 + rates:taps + 2 + 2 * rates]
    at = taps + 2 + 2 * rates
    gbo[...] = small[at]
    gbi[...] = small[at + 1, :h]


def unpack(meta, near, far, small, dp, taps, rates, width, h):
    shapes = [(taps, width), (width,), (rates, width), (rates, width), (width, h), (h,), (h, width), (width,), (width,)]
    return pl.pallas_call(
        functools.partial(unpack_kernel, dp, taps, rates), in_specs=[smem(), vmem(), vmem(), vmem()],
        out_shape=[struct(s, F32) for s in shapes],
        scratch_shapes=[pltpu.VMEM((2 * width * h // LANES, LANES), F32)],
        compiler_params=params())(meta, near, far, small)


def swap(x, step):
    size = lax.axis_size("tp")
    return lax.ppermute(x, "tp", [(i, i ^ step) for i in range(size)])


def across(x, step):
    size = lax.axis_size("dp")
    return lax.ppermute(x, "dp", [(i, i ^ step) for i in range(size)])


def per_device(tokens, frame_counts, rate_groups, conv_weight, conv_bias, norm_scale, norm_shift,
               weight_in, bias_in, weight_out, bias_out, layer_scale, cotangent):
    width, h = weight_in.shape
    n = tokens.shape[0] // 2
    (tokens, cotangent, conv_weight, conv_bias, norm_scale, norm_shift, weight_in, bias_in, weight_out, bias_out,
     layer_scale) = [pltpu.with_memory_space_constraint(v, pltpu.HBM) for v in (
         tokens, cotangent, conv_weight, conv_bias, norm_scale, norm_shift, weight_in, bias_in, weight_out, bias_out,
         layer_scale)]
    taps, rates = conv_weight.shape[0], norm_scale.shape[0]
    dp = lax.axis_size("dp")
    place = jnp.stack([lax.axis_index("tp") & 1, lax.axis_index("dp")]).astype(jnp.int32)
    meta = jnp.concatenate([place, frame_counts, rate_groups])

    buf_a = pack(weight_in, bias_in, weight_out)
    buf_b = swap(buf_a, 1)
    buf_c = swap(buf_a, 2)
    buf_d = swap(buf_c, 1)
    ad, nrm, low, inv, act, pre, win, wout, keep, send, gbo, gbi = front(
        meta, tokens, cotangent, conv_weight, conv_bias, norm_scale, norm_shift, layer_scale, buf_a, buf_b, h)
    stay, leave = combine(meta, keep, swap(send, 1), dp)
    arrived = across(leave, 1)
    branch, ag = mix(meta, ad, low, act, pre, win, wout, bias_out, buf_c, buf_d, n)
    arrived, branch = lax.optimization_barrier((arrived, branch))
    stay = (stay + arrived.astype(F32)).reshape(dp // 2, -1, LANES)
    pieces = [across(stay[d].astype(BF), 2 * d) for d in range(1, dp // 2)]

    def finish_part(sums, branch, first, *more):
        return finish(meta, tokens, cotangent, branch, ag, nrm, inv, sums, gbo, gbi, conv_weight, norm_scale,
                      layer_scale, first, n // 2, *more)

    *parts, both, sums = finish_part(None, branch, 0)
    pieces, sums, branch, both = lax.optimization_barrier((pieces, sums, branch, both))
    other = swap(both, 1)
    shard = make_shard(stay.reshape(-1, LANES), pieces)
    near = [shard] + [across(shard, 2 * d) for d in range(1, dp // 2)]
    *parts, both, small_keep, small_send = finish_part(sums, branch, n // 2, other, parts)
    near, small_send, both = lax.optimization_barrier((near, small_send, both))
    small_got = swap(small_send, 1)
    small_got, both = lax.optimization_barrier((small_got, both))
    near = relay(near)
    far = across(near, 1)
    small = small_keep + small_got
    got = across(small, 2)
    out, gtok = merge(meta, swap(both, 1), parts, n, n // 2)
    got, out, gtok = lax.optimization_barrier((got, out, gtok))
    small = small + got
    for i in range(2, dp.bit_length() - 1):
        small = small + across(small, 1 << i)
    small = small + across(small, 1)
    far, out, gtok = lax.optimization_barrier((far, out, gtok))
    gcw, gcb, gns, gnsh, gwi, gbi, gwo, gbo, gls = unpack(meta, near, far, small, dp, taps, rates, width, h)
    return (out, gtok, gcw, gcb, gns, gnsh, gwi, gbi, gwo, gbo, gls)


def solution(mesh):
    items, copied = P("dp", None, None), P()
    in_specs = (items, P("dp"), P("dp"), copied, copied, copied, copied, P(None, "tp"), P("tp"), P("tp", None),
                copied, copied, items)
    out_specs = (items, items, copied, copied, copied, copied, P(None, "tp"), P("tp"), P("tp", None), copied, copied)
    return jax.shard_map(per_device, mesh=mesh, in_specs=in_specs, out_specs=out_specs, check_vma=False)
```

```python
import functools

import jax
import jax.numpy as jnp
from jax import lax
from jax.experimental import pallas as pl
from jax.experimental.pallas import tpu as pltpu
from jax.sharding import PartitionSpec as P

EPS = 1e-06
BF, F32 = jnp.bfloat16, jnp.float32
TILE = 256
LANES = 128
PAD = 8
CHUNK = 64
WIDE_CHUNK = 128
VMEM_LIMIT = 12 * 1024 * 1024


def params(**more):
    return pltpu.CompilerParams(vmem_limit_bytes=VMEM_LIMIT, **more)


def struct(shape, dtype):
    return jax.ShapeDtypeStruct(shape, dtype)


def whole(shape):
    return pl.BlockSpec(shape, lambda *_: (0,) * len(shape))


def hbm():
    return pl.BlockSpec(memory_space=pltpu.HBM)


def smem():
    return pl.BlockSpec(memory_space=pltpu.SMEM)


def cost(size):
    return pl.CostEstimate(flops=0, transcendentals=0, bytes_accessed=size)


def vmem():
    return pl.BlockSpec(memory_space=pltpu.VMEM)


def lane(q):
    return slice(q * LANES, (q + 1) * LANES)


def fold(x):
    return jnp.sum(x.reshape(x.shape[0] // 8, 8, x.shape[1]), axis=0)


def pick(table, group):
    rows = table[...].astype(F32)
    value = rows[0:1]
    for r in range(1, rows.shape[0]):
        value = jnp.where(group == r, rows[r:r + 1], value)
    return value


def as_row(ref):
    return ref[...].astype(F32).reshape(1, -1)


def gelu_parts(pre):
    cdf = 0.5 + 0.5 * lax.erf(pre * 0.7071067811865476)
    density = jnp.exp(-0.5 * pre * pre) * 0.3989422804014327
    return pre * cdf, cdf + pre * density


def dot(a, b):
    return jnp.dot(a, b, preferred_element_type=F32)


def dot_t(a, b):
    return lax.dot_general(a, b, (((1,), (1,)), ((), ())), preferred_element_type=F32)


def dot_rows(a, b):
    return lax.dot_general(a, b, (((0,), (0,)), ((), ())), preferred_element_type=F32)


def place_items(n, meta, offs):
    end = jnp.int32(0)
    for j in range(n):
        offs[j] = end
        end = end + ((meta[2 + meta[0] * n + j] + 15) & -16)
    offs[n] = end
    offs[n + 1] = (end + TILE - 1) // TILE


def pack_kernel(wi, bi, wo, out):
    width, h = wi.shape
    hq, wq = h // LANES, width // LANES
    for q in range(hq):
        out[q * width:(q + 1) * width, :] = wi[:, lane(q)]
    base = hq * width
    for q in range(wq):
        out[base + q * h:base + (q + 1) * h, :] = wo[:, lane(q)]
    base += wq * h
    bias = bi[...].astype(F32).reshape(1, h)
    rows = [bias[:, lane(q)] for q in range(hq)] + [jnp.zeros((1, LANES), F32)] * (16 - hq)
    out[base:base + 16, :] = jnp.concatenate(rows, axis=0).astype(BF)


def pack(wi, bi, wo):
    rows = 2 * wi.size // LANES + 16
    return pl.pallas_call(pack_kernel, out_shape=struct((rows, LANES), BF),
                          compiler_params=params())(wi, bi, wo)


def weight_copies(buf, side, win, wout, bias, sems):
    width, h = win.shape[0], win.shape[1] // 2
    hq, wq = h // LANES, width // LANES
    copies = []
    for q in range(hq):
        at = side * h + q * LANES
        copies.append((buf.at[pl.ds(q * width, width), :], win.at[:, pl.ds(at, LANES)]))
    base = hq * width
    for q in range(wq):
        copies.append((buf.at[pl.ds(base + q * h, h), :], wout.at[pl.ds(side * h, h), pl.ds(q * LANES, LANES)]))
    copies.append((buf.at[pl.ds(base + wq * h, 16), :], bias.at[side]))
    return [pltpu.make_async_copy(src, dst, sems.at[side, i]) for i, (src, dst) in enumerate(copies)]


def spread_bias(bias, row):
    hq = row.shape[1] // LANES // 2
    for side in range(2):
        for q in range(hq):
            at = side * hq + q
            row[:, lane(at)] = bias[side, q:q + 1, :].astype(F32)


def front_kernel(n, meta, tok, cot, cw, cb, ns, nsh, gamma, buf_a, buf_b,
                 ad, nrm, low, inv, act, pre, win, wout, keep, send, gbo, gbi,
                 offs, pad, ad_s, nrm_s, low_s, inv_s, bias, bias_row, dwo, dwi, sems):
    s = pl.program_id(0)
    frames, width = tok.shape[1], tok.shape[2]
    taps = cw.shape[0]
    half = taps // 2
    wq = width // LANES
    h = win.shape[1] // 2
    copies = weight_copies(buf_a, 0, win, wout, bias, sems) + weight_copies(buf_b, 1, win, wout, bias, sems)

    @pl.when(s == 0)
    def _():
        for c in copies:
            c.start()
        place_items(n, meta, offs)
        offs[n + 2] = 0
        gbo[...] = jnp.zeros_like(gbo)
        pad[...] = jnp.zeros_like(pad)

    def flush(j):
        dst = pl.ds(pl.multiple_of(offs[j], 16), frames)
        for whole_ref, stage in ((ad, ad_s), (nrm, nrm_s), (low, low_s), (inv, inv_s)):
            whole_ref[dst, :] = stage[...]

    @pl.when(s > 0)
    def _():
        flush(s - 1)

    @pl.when(s == 1)
    def _():
        for c in copies:
            c.wait()
        spread_bias(bias, bias_row)
        dwo[...] = jnp.zeros_like(dwo)
        dwi[...] = jnp.zeros_like(dwi)
        gbi[...] = jnp.zeros_like(gbi)

    item = meta[0] * n + s
    count = meta[2 + item]
    group = meta[2 + 2 * n + item]

    def setup():
        rows = lax.broadcasted_iota(jnp.int32, (frames, LANES), 0)
        for q in range(wq):
            pad[q, PAD:PAD + frames, :] = jnp.where(rows < count, tok[0, :, lane(q)].astype(F32), 0.0)
        return pick(ns, group), pick(nsh, group), as_row(gamma), as_row(cb), cw[...].astype(F32)

    def conv_step(i, acc, consts):
        scale, shift, gam, conv_bias, w = consts
        r0 = i * CHUNK if isinstance(i, int) else pl.multiple_of(i * CHUNK, CHUNK)
        here = pl.ds(r0, CHUNK)
        live = (lax.broadcasted_iota(jnp.int32, (CHUNK, LANES), 0) + r0) < count
        convs = []
        for q in range(wq):
            conv = conv_bias[:, lane(q)]
            for k in range(taps):
                conv = conv + w[k:k + 1, lane(q)] * pad[q, pl.ds(r0 + (PAD - half + k), CHUNK), :]
            convs.append(conv)
        mean = jnp.sum(sum(convs[1:], convs[0]), axis=-1, keepdims=True) * (1.0 / width)
        cents = [c - mean for c in convs]
        sq = [c * c for c in cents]
        var = jnp.sum(sum(sq[1:], sq[0]), axis=-1, keepdims=True) * (1.0 / width)
        istd = lax.rsqrt(var + EPS)
        inv_s[here, :] = jnp.broadcast_to(istd, (CHUNK, LANES))
        new = []
        for q in range(wq):
            normed = cents[q] * istd
            ad_s[here, lane(q)] = (normed * scale[:, lane(q)] + shift[:, lane(q)]).astype(BF)
            nrm_s[here, lane(q)] = normed.astype(BF)
            back = jnp.where(live, cot[0, here, lane(q)].astype(F32), 0.0) * gam[:, lane(q)]
            low_s[here, lane(q)] = back.astype(BF)
            new.append(acc[q] + fold(back))
        return tuple(new)

    def add_gbo(accs):
        for q in range(wq):
            gbo[:, lane(q)] += accs[q]

    def tile(t, between=()):
        between = list(between)
        at = pl.ds(pl.multiple_of(t * TILE, TILE), TILE)
        a, b = ad[at, :], low[at, :]
        activation, slope = gelu_parts(dot(a, win[...]) + bias_row[...])
        if between:
            between.pop(0)()
        grad = dot_t(b, wout[...]) * slope
        lo = activation.astype(BF)
        act[at, :] = lo
        if between:
            between.pop(0)()
        dwo[...] += dot_rows(lo, b)
        gbi[...] += fold(grad)
        g = grad.astype(BF)
        pre[at, :] = g
        if between:
            between.pop(0)()
        dwi[...] += dot_rows(a, g)
        if between:
            between.pop(0)()

    done = offs[n + 2]
    ready = offs[s] >= (done + 1) * TILE
    none = (jnp.zeros((8, LANES), F32),) * wq

    @pl.when(ready)
    def _():
        consts = setup()
        state = [none]

        def part(lo_i, hi_i):
            def run():
                for i in range(lo_i, hi_i):
                    state[0] = conv_step(i, state[0], consts)
            return run

        count_c = frames // CHUNK
        cuts = [count_c * k // 4 for k in range(5)]
        tile(done, [part(cuts[k], cuts[k + 1]) for k in range(4)])
        add_gbo(state[0])
        offs[n + 2] = done + 1

    @pl.when(jnp.logical_not(ready))
    def _():
        consts = setup()
        add_gbo(lax.fori_loop(0, pl.cdiv(count, CHUNK), lambda i, acc: conv_step(i, acc, consts), none))

    @pl.when(s == n - 1)
    def _():
        flush(s)
        end = pl.ds(pl.multiple_of(offs[n], 16), TILE)
        ad[end, :] = jnp.zeros((TILE, width), BF)
        low[end, :] = jnp.zeros((TILE, width), BF)

        def rest(t, _):
            tile(t)
            return 0

        lax.fori_loop(offs[n + 2], offs[n + 1], rest, 0)
        for side, dst in ((0, keep), (1, send)):
            for q in range(wq):
                dst[q * h:(q + 1) * h, :] = dwo[side * h:(side + 1) * h, lane(q)].astype(dst.dtype)
            base = wq * h
            for q in range(h // LANES):
                dst[base + q * width:base + (q + 1) * width, :] = dwi[:, lane(side * (h // LANES) + q)].astype(dst.dtype)


def front(meta, tok, cot, cw, cb, ns, nsh, gamma, buf_a, buf_b, h):
    items, frames, width = tok.shape
    n = items // 2
    rows = n * frames + TILE
    packed = 2 * width * h // LANES
    wq, hq = width // LANES, h // LANES
    item = pl.BlockSpec((1, frames, width), lambda s, c: (c[0] * n + s, 0, 0))
    return pl.pallas_call(
        functools.partial(front_kernel, n),
        grid_spec=pltpu.PrefetchScalarGridSpec(
            num_scalar_prefetch=1, grid=(n,),
            in_specs=[item, item] + [whole(v.shape) for v in (cw, cb, ns, nsh, gamma)] + [hbm()] * 2,
            out_specs=[vmem()] * 12,
            scratch_shapes=[pltpu.SMEM((n + 3,), jnp.int32),
                            pltpu.VMEM((wq, frames + 4 * PAD, LANES), F32),
                            pltpu.VMEM((frames, width), BF), pltpu.VMEM((frames, width), BF),
                            pltpu.VMEM((frames, width), BF), pltpu.VMEM((frames, LANES), F32),
                            pltpu.VMEM((2, 16, LANES), BF), pltpu.VMEM((1, 2 * h), F32),
                            pltpu.VMEM((2 * h, width), F32), pltpu.VMEM((width, 2 * h), F32),
                            pltpu.SemaphoreType.DMA((2, hq + wq + 1))]),
        out_shape=[struct((rows, width), BF)] * 3 + [struct((rows, LANES), F32)]
        + [struct((rows, 2 * h), BF)] * 2 + [struct((width, 2 * h), BF), struct((2 * h, width), BF)]
        + [struct((packed, LANES), F32), struct((packed, LANES), BF), struct((8, width), F32), struct((8, 2 * h), F32)],
        compiler_params=params(), cost_estimate=cost(0),
    )(meta, tok, cot, cw, cb, ns, nsh, gamma, buf_a, buf_b)


def combine_kernel(dp, meta, keep, recv, stay, leave):
    m = keep.shape[0] // dp
    for d in range(dp):
        src = pl.ds(pl.multiple_of((meta[1] ^ d) * m, m), m)
        total = keep[src, :] + recv[src, :].astype(F32)
        dst = leave if d % 2 else stay
        dst[d // 2 * m:(d // 2 + 1) * m, :] = total.astype(dst.dtype)


def combine(meta, keep, recv, dp):
    rows = keep.shape[0] // 2
    return pl.pallas_call(
        functools.partial(combine_kernel, dp),
        in_specs=[smem(), vmem(), vmem()], out_specs=[vmem(), vmem()],
        out_shape=[struct((rows, LANES), F32), struct((rows, LANES), BF)],
        compiler_params=params())(meta, keep, recv)


def mix_kernel(n, meta, ad, low, act, pre, win1, wout1, bout, buf_c, buf_d, branch, ag,
               offs, win2, wout2, bias, bias_row, sems):
    copies = weight_copies(buf_c, 0, win2, wout2, bias, sems) + weight_copies(buf_d, 1, win2, wout2, bias, sems)
    for c in copies:
        c.start()
    place_items(n, meta, offs)
    for c in copies:
        c.wait()
    spread_bias(bias, bias_row)

    def tile(t, _):
        at = pl.ds(pl.multiple_of(t * TILE, TILE), TILE)
        a, b = ad[at, :], low[at, :]
        activation, slope = gelu_parts(dot(a, win2[...]) + bias_row[...])
        grad = dot_t(b, wout2[...]) * slope
        branch[at, :] = (dot(act[at, :], wout1[...]) + dot(activation.astype(BF), wout2[...])) + as_row(bout)
        ag[at, :] = dot_t(pre[at, :], win1[...]) + dot_t(grad.astype(BF), win2[...])
        return 0

    lax.fori_loop(0, offs[n + 1], tile, 0)


def mix(meta, ad, low, act, pre, win, wout, bout, buf_c, buf_d, n):
    rows, width = ad.shape
    h = act.shape[1] // 2
    wq, hq = width // LANES, h // LANES
    return pl.pallas_call(
        functools.partial(mix_kernel, n),
        in_specs=[smem()] + [vmem()] * 6 + [whole(bout.shape)] + [hbm()] * 2,
        out_specs=[vmem(), vmem()],
        scratch_shapes=[pltpu.SMEM((n + 2,), jnp.int32),
                        pltpu.VMEM((width, 2 * h), BF), pltpu.VMEM((2 * h, width), BF),
                        pltpu.VMEM((2, 16, LANES), BF), pltpu.VMEM((1, 2 * h), F32),
                        pltpu.SemaphoreType.DMA((2, hq + wq + 1))],
        out_shape=[struct((rows, width), F32)] * 2,
        compiler_params=params(), cost_estimate=cost(0),
    )(meta, ad, low, act, pre, win, wout, bout, buf_c, buf_d)


def norm_grad_kernel(n, meta, tok, cot, branch, ag, nrm, inv, gbo, gbi, cw, ns, gamma,
                     out, out_own, cgp, small_keep, small_send, offs, sums, sems):
    s = pl.program_id(0)
    frames, width = tok.shape[1], tok.shape[2]
    taps, rates = cw.shape[0], ns.shape[0]
    half = taps // 2
    wq = width // LANES
    h = gbi.shape[1] // 2

    def place(j):
        return pltpu.make_async_copy(out_own.at[j], out.at[meta[0] * n + j], sems.at[j])

    @pl.when(s == 0)
    def _():
        place_items(n, meta, offs)
        sums[...] = jnp.zeros_like(sums)

    item = meta[0] * n + s
    count = meta[2 + item]
    group = meta[2 + 2 * n + item]
    off = offs[s]
    scale = pick(ns, group)
    gam = as_row(gamma)
    zero = jnp.zeros((8, LANES), F32)
    steps = pl.cdiv(count, WIDE_CHUNK)

    def step(i, accs):
        r0 = pl.multiple_of(i * WIDE_CHUNK, WIDE_CHUNK)
        here = pl.ds(r0, WIDE_CHUNK)
        live = (lax.broadcasted_iota(jnp.int32, (WIDE_CHUNK, LANES), 0) + r0) < count
        src = pl.ds(pl.multiple_of(off + r0, 16), WIDE_CHUNK)
        new = []
        ngs, nrs = [], []
        for q in range(wq):
            a_ls, a_sc, a_sh = accs[3 * q:3 * q + 3]
            br = jnp.where(live, branch[src, lane(q)], 0.0)
            tk = jnp.where(live, tok[0, here, lane(q)].astype(F32), 0.0)
            out_own[s, here, lane(q)] = (tk + gam[:, lane(q)] * br).astype(BF)
            g = jnp.where(live, ag[src, lane(q)], 0.0)
            nr = nrm[src, lane(q)].astype(F32)
            new += [a_ls + fold(cot[0, here, lane(q)].astype(F32) * br), a_sc + fold(g * nr), a_sh + fold(g)]
            ngs.append(g * scale[:, lane(q)])
            nrs.append(nr)
        cross = [a * b for a, b in zip(ngs, nrs)]
        m1 = jnp.sum(sum(ngs[1:], ngs[0]), axis=-1, keepdims=True) * (1.0 / width)
        m2 = jnp.sum(sum(cross[1:], cross[0]), axis=-1, keepdims=True) * (1.0 / width)
        istd = inv[src, :]
        for q in range(wq):
            cg = istd * (ngs[q] - m1 - nrs[q] * m2)
            cgp[s, q, pl.ds(pl.multiple_of(r0 + PAD, 8), WIDE_CHUNK), :] = jnp.where(live, cg, 0.0)
        return tuple(new)

    accs = lax.fori_loop(0, steps, step, (zero,) * (3 * wq))
    for q in range(wq):
        sums[taps + 1, :, lane(q)] += accs[3 * q]
        sums[taps + 2 + group, :, lane(q)] += accs[3 * q + 1]
        sums[taps + 2 + rates + group, :, lane(q)] += accs[3 * q + 2]

    def clear(i, _):
        r0 = pl.multiple_of(i * WIDE_CHUNK, WIDE_CHUNK)
        out_own[s, pl.ds(r0, WIDE_CHUNK), :] = jnp.zeros((WIDE_CHUNK, width), BF)
        for q in range(wq):
            cgp[s, q, pl.ds(pl.multiple_of(r0 + PAD, 8), WIDE_CHUNK), :] = jnp.zeros((WIDE_CHUNK, LANES), F32)
        return 0

    lax.fori_loop(steps, frames // WIDE_CHUNK, clear, 0)
    place(s).start()
    for q in range(wq):
        cgp[s, q, :PAD, :] = jnp.zeros((PAD, LANES), F32)
        cgp[s, q, PAD + frames:, :] = jnp.zeros((cgp.shape[2] - PAD - frames, LANES), F32)

        def conv_step(i, accs):
            r0 = pl.multiple_of(i * WIDE_CHUNK, WIDE_CHUNK)
            here = pl.ds(r0, WIDE_CHUNK)
            live = (lax.broadcasted_iota(jnp.int32, (WIDE_CHUNK, LANES), 0) + r0) < count
            tk = jnp.where(live, tok[0, here, lane(q)].astype(F32), 0.0)
            new = []
            for k in range(taps):
                sh = cgp[s, q, pl.ds(r0 + (PAD + half - k), WIDE_CHUNK), :]
                new.append(accs[k] + fold(tk * sh))
                if k == half:
                    new_bias = accs[taps] + fold(sh)
            return tuple(new) + (new_bias,)

        accs = lax.fori_loop(0, steps, conv_step, (zero,) * (taps + 1))
        for k in range(taps + 1):
            sums[k, :, lane(q)] += accs[k]

    @pl.when(s == n - 1)
    def _():
        last = taps + 2 + 2 * rates
        rows = [jnp.sum(sums[i], axis=0, keepdims=True) for i in range(last)]
        rows.append(jnp.sum(gbo[...], axis=0, keepdims=True))
        gb = jnp.sum(gbi[...], axis=0, keepdims=True)
        fill = jnp.zeros((1, width - h), F32)
        spare = [jnp.zeros((1, width), F32)] * (small_keep.shape[0] - last - 2)
        for side, dst in ((0, small_keep), (1, small_send)):
            tail = [jnp.concatenate([gb[:, side * h:(side + 1) * h], fill], axis=1)]
            dst[...] = jnp.concatenate(rows + tail + spare, axis=0)
        for j in range(n):
            place(j).wait()


def norm_grad(meta, tok, cot, branch, ag, nrm, inv, gbo, gbi, cw, ns, gamma):
    items, frames, width = tok.shape
    n = items // 2
    wq = width // LANES
    taps, rates = cw.shape[0], ns.shape[0]
    n_small = -(-(taps + 4 + 2 * rates) // 8) * 8
    item = pl.BlockSpec((1, frames, width), lambda s, c: (c[0] * n + s, 0, 0))
    return pl.pallas_call(
        functools.partial(norm_grad_kernel, n),
        grid_spec=pltpu.PrefetchScalarGridSpec(
            num_scalar_prefetch=1, grid=(n,),
            in_specs=[item, item] + [vmem()] * 6 + [whole(v.shape) for v in (cw, ns, gamma)],
            out_specs=[hbm()] + [vmem()] * 4,
            scratch_shapes=[pltpu.SMEM((n + 2,), jnp.int32),
                            pltpu.VMEM((taps + 2 + 2 * rates, 8, width), F32),
                            pltpu.SemaphoreType.DMA((n,))]),
        out_shape=[struct((items, frames, width), BF), struct((n, frames, width), BF),
                   struct((n, wq, frames + 4 * PAD, LANES), F32)] + [struct((n_small, width), F32)] * 2,
        compiler_params=params(), cost_estimate=cost(40000000),
    )(meta, tok, cot, branch, ag, nrm, inv, gbo, gbi, cw, ns, gamma)


def token_grad_kernel(n, meta, cot, cgp, cw, other, out_in, out, gtok, gtok_own, stage, sems, out_sem):
    s = pl.program_id(0)
    frames, width = cot.shape[1], cot.shape[2]
    taps = cw.shape[0]
    half = taps // 2
    wq = width // LANES
    count = meta[2 + meta[0] * n + s]
    w = cw[...].astype(F32)
    steps = pl.cdiv(count, CHUNK)
    other_copy = pltpu.make_async_copy(other, out.at[pl.ds((1 - meta[0]) * n, n)], out_sem)

    def place(j):
        return pltpu.make_async_copy(stage.at[j], gtok.at[meta[0] * n + j], sems.at[j])

    @pl.when(s == 0)
    def _():
        other_copy.start()

    for q in range(wq):
        wl = w[:, lane(q)]

        def conv_step(i, _):
            r0 = pl.multiple_of(i * CHUNK, CHUNK)
            here = pl.ds(r0, CHUNK)
            live = (lax.broadcasted_iota(jnp.int32, (CHUNK, LANES), 0) + r0) < count
            total = cot[0, here, lane(q)].astype(F32)
            for k in range(taps):
                total = total + wl[k:k + 1] * cgp[s, q, pl.ds(r0 + (PAD + half - k), CHUNK), :]
            total = jnp.where(live, total, 0.0).astype(BF)
            gtok_own[s, here, lane(q)] = total
            stage[s, here, lane(q)] = total.astype(F32)
            return 0

        lax.fori_loop(0, steps, conv_step, 0)

    def clear(i, _):
        here = pl.ds(pl.multiple_of(i * CHUNK, CHUNK), CHUNK)
        gtok_own[s, here, :] = jnp.zeros((CHUNK, width), BF)
        stage[s, here, :] = jnp.zeros((CHUNK, width), F32)
        return 0

    lax.fori_loop(steps, frames // CHUNK, clear, 0)
    place(s).start()

    @pl.when(s == n - 1)
    def _():
        other_copy.wait()
        for j in range(n):
            place(j).wait()


def token_grad(meta, cot, cgp, cw, other, out):
    items, frames, width = cot.shape
    n = items // 2
    item = pl.BlockSpec((1, frames, width), lambda s, c: (c[0] * n + s, 0, 0))
    return pl.pallas_call(
        functools.partial(token_grad_kernel, n),
        grid_spec=pltpu.PrefetchScalarGridSpec(
            num_scalar_prefetch=1, grid=(n,),
            in_specs=[item, vmem(), whole(cw.shape), hbm(), hbm()], out_specs=[hbm(), hbm(), vmem()],
            scratch_shapes=[pltpu.VMEM((n, frames, width), F32), pltpu.SemaphoreType.DMA((n,)), pltpu.SemaphoreType.DMA]),
        out_shape=[struct(out.shape, BF), struct(out.shape, F32), struct((n, frames, width), BF)],
        input_output_aliases={5: 0},
        compiler_params=params(), cost_estimate=cost(40000000),
    )(meta, cot, cgp, cw, other, out)


def merge_kernel(n, meta, other, gtok_in, gtok, stage, sems):
    copies = [pltpu.make_async_copy(stage.at[j], gtok.at[(1 - meta[0]) * n + j], sems.at[j]) for j in range(n)]
    for j in range(n):
        stage[j] = other[j].astype(F32)
        copies[j].start()
    for c in copies:
        c.wait()


def merge(meta, other, gtok):
    n = other.shape[0]
    return pl.pallas_call(
        functools.partial(merge_kernel, n),
        in_specs=[smem(), vmem(), hbm()], out_specs=hbm(), out_shape=struct(gtok.shape, F32),
        scratch_shapes=[pltpu.VMEM(other.shape, F32), pltpu.SemaphoreType.DMA((n,))],
        input_output_aliases={2: 0},
        compiler_params=params(), cost_estimate=cost(20000000),
    )(meta, other, gtok)


def put_small(small, dst, base):
    high = small.astype(BF)
    low = (small - high.astype(F32)).astype(BF)
    rows = small.shape[0]
    dst[base:base + rows, :] = high
    dst[base + rows:base + 2 * rows, :] = low


def get_small(src, base):
    rows = (src.shape[0] - base) // 2
    return src[base:base + rows, :].astype(F32) + src[base + rows:base + 2 * rows, :].astype(F32)


def message_kernel(stay, keep, recv, *refs):
    pieces, out = refs[:-1], refs[-1]
    m = pieces[0].shape[0]
    total = stay[:m, :]
    for piece in pieces:
        total = total + piece[...].astype(F32)
    out[:m, :] = total.astype(BF)
    small = keep[...] + recv[...]
    put_small(jnp.concatenate([small[:, lane(q)] for q in range(small.shape[1] // LANES)], axis=0), out, m)


def make_message(stay, keep, recv, pieces):
    rows = pieces[0].shape[0] + 2 * keep.size // LANES
    return pl.pallas_call(message_kernel, in_specs=[vmem()] * (3 + len(pieces)), out_specs=vmem(),
                          out_shape=struct((rows, LANES), BF), compiler_params=params())(stay, keep, recv, *pieces)


def relay_kernel(m, *refs):
    sources, out = refs[:-1], refs[-1]
    sums = []
    for d, src in enumerate(sources):
        out[d * m:(d + 1) * m, :] = src[:m, :]
        sums.append(get_small(src, m))
    while len(sums) > 1:
        sums = [a + b for a, b in zip(sums[::2], sums[1::2])]
    put_small(sums[0], out, len(sources) * m)


def relay(m, sources):
    rows = len(sources) * m + sources[0].shape[0] - m
    return pl.pallas_call(functools.partial(relay_kernel, m), in_specs=[vmem()] * len(sources), out_specs=vmem(),
                          out_shape=struct((rows, LANES), BF), compiler_params=params())(*sources)


def unpack_kernel(dp, taps, rates, meta, near, far, gcw, gcb, gns, gnsh, gwi, gbi, gwo, gbo, gls, full):
    h, width = gwo.shape
    wq, hq = width // LANES, h // LANES
    m = full.shape[0] // dp
    for odd, mess in ((0, near), (1, far)):
        for d in range(dp // 2):
            at = pl.multiple_of((meta[1] ^ (2 * d + odd)) * m, m)
            full[pl.ds(at, m), :] = mess[d * m:(d + 1) * m, :].astype(F32)
    for q in range(wq):
        gwo[:, lane(q)] = full[q * h:(q + 1) * h, :]
    base = wq * h
    for q in range(hq):
        gwi[:, lane(q)] = full[base + q * width:base + (q + 1) * width, :]
    small = get_small(near, dp // 2 * m) + get_small(far, dp // 2 * m)
    rows = small.shape[0] // wq
    small = jnp.concatenate([small[q * rows:(q + 1) * rows] for q in range(wq)], axis=1)
    gcw[...] = small[:taps]
    gcb[...] = small[taps]
    gls[...] = small[taps + 1]
    gns[...] = small[taps + 2:taps + 2 + rates]
    gnsh[...] = small[taps + 2 + rates:taps + 2 + 2 * rates]
    at = taps + 2 + 2 * rates
    gbo[...] = small[at]
    gbi[...] = small[at + 1, :h]


def unpack(meta, near, far, dp, taps, rates, width, h):
    shapes = [(taps, width), (width,), (rates, width), (rates, width), (width, h), (h,), (h, width), (width,), (width,)]
    return pl.pallas_call(
        functools.partial(unpack_kernel, dp, taps, rates), in_specs=[smem(), vmem(), vmem()],
        out_shape=[struct(s, F32) for s in shapes],
        scratch_shapes=[pltpu.VMEM((2 * width * h // LANES, LANES), F32)],
        compiler_params=params())(meta, near, far)


def swap(x, step):
    size = lax.axis_size("tp")
    return lax.ppermute(x, "tp", [(i, i ^ step) for i in range(size)])


def across(x, step):
    size = lax.axis_size("dp")
    return lax.ppermute(x, "dp", [(i, i ^ step) for i in range(size)])


def per_device(tokens, frame_counts, rate_groups, conv_weight, conv_bias, norm_scale, norm_shift,
               weight_in, bias_in, weight_out, bias_out, layer_scale, cotangent):
    width, h = weight_in.shape
    n = tokens.shape[0] // 2
    (tokens, cotangent, conv_weight, conv_bias, norm_scale, norm_shift, weight_in, bias_in, weight_out, bias_out,
     layer_scale) = [pltpu.with_memory_space_constraint(v, pltpu.HBM) for v in (
         tokens, cotangent, conv_weight, conv_bias, norm_scale, norm_shift, weight_in, bias_in, weight_out, bias_out,
         layer_scale)]
    taps, rates = conv_weight.shape[0], norm_scale.shape[0]
    dp = lax.axis_size("dp")
    place = jnp.stack([lax.axis_index("tp") & 1, lax.axis_index("dp")]).astype(jnp.int32)
    meta = jnp.concatenate([place, frame_counts, rate_groups])

    buf_a = pack(weight_in, bias_in, weight_out)
    buf_b = swap(buf_a, 1)
    buf_c = swap(buf_a, 2)
    buf_d = swap(buf_c, 1)
    ad, nrm, low, inv, act, pre, win, wout, keep, send, gbo, gbi = front(
        meta, tokens, cotangent, conv_weight, conv_bias, norm_scale, norm_shift, layer_scale, buf_a, buf_b, h)
    stay, leave = combine(meta, keep, swap(send, 1), dp)
    arrived = across(leave, 1)
    branch, ag = mix(meta, ad, low, act, pre, win, wout, bias_out, buf_c, buf_d, n)
    arrived, branch = lax.optimization_barrier((arrived, branch))
    stay = (stay + arrived.astype(F32)).reshape(dp // 2, -1, LANES)
    pieces = [across(stay[d].astype(BF), 2 * d) for d in range(1, dp // 2)]

    out, out_own, cgp, small_keep, small_send = norm_grad(
        meta, tokens, cotangent, branch, ag, nrm, inv, gbo, gbi, conv_weight, norm_scale, layer_scale)
    pieces, small_send, out_own, cgp = lax.optimization_barrier((pieces, small_send, out_own, cgp))
    small_got = swap(small_send, 1)
    small_got, out_own = lax.optimization_barrier((small_got, out_own))
    message = make_message(stay.reshape(-1, LANES), small_keep, small_got, pieces)
    near = [message] + [across(message, 2 * d) for d in range(1, dp // 2)]
    out, gtok, gtok_own = token_grad(meta, cotangent, cgp, conv_weight, swap(out_own, 1), out)
    near, gtok_own = lax.optimization_barrier((near, gtok_own))
    near = relay(pieces[0].shape[0], near)
    far = across(near, 1)
    gtok = merge(meta, swap(gtok_own, 1), gtok)
    far, gtok = lax.optimization_barrier((far, gtok))
    gcw, gcb, gns, gnsh, gwi, gbi, gwo, gbo, gls = unpack(meta, near, far, dp, taps, rates, width, h)
    return (out, gtok, gcw, gcb, gns, gnsh, gwi, gbi, gwo, gbo, gls)


def solution(mesh):
    items, copied = P("dp", None, None), P()
    in_specs = (items, P("dp"), P("dp"), copied, copied, copied, copied, P(None, "tp"), P("tp"), P("tp", None),
                copied, copied, items)
    out_specs = (items, items, copied, copied, copied, copied, P(None, "tp"), P("tp"), P("tp", None), copied, copied)
    return jax.shard_map(per_device, mesh=mesh, in_specs=in_specs, out_specs=out_specs, check_vma=False)
```

```python
import functools

import jax
import jax.numpy as jnp
from jax import lax
from jax.experimental import pallas as pl
from jax.experimental.pallas import tpu as pltpu
from jax.sharding import PartitionSpec as P

EPS = 1e-06
BF, F32 = jnp.bfloat16, jnp.float32
TILE = 256
LANES = 128
PAD = 8
CHUNK = 64
WIDE_CHUNK = 128
VMEM_LIMIT = 12 * 1024 * 1024


def params(**more):
    return pltpu.CompilerParams(vmem_limit_bytes=VMEM_LIMIT, **more)


def struct(shape, dtype):
    return jax.ShapeDtypeStruct(shape, dtype)


def whole(shape):
    return pl.BlockSpec(shape, lambda *_: (0,) * len(shape))


def hbm():
    return pl.BlockSpec(memory_space=pltpu.HBM)


def smem():
    return pl.BlockSpec(memory_space=pltpu.SMEM)


def cost(size):
    return pl.CostEstimate(flops=0, transcendentals=0, bytes_accessed=size)


def vmem():
    return pl.BlockSpec(memory_space=pltpu.VMEM)


def lane(q):
    return slice(q * LANES, (q + 1) * LANES)


def fold(x):
    return jnp.sum(x.reshape(x.shape[0] // 8, 8, x.shape[1]), axis=0)


def pick(table, group):
    rows = table[...].astype(F32)
    value = rows[0:1]
    for r in range(1, rows.shape[0]):
        value = jnp.where(group == r, rows[r:r + 1], value)
    return value


def as_row(ref):
    return ref[...].astype(F32).reshape(1, -1)


def gelu_parts(pre):
    cdf = 0.5 + 0.5 * lax.erf(pre * 0.7071067811865476)
    density = jnp.exp(-0.5 * pre * pre) * 0.3989422804014327
    return pre * cdf, cdf + pre * density


def dot(a, b):
    return jnp.dot(a, b, preferred_element_type=F32)


def dot_t(a, b):
    return lax.dot_general(a, b, (((1,), (1,)), ((), ())), preferred_element_type=F32)


def dot_rows(a, b):
    return lax.dot_general(a, b, (((0,), (0,)), ((), ())), preferred_element_type=F32)


def place_items(n, meta, offs):
    end = jnp.int32(0)
    for j in range(n):
        offs[j] = end
        end = end + ((meta[2 + meta[0] * n + j] + 15) & -16)
    offs[n] = end
    offs[n + 1] = (end + TILE - 1) // TILE


def pack_kernel(n, wi, bi, wo, counts, groups, out, meta, counts_s, groups_s, sems):
    width, h = wi.shape
    hq, wq = h // LANES, width // LANES
    copies = [pltpu.make_async_copy(counts, counts_s, sems.at[0]), pltpu.make_async_copy(groups, groups_s, sems.at[1])]
    for c in copies:
        c.start()
    for q in range(hq):
        out[q * width:(q + 1) * width, :] = wi[:, lane(q)]
    base = hq * width
    for q in range(wq):
        out[base + q * h:base + (q + 1) * h, :] = wo[:, lane(q)]
    base += wq * h
    bias = bi[...].astype(F32).reshape(1, h)
    rows = [bias[:, lane(q)] for q in range(hq)] + [jnp.zeros((1, LANES), F32)] * (16 - hq)
    out[base:base + 16, :] = jnp.concatenate(rows, axis=0).astype(BF)
    meta[0] = lax.axis_index("tp") & 1
    meta[1] = lax.axis_index("dp")
    for c in copies:
        c.wait()
    for j in range(2 * n):
        meta[2 + j] = counts_s[j]
        meta[2 + 2 * n + j] = groups_s[j]


def pack(wi, bi, wo, counts, groups):
    rows = 2 * wi.size // LANES + 16
    items = counts.shape[0]
    return pl.pallas_call(
        functools.partial(pack_kernel, items // 2),
        in_specs=[whole(wi.shape), whole(bi.shape), whole(wo.shape), hbm(), hbm()],
        out_specs=[whole((rows, LANES)), smem()],
        out_shape=[struct((rows, LANES), BF), struct((2 + 2 * items,), jnp.int32)],
        scratch_shapes=[pltpu.SMEM((items,), jnp.int32), pltpu.SMEM((items,), jnp.int32), pltpu.SemaphoreType.DMA((2,))],
        compiler_params=params())(wi, bi, wo, counts, groups)


def weight_copies(buf, side, win, wout, bias, sems):
    width, h = win.shape[0], win.shape[1] // 2
    hq, wq = h // LANES, width // LANES
    copies = []
    for q in range(hq):
        at = side * h + q * LANES
        copies.append((buf.at[pl.ds(q * width, width), :], win.at[:, pl.ds(at, LANES)]))
    base = hq * width
    for q in range(wq):
        copies.append((buf.at[pl.ds(base + q * h, h), :], wout.at[pl.ds(side * h, h), pl.ds(q * LANES, LANES)]))
    copies.append((buf.at[pl.ds(base + wq * h, 16), :], bias.at[side]))
    return [pltpu.make_async_copy(src, dst, sems.at[side, i]) for i, (src, dst) in enumerate(copies)]


def spread_bias(bias, row):
    hq = row.shape[1] // LANES // 2
    for side in range(2):
        for q in range(hq):
            at = side * hq + q
            row[:, lane(at)] = bias[side, q:q + 1, :].astype(F32)


def front_kernel(n, meta, tok, cot, cw, cb, ns, nsh, gamma, buf_a, buf_b,
                 ad, nrm, low, inv, act, pre, win, wout, keep, send, gbo, gbi,
                 offs, pad, ad_s, nrm_s, low_s, inv_s, bias, bias_row, dwo, dwi, sems):
    s = pl.program_id(0)
    frames, width = tok.shape[1], tok.shape[2]
    taps = cw.shape[0]
    half = taps // 2
    wq = width // LANES
    h = win.shape[1] // 2
    copies = weight_copies(buf_a, 0, win, wout, bias, sems) + weight_copies(buf_b, 1, win, wout, bias, sems)

    @pl.when(s == 0)
    def _():
        for c in copies:
            c.start()
        place_items(n, meta, offs)
        offs[n + 2] = 0
        gbo[...] = jnp.zeros_like(gbo)
        pad[...] = jnp.zeros_like(pad)

    def flush(j):
        dst = pl.ds(pl.multiple_of(offs[j], 16), frames)
        for whole_ref, stage in ((ad, ad_s), (nrm, nrm_s), (low, low_s), (inv, inv_s)):
            whole_ref[dst, :] = stage[...]

    @pl.when(s > 0)
    def _():
        flush(s - 1)

    @pl.when(s == 1)
    def _():
        for c in copies:
            c.wait()
        spread_bias(bias, bias_row)
        dwo[...] = jnp.zeros_like(dwo)
        dwi[...] = jnp.zeros_like(dwi)
        gbi[...] = jnp.zeros_like(gbi)

    item = meta[0] * n + s
    count = meta[2 + item]
    group = meta[2 + 2 * n + item]

    def setup():
        rows = lax.broadcasted_iota(jnp.int32, (frames, LANES), 0)
        for q in range(wq):
            pad[q, PAD:PAD + frames, :] = jnp.where(rows < count, tok[0, :, lane(q)].astype(F32), 0.0)
        return pick(ns, group), pick(nsh, group), as_row(gamma), as_row(cb), cw[...].astype(F32)

    def conv_step(i, acc, consts):
        scale, shift, gam, conv_bias, w = consts
        r0 = i * CHUNK if isinstance(i, int) else pl.multiple_of(i * CHUNK, CHUNK)
        here = pl.ds(r0, CHUNK)
        live = (lax.broadcasted_iota(jnp.int32, (CHUNK, LANES), 0) + r0) < count
        convs = []
        for q in range(wq):
            conv = conv_bias[:, lane(q)]
            for k in range(taps):
                conv = conv + w[k:k + 1, lane(q)] * pad[q, pl.ds(r0 + (PAD - half + k), CHUNK), :]
            convs.append(conv)
        mean = jnp.sum(sum(convs[1:], convs[0]), axis=-1, keepdims=True) * (1.0 / width)
        cents = [c - mean for c in convs]
        sq = [c * c for c in cents]
        var = jnp.sum(sum(sq[1:], sq[0]), axis=-1, keepdims=True) * (1.0 / width)
        istd = lax.rsqrt(var + EPS)
        inv_s[here, :] = jnp.broadcast_to(istd, (CHUNK, LANES))
        new = []
        for q in range(wq):
            normed = cents[q] * istd
            ad_s[here, lane(q)] = (normed * scale[:, lane(q)] + shift[:, lane(q)]).astype(BF)
            nrm_s[here, lane(q)] = normed.astype(BF)
            back = jnp.where(live, cot[0, here, lane(q)].astype(F32), 0.0) * gam[:, lane(q)]
            low_s[here, lane(q)] = back.astype(BF)
            new.append(acc[q] + fold(back))
        return tuple(new)

    def add_gbo(accs):
        for q in range(wq):
            gbo[:, lane(q)] += accs[q]

    def tile(t, between=()):
        between = list(between)
        at = pl.ds(pl.multiple_of(t * TILE, TILE), TILE)
        a, b = ad[at, :], low[at, :]
        activation, slope = gelu_parts(dot(a, win[...]) + bias_row[...])
        if between:
            between.pop(0)()
        grad = dot_t(b, wout[...]) * slope
        lo = activation.astype(BF)
        act[at, :] = lo
        if between:
            between.pop(0)()
        dwo[...] += dot_rows(lo, b)
        gbi[...] += fold(grad)
        g = grad.astype(BF)
        pre[at, :] = g
        if between:
            between.pop(0)()
        dwi[...] += dot_rows(a, g)
        if between:
            between.pop(0)()

    done = offs[n + 2]
    ready = offs[s] >= (done + 1) * TILE
    none = (jnp.zeros((8, LANES), F32),) * wq

    @pl.when(ready)
    def _():
        consts = setup()
        state = [none]

        def part(lo_i, hi_i):
            def run():
                for i in range(lo_i, hi_i):
                    state[0] = conv_step(i, state[0], consts)
            return run

        count_c = frames // CHUNK
        cuts = [count_c * k // 4 for k in range(5)]
        tile(done, [part(cuts[k], cuts[k + 1]) for k in range(4)])
        add_gbo(state[0])
        offs[n + 2] = done + 1

    @pl.when(jnp.logical_not(ready))
    def _():
        consts = setup()
        add_gbo(lax.fori_loop(0, pl.cdiv(count, CHUNK), lambda i, acc: conv_step(i, acc, consts), none))

    @pl.when(s == n - 1)
    def _():
        flush(s)
        end = pl.ds(pl.multiple_of(offs[n], 16), TILE)
        ad[end, :] = jnp.zeros((TILE, width), BF)
        low[end, :] = jnp.zeros((TILE, width), BF)

        def rest(t, _):
            tile(t)
            return 0

        lax.fori_loop(offs[n + 2], offs[n + 1], rest, 0)
        for side, dst in ((0, keep), (1, send)):
            for q in range(wq):
                dst[q * h:(q + 1) * h, :] = dwo[side * h:(side + 1) * h, lane(q)].astype(dst.dtype)
            base = wq * h
            for q in range(h // LANES):
                dst[base + q * width:base + (q + 1) * width, :] = dwi[:, lane(side * (h // LANES) + q)].astype(dst.dtype)


def front(meta, tok, cot, cw, cb, ns, nsh, gamma, buf_a, buf_b, h):
    items, frames, width = tok.shape
    n = items // 2
    rows = n * frames + TILE
    packed = 2 * width * h // LANES
    wq, hq = width // LANES, h // LANES
    item = pl.BlockSpec((1, frames, width), lambda s, c: (c[0] * n + s, 0, 0))
    return pl.pallas_call(
        functools.partial(front_kernel, n),
        grid_spec=pltpu.PrefetchScalarGridSpec(
            num_scalar_prefetch=1, grid=(n,),
            in_specs=[item, item] + [whole(v.shape) for v in (cw, cb, ns, nsh, gamma)] + [hbm()] * 2,
            out_specs=[vmem()] * 12,
            scratch_shapes=[pltpu.SMEM((n + 3,), jnp.int32),
                            pltpu.VMEM((wq, frames + 4 * PAD, LANES), F32),
                            pltpu.VMEM((frames, width), BF), pltpu.VMEM((frames, width), BF),
                            pltpu.VMEM((frames, width), BF), pltpu.VMEM((frames, LANES), F32),
                            pltpu.VMEM((2, 16, LANES), BF), pltpu.VMEM((1, 2 * h), F32),
                            pltpu.VMEM((2 * h, width), F32), pltpu.VMEM((width, 2 * h), F32),
                            pltpu.SemaphoreType.DMA((2, hq + wq + 1))]),
        out_shape=[struct((rows, width), BF)] * 3 + [struct((rows, LANES), F32)]
        + [struct((rows, 2 * h), BF)] * 2 + [struct((width, 2 * h), BF), struct((2 * h, width), BF)]
        + [struct((packed, LANES), F32), struct((packed, LANES), BF), struct((8, width), F32), struct((8, 2 * h), F32)],
        compiler_params=params(), cost_estimate=cost(0),
    )(meta, tok, cot, cw, cb, ns, nsh, gamma, buf_a, buf_b)


def combine_kernel(dp, meta, keep, recv, stay, leave):
    m = keep.shape[0] // dp
    for d in range(dp):
        src = pl.ds(pl.multiple_of((meta[1] ^ d) * m, m), m)
        total = keep[src, :] + recv[src, :].astype(F32)
        dst = leave if d % 2 else stay
        dst[d // 2 * m:(d // 2 + 1) * m, :] = total.astype(dst.dtype)


def combine(meta, keep, recv, dp):
    rows = keep.shape[0] // 2
    return pl.pallas_call(
        functools.partial(combine_kernel, dp),
        in_specs=[smem(), vmem(), vmem()], out_specs=[vmem(), vmem()],
        out_shape=[struct((rows, LANES), F32), struct((rows, LANES), BF)],
        compiler_params=params())(meta, keep, recv)


def mix_kernel(n, meta, ad, low, act, pre, win1, wout1, bout, buf_c, buf_d, branch, ag,
               offs, win2, wout2, bias, bias_row, sems):
    copies = weight_copies(buf_c, 0, win2, wout2, bias, sems) + weight_copies(buf_d, 1, win2, wout2, bias, sems)
    for c in copies:
        c.start()
    place_items(n, meta, offs)
    for c in copies:
        c.wait()
    spread_bias(bias, bias_row)

    def tile(t, _):
        at = pl.ds(pl.multiple_of(t * TILE, TILE), TILE)
        a, b = ad[at, :], low[at, :]
        activation, slope = gelu_parts(dot(a, win2[...]) + bias_row[...])
        grad = dot_t(b, wout2[...]) * slope
        branch[at, :] = (dot(act[at, :], wout1[...]) + dot(activation.astype(BF), wout2[...])) + as_row(bout)
        ag[at, :] = dot_t(pre[at, :], win1[...]) + dot_t(grad.astype(BF), win2[...])
        return 0

    lax.fori_loop(0, offs[n + 1], tile, 0)


def mix(meta, ad, low, act, pre, win, wout, bout, buf_c, buf_d, n):
    rows, width = ad.shape
    h = act.shape[1] // 2
    wq, hq = width // LANES, h // LANES
    return pl.pallas_call(
        functools.partial(mix_kernel, n),
        in_specs=[smem()] + [vmem()] * 6 + [whole(bout.shape)] + [hbm()] * 2,
        out_specs=[vmem(), vmem()],
        scratch_shapes=[pltpu.SMEM((n + 2,), jnp.int32),
                        pltpu.VMEM((width, 2 * h), BF), pltpu.VMEM((2 * h, width), BF),
                        pltpu.VMEM((2, 16, LANES), BF), pltpu.VMEM((1, 2 * h), F32),
                        pltpu.SemaphoreType.DMA((2, hq + wq + 1))],
        out_shape=[struct((rows, width), F32)] * 2,
        compiler_params=params(), cost_estimate=cost(0),
    )(meta, ad, low, act, pre, win, wout, bout, buf_c, buf_d)


def norm_grad_kernel(n, meta, tok, cot, branch, ag, nrm, inv, gbo, gbi, cw, ns, gamma,
                     out, out_own, cgp, small_keep, small_send, offs, sums, sems):
    s = pl.program_id(0)
    frames, width = tok.shape[1], tok.shape[2]
    taps, rates = cw.shape[0], ns.shape[0]
    half = taps // 2
    wq = width // LANES
    h = gbi.shape[1] // 2

    def place(j):
        return pltpu.make_async_copy(out_own.at[j], out.at[meta[0] * n + j], sems.at[j])

    @pl.when(s == 0)
    def _():
        place_items(n, meta, offs)
        sums[...] = jnp.zeros_like(sums)

    item = meta[0] * n + s
    count = meta[2 + item]
    group = meta[2 + 2 * n + item]
    off = offs[s]
    scale = pick(ns, group)
    gam = as_row(gamma)
    zero = jnp.zeros((8, LANES), F32)
    steps = pl.cdiv(count, WIDE_CHUNK)

    def step(i, accs):
        r0 = pl.multiple_of(i * WIDE_CHUNK, WIDE_CHUNK)
        here = pl.ds(r0, WIDE_CHUNK)
        live = (lax.broadcasted_iota(jnp.int32, (WIDE_CHUNK, LANES), 0) + r0) < count
        src = pl.ds(pl.multiple_of(off + r0, 16), WIDE_CHUNK)
        new = []
        ngs, nrs = [], []
        for q in range(wq):
            a_ls, a_sc, a_sh = accs[3 * q:3 * q + 3]
            br = jnp.where(live, branch[src, lane(q)], 0.0)
            tk = jnp.where(live, tok[0, here, lane(q)].astype(F32), 0.0)
            out_own[s, here, lane(q)] = (tk + gam[:, lane(q)] * br).astype(BF)
            g = jnp.where(live, ag[src, lane(q)], 0.0)
            nr = nrm[src, lane(q)].astype(F32)
            new += [a_ls + fold(cot[0, here, lane(q)].astype(F32) * br), a_sc + fold(g * nr), a_sh + fold(g)]
            ngs.append(g * scale[:, lane(q)])
            nrs.append(nr)
        cross = [a * b for a, b in zip(ngs, nrs)]
        m1 = jnp.sum(sum(ngs[1:], ngs[0]), axis=-1, keepdims=True) * (1.0 / width)
        m2 = jnp.sum(sum(cross[1:], cross[0]), axis=-1, keepdims=True) * (1.0 / width)
        istd = inv[src, :]
        for q in range(wq):
            cg = istd * (ngs[q] - m1 - nrs[q] * m2)
            cgp[s, q, pl.ds(pl.multiple_of(r0 + PAD, 8), WIDE_CHUNK), :] = jnp.where(live, cg, 0.0)
        return tuple(new)

    accs = lax.fori_loop(0, steps, step, (zero,) * (3 * wq))
    for q in range(wq):
        sums[taps + 1, :, lane(q)] += accs[3 * q]
        sums[taps + 2 + group, :, lane(q)] += accs[3 * q + 1]
        sums[taps + 2 + rates + group, :, lane(q)] += accs[3 * q + 2]

    def clear(i, _):
        r0 = pl.multiple_of(i * WIDE_CHUNK, WIDE_CHUNK)
        out_own[s, pl.ds(r0, WIDE_CHUNK), :] = jnp.zeros((WIDE_CHUNK, width), BF)
        for q in range(wq):
            cgp[s, q, pl.ds(pl.multiple_of(r0 + PAD, 8), WIDE_CHUNK), :] = jnp.zeros((WIDE_CHUNK, LANES), F32)
        return 0

    lax.fori_loop(steps, frames // WIDE_CHUNK, clear, 0)
    place(s).start()
    for q in range(wq):
        cgp[s, q, :PAD, :] = jnp.zeros((PAD, LANES), F32)
        cgp[s, q, PAD + frames:, :] = jnp.zeros((cgp.shape[2] - PAD - frames, LANES), F32)

        def conv_step(i, accs):
            r0 = pl.multiple_of(i * WIDE_CHUNK, WIDE_CHUNK)
            here = pl.ds(r0, WIDE_CHUNK)
            live = (lax.broadcasted_iota(jnp.int32, (WIDE_CHUNK, LANES), 0) + r0) < count
            tk = jnp.where(live, tok[0, here, lane(q)].astype(F32), 0.0)
            new = []
            for k in range(taps):
                sh = cgp[s, q, pl.ds(r0 + (PAD + half - k), WIDE_CHUNK), :]
                new.append(accs[k] + fold(tk * sh))
                if k == half:
                    new_bias = accs[taps] + fold(sh)
            return tuple(new) + (new_bias,)

        accs = lax.fori_loop(0, steps, conv_step, (zero,) * (taps + 1))
        for k in range(taps + 1):
            sums[k, :, lane(q)] += accs[k]

    @pl.when(s == n - 1)
    def _():
        last = taps + 2 + 2 * rates
        rows = [jnp.sum(sums[i], axis=0, keepdims=True) for i in range(last)]
        rows.append(jnp.sum(gbo[...], axis=0, keepdims=True))
        gb = jnp.sum(gbi[...], axis=0, keepdims=True)
        fill = jnp.zeros((1, width - h), F32)
        spare = [jnp.zeros((1, width), F32)] * (small_keep.shape[0] - last - 2)
        for side, dst in ((0, small_keep), (1, small_send)):
            tail = [jnp.concatenate([gb[:, side * h:(side + 1) * h], fill], axis=1)]
            dst[...] = jnp.concatenate(rows + tail + spare, axis=0)
        for j in range(n):
            place(j).wait()


def norm_grad(meta, tok, cot, branch, ag, nrm, inv, gbo, gbi, cw, ns, gamma):
    items, frames, width = tok.shape
    n = items // 2
    wq = width // LANES
    taps, rates = cw.shape[0], ns.shape[0]
    n_small = -(-(taps + 4 + 2 * rates) // 8) * 8
    item = pl.BlockSpec((1, frames, width), lambda s, c: (c[0] * n + s, 0, 0))
    return pl.pallas_call(
        functools.partial(norm_grad_kernel, n),
        grid_spec=pltpu.PrefetchScalarGridSpec(
            num_scalar_prefetch=1, grid=(n,),
            in_specs=[item, item] + [vmem()] * 6 + [whole(v.shape) for v in (cw, ns, gamma)],
            out_specs=[hbm()] + [vmem()] * 4,
            scratch_shapes=[pltpu.SMEM((n + 2,), jnp.int32),
                            pltpu.VMEM((taps + 2 + 2 * rates, 8, width), F32),
                            pltpu.SemaphoreType.DMA((n,))]),
        out_shape=[struct((items, frames, width), BF), struct((n, frames, width), BF),
                   struct((n, wq, frames + 4 * PAD, LANES), F32)] + [struct((n_small, width), F32)] * 2,
        compiler_params=params(), cost_estimate=cost(40000000),
    )(meta, tok, cot, branch, ag, nrm, inv, gbo, gbi, cw, ns, gamma)


def token_grad_kernel(n, meta, cot, cgp, cw, other, out_in, out, gtok, gtok_own, stage, sems, out_sem):
    s = pl.program_id(0)
    frames, width = cot.shape[1], cot.shape[2]
    taps = cw.shape[0]
    half = taps // 2
    wq = width // LANES
    count = meta[2 + meta[0] * n + s]
    w = cw[...].astype(F32)
    steps = pl.cdiv(count, CHUNK)
    other_copy = pltpu.make_async_copy(other, out.at[pl.ds((1 - meta[0]) * n, n)], out_sem)

    def place(j):
        return pltpu.make_async_copy(stage.at[j], gtok.at[meta[0] * n + j], sems.at[j])

    @pl.when(s == 0)
    def _():
        other_copy.start()

    for q in range(wq):
        wl = w[:, lane(q)]

        def conv_step(i, _):
            r0 = pl.multiple_of(i * CHUNK, CHUNK)
            here = pl.ds(r0, CHUNK)
            live = (lax.broadcasted_iota(jnp.int32, (CHUNK, LANES), 0) + r0) < count
            total = cot[0, here, lane(q)].astype(F32)
            for k in range(taps):
                total = total + wl[k:k + 1] * cgp[s, q, pl.ds(r0 + (PAD + half - k), CHUNK), :]
            total = jnp.where(live, total, 0.0).astype(BF)
            gtok_own[s, here, lane(q)] = total
            stage[s, here, lane(q)] = total.astype(F32)
            return 0

        lax.fori_loop(0, steps, conv_step, 0)

    def clear(i, _):
        here = pl.ds(pl.multiple_of(i * CHUNK, CHUNK), CHUNK)
        gtok_own[s, here, :] = jnp.zeros((CHUNK, width), BF)
        stage[s, here, :] = jnp.zeros((CHUNK, width), F32)
        return 0

    lax.fori_loop(steps, frames // CHUNK, clear, 0)
    place(s).start()

    @pl.when(s == n - 1)
    def _():
        other_copy.wait()
        for j in range(n):
            place(j).wait()


def token_grad(meta, cot, cgp, cw, other, out):
    items, frames, width = cot.shape
    n = items // 2
    item = pl.BlockSpec((1, frames, width), lambda s, c: (c[0] * n + s, 0, 0))
    return pl.pallas_call(
        functools.partial(token_grad_kernel, n),
        grid_spec=pltpu.PrefetchScalarGridSpec(
            num_scalar_prefetch=1, grid=(n,),
            in_specs=[item, vmem(), whole(cw.shape), hbm(), hbm()], out_specs=[hbm(), hbm(), vmem()],
            scratch_shapes=[pltpu.VMEM((n, frames, width), F32), pltpu.SemaphoreType.DMA((n,)), pltpu.SemaphoreType.DMA]),
        out_shape=[struct(out.shape, BF), struct(out.shape, F32), struct((n, frames, width), BF)],
        input_output_aliases={5: 0},
        compiler_params=params(), cost_estimate=cost(40000000),
    )(meta, cot, cgp, cw, other, out)


def merge_kernel(n, meta, other, gtok_in, gtok, stage, sems):
    copies = [pltpu.make_async_copy(stage.at[j], gtok.at[(1 - meta[0]) * n + j], sems.at[j]) for j in range(n)]
    for j in range(n):
        stage[j] = other[j].astype(F32)
        copies[j].start()
    for c in copies:
        c.wait()


def merge(meta, other, gtok):
    n = other.shape[0]
    return pl.pallas_call(
        functools.partial(merge_kernel, n),
        in_specs=[smem(), vmem(), hbm()], out_specs=hbm(), out_shape=struct(gtok.shape, F32),
        scratch_shapes=[pltpu.VMEM(other.shape, F32), pltpu.SemaphoreType.DMA((n,))],
        input_output_aliases={2: 0},
        compiler_params=params(), cost_estimate=cost(20000000),
    )(meta, other, gtok)


def message_kernel(stay, keep, recv, *refs):
    pieces, (out, mine) = refs[:-2], refs[-2:]
    m = pieces[0].shape[0]
    total = stay[:m, :]
    for piece in pieces:
        total = total + piece[...].astype(F32)
    out[:m, :] = total.astype(BF)
    mine[...] = total.astype(BF)
    small = (keep[...] + recv[...]).astype(BF)
    rows = small.shape[0]
    for q in range(small.shape[1] // LANES):
        out[m + q * rows:m + (q + 1) * rows, :] = small[:, lane(q)]


def make_message(stay, keep, recv, pieces):
    rows = pieces[0].shape[0] + keep.size // LANES
    return pl.pallas_call(message_kernel, in_specs=[vmem()] * (3 + len(pieces)), out_specs=[vmem(), vmem()],
                          out_shape=[struct((rows, LANES), BF), struct(pieces[0].shape, BF)],
                          compiler_params=params())(stay, keep, recv, *pieces)


def relay_kernel(m, *refs):
    sources, out = refs[:-1], refs[-1]
    sums = []
    for d, src in enumerate(sources):
        if d > 0:
            out[(d - 1) * m:d * m, :] = src[:m, :]
        sums.append(src[m:, :].astype(F32))
    while len(sums) > 1:
        sums = [a + b for a, b in zip(sums[::2], sums[1::2])]
    out[(len(sources) - 1) * m:, :] = sums[0].astype(BF)


def relay(m, sources):
    rows = (len(sources) - 1) * m + sources[0].shape[0] - m
    return pl.pallas_call(functools.partial(relay_kernel, m), in_specs=[vmem()] * len(sources), out_specs=vmem(),
                          out_shape=struct((rows, LANES), BF), compiler_params=params())(*sources)


def unpack_kernel(dp, taps, rates, meta, mine, theirs, near, far, gcw, gcb, gns, gnsh, gwi, gbi, gwo, gbo, gls, full):
    h, width = gwo.shape
    wq, hq = width // LANES, h // LANES
    m = full.shape[0] // dp
    for odd, first, others in ((0, mine, near), (1, theirs, far)):
        for d in range(dp // 2):
            piece = others[(d - 1) * m:d * m, :] if d else first[:m, :]
            at = pl.multiple_of((meta[1] ^ (2 * d + odd)) * m, m)
            full[pl.ds(at, m), :] = piece.astype(F32)
    for q in range(wq):
        gwo[:, lane(q)] = full[q * h:(q + 1) * h, :]
    base = wq * h
    for q in range(hq):
        gwi[:, lane(q)] = full[base + q * width:base + (q + 1) * width, :]
    behind = (dp // 2 - 1) * m
    small = near[behind:, :].astype(F32) + far[behind:, :].astype(F32)
    rows = small.shape[0] // wq
    small = jnp.concatenate([small[q * rows:(q + 1) * rows] for q in range(wq)], axis=1)
    gcw[...] = small[:taps]
    gcb[...] = small[taps]
    gls[...] = small[taps + 1]
    gns[...] = small[taps + 2:taps + 2 + rates]
    gnsh[...] = small[taps + 2 + rates:taps + 2 + 2 * rates]
    at = taps + 2 + 2 * rates
    gbo[...] = small[at]
    gbi[...] = small[at + 1, :h]


def unpack(meta, mine, theirs, near, far, dp, taps, rates, width, h):
    shapes = [(taps, width), (width,), (rates, width), (rates, width), (width, h), (h,), (h, width), (width,), (width,)]
    return pl.pallas_call(
        functools.partial(unpack_kernel, dp, taps, rates), in_specs=[smem()] + [vmem()] * 4,
        out_shape=[struct(s, F32) for s in shapes],
        scratch_shapes=[pltpu.VMEM((2 * width * h // LANES, LANES), F32)],
        compiler_params=params())(meta, mine, theirs, near, far)


def swap(x, step):
    size = lax.axis_size("tp")
    return lax.ppermute(x, "tp", [(i, i ^ step) for i in range(size)])


def across(x, step):
    size = lax.axis_size("dp")
    return lax.ppermute(x, "dp", [(i, i ^ step) for i in range(size)])


def per_device(tokens, frame_counts, rate_groups, conv_weight, conv_bias, norm_scale, norm_shift,
               weight_in, bias_in, weight_out, bias_out, layer_scale, cotangent):
    width, h = weight_in.shape
    n = tokens.shape[0] // 2
    (tokens, cotangent, conv_weight, conv_bias, norm_scale, norm_shift, weight_in, bias_in, weight_out, bias_out,
     layer_scale, frame_counts, rate_groups) = [pltpu.with_memory_space_constraint(v, pltpu.HBM) for v in (
         tokens, cotangent, conv_weight, conv_bias, norm_scale, norm_shift, weight_in, bias_in, weight_out, bias_out,
         layer_scale, frame_counts, rate_groups)]
    taps, rates = conv_weight.shape[0], norm_scale.shape[0]
    dp = lax.axis_size("dp")
    buf_a, meta = pack(weight_in, bias_in, weight_out, frame_counts, rate_groups)
    buf_b = swap(buf_a, 1)
    buf_c = swap(buf_a, 2)
    buf_d = swap(buf_c, 1)
    ad, nrm, low, inv, act, pre, win, wout, keep, send, gbo, gbi = front(
        meta, tokens, cotangent, conv_weight, conv_bias, norm_scale, norm_shift, layer_scale, buf_a, buf_b, h)
    stay, leave = combine(meta, keep, swap(send, 1), dp)
    arrived = across(leave, 1)
    branch, ag = mix(meta, ad, low, act, pre, win, wout, bias_out, buf_c, buf_d, n)
    arrived, branch = lax.optimization_barrier((arrived, branch))
    stay = (stay + arrived.astype(F32)).reshape(dp // 2, -1, LANES)
    pieces = [across(stay[d].astype(BF), 2 * d) for d in range(1, dp // 2)]

    out, out_own, cgp, small_keep, small_send = norm_grad(
        meta, tokens, cotangent, branch, ag, nrm, inv, gbo, gbi, conv_weight, norm_scale, layer_scale)
    pieces, small_send, out_own, cgp = lax.optimization_barrier((pieces, small_send, out_own, cgp))
    small_got = swap(small_send, 1)
    small_got, out_own = lax.optimization_barrier((small_got, out_own))
    message, mine = make_message(stay.reshape(-1, LANES), small_keep, small_got, pieces)
    m = pieces[0].shape[0]
    near = [message] + [across(message, 2 * d) for d in range(1, dp // 2)]
    theirs = across(mine, 1)
    out, gtok, gtok_own = token_grad(meta, cotangent, cgp, conv_weight, swap(out_own, 1), out)
    near, theirs, gtok_own = lax.optimization_barrier((near, theirs, gtok_own))
    near = relay(m, near)
    far = across(near, 1)
    gtok = merge(meta, swap(gtok_own, 1), gtok)
    far, gtok = lax.optimization_barrier((far, gtok))
    gcw, gcb, gns, gnsh, gwi, gbi, gwo, gbo, gls = unpack(meta, mine, theirs, near, far, dp, taps, rates, width, h)
    return (out, gtok, gcw, gcb, gns, gnsh, gwi, gbi, gwo, gbo, gls)


def solution(mesh):
    items, copied = P("dp", None, None), P()
    in_specs = (items, P("dp"), P("dp"), copied, copied, copied, copied, P(None, "tp"), P("tp"), P("tp", None),
                copied, copied, items)
    out_specs = (items, items, copied, copied, copied, copied, P(None, "tp"), P("tp"), P("tp", None), copied, copied)
    return jax.shard_map(per_device, mesh=mesh, in_specs=in_specs, out_specs=out_specs, check_vma=False)
```

```python
import functools

import jax
import jax.numpy as jnp
from jax import lax
from jax.experimental import pallas as pl
from jax.experimental.pallas import tpu as pltpu
from jax.sharding import PartitionSpec as P

EPS = 1e-06
BF, F32 = jnp.bfloat16, jnp.float32
TILE = 256
LANES = 128
PAD = 8
CHUNK = 64
WIDE_CHUNK = 128
VMEM_LIMIT = 12 * 1024 * 1024


def params(**more):
    return pltpu.CompilerParams(vmem_limit_bytes=VMEM_LIMIT, **more)


def struct(shape, dtype):
    return jax.ShapeDtypeStruct(shape, dtype)


def whole(shape):
    return pl.BlockSpec(shape, lambda *_: (0,) * len(shape))


def hbm():
    return pl.BlockSpec(memory_space=pltpu.HBM)


def smem():
    return pl.BlockSpec(memory_space=pltpu.SMEM)


def cost(size):
    return pl.CostEstimate(flops=0, transcendentals=0, bytes_accessed=size)


def vmem():
    return pl.BlockSpec(memory_space=pltpu.VMEM)


def lane(q):
    return slice(q * LANES, (q + 1) * LANES)


def fold(x):
    return jnp.sum(x.reshape(x.shape[0] // 8, 8, x.shape[1]), axis=0)


def pick(table, group):
    rows = table[...].astype(F32)
    value = rows[0:1]
    for r in range(1, rows.shape[0]):
        value = jnp.where(group == r, rows[r:r + 1], value)
    return value


def as_row(ref):
    return ref[...].astype(F32).reshape(1, -1)


def gelu_parts(pre):
    cdf = 0.5 + 0.5 * lax.erf(pre * 0.7071067811865476)
    density = jnp.exp(-0.5 * pre * pre) * 0.3989422804014327
    return pre * cdf, cdf + pre * density


def dot(a, b):
    return jnp.dot(a, b, preferred_element_type=F32)


def dot_t(a, b):
    return lax.dot_general(a, b, (((1,), (1,)), ((), ())), preferred_element_type=F32)


def dot_rows(a, b):
    return lax.dot_general(a, b, (((0,), (0,)), ((), ())), preferred_element_type=F32)


def place_items(n, meta, offs):
    end = jnp.int32(0)
    for j in range(n):
        offs[j] = end
        end = end + ((meta[2 + meta[0] * n + j] + 15) & -16)
    offs[n] = end
    offs[n + 1] = (end + TILE - 1) // TILE


def pack_kernel(wi, bi, wo, out):
    width, h = wi.shape
    hq, wq = h // LANES, width // LANES
    for q in range(hq):
        out[q * width:(q + 1) * width, :] = wi[:, lane(q)]
    base = hq * width
    for q in range(wq):
        out[base + q * h:base + (q + 1) * h, :] = wo[:, lane(q)]
    base += wq * h
    bias = bi[...].astype(F32).reshape(1, h)
    rows = [bias[:, lane(q)] for q in range(hq)] + [jnp.zeros((1, LANES), F32)] * (16 - hq)
    out[base:base + 16, :] = jnp.concatenate(rows, axis=0).astype(BF)


def pack(wi, bi, wo):
    rows = 2 * wi.size // LANES + 16
    return pl.pallas_call(pack_kernel, out_shape=struct((rows, LANES), BF),
                          compiler_params=params())(wi, bi, wo)


def weight_copies(buf, side, win, wout, bias, sems):
    width, h = win.shape[0], win.shape[1] // 2
    hq, wq = h // LANES, width // LANES
    copies = []
    for q in range(hq):
        at = side * h + q * LANES
        copies.append((buf.at[pl.ds(q * width, width), :], win.at[:, pl.ds(at, LANES)]))
    base = hq * width
    for q in range(wq):
        copies.append((buf.at[pl.ds(base + q * h, h), :], wout.at[pl.ds(side * h, h), pl.ds(q * LANES, LANES)]))
    copies.append((buf.at[pl.ds(base + wq * h, 16), :], bias.at[side]))
    return [pltpu.make_async_copy(src, dst, sems.at[side, i]) for i, (src, dst) in enumerate(copies)]


def spread_bias(bias, row):
    hq = row.shape[1] // LANES // 2
    for side in range(2):
        for q in range(hq):
            at = side * hq + q
            row[:, lane(at)] = bias[side, q:q + 1, :].astype(F32)


def front_kernel(n, meta, tok_hbm, cot_hbm, cw, cb, ns, nsh, gamma, bout, buf_a, buf_b,
                 ad, nrm, low, inv, act, pre, win, wout, keep, send, gbo, gbi, tok, cot, consts,
                 offs, pad, ad_s, nrm_s, low_s, inv_s, bias, bias_row, dwo, dwi, sems, item_sems):
    s = pl.program_id(0)
    frames, width = tok.shape[1], tok.shape[2]
    taps, rates = cw.shape[0], ns.shape[0]
    half = taps // 2
    wq = width // LANES
    h = win.shape[1] // 2
    copies = weight_copies(buf_a, 0, win, wout, bias, sems) + weight_copies(buf_b, 1, win, wout, bias, sems)

    def fetch(j):
        at = meta[0] * n + j
        return [pltpu.make_async_copy(src.at[at], dst.at[j], item_sems.at[i, j])
                for i, (src, dst) in enumerate(((tok_hbm, tok), (cot_hbm, cot)))]

    @pl.when(s == 0)
    def _():
        for c in fetch(0) + fetch(1):
            c.start()
        for c in copies:
            c.start()
        for j in range(2, n):
            for c in fetch(j):
                c.start()
        consts[...] = jnp.zeros_like(consts)
        consts[:taps, :] = cw[...].astype(F32)
        consts[taps:taps + 1, :] = as_row(gamma)
        consts[taps + 1:taps + 2, :] = as_row(bout)
        consts[taps + 2:taps + 2 + rates, :] = ns[...].astype(F32)
        place_items(n, meta, offs)
        offs[n + 2] = 0
        gbo[...] = jnp.zeros_like(gbo)
        pad[...] = jnp.zeros_like(pad)

    def flush(j):
        dst = pl.ds(pl.multiple_of(offs[j], 16), frames)
        for whole_ref, stage in ((ad, ad_s), (nrm, nrm_s), (low, low_s), (inv, inv_s)):
            whole_ref[dst, :] = stage[...]

    @pl.when(s > 0)
    def _():
        flush(s - 1)

    @pl.when(s == 1)
    def _():
        for c in copies:
            c.wait()
        spread_bias(bias, bias_row)
        dwo[...] = jnp.zeros_like(dwo)
        dwi[...] = jnp.zeros_like(dwi)
        gbi[...] = jnp.zeros_like(gbi)

    for c in fetch(s):
        c.wait()
    item = meta[0] * n + s
    count = meta[2 + item]
    group = meta[2 + 2 * n + item]

    def setup():
        rows = lax.broadcasted_iota(jnp.int32, (frames, LANES), 0)
        for q in range(wq):
            pad[q, PAD:PAD + frames, :] = jnp.where(rows < count, tok[s, :, lane(q)].astype(F32), 0.0)
        return pick(ns, group), pick(nsh, group), as_row(gamma), as_row(cb), cw[...].astype(F32)

    def conv_step(i, acc, consts):
        scale, shift, gam, conv_bias, w = consts
        r0 = i * CHUNK if isinstance(i, int) else pl.multiple_of(i * CHUNK, CHUNK)
        here = pl.ds(r0, CHUNK)
        live = (lax.broadcasted_iota(jnp.int32, (CHUNK, LANES), 0) + r0) < count
        convs = []
        for q in range(wq):
            conv = conv_bias[:, lane(q)]
            for k in range(taps):
                conv = conv + w[k:k + 1, lane(q)] * pad[q, pl.ds(r0 + (PAD - half + k), CHUNK), :]
            convs.append(conv)
        mean = jnp.sum(sum(convs[1:], convs[0]), axis=-1, keepdims=True) * (1.0 / width)
        cents = [c - mean for c in convs]
        sq = [c * c for c in cents]
        var = jnp.sum(sum(sq[1:], sq[0]), axis=-1, keepdims=True) * (1.0 / width)
        istd = lax.rsqrt(var + EPS)
        inv_s[here, :] = jnp.broadcast_to(istd, (CHUNK, LANES))
        new = []
        for q in range(wq):
            normed = cents[q] * istd
            ad_s[here, lane(q)] = (normed * scale[:, lane(q)] + shift[:, lane(q)]).astype(BF)
            nrm_s[here, lane(q)] = normed.astype(BF)
            back = jnp.where(live, cot[s, here, lane(q)].astype(F32), 0.0) * gam[:, lane(q)]
            low_s[here, lane(q)] = back.astype(BF)
            new.append(acc[q] + fold(back))
        return tuple(new)

    def add_gbo(accs):
        for q in range(wq):
            gbo[:, lane(q)] += accs[q]

    def tile(t, between=()):
        between = list(between)
        at = pl.ds(pl.multiple_of(t * TILE, TILE), TILE)
        a, b = ad[at, :], low[at, :]
        activation, slope = gelu_parts(dot(a, win[...]) + bias_row[...])
        if between:
            between.pop(0)()
        grad = dot_t(b, wout[...]) * slope
        lo = activation.astype(BF)
        act[at, :] = lo
        if between:
            between.pop(0)()
        dwo[...] += dot_rows(lo, b)
        gbi[...] += fold(grad)
        g = grad.astype(BF)
        pre[at, :] = g
        if between:
            between.pop(0)()
        dwi[...] += dot_rows(a, g)
        if between:
            between.pop(0)()

    done = offs[n + 2]
    ready = offs[s] >= (done + 1) * TILE
    none = (jnp.zeros((8, LANES), F32),) * wq

    @pl.when(ready)
    def _():
        consts = setup()
        state = [none]

        def part(lo_i, hi_i):
            def run():
                for i in range(lo_i, hi_i):
                    state[0] = conv_step(i, state[0], consts)
            return run

        count_c = frames // CHUNK
        cuts = [count_c * k // 4 for k in range(5)]
        tile(done, [part(cuts[k], cuts[k + 1]) for k in range(4)])
        add_gbo(state[0])
        offs[n + 2] = done + 1

    @pl.when(jnp.logical_not(ready))
    def _():
        consts = setup()
        add_gbo(lax.fori_loop(0, pl.cdiv(count, CHUNK), lambda i, acc: conv_step(i, acc, consts), none))

    @pl.when(s == n - 1)
    def _():
        flush(s)
        end = pl.ds(pl.multiple_of(offs[n], 16), TILE)
        ad[end, :] = jnp.zeros((TILE, width), BF)
        low[end, :] = jnp.zeros((TILE, width), BF)

        def rest(t, _):
            tile(t)
            return 0

        lax.fori_loop(offs[n + 2], offs[n + 1], rest, 0)
        for side, dst in ((0, keep), (1, send)):
            for q in range(wq):
                dst[q * h:(q + 1) * h, :] = dwo[side * h:(side + 1) * h, lane(q)].astype(dst.dtype)
            base = wq * h
            for q in range(h // LANES):
                dst[base + q * width:base + (q + 1) * width, :] = dwi[:, lane(side * (h // LANES) + q)].astype(dst.dtype)


def front(meta, tok, cot, cw, cb, ns, nsh, gamma, bout, buf_a, buf_b, h):
    items, frames, width = tok.shape
    n = items // 2
    rows = n * frames + TILE
    packed = 2 * width * h // LANES
    wq, hq = width // LANES, h // LANES
    n_consts = -(-(cw.shape[0] + 2 + ns.shape[0]) // 8) * 8
    return pl.pallas_call(
        functools.partial(front_kernel, n),
        grid_spec=pltpu.PrefetchScalarGridSpec(
            num_scalar_prefetch=1, grid=(n,),
            in_specs=[hbm()] * 2 + [whole(v.shape) for v in (cw, cb, ns, nsh, gamma, bout)] + [hbm()] * 2,
            out_specs=[vmem()] * 15,
            scratch_shapes=[pltpu.SMEM((n + 3,), jnp.int32),
                            pltpu.VMEM((wq, frames + 4 * PAD, LANES), F32),
                            pltpu.VMEM((frames, width), BF), pltpu.VMEM((frames, width), BF),
                            pltpu.VMEM((frames, width), BF), pltpu.VMEM((frames, LANES), F32),
                            pltpu.VMEM((2, 16, LANES), BF), pltpu.VMEM((1, 2 * h), F32),
                            pltpu.VMEM((2 * h, width), F32), pltpu.VMEM((width, 2 * h), F32),
                            pltpu.SemaphoreType.DMA((2, hq + wq + 1)), pltpu.SemaphoreType.DMA((2, n))]),
        out_shape=[struct((rows, width), BF)] * 3 + [struct((rows, LANES), F32)]
        + [struct((rows, 2 * h), BF)] * 2 + [struct((width, 2 * h), BF), struct((2 * h, width), BF)]
        + [struct((packed, LANES), F32), struct((packed, LANES), BF), struct((8, width), F32), struct((8, 2 * h), F32)]
        + [struct((n, frames, width), BF)] * 2 + [struct((n_consts, width), F32)],
        compiler_params=params(), cost_estimate=cost(0),
    )(meta, tok, cot, cw, cb, ns, nsh, gamma, bout, buf_a, buf_b)


def combine_kernel(dp, meta, keep, recv, stay, leave):
    m = keep.shape[0] // dp
    for d in range(dp):
        src = pl.ds(pl.multiple_of((meta[1] ^ d) * m, m), m)
        total = keep[src, :] + recv[src, :].astype(F32)
        dst = leave if d % 2 else stay
        dst[d // 2 * m:(d // 2 + 1) * m, :] = total.astype(dst.dtype)


def combine(meta, keep, recv, dp):
    rows = keep.shape[0] // 2
    return pl.pallas_call(
        functools.partial(combine_kernel, dp),
        in_specs=[smem(), vmem(), vmem()], out_specs=[vmem(), vmem()],
        out_shape=[struct((rows, LANES), F32), struct((rows, LANES), BF)],
        compiler_params=params())(meta, keep, recv)


def mix_kernel(n, taps, meta, ad, low, act, pre, win1, wout1, consts, buf_c, buf_d, branch, ag,
               offs, win2, wout2, bias, bias_row, sems):
    copies = weight_copies(buf_c, 0, win2, wout2, bias, sems) + weight_copies(buf_d, 1, win2, wout2, bias, sems)
    for c in copies:
        c.start()
    place_items(n, meta, offs)
    for c in copies:
        c.wait()
    spread_bias(bias, bias_row)

    def tile(t, _):
        at = pl.ds(pl.multiple_of(t * TILE, TILE), TILE)
        a, b = ad[at, :], low[at, :]
        activation, slope = gelu_parts(dot(a, win2[...]) + bias_row[...])
        grad = dot_t(b, wout2[...]) * slope
        branch[at, :] = (dot(act[at, :], wout1[...]) + dot(activation.astype(BF), wout2[...])) + consts[taps + 1:taps + 2, :]
        ag[at, :] = dot_t(pre[at, :], win1[...]) + dot_t(grad.astype(BF), win2[...])
        return 0

    lax.fori_loop(0, offs[n + 1], tile, 0)


def mix(meta, ad, low, act, pre, win, wout, consts, buf_c, buf_d, n, taps):
    rows, width = ad.shape
    h = act.shape[1] // 2
    wq, hq = width // LANES, h // LANES
    return pl.pallas_call(
        functools.partial(mix_kernel, n, taps),
        in_specs=[smem()] + [vmem()] * 7 + [hbm()] * 2,
        out_specs=[vmem(), vmem()],
        scratch_shapes=[pltpu.SMEM((n + 2,), jnp.int32),
                        pltpu.VMEM((width, 2 * h), BF), pltpu.VMEM((2 * h, width), BF),
                        pltpu.VMEM((2, 16, LANES), BF), pltpu.VMEM((1, 2 * h), F32),
                        pltpu.SemaphoreType.DMA((2, hq + wq + 1))],
        out_shape=[struct((rows, width), F32)] * 2,
        compiler_params=params(), cost_estimate=cost(0),
    )(meta, ad, low, act, pre, win, wout, consts, buf_c, buf_d)


def norm_grad_kernel(n, taps, rates, meta, tok, cot, branch, ag, nrm, inv, gbo, gbi, consts,
                     out, out_own, cgp, small_keep, small_send, offs, sums, sems):
    s = pl.program_id(0)
    frames, width = tok.shape[1], tok.shape[2]
    half = taps // 2
    wq = width // LANES
    h = gbi.shape[1] // 2

    def place(j):
        return pltpu.make_async_copy(out_own.at[j], out.at[meta[0] * n + j], sems.at[j])

    @pl.when(s == 0)
    def _():
        place_items(n, meta, offs)
        sums[...] = jnp.zeros_like(sums)

    item = meta[0] * n + s
    count = meta[2 + item]
    group = meta[2 + 2 * n + item]
    off = offs[s]
    scale = pick(consts.at[taps + 2:taps + 2 + rates], group)
    gam = consts[taps:taps + 1, :]
    zero = jnp.zeros((8, LANES), F32)
    steps = pl.cdiv(count, WIDE_CHUNK)

    def step(i, accs):
        r0 = pl.multiple_of(i * WIDE_CHUNK, WIDE_CHUNK)
        here = pl.ds(r0, WIDE_CHUNK)
        live = (lax.broadcasted_iota(jnp.int32, (WIDE_CHUNK, LANES), 0) + r0) < count
        src = pl.ds(pl.multiple_of(off + r0, 16), WIDE_CHUNK)
        new = []
        ngs, nrs = [], []
        for q in range(wq):
            a_ls, a_sc, a_sh = accs[3 * q:3 * q + 3]
            br = jnp.where(live, branch[src, lane(q)], 0.0)
            tk = jnp.where(live, tok[s, here, lane(q)].astype(F32), 0.0)
            out_own[s, here, lane(q)] = (tk + gam[:, lane(q)] * br).astype(BF)
            g = jnp.where(live, ag[src, lane(q)], 0.0)
            nr = nrm[src, lane(q)].astype(F32)
            new += [a_ls + fold(cot[s, here, lane(q)].astype(F32) * br), a_sc + fold(g * nr), a_sh + fold(g)]
            ngs.append(g * scale[:, lane(q)])
            nrs.append(nr)
        cross = [a * b for a, b in zip(ngs, nrs)]
        m1 = jnp.sum(sum(ngs[1:], ngs[0]), axis=-1, keepdims=True) * (1.0 / width)
        m2 = jnp.sum(sum(cross[1:], cross[0]), axis=-1, keepdims=True) * (1.0 / width)
        istd = inv[src, :]
        for q in range(wq):
            cg = istd * (ngs[q] - m1 - nrs[q] * m2)
            cgp[s, q, pl.ds(pl.multiple_of(r0 + PAD, 8), WIDE_CHUNK), :] = jnp.where(live, cg, 0.0)
        return tuple(new)

    accs = lax.fori_loop(0, steps, step, (zero,) * (3 * wq))
    for q in range(wq):
        sums[taps + 1, :, lane(q)] += accs[3 * q]
        sums[taps + 2 + group, :, lane(q)] += accs[3 * q + 1]
        sums[taps + 2 + rates + group, :, lane(q)] += accs[3 * q + 2]

    def clear(i, _):
        r0 = pl.multiple_of(i * WIDE_CHUNK, WIDE_CHUNK)
        out_own[s, pl.ds(r0, WIDE_CHUNK), :] = jnp.zeros((WIDE_CHUNK, width), BF)
        for q in range(wq):
            cgp[s, q, pl.ds(pl.multiple_of(r0 + PAD, 8), WIDE_CHUNK), :] = jnp.zeros((WIDE_CHUNK, LANES), F32)
        return 0

    lax.fori_loop(steps, frames // WIDE_CHUNK, clear, 0)
    place(s).start()
    for q in range(wq):
        cgp[s, q, :PAD, :] = jnp.zeros((PAD, LANES), F32)
        cgp[s, q, PAD + frames:, :] = jnp.zeros((cgp.shape[2] - PAD - frames, LANES), F32)

        def conv_step(i, accs):
            r0 = pl.multiple_of(i * WIDE_CHUNK, WIDE_CHUNK)
            here = pl.ds(r0, WIDE_CHUNK)
            live = (lax.broadcasted_iota(jnp.int32, (WIDE_CHUNK, LANES), 0) + r0) < count
            tk = jnp.where(live, tok[s, here, lane(q)].astype(F32), 0.0)
            new = []
            for k in range(taps):
                sh = cgp[s, q, pl.ds(r0 + (PAD + half - k), WIDE_CHUNK), :]
                new.append(accs[k] + fold(tk * sh))
                if k == half:
                    new_bias = accs[taps] + fold(sh)
            return tuple(new) + (new_bias,)

        accs = lax.fori_loop(0, steps, conv_step, (zero,) * (taps + 1))
        for k in range(taps + 1):
            sums[k, :, lane(q)] += accs[k]

    @pl.when(s == n - 1)
    def _():
        last = taps + 2 + 2 * rates
        rows = [jnp.sum(sums[i], axis=0, keepdims=True) for i in range(last)]
        rows.append(jnp.sum(gbo[...], axis=0, keepdims=True))
        gb = jnp.sum(gbi[...], axis=0, keepdims=True)
        fill = jnp.zeros((1, width - h), F32)
        spare = [jnp.zeros((1, width), F32)] * (small_keep.shape[0] - last - 2)
        for side, dst in ((0, small_keep), (1, small_send)):
            tail = [jnp.concatenate([gb[:, side * h:(side + 1) * h], fill], axis=1)]
            dst[...] = jnp.concatenate(rows + tail + spare, axis=0)
        for j in range(n):
            place(j).wait()


def norm_grad(meta, tok, cot, branch, ag, nrm, inv, gbo, gbi, consts, taps, rates):
    n, frames, width = tok.shape
    wq = width // LANES
    n_small = -(-(taps + 4 + 2 * rates) // 8) * 8
    return pl.pallas_call(
        functools.partial(norm_grad_kernel, n, taps, rates), grid=(n,),
        in_specs=[smem()] + [vmem()] * 9, out_specs=[hbm()] + [vmem()] * 4,
        scratch_shapes=[pltpu.SMEM((n + 2,), jnp.int32),
                        pltpu.VMEM((taps + 2 + 2 * rates, 8, width), F32),
                        pltpu.SemaphoreType.DMA((n,))],
        out_shape=[struct((2 * n, frames, width), BF), struct((n, frames, width), BF),
                   struct((n, wq, frames + 4 * PAD, LANES), F32)] + [struct((n_small, width), F32)] * 2,
        compiler_params=params(), cost_estimate=cost(40000000),
    )(meta, tok, cot, branch, ag, nrm, inv, gbo, gbi, consts)


def token_grad_kernel(n, taps, meta, cot, cgp, consts, other, out_in, out, gtok, gtok_own, stage, sems, out_sem):
    s = pl.program_id(0)
    frames, width = cot.shape[1], cot.shape[2]
    half = taps // 2
    wq = width // LANES
    count = meta[2 + meta[0] * n + s]
    w = consts[:taps, :]
    steps = pl.cdiv(count, CHUNK)
    other_copy = pltpu.make_async_copy(other, out.at[pl.ds((1 - meta[0]) * n, n)], out_sem)

    def place(j):
        return pltpu.make_async_copy(stage.at[j], gtok.at[meta[0] * n + j], sems.at[j])

    @pl.when(s == 0)
    def _():
        other_copy.start()

    def conv_step(i, _):
        r0 = pl.multiple_of(i * CHUNK, CHUNK)
        here = pl.ds(r0, CHUNK)
        live = (lax.broadcasted_iota(jnp.int32, (CHUNK, LANES), 0) + r0) < count
        for q in range(wq):
            total = cot[s, here, lane(q)].astype(F32)
            for k in range(taps):
                total = total + w[k:k + 1, lane(q)] * cgp[s, q, pl.ds(r0 + (PAD + half - k), CHUNK), :]
            total = jnp.where(live, total, 0.0).astype(BF)
            gtok_own[s, here, lane(q)] = total
            stage[s, here, lane(q)] = total.astype(F32)
        return 0

    lax.fori_loop(0, steps, conv_step, 0)

    def clear(i, _):
        here = pl.ds(pl.multiple_of(i * CHUNK, CHUNK), CHUNK)
        gtok_own[s, here, :] = jnp.zeros((CHUNK, width), BF)
        stage[s, here, :] = jnp.zeros((CHUNK, width), F32)
        return 0

    lax.fori_loop(steps, frames // CHUNK, clear, 0)
    place(s).start()

    @pl.when(s == n - 1)
    def _():
        other_copy.wait()
        for j in range(n):
            place(j).wait()


def token_grad(meta, cot, cgp, consts, other, out, taps):
    n, frames, width = cot.shape
    return pl.pallas_call(
        functools.partial(token_grad_kernel, n, taps), grid=(n,),
        in_specs=[smem()] + [vmem()] * 3 + [hbm()] * 2, out_specs=[hbm(), hbm(), vmem()],
        scratch_shapes=[pltpu.VMEM((n, frames, width), F32), pltpu.SemaphoreType.DMA((n,)), pltpu.SemaphoreType.DMA],
        out_shape=[struct(out.shape, BF), struct(out.shape, F32), struct((n, frames, width), BF)],
        input_output_aliases={5: 0},
        compiler_params=params(), cost_estimate=cost(40000000),
    )(meta, cot, cgp, consts, other, out)


def merge_kernel(n, meta, other, gtok_in, gtok, stage, sems):
    copies = [pltpu.make_async_copy(stage.at[j], gtok.at[(1 - meta[0]) * n + j], sems.at[j]) for j in range(n)]
    for j in range(n):
        stage[j] = other[j].astype(F32)
        copies[j].start()
    for c in copies:
        c.wait()


def merge(meta, other, gtok):
    n = other.shape[0]
    return pl.pallas_call(
        functools.partial(merge_kernel, n),
        in_specs=[smem(), vmem(), hbm()], out_specs=hbm(), out_shape=struct(gtok.shape, F32),
        scratch_shapes=[pltpu.VMEM(other.shape, F32), pltpu.SemaphoreType.DMA((n,))],
        input_output_aliases={2: 0},
        compiler_params=params(), cost_estimate=cost(20000000),
    )(meta, other, gtok)


def message_kernel(stay, keep, recv, *refs):
    pieces, (out, mine) = refs[:-2], refs[-2:]
    m = pieces[0].shape[0]
    total = stay[:m, :]
    for piece in pieces:
        total = total + piece[...].astype(F32)
    out[:m, :] = total.astype(BF)
    mine[...] = total.astype(BF)
    small = (keep[...] + recv[...]).astype(BF)
    rows = small.shape[0]
    for q in range(small.shape[1] // LANES):
        out[m + q * rows:m + (q + 1) * rows, :] = small[:, lane(q)]


def make_message(stay, keep, recv, pieces):
    rows = pieces[0].shape[0] + keep.size // LANES
    return pl.pallas_call(message_kernel, in_specs=[vmem()] * (3 + len(pieces)), out_specs=[vmem(), vmem()],
                          out_shape=[struct((rows, LANES), BF), struct(pieces[0].shape, BF)],
                          compiler_params=params())(stay, keep, recv, *pieces)


def relay_kernel(m, *refs):
    sources, out = refs[:-1], refs[-1]
    sums = []
    for d, src in enumerate(sources):
        if d > 0:
            out[(d - 1) * m:d * m, :] = src[:m, :]
        sums.append(src[m:, :].astype(F32))
    while len(sums) > 1:
        sums = [a + b for a, b in zip(sums[::2], sums[1::2])]
    out[(len(sources) - 1) * m:, :] = sums[0].astype(BF)


def relay(m, sources):
    rows = (len(sources) - 1) * m + sources[0].shape[0] - m
    return pl.pallas_call(functools.partial(relay_kernel, m), in_specs=[vmem()] * len(sources), out_specs=vmem(),
                          out_shape=struct((rows, LANES), BF), compiler_params=params())(*sources)


def unpack_kernel(dp, taps, rates, meta, mine, theirs, near, far, gcw, gcb, gns, gnsh, gwi, gbi, gwo, gbo, gls, full):
    h, width = gwo.shape
    wq, hq = width // LANES, h // LANES
    m = full.shape[0] // dp
    for odd, first, others in ((0, mine, near), (1, theirs, far)):
        for d in range(dp // 2):
            piece = others[(d - 1) * m:d * m, :] if d else first[:m, :]
            at = pl.multiple_of((meta[1] ^ (2 * d + odd)) * m, m)
            full[pl.ds(at, m), :] = piece.astype(F32)
    for q in range(wq):
        gwo[:, lane(q)] = full[q * h:(q + 1) * h, :]
    base = wq * h
    for q in range(hq):
        gwi[:, lane(q)] = full[base + q * width:base + (q + 1) * width, :]
    behind = (dp // 2 - 1) * m
    small = near[behind:, :].astype(F32) + far[behind:, :].astype(F32)
    rows = small.shape[0] // wq
    small = jnp.concatenate([small[q * rows:(q + 1) * rows] for q in range(wq)], axis=1)
    gcw[...] = small[:taps]
    gcb[...] = small[taps]
    gls[...] = small[taps + 1]
    gns[...] = small[taps + 2:taps + 2 + rates]
    gnsh[...] = small[taps + 2 + rates:taps + 2 + 2 * rates]
    at = taps + 2 + 2 * rates
    gbo[...] = small[at]
    gbi[...] = small[at + 1, :h]


def unpack(meta, mine, theirs, near, far, dp, taps, rates, width, h):
    shapes = [(taps, width), (width,), (rates, width), (rates, width), (width, h), (h,), (h, width), (width,), (width,)]
    return pl.pallas_call(
        functools.partial(unpack_kernel, dp, taps, rates), in_specs=[smem()] + [vmem()] * 4,
        out_shape=[struct(s, F32) for s in shapes],
        scratch_shapes=[pltpu.VMEM((2 * width * h // LANES, LANES), F32)],
        compiler_params=params())(meta, mine, theirs, near, far)


def swap(x, step):
    size = lax.axis_size("tp")
    return lax.ppermute(x, "tp", [(i, i ^ step) for i in range(size)])


def across(x, step):
    size = lax.axis_size("dp")
    return lax.ppermute(x, "dp", [(i, i ^ step) for i in range(size)])


def per_device(tokens, frame_counts, rate_groups, conv_weight, conv_bias, norm_scale, norm_shift,
               weight_in, bias_in, weight_out, bias_out, layer_scale, cotangent):
    width, h = weight_in.shape
    n = tokens.shape[0] // 2
    (tokens, cotangent, conv_weight, conv_bias, norm_scale, norm_shift, weight_in, bias_in, weight_out, bias_out,
     layer_scale) = [pltpu.with_memory_space_constraint(v, pltpu.HBM) for v in (
         tokens, cotangent, conv_weight, conv_bias, norm_scale, norm_shift, weight_in, bias_in, weight_out, bias_out,
         layer_scale)]
    taps, rates = conv_weight.shape[0], norm_scale.shape[0]
    dp = lax.axis_size("dp")
    place = jnp.stack([lax.axis_index("tp") & 1, lax.axis_index("dp")]).astype(jnp.int32)
    meta = jnp.concatenate([place, frame_counts, rate_groups])

    buf_a = pack(weight_in, bias_in, weight_out)
    buf_b = swap(buf_a, 1)
    buf_c = swap(buf_a, 2)
    buf_d = swap(buf_c, 1)
    ad, nrm, low, inv, act, pre, win, wout, keep, send, gbo, gbi, tok, cot, consts = front(
        meta, tokens, cotangent, conv_weight, conv_bias, norm_scale, norm_shift, layer_scale, bias_out, buf_a, buf_b, h)
    stay, leave = combine(meta, keep, swap(send, 1), dp)
    arrived = across(leave, 1)
    branch, ag = mix(meta, ad, low, act, pre, win, wout, consts, buf_c, buf_d, n, taps)
    arrived, branch = lax.optimization_barrier((arrived, branch))
    stay = (stay + arrived.astype(F32)).reshape(dp // 2, -1, LANES)
    pieces = [across(stay[d].astype(BF), 2 * d) for d in range(1, dp // 2)]

    out, out_own, cgp, small_keep, small_send = norm_grad(
        meta, tok, cot, branch, ag, nrm, inv, gbo, gbi, consts, taps, rates)
    pieces, small_send, out_own, cgp = lax.optimization_barrier((pieces, small_send, out_own, cgp))
    small_got = swap(small_send, 1)
    small_got, out_own = lax.optimization_barrier((small_got, out_own))
    message, mine = make_message(stay.reshape(-1, LANES), small_keep, small_got, pieces)
    m = pieces[0].shape[0]
    near = [message] + [across(message, 2 * d) for d in range(1, dp // 2)]
    theirs = across(mine, 1)
    out, gtok, gtok_own = token_grad(meta, cot, cgp, consts, swap(out_own, 1), out, taps)
    near, theirs, gtok_own = lax.optimization_barrier((near, theirs, gtok_own))
    near = relay(m, near)
    far = across(near, 1)
    gtok = merge(meta, swap(gtok_own, 1), gtok)
    far, gtok = lax.optimization_barrier((far, gtok))
    gcw, gcb, gns, gnsh, gwi, gbi, gwo, gbo, gls = unpack(meta, mine, theirs, near, far, dp, taps, rates, width, h)
    return (out, gtok, gcw, gcb, gns, gnsh, gwi, gbi, gwo, gbo, gls)


def solution(mesh):
    items, copied = P("dp", None, None), P()
    in_specs = (items, P("dp"), P("dp"), copied, copied, copied, copied, P(None, "tp"), P("tp"), P("tp", None),
                copied, copied, items)
    out_specs = (items, items, copied, copied, copied, copied, P(None, "tp"), P("tp"), P("tp", None), copied, copied)
    return jax.shard_map(per_device, mesh=mesh, in_specs=in_specs, out_specs=out_specs, check_vma=False)
```

```python
import functools

import jax
import jax.numpy as jnp
from jax import lax
from jax.experimental import pallas as pl
from jax.experimental.pallas import tpu as pltpu
from jax.sharding import PartitionSpec as P

EPS = 1e-06
BF, F32 = jnp.bfloat16, jnp.float32
TILE = 256
LANES = 128
PAD = 8
CHUNK = 64
WIDE_CHUNK = 128
VMEM_LIMIT = 12 * 1024 * 1024


def params(**more):
    return pltpu.CompilerParams(vmem_limit_bytes=VMEM_LIMIT, **more)


def struct(shape, dtype):
    return jax.ShapeDtypeStruct(shape, dtype)


def whole(shape):
    return pl.BlockSpec(shape, lambda *_: (0,) * len(shape))


def hbm():
    return pl.BlockSpec(memory_space=pltpu.HBM)


def smem():
    return pl.BlockSpec(memory_space=pltpu.SMEM)


def cost(size):
    return pl.CostEstimate(flops=0, transcendentals=0, bytes_accessed=size)


def vmem():
    return pl.BlockSpec(memory_space=pltpu.VMEM)


def lane(q):
    return slice(q * LANES, (q + 1) * LANES)


def fold(x):
    return jnp.sum(x.reshape(x.shape[0] // 8, 8, x.shape[1]), axis=0)


def pick(table, group):
    rows = table[...].astype(F32)
    value = rows[0:1]
    for r in range(1, rows.shape[0]):
        value = jnp.where(group == r, rows[r:r + 1], value)
    return value


def as_row(ref):
    return ref[...].astype(F32).reshape(1, -1)


def gelu_parts(pre):
    cdf = 0.5 + 0.5 * lax.erf(pre * 0.7071067811865476)
    density = jnp.exp(-0.5 * pre * pre) * 0.3989422804014327
    return pre * cdf, cdf + pre * density


def dot(a, b):
    return jnp.dot(a, b, preferred_element_type=F32)


def dot_t(a, b):
    return lax.dot_general(a, b, (((1,), (1,)), ((), ())), preferred_element_type=F32)


def dot_rows(a, b):
    return lax.dot_general(a, b, (((0,), (0,)), ((), ())), preferred_element_type=F32)


def place_items(n, meta, offs):
    end = jnp.int32(0)
    for j in range(n):
        offs[j] = end
        end = end + ((meta[2 + meta[0] * n + j] + 15) & -16)
    offs[n] = end
    offs[n + 1] = (end + TILE - 1) // TILE


def pack_kernel(wi, bi, wo, out):
    width, h = wi.shape
    hq, wq = h // LANES, width // LANES
    for q in range(hq):
        out[q * width:(q + 1) * width, :] = wi[:, lane(q)]
    base = hq * width
    for q in range(wq):
        out[base + q * h:base + (q + 1) * h, :] = wo[:, lane(q)]
    base += wq * h
    bias = bi[...].astype(F32).reshape(1, h)
    rows = [bias[:, lane(q)] for q in range(hq)] + [jnp.zeros((1, LANES), F32)] * (16 - hq)
    out[base:base + 16, :] = jnp.concatenate(rows, axis=0).astype(BF)


def pack(wi, bi, wo):
    rows = 2 * wi.size // LANES + 16
    return pl.pallas_call(pack_kernel, out_shape=struct((rows, LANES), BF),
                          compiler_params=params())(wi, bi, wo)


def weight_copies(buf, side, win, wout, bias, sems):
    width, h = win.shape[0], win.shape[1] // 2
    hq, wq = h // LANES, width // LANES
    copies = []
    for q in range(hq):
        at = side * h + q * LANES
        copies.append((buf.at[pl.ds(q * width, width), :], win.at[:, pl.ds(at, LANES)]))
    base = hq * width
    for q in range(wq):
        copies.append((buf.at[pl.ds(base + q * h, h), :], wout.at[pl.ds(side * h, h), pl.ds(q * LANES, LANES)]))
    copies.append((buf.at[pl.ds(base + wq * h, 16), :], bias.at[side]))
    return [pltpu.make_async_copy(src, dst, sems.at[side, i]) for i, (src, dst) in enumerate(copies)]


def spread_bias(bias, row):
    hq = row.shape[1] // LANES // 2
    for side in range(2):
        for q in range(hq):
            at = side * hq + q
            row[:, lane(at)] = bias[side, q:q + 1, :].astype(F32)


def front_kernel(n, counts_hbm, groups_hbm, tok_hbm, cot_hbm, cw, cb, ns, nsh, gamma, bout, buf_a, buf_b,
                 ad, nrm, low, inv, act, pre, win, wout, keep, send, gbo, gbi, tok, cot, consts, meta,
                 offs, counts_s, groups_s, pad, ad_s, nrm_s, low_s, inv_s, bias, bias_row, dwo, dwi, sems, item_sems, meta_sems):
    s = pl.program_id(0)
    frames, width = tok.shape[1], tok.shape[2]
    taps, rates = cw.shape[0], ns.shape[0]
    half = taps // 2
    wq = width // LANES
    h = win.shape[1] // 2
    copies = weight_copies(buf_a, 0, win, wout, bias, sems) + weight_copies(buf_b, 1, win, wout, bias, sems)

    def fetch(j):
        at = (lax.axis_index("tp") & 1) * n + j
        return [pltpu.make_async_copy(src.at[at], dst.at[j], item_sems.at[i, j])
                for i, (src, dst) in enumerate(((tok_hbm, tok), (cot_hbm, cot)))]

    @pl.when(s == 0)
    def _():
        tables = [pltpu.make_async_copy(counts_hbm, counts_s, meta_sems.at[0]),
                  pltpu.make_async_copy(groups_hbm, groups_s, meta_sems.at[1])]
        for c in tables + fetch(0) + fetch(1):
            c.start()
        for c in copies:
            c.start()
        for j in range(2, n):
            for c in fetch(j):
                c.start()
        consts[...] = jnp.zeros_like(consts)
        consts[:taps, :] = cw[...].astype(F32)
        consts[taps:taps + 1, :] = as_row(gamma)
        consts[taps + 1:taps + 2, :] = as_row(bout)
        consts[taps + 2:taps + 2 + rates, :] = ns[...].astype(F32)
        offs[n + 2] = 0
        gbo[...] = jnp.zeros_like(gbo)
        pad[...] = jnp.zeros_like(pad)
        meta[0] = lax.axis_index("tp") & 1
        meta[1] = lax.axis_index("dp")
        for c in tables:
            c.wait()
        for j in range(2 * n):
            meta[2 + j] = counts_s[j]
            meta[2 + 2 * n + j] = groups_s[j]
        place_items(n, meta, offs)

    def flush(j):
        dst = pl.ds(pl.multiple_of(offs[j], 16), frames)
        for whole_ref, stage in ((ad, ad_s), (nrm, nrm_s), (low, low_s), (inv, inv_s)):
            whole_ref[dst, :] = stage[...]

    @pl.when(s > 0)
    def _():
        flush(s - 1)

    @pl.when(s == 1)
    def _():
        for c in copies:
            c.wait()
        spread_bias(bias, bias_row)
        dwo[...] = jnp.zeros_like(dwo)
        dwi[...] = jnp.zeros_like(dwi)
        gbi[...] = jnp.zeros_like(gbi)

    for c in fetch(s):
        c.wait()
    item = meta[0] * n + s
    count = meta[2 + item]
    group = meta[2 + 2 * n + item]

    def setup():
        rows = lax.broadcasted_iota(jnp.int32, (frames, LANES), 0)
        for q in range(wq):
            pad[q, PAD:PAD + frames, :] = jnp.where(rows < count, tok[s, :, lane(q)].astype(F32), 0.0)
        return pick(ns, group), pick(nsh, group), as_row(gamma), as_row(cb), cw[...].astype(F32)

    def conv_step(i, acc, consts):
        scale, shift, gam, conv_bias, w = consts
        r0 = i * CHUNK if isinstance(i, int) else pl.multiple_of(i * CHUNK, CHUNK)
        here = pl.ds(r0, CHUNK)
        live = (lax.broadcasted_iota(jnp.int32, (CHUNK, LANES), 0) + r0) < count
        convs = []
        for q in range(wq):
            conv = conv_bias[:, lane(q)]
            for k in range(taps):
                conv = conv + w[k:k + 1, lane(q)] * pad[q, pl.ds(r0 + (PAD - half + k), CHUNK), :]
            convs.append(conv)
        mean = jnp.sum(sum(convs[1:], convs[0]), axis=-1, keepdims=True) * (1.0 / width)
        cents = [c - mean for c in convs]
        sq = [c * c for c in cents]
        var = jnp.sum(sum(sq[1:], sq[0]), axis=-1, keepdims=True) * (1.0 / width)
        istd = lax.rsqrt(var + EPS)
        inv_s[here, :] = jnp.broadcast_to(istd, (CHUNK, LANES))
        new = []
        for q in range(wq):
            normed = cents[q] * istd
            ad_s[here, lane(q)] = (normed * scale[:, lane(q)] + shift[:, lane(q)]).astype(BF)
            nrm_s[here, lane(q)] = normed.astype(BF)
            back = jnp.where(live, cot[s, here, lane(q)].astype(F32), 0.0) * gam[:, lane(q)]
            low_s[here, lane(q)] = back.astype(BF)
            new.append(acc[q] + fold(back))
        return tuple(new)

    def add_gbo(accs):
        for q in range(wq):
            gbo[:, lane(q)] += accs[q]

    def tile(t, between=()):
        between = list(between)
        at = pl.ds(pl.multiple_of(t * TILE, TILE), TILE)
        a, b = ad[at, :], low[at, :]
        activation, slope = gelu_parts(dot(a, win[...]) + bias_row[...])
        if between:
            between.pop(0)()
        grad = dot_t(b, wout[...]) * slope
        lo = activation.astype(BF)
        act[at, :] = lo
        if between:
            between.pop(0)()
        dwo[...] += dot_rows(lo, b)
        gbi[...] += fold(grad)
        g = grad.astype(BF)
        pre[at, :] = g
        if between:
            between.pop(0)()
        dwi[...] += dot_rows(a, g)
        if between:
            between.pop(0)()

    done = offs[n + 2]
    ready = offs[s] >= (done + 1) * TILE
    none = (jnp.zeros((8, LANES), F32),) * wq

    @pl.when(ready)
    def _():
        consts = setup()
        state = [none]

        def part(lo_i, hi_i):
            def run():
                for i in range(lo_i, hi_i):
                    state[0] = conv_step(i, state[0], consts)
            return run

        count_c = frames // CHUNK
        cuts = [count_c * k // 4 for k in range(5)]
        tile(done, [part(cuts[k], cuts[k + 1]) for k in range(4)])
        add_gbo(state[0])
        offs[n + 2] = done + 1

    @pl.when(jnp.logical_not(ready))
    def _():
        consts = setup()
        state = none
        for i in range(frames // CHUNK):
            state = conv_step(i, state, consts)
        add_gbo(state)

    @pl.when(s == n - 1)
    def _():
        flush(s)
        end = pl.ds(pl.multiple_of(offs[n], 16), TILE)
        ad[end, :] = jnp.zeros((TILE, width), BF)
        low[end, :] = jnp.zeros((TILE, width), BF)

        def rest(t, _):
            tile(t)
            return 0

        lax.fori_loop(offs[n + 2], offs[n + 1], rest, 0)
        for side, dst in ((0, keep), (1, send)):
            for q in range(wq):
                dst[q * h:(q + 1) * h, :] = dwo[side * h:(side + 1) * h, lane(q)].astype(dst.dtype)
            base = wq * h
            for q in range(h // LANES):
                dst[base + q * width:base + (q + 1) * width, :] = dwi[:, lane(side * (h // LANES) + q)].astype(dst.dtype)


def front(counts, groups, tok, cot, cw, cb, ns, nsh, gamma, bout, buf_a, buf_b, h):
    items, frames, width = tok.shape
    n = items // 2
    rows = n * frames + TILE
    packed = 2 * width * h // LANES
    wq, hq = width // LANES, h // LANES
    n_consts = -(-(cw.shape[0] + 2 + ns.shape[0]) // 8) * 8
    return pl.pallas_call(
        functools.partial(front_kernel, n),
        grid_spec=pl.GridSpec(
            grid=(n,),
            in_specs=[hbm()] * 4 + [whole(v.shape) for v in (cw, cb, ns, nsh, gamma, bout)] + [hbm()] * 2,
            out_specs=[vmem()] * 15 + [smem()],
            scratch_shapes=[pltpu.SMEM((n + 3,), jnp.int32), pltpu.SMEM((items,), jnp.int32), pltpu.SMEM((items,), jnp.int32),
                            pltpu.VMEM((wq, frames + 4 * PAD, LANES), F32),
                            pltpu.VMEM((frames, width), BF), pltpu.VMEM((frames, width), BF),
                            pltpu.VMEM((frames, width), BF), pltpu.VMEM((frames, LANES), F32),
                            pltpu.VMEM((2, 16, LANES), BF), pltpu.VMEM((1, 2 * h), F32),
                            pltpu.VMEM((2 * h, width), F32), pltpu.VMEM((width, 2 * h), F32),
                            pltpu.SemaphoreType.DMA((2, hq + wq + 1)), pltpu.SemaphoreType.DMA((2, n)),
                            pltpu.SemaphoreType.DMA((2,))]),
        out_shape=[struct((rows, width), BF)] * 3 + [struct((rows, LANES), F32)]
        + [struct((rows, 2 * h), BF)] * 2 + [struct((width, 2 * h), BF), struct((2 * h, width), BF)]
        + [struct((packed, LANES), F32), struct((packed, LANES), BF), struct((8, width), F32), struct((8, 2 * h), F32)]
        + [struct((n, frames, width), BF)] * 2 + [struct((n_consts, width), F32), struct((2 + 2 * items,), jnp.int32)],
        compiler_params=params(), cost_estimate=cost(0),
    )(counts, groups, tok, cot, cw, cb, ns, nsh, gamma, bout, buf_a, buf_b)


def combine_kernel(dp, meta, keep, recv, stay, leave):
    m = keep.shape[0] // dp
    for d in range(dp):
        src = pl.ds(pl.multiple_of((meta[1] ^ d) * m, m), m)
        total = keep[src, :] + recv[src, :].astype(F32)
        dst = leave if d % 2 else stay
        dst[d // 2 * m:(d // 2 + 1) * m, :] = total.astype(dst.dtype)


def combine(meta, keep, recv, dp):
    rows = keep.shape[0] // 2
    return pl.pallas_call(
        functools.partial(combine_kernel, dp),
        in_specs=[smem(), vmem(), vmem()], out_specs=[vmem(), vmem()],
        out_shape=[struct((rows, LANES), F32), struct((rows, LANES), BF)],
        compiler_params=params())(meta, keep, recv)


def mix_kernel(n, taps, meta, ad, low, act, pre, win1, wout1, consts, buf_c, buf_d, branch, ag,
               offs, win2, wout2, bias, bias_row, sems):
    copies = weight_copies(buf_c, 0, win2, wout2, bias, sems) + weight_copies(buf_d, 1, win2, wout2, bias, sems)
    for c in copies:
        c.start()
    place_items(n, meta, offs)
    for c in copies:
        c.wait()
    spread_bias(bias, bias_row)

    def tile(t, _):
        at = pl.ds(pl.multiple_of(t * TILE, TILE), TILE)
        a, b = ad[at, :], low[at, :]
        activation, slope = gelu_parts(dot(a, win2[...]) + bias_row[...])
        grad = dot_t(b, wout2[...]) * slope
        branch[at, :] = (dot(act[at, :], wout1[...]) + dot(activation.astype(BF), wout2[...])) + consts[taps + 1:taps + 2, :]
        ag[at, :] = dot_t(pre[at, :], win1[...]) + dot_t(grad.astype(BF), win2[...])
        return 0

    lax.fori_loop(0, offs[n + 1], tile, 0)


def mix(meta, ad, low, act, pre, win, wout, consts, buf_c, buf_d, n, taps):
    rows, width = ad.shape
    h = act.shape[1] // 2
    wq, hq = width // LANES, h // LANES
    return pl.pallas_call(
        functools.partial(mix_kernel, n, taps),
        in_specs=[smem()] + [vmem()] * 7 + [hbm()] * 2,
        out_specs=[vmem(), vmem()],
        scratch_shapes=[pltpu.SMEM((n + 2,), jnp.int32),
                        pltpu.VMEM((width, 2 * h), BF), pltpu.VMEM((2 * h, width), BF),
                        pltpu.VMEM((2, 16, LANES), BF), pltpu.VMEM((1, 2 * h), F32),
                        pltpu.SemaphoreType.DMA((2, hq + wq + 1))],
        out_shape=[struct((rows, width), F32)] * 2,
        compiler_params=params(), cost_estimate=cost(0),
    )(meta, ad, low, act, pre, win, wout, consts, buf_c, buf_d)


def norm_grad_kernel(n, taps, rates, meta, tok, cot, branch, ag, nrm, inv, gbo, gbi, consts,
                     cgp, small_keep, small_send, offs, sums):
    s = pl.program_id(0)
    frames, width = tok.shape[1], tok.shape[2]
    half = taps // 2
    wq = width // LANES
    h = gbi.shape[1] // 2

    @pl.when(s == 0)
    def _():
        place_items(n, meta, offs)
        sums[...] = jnp.zeros_like(sums)

    item = meta[0] * n + s
    count = meta[2 + item]
    group = meta[2 + 2 * n + item]
    off = offs[s]
    scale = pick(consts.at[taps + 2:taps + 2 + rates], group)
    zero = jnp.zeros((8, LANES), F32)
    steps = pl.cdiv(count, WIDE_CHUNK)

    def step(i, accs):
        r0 = pl.multiple_of(i * WIDE_CHUNK, WIDE_CHUNK)
        here = pl.ds(r0, WIDE_CHUNK)
        live = (lax.broadcasted_iota(jnp.int32, (WIDE_CHUNK, LANES), 0) + r0) < count
        src = pl.ds(pl.multiple_of(off + r0, 16), WIDE_CHUNK)
        new = []
        ngs, nrs = [], []
        for q in range(wq):
            a_ls, a_sc, a_sh = accs[3 * q:3 * q + 3]
            br = jnp.where(live, branch[src, lane(q)], 0.0)
            g = jnp.where(live, ag[src, lane(q)], 0.0)
            nr = nrm[src, lane(q)].astype(F32)
            new += [a_ls + fold(cot[s, here, lane(q)].astype(F32) * br), a_sc + fold(g * nr), a_sh + fold(g)]
            ngs.append(g * scale[:, lane(q)])
            nrs.append(nr)
        cross = [a * b for a, b in zip(ngs, nrs)]
        m1 = jnp.sum(sum(ngs[1:], ngs[0]), axis=-1, keepdims=True) * (1.0 / width)
        m2 = jnp.sum(sum(cross[1:], cross[0]), axis=-1, keepdims=True) * (1.0 / width)
        istd = inv[src, :]
        for q in range(wq):
            cg = istd * (ngs[q] - m1 - nrs[q] * m2)
            cgp[s, q, pl.ds(pl.multiple_of(r0 + PAD, 8), WIDE_CHUNK), :] = jnp.where(live, cg, 0.0)
        return tuple(new)

    accs = lax.fori_loop(0, steps, step, (zero,) * (3 * wq))
    for q in range(wq):
        sums[taps + 1, :, lane(q)] += accs[3 * q]
        sums[taps + 2 + group, :, lane(q)] += accs[3 * q + 1]
        sums[taps + 2 + rates + group, :, lane(q)] += accs[3 * q + 2]

    def clear(i, _):
        r0 = pl.multiple_of(i * WIDE_CHUNK, WIDE_CHUNK)
        for q in range(wq):
            cgp[s, q, pl.ds(pl.multiple_of(r0 + PAD, 8), WIDE_CHUNK), :] = jnp.zeros((WIDE_CHUNK, LANES), F32)
        return 0

    lax.fori_loop(steps, frames // WIDE_CHUNK, clear, 0)
    for q in range(wq):
        cgp[s, q, :PAD, :] = jnp.zeros((PAD, LANES), F32)
        cgp[s, q, PAD + frames:, :] = jnp.zeros((cgp.shape[2] - PAD - frames, LANES), F32)

        def conv_step(i, accs):
            r0 = pl.multiple_of(i * WIDE_CHUNK, WIDE_CHUNK)
            here = pl.ds(r0, WIDE_CHUNK)
            live = (lax.broadcasted_iota(jnp.int32, (WIDE_CHUNK, LANES), 0) + r0) < count
            tk = jnp.where(live, tok[s, here, lane(q)].astype(F32), 0.0)
            new = []
            for k in range(taps):
                sh = cgp[s, q, pl.ds(r0 + (PAD + half - k), WIDE_CHUNK), :]
                new.append(accs[k] + fold(tk * sh))
                if k == half:
                    new_bias = accs[taps] + fold(sh)
            return tuple(new) + (new_bias,)

        accs = lax.fori_loop(0, steps, conv_step, (zero,) * (taps + 1))
        for k in range(taps + 1):
            sums[k, :, lane(q)] += accs[k]

    @pl.when(s == n - 1)
    def _():
        last = taps + 2 + 2 * rates
        rows = [jnp.sum(sums[i], axis=0, keepdims=True) for i in range(last)]
        rows.append(jnp.sum(gbo[...], axis=0, keepdims=True))
        gb = jnp.sum(gbi[...], axis=0, keepdims=True)
        fill = jnp.zeros((1, width - h), F32)
        spare = [jnp.zeros((1, width), F32)] * (small_keep.shape[0] - last - 2)
        for side, dst in ((0, small_keep), (1, small_send)):
            tail = [jnp.concatenate([gb[:, side * h:(side + 1) * h], fill], axis=1)]
            dst[...] = jnp.concatenate(rows + tail + spare, axis=0)


def norm_grad(meta, tok, cot, branch, ag, nrm, inv, gbo, gbi, consts, taps, rates):
    n, frames, width = tok.shape
    wq = width // LANES
    n_small = -(-(taps + 4 + 2 * rates) // 8) * 8
    return pl.pallas_call(
        functools.partial(norm_grad_kernel, n, taps, rates), grid=(n,),
        in_specs=[smem()] + [vmem()] * 9, out_specs=[vmem()] * 3,
        scratch_shapes=[pltpu.SMEM((n + 2,), jnp.int32),
                        pltpu.VMEM((taps + 2 + 2 * rates, 8, width), F32)],
        out_shape=[struct((n, wq, frames + 4 * PAD, LANES), F32)] + [struct((n_small, width), F32)] * 2,
        compiler_params=params(), cost_estimate=cost(40000000),
    )(meta, tok, cot, branch, ag, nrm, inv, gbo, gbi, consts)


def block_out_kernel(n, taps, meta, tok, branch, consts, out, own, offs, sems):
    s = pl.program_id(0)
    frames, width = tok.shape[1], tok.shape[2]

    def place(j):
        return pltpu.make_async_copy(own.at[j], out.at[meta[0] * n + j], sems.at[j])

    @pl.when(s == 0)
    def _():
        place_items(n, meta, offs)

    count = meta[2 + meta[0] * n + s]
    off = offs[s]
    gam = consts[taps:taps + 1, :]
    for i in range(frames // CHUNK):
        here = pl.ds(i * CHUNK, CHUNK)
        live = (lax.broadcasted_iota(jnp.int32, (CHUNK, LANES), 0) + i * CHUNK) < count
        src = pl.ds(pl.multiple_of(off + i * CHUNK, 16), CHUNK)
        for q in range(width // LANES):
            value = tok[s, here, lane(q)].astype(F32) + gam[:, lane(q)] * branch[src, lane(q)]
            own[s, here, lane(q)] = jnp.where(live, value, 0.0).astype(BF)
    place(s).start()

    @pl.when(s == n - 1)
    def _():
        for j in range(n):
            place(j).wait()


def block_out(meta, tok, branch, consts, taps):
    n, frames, width = tok.shape
    return pl.pallas_call(
        functools.partial(block_out_kernel, n, taps), grid=(n,),
        in_specs=[smem()] + [vmem()] * 3, out_specs=[hbm(), vmem()],
        scratch_shapes=[pltpu.SMEM((n + 2,), jnp.int32), pltpu.SemaphoreType.DMA((n,))],
        out_shape=[struct((2 * n, frames, width), BF), struct((n, frames, width), BF)],
        compiler_params=params(), cost_estimate=cost(40000000),
    )(meta, tok, branch, consts)


def token_grad_kernel(n, taps, meta, cot, cgp, consts, gtok, gtok_own, stage, sems):
    s = pl.program_id(0)
    frames, width = cot.shape[1], cot.shape[2]
    half = taps // 2
    wq = width // LANES
    count = meta[2 + meta[0] * n + s]
    w = consts[:taps, :]
    steps = pl.cdiv(count, CHUNK)

    def place(j):
        return pltpu.make_async_copy(stage.at[j], gtok.at[meta[0] * n + j], sems.at[j])

    def conv_step(i, _):
        r0 = pl.multiple_of(i * CHUNK, CHUNK)
        here = pl.ds(r0, CHUNK)
        live = (lax.broadcasted_iota(jnp.int32, (CHUNK, LANES), 0) + r0) < count
        for q in range(wq):
            total = cot[s, here, lane(q)].astype(F32)
            for k in range(taps):
                total = total + w[k:k + 1, lane(q)] * cgp[s, q, pl.ds(r0 + (PAD + half - k), CHUNK), :]
            total = jnp.where(live, total, 0.0).astype(BF)
            gtok_own[s, here, lane(q)] = total
            stage[s, here, lane(q)] = total.astype(F32)
        return 0

    lax.fori_loop(0, steps, conv_step, 0)

    def clear(i, _):
        here = pl.ds(pl.multiple_of(i * CHUNK, CHUNK), CHUNK)
        gtok_own[s, here, :] = jnp.zeros((CHUNK, width), BF)
        stage[s, here, :] = jnp.zeros((CHUNK, width), F32)
        return 0

    lax.fori_loop(steps, frames // CHUNK, clear, 0)
    place(s).start()

    @pl.when(s == n - 1)
    def _():
        for j in range(n):
            place(j).wait()


def token_grad(meta, cot, cgp, consts, taps):
    n, frames, width = cot.shape
    return pl.pallas_call(
        functools.partial(token_grad_kernel, n, taps), grid=(n,),
        in_specs=[smem()] + [vmem()] * 3, out_specs=[hbm(), vmem()],
        scratch_shapes=[pltpu.VMEM((n, frames, width), F32), pltpu.SemaphoreType.DMA((n,))],
        out_shape=[struct((2 * n, frames, width), F32), struct((n, frames, width), BF)],
        compiler_params=params(), cost_estimate=cost(40000000),
    )(meta, cot, cgp, consts)


def merge_kernel(n, meta, out_b, gtok_b, out_in, gtok_in, out, gtok, stage, sems, out_sem):
    first = (1 - meta[0]) * n
    whole_copy = pltpu.make_async_copy(out_b, out.at[pl.ds(first, n)], out_sem)
    whole_copy.start()
    copies = [pltpu.make_async_copy(stage.at[j], gtok.at[first + j], sems.at[j]) for j in range(n)]
    for j in range(n):
        stage[j] = gtok_b[j].astype(F32)
        copies[j].start()
    whole_copy.wait()
    for c in copies:
        c.wait()


def merge(meta, out_b, gtok_b, out, gtok):
    n = out_b.shape[0]
    return pl.pallas_call(
        functools.partial(merge_kernel, n),
        in_specs=[smem(), hbm(), vmem(), hbm(), hbm()], out_specs=[hbm(), hbm()],
        out_shape=[struct(out.shape, BF), struct(gtok.shape, F32)],
        scratch_shapes=[pltpu.VMEM(gtok_b.shape, F32), pltpu.SemaphoreType.DMA((n,)), pltpu.SemaphoreType.DMA],
        input_output_aliases={3: 0, 4: 1},
        compiler_params=params(), cost_estimate=cost(20000000),
    )(meta, out_b, gtok_b, out, gtok)


def message_kernel(stay, keep, recv, *refs):
    pieces, (out, mine) = refs[:-2], refs[-2:]
    m = pieces[0].shape[0]
    total = stay[:m, :]
    for piece in pieces:
        total = total + piece[...].astype(F32)
    out[:m, :] = total.astype(BF)
    mine[...] = total.astype(BF)
    small = (keep[...] + recv[...]).astype(BF)
    rows = small.shape[0]
    for q in range(small.shape[1] // LANES):
        out[m + q * rows:m + (q + 1) * rows, :] = small[:, lane(q)]


def make_message(stay, keep, recv, pieces):
    rows = pieces[0].shape[0] + keep.size // LANES
    return pl.pallas_call(message_kernel, in_specs=[vmem()] * (3 + len(pieces)), out_specs=[vmem(), vmem()],
                          out_shape=[struct((rows, LANES), BF), struct(pieces[0].shape, BF)],
                          compiler_params=params())(stay, keep, recv, *pieces)


def relay_kernel(m, *refs):
    sources, out = refs[:-1], refs[-1]
    sums = []
    for d, src in enumerate(sources):
        if d > 0:
            out[(d - 1) * m:d * m, :] = src[:m, :]
        sums.append(src[m:, :].astype(F32))
    while len(sums) > 1:
        sums = [a + b for a, b in zip(sums[::2], sums[1::2])]
    out[(len(sources) - 1) * m:, :] = sums[0].astype(BF)


def relay(m, sources):
    rows = (len(sources) - 1) * m + sources[0].shape[0] - m
    return pl.pallas_call(functools.partial(relay_kernel, m), in_specs=[vmem()] * len(sources), out_specs=vmem(),
                          out_shape=struct((rows, LANES), BF), compiler_params=params())(*sources)


def unpack_kernel(dp, taps, rates, meta, mine, theirs, near, far, gcw, gcb, gns, gnsh, gwi, gbi, gwo, gbo, gls, full):
    h, width = gwo.shape
    wq, hq = width // LANES, h // LANES
    m = full.shape[0] // dp
    for odd, first, others in ((0, mine, near), (1, theirs, far)):
        for d in range(dp // 2):
            piece = others[(d - 1) * m:d * m, :] if d else first[:m, :]
            at = pl.multiple_of((meta[1] ^ (2 * d + odd)) * m, m)
            full[pl.ds(at, m), :] = piece.astype(F32)
    for q in range(wq):
        gwo[:, lane(q)] = full[q * h:(q + 1) * h, :]
    base = wq * h
    for q in range(hq):
        gwi[:, lane(q)] = full[base + q * width:base + (q + 1) * width, :]
    behind = (dp // 2 - 1) * m
    small = near[behind:, :].astype(F32) + far[behind:, :].astype(F32)
    rows = small.shape[0] // wq
    small = jnp.concatenate([small[q * rows:(q + 1) * rows] for q in range(wq)], axis=1)
    gcw[...] = small[:taps]
    gcb[...] = small[taps]
    gls[...] = small[taps + 1]
    gns[...] = small[taps + 2:taps + 2 + rates]
    gnsh[...] = small[taps + 2 + rates:taps + 2 + 2 * rates]
    at = taps + 2 + 2 * rates
    gbo[...] = small[at]
    gbi[...] = small[at + 1, :h]


def unpack(meta, mine, theirs, near, far, dp, taps, rates, width, h):
    shapes = [(taps, width), (width,), (rates, width), (rates, width), (width, h), (h,), (h, width), (width,), (width,)]
    return pl.pallas_call(
        functools.partial(unpack_kernel, dp, taps, rates), in_specs=[smem()] + [vmem()] * 4,
        out_shape=[struct(s, F32) for s in shapes],
        scratch_shapes=[pltpu.VMEM((2 * width * h // LANES, LANES), F32)],
        compiler_params=params())(meta, mine, theirs, near, far)


def swap(x, step):
    size = lax.axis_size("tp")
    return lax.ppermute(x, "tp", [(i, i ^ step) for i in range(size)])


def across(x, step):
    size = lax.axis_size("dp")
    return lax.ppermute(x, "dp", [(i, i ^ step) for i in range(size)])


def per_device(tokens, frame_counts, rate_groups, conv_weight, conv_bias, norm_scale, norm_shift,
               weight_in, bias_in, weight_out, bias_out, layer_scale, cotangent):
    width, h = weight_in.shape
    n = tokens.shape[0] // 2
    (tokens, cotangent, conv_weight, conv_bias, norm_scale, norm_shift, weight_in, bias_in, weight_out, bias_out,
     layer_scale, frame_counts, rate_groups) = [pltpu.with_memory_space_constraint(v, pltpu.HBM) for v in (
         tokens, cotangent, conv_weight, conv_bias, norm_scale, norm_shift, weight_in, bias_in, weight_out, bias_out,
         layer_scale, frame_counts, rate_groups)]
    taps, rates = conv_weight.shape[0], norm_scale.shape[0]
    dp = lax.axis_size("dp")
    buf_a = pack(weight_in, bias_in, weight_out)
    buf_b = swap(buf_a, 1)
    buf_c = swap(buf_a, 2)
    buf_d = swap(buf_c, 1)
    ad, nrm, low, inv, act, pre, win, wout, keep, send, gbo, gbi, tok, cot, consts, meta = front(
        frame_counts, rate_groups, tokens, cotangent, conv_weight, conv_bias, norm_scale, norm_shift, layer_scale, bias_out, buf_a, buf_b, h)
    stay, leave = combine(meta, keep, swap(send, 1), dp)
    arrived = across(leave, 1)
    branch, ag = mix(meta, ad, low, act, pre, win, wout, consts, buf_c, buf_d, n, taps)
    arrived, branch = lax.optimization_barrier((arrived, branch))
    stay = (stay + arrived.astype(F32)).reshape(dp // 2, -1, LANES)
    pieces = [across(stay[d].astype(BF), 2 * d) for d in range(1, dp // 2)]

    cgp, small_keep, small_send = norm_grad(meta, tok, cot, branch, ag, nrm, inv, gbo, gbi, consts, taps, rates)
    pieces, small_send, cgp, branch = lax.optimization_barrier((pieces, small_send, cgp, branch))
    small_got = swap(small_send, 1)
    message, mine = make_message(stay.reshape(-1, LANES), small_keep, small_got, pieces)
    m = pieces[0].shape[0]
    near = [message] + [across(message, 2 * d) for d in range(1, dp // 2)]
    theirs = across(mine, 1)
    out, out_own = block_out(meta, tok, branch, consts, taps)
    cgp, out, out_own = lax.optimization_barrier((cgp, out, out_own))
    out_b = swap(out_own, 1)
    gtok, gtok_own = token_grad(meta, cot, cgp, consts, taps)
    near, theirs, gtok_own = lax.optimization_barrier((near, theirs, gtok_own))
    near = relay(m, near)
    far = across(near, 1)
    out, gtok = merge(meta, out_b, swap(gtok_own, 1), out, gtok)
    far, gtok = lax.optimization_barrier((far, gtok))
    gcw, gcb, gns, gnsh, gwi, gbi, gwo, gbo, gls = unpack(meta, mine, theirs, near, far, dp, taps, rates, width, h)
    return (out, gtok, gcw, gcb, gns, gnsh, gwi, gbi, gwo, gbo, gls)


def solution(mesh):
    items, copied = P("dp", None, None), P()
    in_specs = (items, P("dp"), P("dp"), copied, copied, copied, copied, P(None, "tp"), P("tp"), P("tp", None),
                copied, copied, items)
    out_specs = (items, items, copied, copied, copied, copied, P(None, "tp"), P("tp"), P("tp", None), copied, copied)
    return jax.shard_map(per_device, mesh=mesh, in_specs=in_specs, out_specs=out_specs, check_vma=False)
```

```python
import functools

import jax
import jax.numpy as jnp
from jax import lax
from jax.experimental import pallas as pl
from jax.experimental.pallas import tpu as pltpu
from jax.sharding import PartitionSpec as P

EPS = 1e-06
BF, F32 = jnp.bfloat16, jnp.float32
TILE = 256
LANES = 128
PAD = 8
CHUNK = 64
WIDE_CHUNK = 128
VMEM_LIMIT = 12 * 1024 * 1024


def params(**more):
    return pltpu.CompilerParams(vmem_limit_bytes=VMEM_LIMIT, **more)


def struct(shape, dtype):
    return jax.ShapeDtypeStruct(shape, dtype)


def whole(shape):
    return pl.BlockSpec(shape, lambda *_: (0,) * len(shape))


def hbm():
    return pl.BlockSpec(memory_space=pltpu.HBM)


def smem():
    return pl.BlockSpec(memory_space=pltpu.SMEM)


def cost(size):
    return pl.CostEstimate(flops=0, transcendentals=0, bytes_accessed=size)


def vmem():
    return pl.BlockSpec(memory_space=pltpu.VMEM)


def lane(q):
    return slice(q * LANES, (q + 1) * LANES)


def fold(x):
    return jnp.sum(x.reshape(x.shape[0] // 8, 8, x.shape[1]), axis=0)


def pick(table, group):
    rows = table[...].astype(F32)
    value = rows[0:1]
    for r in range(1, rows.shape[0]):
        value = jnp.where(group == r, rows[r:r + 1], value)
    return value


def as_row(ref):
    return ref[...].astype(F32).reshape(1, -1)


def gelu_parts(pre):
    cdf = 0.5 + 0.5 * lax.erf(pre * 0.7071067811865476)
    density = jnp.exp(-0.5 * pre * pre) * 0.3989422804014327
    return pre * cdf, cdf + pre * density


def dot(a, b):
    return jnp.dot(a, b, preferred_element_type=F32)


def dot_t(a, b):
    return lax.dot_general(a, b, (((1,), (1,)), ((), ())), preferred_element_type=F32)


def dot_rows(a, b):
    return lax.dot_general(a, b, (((0,), (0,)), ((), ())), preferred_element_type=F32)


def place_items(n, meta, offs):
    end = jnp.int32(0)
    for j in range(n):
        offs[j] = end
        end = end + ((meta[2 + meta[0] * n + j] + 15) & -16)
    offs[n] = end
    offs[n + 1] = (end + TILE - 1) // TILE


def pack_kernel(wi, bi, wo, out):
    width, h = wi.shape
    hq, wq = h // LANES, width // LANES
    for q in range(hq):
        out[q * width:(q + 1) * width, :] = wi[:, lane(q)]
    base = hq * width
    for q in range(wq):
        out[base + q * h:base + (q + 1) * h, :] = wo[:, lane(q)]
    base += wq * h
    bias = bi[...].astype(F32).reshape(1, h)
    rows = [bias[:, lane(q)] for q in range(hq)] + [jnp.zeros((1, LANES), F32)] * (16 - hq)
    out[base:base + 16, :] = jnp.concatenate(rows, axis=0).astype(BF)


def pack(wi, bi, wo):
    rows = 2 * wi.size // LANES + 16
    return pl.pallas_call(pack_kernel, out_shape=struct((rows, LANES), BF),
                          compiler_params=params())(wi, bi, wo)


def weight_copies(buf, side, win, wout, bias, sems):
    width, h = win.shape[0], win.shape[1] // 2
    hq, wq = h // LANES, width // LANES
    copies = []
    for q in range(hq):
        at = side * h + q * LANES
        copies.append((buf.at[pl.ds(q * width, width), :], win.at[:, pl.ds(at, LANES)]))
    base = hq * width
    for q in range(wq):
        copies.append((buf.at[pl.ds(base + q * h, h), :], wout.at[pl.ds(side * h, h), pl.ds(q * LANES, LANES)]))
    copies.append((buf.at[pl.ds(base + wq * h, 16), :], bias.at[side]))
    return [pltpu.make_async_copy(src, dst, sems.at[side, i]) for i, (src, dst) in enumerate(copies)]


def spread_bias(bias, row):
    hq = row.shape[1] // LANES // 2
    for side in range(2):
        for q in range(hq):
            at = side * hq + q
            row[:, lane(at)] = bias[side, q:q + 1, :].astype(F32)


def front_kernel(n, counts_hbm, groups_hbm, tok_hbm, cot_hbm, cw, cb, ns, nsh, gamma, bout, buf_a, buf_b,
                 ad, nrm, low, inv, act, pre, win, wout, keep, send, gbo, gbi, tok, cot, consts, meta,
                 offs, counts_s, groups_s, pad, ad_s, nrm_s, low_s, inv_s, bias, bias_row, dwo, dwi, sems, item_sems, meta_sems):
    s = pl.program_id(0)
    frames, width = tok.shape[1], tok.shape[2]
    taps, rates = cw.shape[0], ns.shape[0]
    half = taps // 2
    wq = width // LANES
    h = win.shape[1] // 2
    copies = weight_copies(buf_a, 0, win, wout, bias, sems) + weight_copies(buf_b, 1, win, wout, bias, sems)

    def fetch(j):
        at = (lax.axis_index("tp") & 1) * n + j
        return [pltpu.make_async_copy(src.at[at], dst.at[j], item_sems.at[i, j])
                for i, (src, dst) in enumerate(((tok_hbm, tok), (cot_hbm, cot)))]

    @pl.when(s == 0)
    def _():
        tables = [pltpu.make_async_copy(counts_hbm, counts_s, meta_sems.at[0]),
                  pltpu.make_async_copy(groups_hbm, groups_s, meta_sems.at[1])]
        for c in tables + fetch(0) + fetch(1):
            c.start()
        for c in copies:
            c.start()
        for j in range(2, n):
            for c in fetch(j):
                c.start()
        consts[...] = jnp.zeros_like(consts)
        consts[:taps, :] = cw[...].astype(F32)
        consts[taps:taps + 1, :] = as_row(gamma)
        consts[taps + 1:taps + 2, :] = as_row(bout)
        consts[taps + 2:taps + 2 + rates, :] = ns[...].astype(F32)
        offs[n + 2] = 0
        gbo[...] = jnp.zeros_like(gbo)
        pad[...] = jnp.zeros_like(pad)
        meta[0] = lax.axis_index("tp") & 1
        meta[1] = lax.axis_index("dp")
        for c in tables:
            c.wait()
        for j in range(2 * n):
            meta[2 + j] = counts_s[j]
            meta[2 + 2 * n + j] = groups_s[j]
        place_items(n, meta, offs)

    def flush(j):
        dst = pl.ds(pl.multiple_of(offs[j], 16), frames)
        for whole_ref, stage in ((ad, ad_s), (nrm, nrm_s), (low, low_s), (inv, inv_s)):
            whole_ref[dst, :] = stage[...]

    @pl.when(s > 0)
    def _():
        flush(s - 1)

    @pl.when(s == 1)
    def _():
        for c in copies:
            c.wait()
        spread_bias(bias, bias_row)
        dwo[...] = jnp.zeros_like(dwo)
        dwi[...] = jnp.zeros_like(dwi)
        gbi[...] = jnp.zeros_like(gbi)

    for c in fetch(s):
        c.wait()
    item = meta[0] * n + s
    count = meta[2 + item]
    group = meta[2 + 2 * n + item]

    def setup():
        rows = lax.broadcasted_iota(jnp.int32, (frames, LANES), 0)
        for q in range(wq):
            pad[q, PAD:PAD + frames, :] = jnp.where(rows < count, tok[s, :, lane(q)].astype(F32), 0.0)
        return pick(ns, group), pick(nsh, group), as_row(gamma), as_row(cb), cw[...].astype(F32)

    def conv_step(i, acc, consts):
        scale, shift, gam, conv_bias, w = consts
        r0 = i * CHUNK if isinstance(i, int) else pl.multiple_of(i * CHUNK, CHUNK)
        here = pl.ds(r0, CHUNK)
        live = (lax.broadcasted_iota(jnp.int32, (CHUNK, LANES), 0) + r0) < count
        convs = []
        for q in range(wq):
            conv = conv_bias[:, lane(q)]
            for k in range(taps):
                conv = conv + w[k:k + 1, lane(q)] * pad[q, pl.ds(r0 + (PAD - half + k), CHUNK), :]
            convs.append(conv)
        mean = jnp.sum(sum(convs[1:], convs[0]), axis=-1, keepdims=True) * (1.0 / width)
        cents = [c - mean for c in convs]
        sq = [c * c for c in cents]
        var = jnp.sum(sum(sq[1:], sq[0]), axis=-1, keepdims=True) * (1.0 / width)
        istd = lax.rsqrt(var + EPS)
        inv_s[here, :] = jnp.broadcast_to(istd, (CHUNK, LANES))
        new = []
        for q in range(wq):
            normed = cents[q] * istd
            ad_s[here, lane(q)] = (normed * scale[:, lane(q)] + shift[:, lane(q)]).astype(BF)
            nrm_s[here, lane(q)] = normed.astype(BF)
            back = jnp.where(live, cot[s, here, lane(q)].astype(F32), 0.0) * gam[:, lane(q)]
            low_s[here, lane(q)] = back.astype(BF)
            new.append(acc[q] + fold(back))
        return tuple(new)

    def add_gbo(accs):
        for q in range(wq):
            gbo[:, lane(q)] += accs[q]

    def tile(t, between=()):
        between = list(between)
        at = pl.ds(pl.multiple_of(t * TILE, TILE), TILE)
        a, b = ad[at, :], low[at, :]
        activation, slope = gelu_parts(dot(a, win[...]) + bias_row[...])
        if between:
            between.pop(0)()
        grad = dot_t(b, wout[...]) * slope
        lo = activation.astype(BF)
        act[at, :] = lo
        if between:
            between.pop(0)()
        dwo[...] += dot_rows(lo, b)
        gbi[...] += fold(grad)
        g = grad.astype(BF)
        pre[at, :] = g
        if between:
            between.pop(0)()
        dwi[...] += dot_rows(a, g)
        if between:
            between.pop(0)()

    done = offs[n + 2]
    ready = offs[s] >= (done + 1) * TILE
    none = (jnp.zeros((8, LANES), F32),) * wq

    @pl.when(ready)
    def _():
        consts = setup()
        state = [none]

        def part(lo_i, hi_i):
            def run():
                for i in range(lo_i, hi_i):
                    state[0] = conv_step(i, state[0], consts)
            return run

        count_c = frames // CHUNK
        cuts = [count_c * k // 4 for k in range(5)]
        tile(done, [part(cuts[k], cuts[k + 1]) for k in range(4)])
        add_gbo(state[0])
        offs[n + 2] = done + 1

    @pl.when(jnp.logical_not(ready))
    def _():
        consts = setup()
        state = none
        for i in range(frames // CHUNK):
            state = conv_step(i, state, consts)
        add_gbo(state)

    @pl.when(s == n - 1)
    def _():
        flush(s)
        end = pl.ds(pl.multiple_of(offs[n], 16), TILE)
        ad[end, :] = jnp.zeros((TILE, width), BF)
        low[end, :] = jnp.zeros((TILE, width), BF)

        def rest(t, _):
            tile(t)
            return 0

        lax.fori_loop(offs[n + 2], offs[n + 1], rest, 0)
        for side, dst in ((0, keep), (1, send)):
            for q in range(wq):
                dst[q * h:(q + 1) * h, :] = dwo[side * h:(side + 1) * h, lane(q)].astype(dst.dtype)
            base = wq * h
            for q in range(h // LANES):
                dst[base + q * width:base + (q + 1) * width, :] = dwi[:, lane(side * (h // LANES) + q)].astype(dst.dtype)


def front(counts, groups, tok, cot, cw, cb, ns, nsh, gamma, bout, buf_a, buf_b, h):
    items, frames, width = tok.shape
    n = items // 2
    rows = n * frames + TILE
    packed = 2 * width * h // LANES
    wq, hq = width // LANES, h // LANES
    n_consts = -(-(cw.shape[0] + 2 + ns.shape[0]) // 8) * 8
    return pl.pallas_call(
        functools.partial(front_kernel, n),
        grid_spec=pl.GridSpec(
            grid=(n,),
            in_specs=[hbm()] * 4 + [whole(v.shape) for v in (cw, cb, ns, nsh, gamma, bout)] + [hbm()] * 2,
            out_specs=[vmem()] * 15 + [smem()],
            scratch_shapes=[pltpu.SMEM((n + 3,), jnp.int32), pltpu.SMEM((items,), jnp.int32), pltpu.SMEM((items,), jnp.int32),
                            pltpu.VMEM((wq, frames + 4 * PAD, LANES), F32),
                            pltpu.VMEM((frames, width), BF), pltpu.VMEM((frames, width), BF),
                            pltpu.VMEM((frames, width), BF), pltpu.VMEM((frames, LANES), F32),
                            pltpu.VMEM((2, 16, LANES), BF), pltpu.VMEM((1, 2 * h), F32),
                            pltpu.VMEM((2 * h, width), F32), pltpu.VMEM((width, 2 * h), F32),
                            pltpu.SemaphoreType.DMA((2, hq + wq + 1)), pltpu.SemaphoreType.DMA((2, n)),
                            pltpu.SemaphoreType.DMA((2,))]),
        out_shape=[struct((rows, width), BF)] * 3 + [struct((rows, LANES), F32)]
        + [struct((rows, 2 * h), BF)] * 2 + [struct((width, 2 * h), BF), struct((2 * h, width), BF)]
        + [struct((packed, LANES), F32), struct((packed, LANES), BF), struct((8, width), F32), struct((8, 2 * h), F32)]
        + [struct((n, frames, width), BF)] * 2 + [struct((n_consts, width), F32), struct((2 + 2 * items,), jnp.int32)],
        compiler_params=params(), cost_estimate=cost(0),
    )(counts, groups, tok, cot, cw, cb, ns, nsh, gamma, bout, buf_a, buf_b)


def combine_kernel(dp, meta, keep, recv, stay, leave):
    m = keep.shape[0] // dp
    for d in range(dp):
        src = pl.ds(pl.multiple_of((meta[1] ^ d) * m, m), m)
        total = keep[src, :] + recv[src, :].astype(F32)
        dst = leave if d % 2 else stay
        dst[d // 2 * m:(d // 2 + 1) * m, :] = total.astype(dst.dtype)


def combine(meta, keep, recv, dp):
    rows = keep.shape[0] // 2
    return pl.pallas_call(
        functools.partial(combine_kernel, dp),
        in_specs=[smem(), vmem(), vmem()], out_specs=[vmem(), vmem()],
        out_shape=[struct((rows, LANES), F32), struct((rows, LANES), BF)],
        compiler_params=params())(meta, keep, recv)


def mix_kernel(n, taps, meta, ad, low, act, pre, win1, wout1, consts, buf_c, buf_d, branch, ag,
               offs, win2, wout2, bias, bias_row, sems):
    copies = weight_copies(buf_c, 0, win2, wout2, bias, sems) + weight_copies(buf_d, 1, win2, wout2, bias, sems)
    for c in copies:
        c.start()
    place_items(n, meta, offs)
    for c in copies:
        c.wait()
    spread_bias(bias, bias_row)

    def tile(t, _):
        at = pl.ds(pl.multiple_of(t * TILE, TILE), TILE)
        a, b = ad[at, :], low[at, :]
        activation, slope = gelu_parts(dot(a, win2[...]) + bias_row[...])
        grad = dot_t(b, wout2[...]) * slope
        branch[at, :] = (dot(act[at, :], wout1[...]) + dot(activation.astype(BF), wout2[...])) + consts[taps + 1:taps + 2, :]
        ag[at, :] = dot_t(pre[at, :], win1[...]) + dot_t(grad.astype(BF), win2[...])
        return 0

    lax.fori_loop(0, offs[n + 1], tile, 0)


def mix(meta, ad, low, act, pre, win, wout, consts, buf_c, buf_d, n, taps):
    rows, width = ad.shape
    h = act.shape[1] // 2
    wq, hq = width // LANES, h // LANES
    return pl.pallas_call(
        functools.partial(mix_kernel, n, taps),
        in_specs=[smem()] + [vmem()] * 7 + [hbm()] * 2,
        out_specs=[vmem(), vmem()],
        scratch_shapes=[pltpu.SMEM((n + 2,), jnp.int32),
                        pltpu.VMEM((width, 2 * h), BF), pltpu.VMEM((2 * h, width), BF),
                        pltpu.VMEM((2, 16, LANES), BF), pltpu.VMEM((1, 2 * h), F32),
                        pltpu.SemaphoreType.DMA((2, hq + wq + 1))],
        out_shape=[struct((rows, width), F32)] * 2,
        compiler_params=params(), cost_estimate=cost(0),
    )(meta, ad, low, act, pre, win, wout, consts, buf_c, buf_d)


def norm_grad_kernel(n, taps, rates, meta, tok, cot, branch, ag, nrm, inv, gbo, gbi, consts,
                     cgp, small_keep, small_send, offs, sums):
    s = pl.program_id(0)
    frames, width = tok.shape[1], tok.shape[2]
    half = taps // 2
    wq = width // LANES
    h = gbi.shape[1] // 2

    @pl.when(s == 0)
    def _():
        place_items(n, meta, offs)
        sums[...] = jnp.zeros_like(sums)

    item = meta[0] * n + s
    count = meta[2 + item]
    group = meta[2 + 2 * n + item]
    off = offs[s]
    scale = pick(consts.at[taps + 2:taps + 2 + rates], group)
    zero = jnp.zeros((8, LANES), F32)
    steps = pl.cdiv(count, WIDE_CHUNK)

    def step(i, accs):
        r0 = pl.multiple_of(i * WIDE_CHUNK, WIDE_CHUNK)
        here = pl.ds(r0, WIDE_CHUNK)
        live = (lax.broadcasted_iota(jnp.int32, (WIDE_CHUNK, LANES), 0) + r0) < count
        src = pl.ds(pl.multiple_of(off + r0, 16), WIDE_CHUNK)
        new = []
        ngs, nrs = [], []
        for q in range(wq):
            a_ls, a_sc, a_sh = accs[3 * q:3 * q + 3]
            br = jnp.where(live, branch[src, lane(q)], 0.0)
            g = jnp.where(live, ag[src, lane(q)], 0.0)
            nr = nrm[src, lane(q)].astype(F32)
            new += [a_ls + fold(cot[s, here, lane(q)].astype(F32) * br), a_sc + fold(g * nr), a_sh + fold(g)]
            ngs.append(g * scale[:, lane(q)])
            nrs.append(nr)
        cross = [a * b for a, b in zip(ngs, nrs)]
        m1 = jnp.sum(sum(ngs[1:], ngs[0]), axis=-1, keepdims=True) * (1.0 / width)
        m2 = jnp.sum(sum(cross[1:], cross[0]), axis=-1, keepdims=True) * (1.0 / width)
        istd = inv[src, :]
        for q in range(wq):
            cg = istd * (ngs[q] - m1 - nrs[q] * m2)
            cgp[s, q, pl.ds(pl.multiple_of(r0 + PAD, 8), WIDE_CHUNK), :] = jnp.where(live, cg, 0.0)
        return tuple(new)

    accs = lax.fori_loop(0, steps, step, (zero,) * (3 * wq))
    for q in range(wq):
        sums[taps + 1, :, lane(q)] += accs[3 * q]
        sums[taps + 2 + group, :, lane(q)] += accs[3 * q + 1]
        sums[taps + 2 + rates + group, :, lane(q)] += accs[3 * q + 2]

    def clear(i, _):
        r0 = pl.multiple_of(i * WIDE_CHUNK, WIDE_CHUNK)
        for q in range(wq):
            cgp[s, q, pl.ds(pl.multiple_of(r0 + PAD, 8), WIDE_CHUNK), :] = jnp.zeros((WIDE_CHUNK, LANES), F32)
        return 0

    lax.fori_loop(steps, frames // WIDE_CHUNK, clear, 0)
    for q in range(wq):
        cgp[s, q, :PAD, :] = jnp.zeros((PAD, LANES), F32)
        cgp[s, q, PAD + frames:, :] = jnp.zeros((cgp.shape[2] - PAD - frames, LANES), F32)

        def conv_step(i, accs):
            r0 = pl.multiple_of(i * WIDE_CHUNK, WIDE_CHUNK)
            here = pl.ds(r0, WIDE_CHUNK)
            live = (lax.broadcasted_iota(jnp.int32, (WIDE_CHUNK, LANES), 0) + r0) < count
            tk = jnp.where(live, tok[s, here, lane(q)].astype(F32), 0.0)
            new = []
            for k in range(taps):
                sh = cgp[s, q, pl.ds(r0 + (PAD + half - k), WIDE_CHUNK), :]
                new.append(accs[k] + fold(tk * sh))
                if k == half:
                    new_bias = accs[taps] + fold(sh)
            return tuple(new) + (new_bias,)

        accs = lax.fori_loop(0, steps, conv_step, (zero,) * (taps + 1))
        for k in range(taps + 1):
            sums[k, :, lane(q)] += accs[k]

    @pl.when(s == n - 1)
    def _():
        last = taps + 2 + 2 * rates
        rows = [jnp.sum(sums[i], axis=0, keepdims=True) for i in range(last)]
        rows.append(jnp.sum(gbo[...], axis=0, keepdims=True))
        gb = jnp.sum(gbi[...], axis=0, keepdims=True)
        fill = jnp.zeros((1, width - h), F32)
        spare = [jnp.zeros((1, width), F32)] * (small_keep.shape[0] - last - 2)
        for side, dst in ((0, small_keep), (1, small_send)):
            tail = [jnp.concatenate([gb[:, side * h:(side + 1) * h], fill], axis=1)]
            dst[...] = jnp.concatenate(rows + tail + spare, axis=0)


def norm_grad(meta, tok, cot, branch, ag, nrm, inv, gbo, gbi, consts, taps, rates):
    n, frames, width = tok.shape
    wq = width // LANES
    n_small = -(-(taps + 4 + 2 * rates) // 8) * 8
    return pl.pallas_call(
        functools.partial(norm_grad_kernel, n, taps, rates), grid=(n,),
        in_specs=[smem()] + [vmem()] * 9, out_specs=[vmem()] * 3,
        scratch_shapes=[pltpu.SMEM((n + 2,), jnp.int32),
                        pltpu.VMEM((taps + 2 + 2 * rates, 8, width), F32)],
        out_shape=[struct((n, wq, frames + 4 * PAD, LANES), F32)] + [struct((n_small, width), F32)] * 2,
        compiler_params=params(), cost_estimate=cost(40000000),
    )(meta, tok, cot, branch, ag, nrm, inv, gbo, gbi, consts)


def block_out_kernel(n, taps, meta, tok, branch, consts, out, own, offs, sems):
    s = pl.program_id(0)
    frames, width = tok.shape[1], tok.shape[2]

    def place(j):
        return pltpu.make_async_copy(own.at[j], out.at[meta[0] * n + j], sems.at[j])

    @pl.when(s == 0)
    def _():
        place_items(n, meta, offs)

    count = meta[2 + meta[0] * n + s]
    off = offs[s]
    gam = consts[taps:taps + 1, :]
    for i in range(frames // CHUNK):
        here = pl.ds(i * CHUNK, CHUNK)
        live = (lax.broadcasted_iota(jnp.int32, (CHUNK, LANES), 0) + i * CHUNK) < count
        src = pl.ds(pl.multiple_of(off + i * CHUNK, 16), CHUNK)
        for q in range(width // LANES):
            value = tok[s, here, lane(q)].astype(F32) + gam[:, lane(q)] * branch[src, lane(q)]
            own[s, here, lane(q)] = jnp.where(live, value, 0.0).astype(BF)
    place(s).start()

    @pl.when(s == n - 1)
    def _():
        for j in range(n):
            place(j).wait()


def block_out(meta, tok, branch, consts, taps):
    n, frames, width = tok.shape
    return pl.pallas_call(
        functools.partial(block_out_kernel, n, taps), grid=(n,),
        in_specs=[smem()] + [vmem()] * 3, out_specs=[hbm(), vmem()],
        scratch_shapes=[pltpu.SMEM((n + 2,), jnp.int32), pltpu.SemaphoreType.DMA((n,))],
        out_shape=[struct((2 * n, frames, width), BF), struct((n, frames, width), BF)],
        compiler_params=params(), cost_estimate=cost(40000000),
    )(meta, tok, branch, consts)


def token_grad_kernel(n, taps, meta, cot, cgp, consts, gtok, gtok_own, stage, sems):
    s = pl.program_id(0)
    frames, width = cot.shape[1], cot.shape[2]
    half = taps // 2
    wq = width // LANES
    count = meta[2 + meta[0] * n + s]
    w = consts[:taps, :]
    steps = pl.cdiv(count, CHUNK)

    def place(j):
        return pltpu.make_async_copy(stage.at[j], gtok.at[meta[0] * n + j], sems.at[j])

    def conv_step(i, _):
        r0 = pl.multiple_of(i * CHUNK, CHUNK)
        here = pl.ds(r0, CHUNK)
        live = (lax.broadcasted_iota(jnp.int32, (CHUNK, LANES), 0) + r0) < count
        for q in range(wq):
            total = cot[s, here, lane(q)].astype(F32)
            for k in range(taps):
                total = total + w[k:k + 1, lane(q)] * cgp[s, q, pl.ds(r0 + (PAD + half - k), CHUNK), :]
            total = jnp.where(live, total, 0.0).astype(BF)
            gtok_own[s, here, lane(q)] = total
            stage[s, here, lane(q)] = total.astype(F32)
        return 0

    lax.fori_loop(0, steps, conv_step, 0)

    def clear(i, _):
        here = pl.ds(pl.multiple_of(i * CHUNK, CHUNK), CHUNK)
        gtok_own[s, here, :] = jnp.zeros((CHUNK, width), BF)
        stage[s, here, :] = jnp.zeros((CHUNK, width), F32)
        return 0

    lax.fori_loop(steps, frames // CHUNK, clear, 0)
    place(s).start()

    @pl.when(s == n - 1)
    def _():
        for j in range(n):
            place(j).wait()


def token_grad(meta, cot, cgp, consts, taps):
    n, frames, width = cot.shape
    return pl.pallas_call(
        functools.partial(token_grad_kernel, n, taps), grid=(n,),
        in_specs=[smem()] + [vmem()] * 3, out_specs=[hbm(), vmem()],
        scratch_shapes=[pltpu.VMEM((n, frames, width), F32), pltpu.SemaphoreType.DMA((n,))],
        out_shape=[struct((2 * n, frames, width), F32), struct((n, frames, width), BF)],
        compiler_params=params(), cost_estimate=cost(40000000),
    )(meta, cot, cgp, consts)


def merge_gtok_kernel(n, meta, other, gtok_in, gtok, stage, sems):
    copies = [pltpu.make_async_copy(stage.at[j], gtok.at[(1 - meta[0]) * n + j], sems.at[j]) for j in range(n)]
    for j in range(n):
        stage[j] = other[j].astype(F32)
        copies[j].start()
    for c in copies:
        c.wait()


def merge_gtok(meta, other, gtok):
    n = other.shape[0]
    return pl.pallas_call(
        functools.partial(merge_gtok_kernel, n),
        in_specs=[smem(), vmem(), hbm()], out_specs=hbm(), out_shape=struct(gtok.shape, F32),
        scratch_shapes=[pltpu.VMEM(other.shape, F32), pltpu.SemaphoreType.DMA((n,))],
        input_output_aliases={2: 0},
        compiler_params=params(), cost_estimate=cost(20000000),
    )(meta, other, gtok)


def merge_out_kernel(n, meta, other, out_in, out, sems):
    copies = [pltpu.make_async_copy(other.at[j], out.at[(1 - meta[0]) * n + j], sems.at[j]) for j in range(n)]
    for c in copies:
        c.start()
    for c in copies:
        c.wait()


def merge_out(meta, other, out):
    n = other.shape[0]
    return pl.pallas_call(
        functools.partial(merge_out_kernel, n),
        in_specs=[smem(), vmem(), hbm()], out_specs=hbm(), out_shape=struct(out.shape, BF),
        scratch_shapes=[pltpu.SemaphoreType.DMA((n,))],
        input_output_aliases={2: 0},
        compiler_params=params(), cost_estimate=cost(10000000),
    )(meta, other, out)


def message_kernel(stay, keep, recv, *refs):
    pieces, (out, mine) = refs[:-2], refs[-2:]
    m = pieces[0].shape[0]
    total = stay[:m, :]
    for piece in pieces:
        total = total + piece[...].astype(F32)
    out[:m, :] = total.astype(BF)
    mine[...] = total.astype(BF)
    small = (keep[...] + recv[...]).astype(BF)
    rows = small.shape[0]
    for q in range(small.shape[1] // LANES):
        out[m + q * rows:m + (q + 1) * rows, :] = small[:, lane(q)]


def make_message(stay, keep, recv, pieces):
    rows = pieces[0].shape[0] + keep.size // LANES
    return pl.pallas_call(message_kernel, in_specs=[vmem()] * (3 + len(pieces)), out_specs=[vmem(), vmem()],
                          out_shape=[struct((rows, LANES), BF), struct(pieces[0].shape, BF)],
                          compiler_params=params())(stay, keep, recv, *pieces)


def relay_kernel(m, *refs):
    sources, out = refs[:-1], refs[-1]
    sums = []
    for d, src in enumerate(sources):
        if d > 1:
            out[(d - 2) * m:(d - 1) * m, :] = src[:m, :]
        sums.append(src[m:, :].astype(F32))
    while len(sums) > 1:
        sums = [a + b for a, b in zip(sums[::2], sums[1::2])]
    out[(len(sources) - 2) * m:, :] = sums[0].astype(BF)


def relay(m, sources):
    rows = (len(sources) - 2) * m + sources[0].shape[0] - m
    return pl.pallas_call(functools.partial(relay_kernel, m), in_specs=[vmem()] * len(sources), out_specs=vmem(),
                          out_shape=struct((rows, LANES), BF), compiler_params=params())(*sources)


def unpack_kernel(dp, taps, rates, meta, mine, theirs, near_1, far_1, near, far, gcw, gcb, gns, gnsh, gwi, gbi, gwo, gbo, gls, full):
    h, width = gwo.shape
    wq, hq = width // LANES, h // LANES
    m = full.shape[0] // dp
    for odd, early, others in ((0, (mine, near_1), near), (1, (theirs, far_1), far)):
        for d in range(dp // 2):
            piece = others[(d - 2) * m:(d - 1) * m, :] if d > 1 else early[d][:m, :]
            at = pl.multiple_of((meta[1] ^ (2 * d + odd)) * m, m)
            full[pl.ds(at, m), :] = piece.astype(F32)
    for q in range(wq):
        gwo[:, lane(q)] = full[q * h:(q + 1) * h, :]
    base = wq * h
    for q in range(hq):
        gwi[:, lane(q)] = full[base + q * width:base + (q + 1) * width, :]
    behind = (dp // 2 - 2) * m
    small = near[behind:, :].astype(F32) + far[behind:, :].astype(F32)
    rows = small.shape[0] // wq
    small = jnp.concatenate([small[q * rows:(q + 1) * rows] for q in range(wq)], axis=1)
    gcw[...] = small[:taps]
    gcb[...] = small[taps]
    gls[...] = small[taps + 1]
    gns[...] = small[taps + 2:taps + 2 + rates]
    gnsh[...] = small[taps + 2 + rates:taps + 2 + 2 * rates]
    at = taps + 2 + 2 * rates
    gbo[...] = small[at]
    gbi[...] = small[at + 1, :h]


def unpack(meta, mine, theirs, near_1, far_1, near, far, dp, taps, rates, width, h):
    shapes = [(taps, width), (width,), (rates, width), (rates, width), (width, h), (h,), (h, width), (width,), (width,)]
    return pl.pallas_call(
        functools.partial(unpack_kernel, dp, taps, rates), in_specs=[smem()] + [vmem()] * 6,
        out_shape=[struct(s, F32) for s in shapes],
        scratch_shapes=[pltpu.VMEM((2 * width * h // LANES, LANES), F32)],
        compiler_params=params())(meta, mine, theirs, near_1, far_1, near, far)


def swap(x, step):
    size = lax.axis_size("tp")
    return lax.ppermute(x, "tp", [(i, i ^ step) for i in range(size)])


def across(x, step):
    size = lax.axis_size("dp")
    return lax.ppermute(x, "dp", [(i, i ^ step) for i in range(size)])


def per_device(tokens, frame_counts, rate_groups, conv_weight, conv_bias, norm_scale, norm_shift,
               weight_in, bias_in, weight_out, bias_out, layer_scale, cotangent):
    width, h = weight_in.shape
    n = tokens.shape[0] // 2
    (tokens, cotangent, conv_weight, conv_bias, norm_scale, norm_shift, weight_in, bias_in, weight_out, bias_out,
     layer_scale, frame_counts, rate_groups) = [pltpu.with_memory_space_constraint(v, pltpu.HBM) for v in (
         tokens, cotangent, conv_weight, conv_bias, norm_scale, norm_shift, weight_in, bias_in, weight_out, bias_out,
         layer_scale, frame_counts, rate_groups)]
    taps, rates = conv_weight.shape[0], norm_scale.shape[0]
    dp = lax.axis_size("dp")
    buf_a = pack(weight_in, bias_in, weight_out)
    buf_b = swap(buf_a, 1)
    buf_c = swap(buf_a, 2)
    buf_d = swap(buf_c, 1)
    ad, nrm, low, inv, act, pre, win, wout, keep, send, gbo, gbi, tok, cot, consts, meta = front(
        frame_counts, rate_groups, tokens, cotangent, conv_weight, conv_bias, norm_scale, norm_shift, layer_scale, bias_out, buf_a, buf_b, h)
    stay, leave = combine(meta, keep, swap(send, 1), dp)
    arrived = across(leave, 1)
    branch, ag = mix(meta, ad, low, act, pre, win, wout, consts, buf_c, buf_d, n, taps)
    arrived, branch = lax.optimization_barrier((arrived, branch))
    stay = (stay + arrived.astype(F32)).reshape(dp // 2, -1, LANES)
    pieces = [across(stay[d].astype(BF), 2 * d) for d in range(1, dp // 2)]

    cgp, small_keep, small_send = norm_grad(meta, tok, cot, branch, ag, nrm, inv, gbo, gbi, consts, taps, rates)
    pieces, small_send, cgp, branch = lax.optimization_barrier((pieces, small_send, cgp, branch))
    small_got = swap(small_send, 1)
    message, mine = make_message(stay.reshape(-1, LANES), small_keep, small_got, pieces)
    m = pieces[0].shape[0]
    near = [message] + [across(message, 2 * d) for d in range(1, dp // 2)]
    theirs = across(mine, 1)
    far_1 = across(message, 3)
    gtok, gtok_own = token_grad(meta, cot, cgp, consts, taps)
    gtok_own, branch = lax.optimization_barrier((gtok_own, branch))
    out, out_own = block_out(meta, tok, branch, consts, taps)
    near, theirs, far_1, out_own = lax.optimization_barrier((near, theirs, far_1, out_own))
    late = relay(m, near)
    far = across(late, 1)
    gtok = merge_gtok(meta, swap(gtok_own, 1), gtok)
    out_b, gtok = lax.optimization_barrier((swap(out_own, 1), gtok))
    out = merge_out(meta, out_b, out)
    far, out, gtok = lax.optimization_barrier((far, out, gtok))
    gcw, gcb, gns, gnsh, gwi, gbi, gwo, gbo, gls = unpack(meta, mine, theirs, near[1], far_1, late, far, dp, taps, rates,
                                                          width, h)
    return (out, gtok, gcw, gcb, gns, gnsh, gwi, gbi, gwo, gbo, gls)


def solution(mesh):
    items, copied = P("dp", None, None), P()
    in_specs = (items, P("dp"), P("dp"), copied, copied, copied, copied, P(None, "tp"), P("tp"), P("tp", None),
                copied, copied, items)
    out_specs = (items, items, copied, copied, copied, copied, P(None, "tp"), P("tp"), P("tp", None), copied, copied)
    return jax.shard_map(per_device, mesh=mesh, in_specs=in_specs, out_specs=out_specs, check_vma=False)
```

```python
import functools

import jax
import jax.numpy as jnp
from jax import lax
from jax.experimental import pallas as pl
from jax.experimental.pallas import tpu as pltpu
from jax.sharding import PartitionSpec as P

EPS = 1e-06
BF, F32 = jnp.bfloat16, jnp.float32
TILE = 256
LANES = 128
PAD = 8
CHUNK = 64
VMEM_LIMIT = 12 * 1024 * 1024


def params(**more):
    return pltpu.CompilerParams(vmem_limit_bytes=VMEM_LIMIT, **more)


def struct(shape, dtype):
    return jax.ShapeDtypeStruct(shape, dtype)


def whole(shape):
    return pl.BlockSpec(shape, lambda *_: (0,) * len(shape))


def hbm():
    return pl.BlockSpec(memory_space=pltpu.HBM)


def smem():
    return pl.BlockSpec(memory_space=pltpu.SMEM)


def cost(size):
    return pl.CostEstimate(flops=0, transcendentals=0, bytes_accessed=size)


def vmem():
    return pl.BlockSpec(memory_space=pltpu.VMEM)


def lane(q):
    return slice(q * LANES, (q + 1) * LANES)


def fold(x):
    return jnp.sum(x.reshape(x.shape[0] // 8, 8, x.shape[1]), axis=0)


def pick(table, group):
    rows = table[...].astype(F32)
    value = rows[0:1]
    for r in range(1, rows.shape[0]):
        value = jnp.where(group == r, rows[r:r + 1], value)
    return value


def as_row(ref):
    return ref[...].astype(F32).reshape(1, -1)


def gelu_parts(pre):
    cdf = 0.5 + 0.5 * lax.erf(pre * 0.7071067811865476)
    density = jnp.exp(-0.5 * pre * pre) * 0.3989422804014327
    return pre * cdf, cdf + pre * density


def dot(a, b):
    return jnp.dot(a, b, preferred_element_type=F32)


def dot_t(a, b):
    return lax.dot_general(a, b, (((1,), (1,)), ((), ())), preferred_element_type=F32)


def dot_rows(a, b):
    return lax.dot_general(a, b, (((0,), (0,)), ((), ())), preferred_element_type=F32)


def place_items(n, meta, offs):
    end = jnp.int32(0)
    for j in range(n):
        offs[j] = end
        end = end + ((meta[2 + meta[0] * n + j] + 15) & -16)
    offs[n] = end
    offs[n + 1] = (end + TILE - 1) // TILE


def pack_kernel(wi, bi, wo, out):
    width, h = wi.shape
    hq, wq = h // LANES, width // LANES
    for q in range(hq):
        out[q * width:(q + 1) * width, :] = wi[:, lane(q)]
    base = hq * width
    for q in range(wq):
        out[base + q * h:base + (q + 1) * h, :] = wo[:, lane(q)]
    base += wq * h
    bias = bi[...].astype(F32).reshape(1, h)
    rows = [bias[:, lane(q)] for q in range(hq)] + [jnp.zeros((1, LANES), F32)] * (16 - hq)
    out[base:base + 16, :] = jnp.concatenate(rows, axis=0).astype(BF)


def pack(wi, bi, wo):
    rows = 2 * wi.size // LANES + 16
    return pl.pallas_call(pack_kernel, out_shape=struct((rows, LANES), BF),
                          compiler_params=params())(wi, bi, wo)


def weight_copies(buf, side, win, wout, bias, sems):
    width, h = win.shape[0], win.shape[1] // 2
    hq, wq = h // LANES, width // LANES
    copies = []
    for q in range(hq):
        at = side * h + q * LANES
        copies.append((buf.at[pl.ds(q * width, width), :], win.at[:, pl.ds(at, LANES)]))
    base = hq * width
    for q in range(wq):
        copies.append((buf.at[pl.ds(base + q * h, h), :], wout.at[pl.ds(side * h, h), pl.ds(q * LANES, LANES)]))
    copies.append((buf.at[pl.ds(base + wq * h, 16), :], bias.at[side]))
    return [pltpu.make_async_copy(src, dst, sems.at[side, i]) for i, (src, dst) in enumerate(copies)]


def spread_bias(bias, row):
    hq = row.shape[1] // LANES // 2
    for side in range(2):
        for q in range(hq):
            at = side * hq + q
            row[:, lane(at)] = bias[side, q:q + 1, :].astype(F32)


def front_kernel(n, counts_hbm, groups_hbm, tok_hbm, cot_hbm, cw, cb, ns, nsh, gamma, bout, buf_a, buf_b,
                 ad, nrm, low, inv, act, pre, win, wout, keep, send, gbo, gbi, tok, cot, consts, meta,
                 offs, counts_s, groups_s, pad, ad_s, nrm_s, low_s, inv_s, bias, bias_row, dwo, dwi, sems, item_sems, meta_sems):
    s = pl.program_id(0)
    frames, width = tok.shape[1], tok.shape[2]
    taps, rates = cw.shape[0], ns.shape[0]
    half = taps // 2
    wq = width // LANES
    h = win.shape[1] // 2
    copies = weight_copies(buf_a, 0, win, wout, bias, sems) + weight_copies(buf_b, 1, win, wout, bias, sems)

    def fetch(j):
        at = (lax.axis_index("tp") & 1) * n + j
        return [pltpu.make_async_copy(src.at[at], dst.at[j], item_sems.at[i, j])
                for i, (src, dst) in enumerate(((tok_hbm, tok), (cot_hbm, cot)))]

    @pl.when(s == 0)
    def _():
        tables = [pltpu.make_async_copy(counts_hbm, counts_s, meta_sems.at[0]),
                  pltpu.make_async_copy(groups_hbm, groups_s, meta_sems.at[1])]
        for c in tables + fetch(0) + fetch(1):
            c.start()
        for c in copies:
            c.start()
        for j in range(2, n):
            for c in fetch(j):
                c.start()
        consts[...] = jnp.zeros_like(consts)
        consts[:taps, :] = cw[...].astype(F32)
        consts[taps:taps + 1, :] = as_row(gamma)
        consts[taps + 1:taps + 2, :] = as_row(bout)
        consts[taps + 2:taps + 2 + rates, :] = ns[...].astype(F32)
        offs[n + 2] = 0
        gbo[...] = jnp.zeros_like(gbo)
        pad[...] = jnp.zeros_like(pad)
        for stage in (ad_s, nrm_s, low_s, inv_s):
            stage[...] = jnp.zeros_like(stage)
        meta[0] = lax.axis_index("tp") & 1
        meta[1] = lax.axis_index("dp")
        for c in tables:
            c.wait()
        for j in range(2 * n):
            meta[2 + j] = counts_s[j]
            meta[2 + 2 * n + j] = groups_s[j]
        place_items(n, meta, offs)

    def flush(j):
        dst = pl.ds(pl.multiple_of(offs[j], 16), frames)
        for whole_ref, stage in ((ad, ad_s), (nrm, nrm_s), (low, low_s), (inv, inv_s)):
            whole_ref[dst, :] = stage[...]

    @pl.when(s > 0)
    def _():
        flush(s - 1)

    @pl.when(s == 1)
    def _():
        for c in copies:
            c.wait()
        spread_bias(bias, bias_row)
        dwo[...] = jnp.zeros_like(dwo)
        dwi[...] = jnp.zeros_like(dwi)
        gbi[...] = jnp.zeros_like(gbi)

    for c in fetch(s):
        c.wait()
    item = meta[0] * n + s
    count = meta[2 + item]
    group = meta[2 + 2 * n + item]

    def setup():
        rows = lax.broadcasted_iota(jnp.int32, (frames, LANES), 0)
        for q in range(wq):
            pad[q, PAD:PAD + frames, :] = jnp.where(rows < count, tok[s, :, lane(q)].astype(F32), 0.0)
        return pick(ns, group), pick(nsh, group), as_row(gamma), as_row(cb), cw[...].astype(F32)

    def conv_step(i, acc, consts):
        scale, shift, gam, conv_bias, w = consts
        r0 = i * CHUNK if isinstance(i, int) else pl.multiple_of(i * CHUNK, CHUNK)
        here = pl.ds(r0, CHUNK)
        live = (lax.broadcasted_iota(jnp.int32, (CHUNK, LANES), 0) + r0) < count
        convs = []
        for q in range(wq):
            conv = conv_bias[:, lane(q)]
            for k in range(taps):
                conv = conv + w[k:k + 1, lane(q)] * pad[q, pl.ds(r0 + (PAD - half + k), CHUNK), :]
            convs.append(conv)
        mean = jnp.sum(sum(convs[1:], convs[0]), axis=-1, keepdims=True) * (1.0 / width)
        cents = [c - mean for c in convs]
        sq = [c * c for c in cents]
        var = jnp.sum(sum(sq[1:], sq[0]), axis=-1, keepdims=True) * (1.0 / width)
        istd = lax.rsqrt(var + EPS)
        inv_s[here, :] = jnp.broadcast_to(istd, (CHUNK, LANES))
        new = []
        for q in range(wq):
            normed = cents[q] * istd
            ad_s[here, lane(q)] = (normed * scale[:, lane(q)] + shift[:, lane(q)]).astype(BF)
            nrm_s[here, lane(q)] = normed.astype(BF)
            back = jnp.where(live, cot[s, here, lane(q)].astype(F32), 0.0) * gam[:, lane(q)]
            low_s[here, lane(q)] = back.astype(BF)
            new.append(acc[q] + fold(back))
        return tuple(new)

    def add_gbo(accs):
        for q in range(wq):
            gbo[:, lane(q)] += accs[q]

    def tile(t, between=()):
        between = list(between)
        at = pl.ds(pl.multiple_of(t * TILE, TILE), TILE)
        a, b = ad[at, :], low[at, :]
        activation, slope = gelu_parts(dot(a, win[...]) + bias_row[...])
        if between:
            between.pop(0)()
        grad = dot_t(b, wout[...]) * slope
        lo = activation.astype(BF)
        act[at, :] = lo
        if between:
            between.pop(0)()
        dwo[...] += dot_rows(lo, b)
        gbi[...] += fold(grad)
        g = grad.astype(BF)
        pre[at, :] = g
        if between:
            between.pop(0)()
        dwi[...] += dot_rows(a, g)
        if between:
            between.pop(0)()

    done = offs[n + 2]
    ready = offs[s] >= (done + 1) * TILE
    none = (jnp.zeros((8, LANES), F32),) * wq

    def conv_with(chunks, with_tile):
        consts = setup()
        state = [none]

        def part(lo_i, hi_i):
            def run():
                for i in range(lo_i, hi_i):
                    state[0] = conv_step(i, state[0], consts)
            return run

        cuts = [chunks * k // 4 for k in range(5)]
        parts = [part(cuts[k], cuts[k + 1]) for k in range(4)]
        if with_tile:
            tile(done, parts)
        else:
            for run in parts:
                run()
        add_gbo(state[0])
        if with_tile:
            offs[n + 2] = done + 1

    all_chunks = frames // CHUNK
    short = count <= (all_chunks - 1) * CHUNK
    for with_tile in (True, False):
        for chunks in (all_chunks - 1, all_chunks):
            fits = short if chunks < all_chunks else jnp.logical_not(short)
            pl.when((ready == with_tile) & fits)(functools.partial(conv_with, chunks, with_tile))

    @pl.when(s == n - 1)
    def _():
        flush(s)
        end = pl.ds(pl.multiple_of(offs[n], 16), TILE)
        ad[end, :] = jnp.zeros((TILE, width), BF)
        low[end, :] = jnp.zeros((TILE, width), BF)

        def rest(t, _):
            tile(t)
            return 0

        lax.fori_loop(offs[n + 2], offs[n + 1], rest, 0)
        for side, dst in ((0, keep), (1, send)):
            for q in range(wq):
                dst[q * h:(q + 1) * h, :] = dwo[side * h:(side + 1) * h, lane(q)].astype(dst.dtype)
            base = wq * h
            for q in range(h // LANES):
                dst[base + q * width:base + (q + 1) * width, :] = dwi[:, lane(side * (h // LANES) + q)].astype(dst.dtype)


def front(counts, groups, tok, cot, cw, cb, ns, nsh, gamma, bout, buf_a, buf_b, h):
    items, frames, width = tok.shape
    n = items // 2
    rows = n * frames + TILE
    packed = 2 * width * h // LANES
    wq, hq = width // LANES, h // LANES
    n_consts = -(-(cw.shape[0] + 2 + ns.shape[0]) // 8) * 8
    return pl.pallas_call(
        functools.partial(front_kernel, n),
        grid_spec=pl.GridSpec(
            grid=(n,),
            in_specs=[hbm()] * 4 + [whole(v.shape) for v in (cw, cb, ns, nsh, gamma, bout)] + [hbm()] * 2,
            out_specs=[vmem()] * 15 + [smem()],
            scratch_shapes=[pltpu.SMEM((n + 3,), jnp.int32), pltpu.SMEM((items,), jnp.int32), pltpu.SMEM((items,), jnp.int32),
                            pltpu.VMEM((wq, frames + 4 * PAD, LANES), F32),
                            pltpu.VMEM((frames, width), BF), pltpu.VMEM((frames, width), BF),
                            pltpu.VMEM((frames, width), BF), pltpu.VMEM((frames, LANES), F32),
                            pltpu.VMEM((2, 16, LANES), BF), pltpu.VMEM((1, 2 * h), F32),
                            pltpu.VMEM((2 * h, width), F32), pltpu.VMEM((width, 2 * h), F32),
                            pltpu.SemaphoreType.DMA((2, hq + wq + 1)), pltpu.SemaphoreType.DMA((2, n)),
                            pltpu.SemaphoreType.DMA((2,))]),
        out_shape=[struct((rows, width), BF)] * 3 + [struct((rows, LANES), F32)]
        + [struct((rows, 2 * h), BF)] * 2 + [struct((width, 2 * h), BF), struct((2 * h, width), BF)]
        + [struct((packed, LANES), F32), struct((packed, LANES), BF), struct((8, width), F32), struct((8, 2 * h), F32)]
        + [struct((n, frames, width), BF)] * 2 + [struct((n_consts, width), F32), struct((2 + 2 * items,), jnp.int32)],
        compiler_params=params(), cost_estimate=cost(0),
    )(counts, groups, tok, cot, cw, cb, ns, nsh, gamma, bout, buf_a, buf_b)


def combine_kernel(dp, meta, keep, recv, stay, leave):
    m = keep.shape[0] // dp
    for d in range(dp):
        src = pl.ds(pl.multiple_of((meta[1] ^ d) * m, m), m)
        total = keep[src, :] + recv[src, :].astype(F32)
        dst = leave if d % 2 else stay
        dst[d // 2 * m:(d // 2 + 1) * m, :] = total.astype(dst.dtype)


def combine(meta, keep, recv, dp):
    rows = keep.shape[0] // 2
    return pl.pallas_call(
        functools.partial(combine_kernel, dp),
        in_specs=[smem(), vmem(), vmem()], out_specs=[vmem(), vmem()],
        out_shape=[struct((rows, LANES), F32), struct((rows, LANES), BF)],
        compiler_params=params())(meta, keep, recv)


def mix_kernel(n, taps, meta, ad, low, act, pre, win1, wout1, consts, buf_c, buf_d, branch, ag,
               offs, win2, wout2, bias, bias_row, sems):
    copies = weight_copies(buf_c, 0, win2, wout2, bias, sems) + weight_copies(buf_d, 1, win2, wout2, bias, sems)
    for c in copies:
        c.start()
    place_items(n, meta, offs)

    def own(at):
        return dot(act[at, :], wout1[...]), dot_t(pre[at, :], win1[...])

    def rest(at, own_branch, own_ag):
        a, b = ad[at, :], low[at, :]
        activation, slope = gelu_parts(dot(a, win2[...]) + bias_row[...])
        grad = dot_t(b, wout2[...]) * slope
        branch[at, :] = (own_branch + dot(activation.astype(BF), wout2[...])) + consts[taps + 1:taps + 2, :]
        ag[at, :] = own_ag + dot_t(grad.astype(BF), win2[...])

    first = pl.ds(0, TILE)
    branch[first, :], ag[first, :] = own(first)
    for c in copies:
        c.wait()
    spread_bias(bias, bias_row)
    rest(first, branch[first, :], ag[first, :])

    def tile(t, _):
        at = pl.ds(pl.multiple_of(t * TILE, TILE), TILE)
        rest(at, *own(at))
        return 0

    lax.fori_loop(1, offs[n + 1], tile, 0)


def mix(meta, ad, low, act, pre, win, wout, consts, buf_c, buf_d, n, taps):
    rows, width = ad.shape
    h = act.shape[1] // 2
    wq, hq = width // LANES, h // LANES
    return pl.pallas_call(
        functools.partial(mix_kernel, n, taps),
        in_specs=[smem()] + [vmem()] * 7 + [hbm()] * 2,
        out_specs=[vmem(), vmem()],
        scratch_shapes=[pltpu.SMEM((n + 2,), jnp.int32),
                        pltpu.VMEM((width, 2 * h), BF), pltpu.VMEM((2 * h, width), BF),
                        pltpu.VMEM((2, 16, LANES), BF), pltpu.VMEM((1, 2 * h), F32),
                        pltpu.SemaphoreType.DMA((2, hq + wq + 1))],
        out_shape=[struct((rows, width), F32)] * 2,
        compiler_params=params(), cost_estimate=cost(0),
    )(meta, ad, low, act, pre, win, wout, consts, buf_c, buf_d)


def norm_grad_kernel(n, taps, rates, meta, tok, cot, branch, ag, nrm, inv, gbo, gbi, consts,
                     cgp, small_keep, small_send, offs, sums):
    s = pl.program_id(0)
    frames, width = tok.shape[1], tok.shape[2]
    half = taps // 2
    wq = width // LANES
    h = gbi.shape[1] // 2

    @pl.when(s == 0)
    def _():
        place_items(n, meta, offs)
        sums[...] = jnp.zeros_like(sums)

    item = meta[0] * n + s
    count = meta[2 + item]
    group = meta[2 + 2 * n + item]
    off = offs[s]
    scale = pick(consts.at[taps + 2:taps + 2 + rates], group)
    zero = jnp.zeros((8, LANES), F32)
    steps = pl.cdiv(count, CHUNK)
    wide = steps // 2

    def step(r0, size, accs):
        here = pl.ds(r0, size)
        live = (lax.broadcasted_iota(jnp.int32, (size, LANES), 0) + r0) < count
        src = pl.ds(pl.multiple_of(off + r0, 16), size)
        new = []
        ngs, nrs = [], []
        for q in range(wq):
            a_ls, a_sc, a_sh = accs[3 * q:3 * q + 3]
            br = jnp.where(live, branch[src, lane(q)], 0.0)
            g = jnp.where(live, ag[src, lane(q)], 0.0)
            nr = nrm[src, lane(q)].astype(F32)
            new += [a_ls + fold(cot[s, here, lane(q)].astype(F32) * br), a_sc + fold(g * nr), a_sh + fold(g)]
            ngs.append(g * scale[:, lane(q)])
            nrs.append(nr)
        cross = [a * b for a, b in zip(ngs, nrs)]
        m1 = jnp.sum(sum(ngs[1:], ngs[0]), axis=-1, keepdims=True) * (1.0 / width)
        m2 = jnp.sum(sum(cross[1:], cross[0]), axis=-1, keepdims=True) * (1.0 / width)
        istd = inv[src, :]
        for q in range(wq):
            cg = istd * (ngs[q] - m1 - nrs[q] * m2)
            cgp[s, q, pl.ds(pl.multiple_of(r0 + PAD, 8), size), :] = jnp.where(live, cg, 0.0)
        return tuple(new)

    def both_sizes(run, width_of_state, add):
        add(lax.fori_loop(0, wide, lambda i, accs: run(pl.multiple_of(i * 2 * CHUNK, 2 * CHUNK), 2 * CHUNK, accs),
                          (zero,) * width_of_state))

        @pl.when(steps > 2 * wide)
        def _():
            add(run(pl.multiple_of(wide * 2 * CHUNK, 2 * CHUNK), CHUNK, (zero,) * width_of_state))

    def add_norm(accs):
        for q in range(wq):
            sums[taps + 1, :, lane(q)] += accs[3 * q]
            sums[taps + 2 + group, :, lane(q)] += accs[3 * q + 1]
            sums[taps + 2 + rates + group, :, lane(q)] += accs[3 * q + 2]

    both_sizes(step, 3 * wq, add_norm)

    def clear(i, _):
        r0 = pl.multiple_of(i * CHUNK, CHUNK)
        for q in range(wq):
            cgp[s, q, pl.ds(pl.multiple_of(r0 + PAD, 8), CHUNK), :] = jnp.zeros((CHUNK, LANES), F32)
        return 0

    lax.fori_loop(steps, frames // CHUNK, clear, 0)
    for q in range(wq):
        cgp[s, q, :PAD, :] = jnp.zeros((PAD, LANES), F32)
        cgp[s, q, PAD + frames:, :] = jnp.zeros((cgp.shape[2] - PAD - frames, LANES), F32)

        def conv_step(r0, size, accs):
            here = pl.ds(r0, size)
            live = (lax.broadcasted_iota(jnp.int32, (size, LANES), 0) + r0) < count
            tk = jnp.where(live, tok[s, here, lane(q)].astype(F32), 0.0)
            new = []
            for k in range(taps):
                sh = cgp[s, q, pl.ds(r0 + (PAD + half - k), size), :]
                new.append(accs[k] + fold(tk * sh))
                if k == half:
                    new_bias = accs[taps] + fold(sh)
            return tuple(new) + (new_bias,)

        def add_conv(accs):
            for k in range(taps + 1):
                sums[k, :, lane(q)] += accs[k]

        both_sizes(conv_step, taps + 1, add_conv)

    @pl.when(s == n - 1)
    def _():
        last = taps + 2 + 2 * rates
        rows = [jnp.sum(sums[i], axis=0, keepdims=True) for i in range(last)]
        rows.append(jnp.sum(gbo[...], axis=0, keepdims=True))
        gb = jnp.sum(gbi[...], axis=0, keepdims=True)
        fill = jnp.zeros((1, width - h), F32)
        spare = [jnp.zeros((1, width), F32)] * (small_keep.shape[0] - last - 2)
        for side, dst in ((0, small_keep), (1, small_send)):
            tail = [jnp.concatenate([gb[:, side * h:(side + 1) * h], fill], axis=1)]
            dst[...] = jnp.concatenate(rows + tail + spare, axis=0)


def norm_grad(meta, tok, cot, branch, ag, nrm, inv, gbo, gbi, consts, taps, rates):
    n, frames, width = tok.shape
    wq = width // LANES
    n_small = -(-(taps + 4 + 2 * rates) // 8) * 8
    return pl.pallas_call(
        functools.partial(norm_grad_kernel, n, taps, rates), grid=(n,),
        in_specs=[smem()] + [vmem()] * 9, out_specs=[vmem()] * 3,
        scratch_shapes=[pltpu.SMEM((n + 2,), jnp.int32),
                        pltpu.VMEM((taps + 2 + 2 * rates, 8, width), F32)],
        out_shape=[struct((n, wq, frames + 4 * PAD, LANES), F32)] + [struct((n_small, width), F32)] * 2,
        compiler_params=params(), cost_estimate=cost(40000000),
    )(meta, tok, cot, branch, ag, nrm, inv, gbo, gbi, consts)


def block_out_kernel(n, taps, meta, tok, branch, consts, out, own, offs, sems):
    s = pl.program_id(0)
    frames, width = tok.shape[1], tok.shape[2]

    def place(j):
        return pltpu.make_async_copy(own.at[j], out.at[meta[0] * n + j], sems.at[j])

    @pl.when(s == 0)
    def _():
        place_items(n, meta, offs)

    count = meta[2 + meta[0] * n + s]
    off = offs[s]
    gam = consts[taps:taps + 1, :]
    for i in range(frames // CHUNK):
        here = pl.ds(i * CHUNK, CHUNK)
        live = (lax.broadcasted_iota(jnp.int32, (CHUNK, LANES), 0) + i * CHUNK) < count
        src = pl.ds(pl.multiple_of(off + i * CHUNK, 16), CHUNK)
        for q in range(width // LANES):
            value = tok[s, here, lane(q)].astype(F32) + gam[:, lane(q)] * branch[src, lane(q)]
            own[s, here, lane(q)] = jnp.where(live, value, 0.0).astype(BF)
    place(s).start()

    @pl.when(s == n - 1)
    def _():
        for j in range(n):
            place(j).wait()


def block_out(meta, tok, branch, consts, taps):
    n, frames, width = tok.shape
    return pl.pallas_call(
        functools.partial(block_out_kernel, n, taps), grid=(n,),
        in_specs=[smem()] + [vmem()] * 3, out_specs=[hbm(), vmem()],
        scratch_shapes=[pltpu.SMEM((n + 2,), jnp.int32), pltpu.SemaphoreType.DMA((n,))],
        out_shape=[struct((2 * n, frames, width), BF), struct((n, frames, width), BF)],
        compiler_params=params(), cost_estimate=cost(40000000),
    )(meta, tok, branch, consts)


def token_grad_kernel(n, taps, meta, cot, cgp, consts, gtok, gtok_own, stage, sems):
    s = pl.program_id(0)
    frames, width = cot.shape[1], cot.shape[2]
    half = taps // 2
    wq = width // LANES
    count = meta[2 + meta[0] * n + s]
    w = consts[:taps, :]
    steps = pl.cdiv(count, CHUNK)

    def place(j):
        return pltpu.make_async_copy(stage.at[j], gtok.at[meta[0] * n + j], sems.at[j])

    def conv_step(i, _):
        r0 = pl.multiple_of(i * CHUNK, CHUNK)
        here = pl.ds(r0, CHUNK)
        live = (lax.broadcasted_iota(jnp.int32, (CHUNK, LANES), 0) + r0) < count
        for q in range(wq):
            total = cot[s, here, lane(q)].astype(F32)
            for k in range(taps):
                total = total + w[k:k + 1, lane(q)] * cgp[s, q, pl.ds(r0 + (PAD + half - k), CHUNK), :]
            total = jnp.where(live, total, 0.0).astype(BF)
            gtok_own[s, here, lane(q)] = total
            stage[s, here, lane(q)] = total.astype(F32)
        return 0

    lax.fori_loop(0, steps, conv_step, 0)

    def clear(i, _):
        here = pl.ds(pl.multiple_of(i * CHUNK, CHUNK), CHUNK)
        gtok_own[s, here, :] = jnp.zeros((CHUNK, width), BF)
        stage[s, here, :] = jnp.zeros((CHUNK, width), F32)
        return 0

    lax.fori_loop(steps, frames // CHUNK, clear, 0)
    place(s).start()

    @pl.when(s == n - 1)
    def _():
        for j in range(n):
            place(j).wait()


def token_grad(meta, cot, cgp, consts, taps):
    n, frames, width = cot.shape
    return pl.pallas_call(
        functools.partial(token_grad_kernel, n, taps), grid=(n,),
        in_specs=[smem()] + [vmem()] * 3, out_specs=[hbm(), vmem()],
        scratch_shapes=[pltpu.VMEM((n, frames, width), F32), pltpu.SemaphoreType.DMA((n,))],
        out_shape=[struct((2 * n, frames, width), F32), struct((n, frames, width), BF)],
        compiler_params=params(), cost_estimate=cost(40000000),
    )(meta, cot, cgp, consts)


def merge_gtok_kernel(n, meta, other, gtok_in, gtok, stage, sems):
    copies = [pltpu.make_async_copy(stage.at[j], gtok.at[(1 - meta[0]) * n + j], sems.at[j]) for j in range(n)]
    for j in range(n):
        stage[j] = other[j].astype(F32)
        copies[j].start()
    for c in copies:
        c.wait()


def merge_gtok(meta, other, gtok):
    n = other.shape[0]
    return pl.pallas_call(
        functools.partial(merge_gtok_kernel, n),
        in_specs=[smem(), vmem(), hbm()], out_specs=hbm(), out_shape=struct(gtok.shape, F32),
        scratch_shapes=[pltpu.VMEM(other.shape, F32), pltpu.SemaphoreType.DMA((n,))],
        input_output_aliases={2: 0},
        compiler_params=params(), cost_estimate=cost(20000000),
    )(meta, other, gtok)


def merge_out_kernel(n, meta, other, out_in, out, sems):
    copies = [pltpu.make_async_copy(other.at[j], out.at[(1 - meta[0]) * n + j], sems.at[j]) for j in range(n)]
    for c in copies:
        c.start()
    for c in copies:
        c.wait()


def merge_out(meta, other, out):
    n = other.shape[0]
    return pl.pallas_call(
        functools.partial(merge_out_kernel, n),
        in_specs=[smem(), vmem(), hbm()], out_specs=hbm(), out_shape=struct(out.shape, BF),
        scratch_shapes=[pltpu.SemaphoreType.DMA((n,))],
        input_output_aliases={2: 0},
        compiler_params=params(), cost_estimate=cost(10000000),
    )(meta, other, out)


def message_kernel(stay, keep, recv, *refs):
    pieces, (out, mine) = refs[:-2], refs[-2:]
    m = pieces[0].shape[0]
    total = stay[:m, :]
    for piece in pieces:
        total = total + piece[...].astype(F32)
    out[:m, :] = total.astype(BF)
    mine[...] = total.astype(BF)
    small = (keep[...] + recv[...]).astype(BF)
    rows = small.shape[0]
    for q in range(small.shape[1] // LANES):
        out[m + q * rows:m + (q + 1) * rows, :] = small[:, lane(q)]


def make_message(stay, keep, recv, pieces):
    rows = pieces[0].shape[0] + keep.size // LANES
    return pl.pallas_call(message_kernel, in_specs=[vmem()] * (3 + len(pieces)), out_specs=[vmem(), vmem()],
                          out_shape=[struct((rows, LANES), BF), struct(pieces[0].shape, BF)],
                          compiler_params=params())(stay, keep, recv, *pieces)


def relay_kernel(m, *refs):
    sources, out = refs[:-1], refs[-1]
    sums = []
    for d, src in enumerate(sources):
        if d > 1:
            out[(d - 2) * m:(d - 1) * m, :] = src[:m, :]
        sums.append(src[m:, :].astype(F32))
    while len(sums) > 1:
        sums = [a + b for a, b in zip(sums[::2], sums[1::2])]
    out[(len(sources) - 2) * m:, :] = sums[0].astype(BF)


def relay(m, sources):
    rows = (len(sources) - 2) * m + sources[0].shape[0] - m
    return pl.pallas_call(functools.partial(relay_kernel, m), in_specs=[vmem()] * len(sources), out_specs=vmem(),
                          out_shape=struct((rows, LANES), BF), compiler_params=params())(*sources)


def unpack_kernel(dp, taps, rates, meta, mine, theirs, near_1, far_1, near, far, gcw, gcb, gns, gnsh, gwi, gbi, gwo, gbo, gls, full):
    h, width = gwo.shape
    wq, hq = width // LANES, h // LANES
    m = full.shape[0] // dp
    for odd, early, others in ((0, (mine, near_1), near), (1, (theirs, far_1), far)):
        for d in range(dp // 2):
            piece = others[(d - 2) * m:(d - 1) * m, :] if d > 1 else early[d][:m, :]
            at = pl.multiple_of((meta[1] ^ (2 * d + odd)) * m, m)
            full[pl.ds(at, m), :] = piece.astype(F32)
    for q in range(wq):
        gwo[:, lane(q)] = full[q * h:(q + 1) * h, :]
    base = wq * h
    for q in range(hq):
        gwi[:, lane(q)] = full[base + q * width:base + (q + 1) * width, :]
    behind = (dp // 2 - 2) * m
    small = near[behind:, :].astype(F32) + far[behind:, :].astype(F32)
    rows = small.shape[0] // wq
    small = jnp.concatenate([small[q * rows:(q + 1) * rows] for q in range(wq)], axis=1)
    gcw[...] = small[:taps]
    gcb[...] = small[taps]
    gls[...] = small[taps + 1]
    gns[...] = small[taps + 2:taps + 2 + rates]
    gnsh[...] = small[taps + 2 + rates:taps + 2 + 2 * rates]
    at = taps + 2 + 2 * rates
    gbo[...] = small[at]
    gbi[...] = small[at + 1, :h]


def unpack(meta, mine, theirs, near_1, far_1, near, far, dp, taps, rates, width, h):
    shapes = [(taps, width), (width,), (rates, width), (rates, width), (width, h), (h,), (h, width), (width,), (width,)]
    return pl.pallas_call(
        functools.partial(unpack_kernel, dp, taps, rates), in_specs=[smem()] + [vmem()] * 6,
        out_shape=[struct(s, F32) for s in shapes],
        scratch_shapes=[pltpu.VMEM((2 * width * h // LANES, LANES), F32)],
        compiler_params=params())(meta, mine, theirs, near_1, far_1, near, far)


def swap(x, step):
    size = lax.axis_size("tp")
    return lax.ppermute(x, "tp", [(i, i ^ step) for i in range(size)])


def across(x, step):
    size = lax.axis_size("dp")
    return lax.ppermute(x, "dp", [(i, i ^ step) for i in range(size)])


def per_device(tokens, frame_counts, rate_groups, conv_weight, conv_bias, norm_scale, norm_shift,
               weight_in, bias_in, weight_out, bias_out, layer_scale, cotangent):
    width, h = weight_in.shape
    n = tokens.shape[0] // 2
    (tokens, cotangent, conv_weight, conv_bias, norm_scale, norm_shift, weight_in, bias_in, weight_out, bias_out,
     layer_scale, frame_counts, rate_groups) = [pltpu.with_memory_space_constraint(v, pltpu.HBM) for v in (
         tokens, cotangent, conv_weight, conv_bias, norm_scale, norm_shift, weight_in, bias_in, weight_out, bias_out,
         layer_scale, frame_counts, rate_groups)]
    taps, rates = conv_weight.shape[0], norm_scale.shape[0]
    dp = lax.axis_size("dp")
    buf_a = pack(weight_in, bias_in, weight_out)
    buf_b = swap(buf_a, 1)
    buf_c = swap(buf_a, 2)
    buf_d = swap(buf_c, 1)
    ad, nrm, low, inv, act, pre, win, wout, keep, send, gbo, gbi, tok, cot, consts, meta = front(
        frame_counts, rate_groups, tokens, cotangent, conv_weight, conv_bias, norm_scale, norm_shift, layer_scale, bias_out, buf_a, buf_b, h)
    stay, leave = combine(meta, keep, swap(send, 1), dp)
    arrived = across(leave, 1)
    branch, ag = mix(meta, ad, low, act, pre, win, wout, consts, buf_c, buf_d, n, taps)
    arrived, branch = lax.optimization_barrier((arrived, branch))
    stay = (stay + arrived.astype(F32)).reshape(dp // 2, -1, LANES)
    pieces = [across(stay[d].astype(BF), 2 * d) for d in range(1, dp // 2)]

    cgp, small_keep, small_send = norm_grad(meta, tok, cot, branch, ag, nrm, inv, gbo, gbi, consts, taps, rates)
    pieces, small_send, cgp, branch = lax.optimization_barrier((pieces, small_send, cgp, branch))
    small_got = swap(small_send, 1)
    message, mine = make_message(stay.reshape(-1, LANES), small_keep, small_got, pieces)
    m = pieces[0].shape[0]
    near = [message] + [across(message, 2 * d) for d in range(1, dp // 2)]
    theirs = across(mine, 1)
    far_1 = across(message, 3)
    gtok, gtok_own = token_grad(meta, cot, cgp, consts, taps)
    gtok_own, branch = lax.optimization_barrier((gtok_own, branch))
    out, out_own = block_out(meta, tok, branch, consts, taps)
    near, theirs, far_1, out_own = lax.optimization_barrier((near, theirs, far_1, out_own))
    late = relay(m, near)
    far = across(late, 1)
    gtok = merge_gtok(meta, swap(gtok_own, 1), gtok)
    out_b, gtok = lax.optimization_barrier((swap(out_own, 1), gtok))
    out = merge_out(meta, out_b, out)
    far, out, gtok = lax.optimization_barrier((far, out, gtok))
    gcw, gcb, gns, gnsh, gwi, gbi, gwo, gbo, gls = unpack(meta, mine, theirs, near[1], far_1, late, far, dp, taps, rates,
                                                          width, h)
    return (out, gtok, gcw, gcb, gns, gnsh, gwi, gbi, gwo, gbo, gls)


def solution(mesh):
    items, copied = P("dp", None, None), P()
    in_specs = (items, P("dp"), P("dp"), copied, copied, copied, copied, P(None, "tp"), P("tp"), P("tp", None),
                copied, copied, items)
    out_specs = (items, items, copied, copied, copied, copied, P(None, "tp"), P("tp"), P("tp", None), copied, copied)
    return jax.shard_map(per_device, mesh=mesh, in_specs=in_specs, out_specs=out_specs, check_vma=False)
```

```python
import functools

import jax
import jax.numpy as jnp
from jax import lax
from jax.experimental import pallas as pl
from jax.experimental.pallas import tpu as pltpu
from jax.sharding import PartitionSpec as P

EPS = 1e-06
BF, F32 = jnp.bfloat16, jnp.float32
TILE = 256
LANES = 128
PAD = 8
CHUNK = 64
VMEM_LIMIT = 12 * 1024 * 1024


def params(**more):
    return pltpu.CompilerParams(vmem_limit_bytes=VMEM_LIMIT, **more)


def struct(shape, dtype):
    return jax.ShapeDtypeStruct(shape, dtype)


def whole(shape):
    return pl.BlockSpec(shape, lambda *_: (0,) * len(shape))


def hbm():
    return pl.BlockSpec(memory_space=pltpu.HBM)


def smem():
    return pl.BlockSpec(memory_space=pltpu.SMEM)


def cost(size):
    return pl.CostEstimate(flops=0, transcendentals=0, bytes_accessed=size)


def vmem():
    return pl.BlockSpec(memory_space=pltpu.VMEM)


def lane(q):
    return slice(q * LANES, (q + 1) * LANES)


def fold(x):
    return jnp.sum(x.reshape(x.shape[0] // 8, 8, x.shape[1]), axis=0)


def pick(table, group):
    rows = table[...].astype(F32)
    value = rows[0:1]
    for r in range(1, rows.shape[0]):
        value = jnp.where(group == r, rows[r:r + 1], value)
    return value


def as_row(ref):
    return ref[...].astype(F32).reshape(1, -1)


def gelu_parts(pre):
    cdf = 0.5 + 0.5 * lax.erf(pre * 0.7071067811865476)
    density = jnp.exp(-0.5 * pre * pre) * 0.3989422804014327
    return pre * cdf, cdf + pre * density


def dot(a, b):
    return jnp.dot(a, b, preferred_element_type=F32)


def dot_t(a, b):
    return lax.dot_general(a, b, (((1,), (1,)), ((), ())), preferred_element_type=F32)


def dot_rows(a, b):
    return lax.dot_general(a, b, (((0,), (0,)), ((), ())), preferred_element_type=F32)


def place_items(n, meta, offs):
    end = jnp.int32(0)
    for j in range(n):
        offs[j] = end
        end = end + ((meta[2 + meta[0] * n + j] + 15) & -16)
    offs[n] = end
    offs[n + 1] = (end + TILE - 1) // TILE


def pack_kernel(wi, bi, wo, out):
    width, h = wi.shape
    hq, wq = h // LANES, width // LANES
    for q in range(hq):
        out[q * width:(q + 1) * width, :] = wi[:, lane(q)]
    base = hq * width
    for q in range(wq):
        out[base + q * h:base + (q + 1) * h, :] = wo[:, lane(q)]
    base += wq * h
    bias = bi[...].astype(F32).reshape(1, h)
    rows = [bias[:, lane(q)] for q in range(hq)] + [jnp.zeros((1, LANES), F32)] * (16 - hq)
    out[base:base + 16, :] = jnp.concatenate(rows, axis=0).astype(BF)


def pack(wi, bi, wo):
    rows = 2 * wi.size // LANES + 16
    return pl.pallas_call(pack_kernel, out_shape=struct((rows, LANES), BF),
                          compiler_params=params())(wi, bi, wo)


def weight_copies(buf, side, win, wout, bias, sems):
    width, h = win.shape[0], win.shape[1] // 2
    hq, wq = h // LANES, width // LANES
    copies = []
    for q in range(hq):
        at = side * h + q * LANES
        copies.append((buf.at[pl.ds(q * width, width), :], win.at[:, pl.ds(at, LANES)]))
    base = hq * width
    for q in range(wq):
        copies.append((buf.at[pl.ds(base + q * h, h), :], wout.at[pl.ds(side * h, h), pl.ds(q * LANES, LANES)]))
    copies.append((buf.at[pl.ds(base + wq * h, 16), :], bias.at[side]))
    return [pltpu.make_async_copy(src, dst, sems.at[side, i]) for i, (src, dst) in enumerate(copies)]


def spread_bias(bias, row):
    hq = row.shape[1] // LANES // 2
    for side in range(2):
        for q in range(hq):
            at = side * hq + q
            row[:, lane(at)] = bias[side, q:q + 1, :].astype(F32)


def front_kernel(n, counts_hbm, groups_hbm, tok_hbm, cot_hbm, cw, cb, ns, nsh, gamma, bout, buf_a, buf_b,
                 ad, nrm, low, inv, act, pre, win, wout, keep, send, gbo, gbi, tok, cot, consts, tokp, meta,
                 offs, counts_s, groups_s, pad, ad_s, nrm_s, low_s, inv_s, bias, bias_row, dwo, dwi, sems, item_sems, meta_sems, packed_sem):
    s = pl.program_id(0)
    frames, width = tok.shape[1], tok.shape[2]
    taps, rates = cw.shape[0], ns.shape[0]
    half = taps // 2
    wq = width // LANES
    h = win.shape[1] // 2
    copies = weight_copies(buf_a, 0, win, wout, bias, sems) + weight_copies(buf_b, 1, win, wout, bias, sems)

    def fetch(j):
        at = (lax.axis_index("tp") & 1) * n + j
        return [pltpu.make_async_copy(src.at[at], dst.at[j], item_sems.at[i, j])
                for i, (src, dst) in enumerate(((tok_hbm, tok), (cot_hbm, cot)))]

    @pl.when(s == 0)
    def _():
        tables = [pltpu.make_async_copy(counts_hbm, counts_s, meta_sems.at[0]),
                  pltpu.make_async_copy(groups_hbm, groups_s, meta_sems.at[1])]
        for c in tables + fetch(0) + fetch(1):
            c.start()
        for c in copies:
            c.start()
        for j in range(2, n):
            for c in fetch(j):
                c.start()
        consts[...] = jnp.zeros_like(consts)
        consts[:taps, :] = cw[...].astype(F32)
        consts[taps:taps + 1, :] = as_row(gamma)
        consts[taps + 1:taps + 2, :] = as_row(bout)
        consts[taps + 2:taps + 2 + rates, :] = ns[...].astype(F32)
        offs[n + 2] = 0
        gbo[...] = jnp.zeros_like(gbo)
        pad[...] = jnp.zeros_like(pad)
        for stage in (ad_s, nrm_s, low_s, inv_s):
            stage[...] = jnp.zeros_like(stage)
        meta[0] = lax.axis_index("tp") & 1
        meta[1] = lax.axis_index("dp")
        for c in tables:
            c.wait()
        for j in range(2 * n):
            meta[2 + j] = counts_s[j]
            meta[2 + 2 * n + j] = groups_s[j]
        place_items(n, meta, offs)

    def flush(j):
        dst = pl.ds(pl.multiple_of(offs[j], 16), frames)
        for whole_ref, stage in ((ad, ad_s), (nrm, nrm_s), (low, low_s), (inv, inv_s)):
            whole_ref[dst, :] = stage[...]

    @pl.when(s > 0)
    def _():
        flush(s - 1)

    @pl.when(s == 1)
    def _():
        for c in copies:
            c.wait()
        spread_bias(bias, bias_row)
        dwo[...] = jnp.zeros_like(dwo)
        dwi[...] = jnp.zeros_like(dwi)
        gbi[...] = jnp.zeros_like(gbi)

    for c in fetch(s):
        c.wait()

    def fetch_packed(j):
        dst = pl.ds(pl.multiple_of(offs[j], 16), frames)
        return pltpu.make_async_copy(tok_hbm.at[(lax.axis_index("tp") & 1) * n + j], tokp.at[dst, :], packed_sem)

    @pl.when(s > 0)
    def _():
        fetch_packed(s - 1).wait()

    fetch_packed(s).start()

    @pl.when(s == n - 1)
    def _():
        fetch_packed(s).wait()

    item = meta[0] * n + s
    count = meta[2 + item]
    group = meta[2 + 2 * n + item]

    def setup():
        rows = lax.broadcasted_iota(jnp.int32, (frames, LANES), 0)
        for q in range(wq):
            pad[q, PAD:PAD + frames, :] = jnp.where(rows < count, tok[s, :, lane(q)].astype(F32), 0.0)
        return pick(ns, group), pick(nsh, group), as_row(gamma), as_row(cb), cw[...].astype(F32)

    def conv_step(i, acc, consts):
        scale, shift, gam, conv_bias, w = consts
        r0 = i * CHUNK if isinstance(i, int) else pl.multiple_of(i * CHUNK, CHUNK)
        here = pl.ds(r0, CHUNK)
        live = (lax.broadcasted_iota(jnp.int32, (CHUNK, LANES), 0) + r0) < count
        convs = []
        for q in range(wq):
            conv = conv_bias[:, lane(q)]
            for k in range(taps):
                conv = conv + w[k:k + 1, lane(q)] * pad[q, pl.ds(r0 + (PAD - half + k), CHUNK), :]
            convs.append(conv)
        mean = jnp.sum(sum(convs[1:], convs[0]), axis=-1, keepdims=True) * (1.0 / width)
        cents = [c - mean for c in convs]
        sq = [c * c for c in cents]
        var = jnp.sum(sum(sq[1:], sq[0]), axis=-1, keepdims=True) * (1.0 / width)
        istd = lax.rsqrt(var + EPS)
        inv_s[here, :] = jnp.broadcast_to(istd, (CHUNK, LANES))
        new = []
        for q in range(wq):
            normed = cents[q] * istd
            ad_s[here, lane(q)] = (normed * scale[:, lane(q)] + shift[:, lane(q)]).astype(BF)
            nrm_s[here, lane(q)] = normed.astype(BF)
            back = jnp.where(live, cot[s, here, lane(q)].astype(F32), 0.0) * gam[:, lane(q)]
            low_s[here, lane(q)] = back.astype(BF)
            new.append(acc[q] + fold(back))
        return tuple(new)

    def add_gbo(accs):
        for q in range(wq):
            gbo[:, lane(q)] += accs[q]

    def tile(t, between=()):
        between = list(between)
        at = pl.ds(pl.multiple_of(t * TILE, TILE), TILE)
        a, b = ad[at, :], low[at, :]
        activation, slope = gelu_parts(dot(a, win[...]) + bias_row[...])
        if between:
            between.pop(0)()
        grad = dot_t(b, wout[...]) * slope
        lo = activation.astype(BF)
        act[at, :] = lo
        if between:
            between.pop(0)()
        dwo[...] += dot_rows(lo, b)
        gbi[...] += fold(grad)
        g = grad.astype(BF)
        pre[at, :] = g
        if between:
            between.pop(0)()
        dwi[...] += dot_rows(a, g)
        if between:
            between.pop(0)()

    done = offs[n + 2]
    ready = offs[s] >= (done + 1) * TILE
    none = (jnp.zeros((8, LANES), F32),) * wq

    def conv_with(chunks, with_tile):
        consts = setup()
        state = [none]

        def part(lo_i, hi_i):
            def run():
                for i in range(lo_i, hi_i):
                    state[0] = conv_step(i, state[0], consts)
            return run

        cuts = [chunks * k // 4 for k in range(5)]
        parts = [part(cuts[k], cuts[k + 1]) for k in range(4)]
        if with_tile:
            tile(done, parts)
        else:
            for run in parts:
                run()
        add_gbo(state[0])
        if with_tile:
            offs[n + 2] = done + 1

    all_chunks = frames // CHUNK
    short = count <= (all_chunks - 1) * CHUNK
    for with_tile in (True, False):
        for chunks in (all_chunks - 1, all_chunks):
            fits = short if chunks < all_chunks else jnp.logical_not(short)
            pl.when((ready == with_tile) & fits)(functools.partial(conv_with, chunks, with_tile))

    @pl.when(s == n - 1)
    def _():
        flush(s)
        end = pl.ds(pl.multiple_of(offs[n], 16), TILE)
        ad[end, :] = jnp.zeros((TILE, width), BF)
        low[end, :] = jnp.zeros((TILE, width), BF)

        def rest(t, _):
            tile(t)
            return 0

        lax.fori_loop(offs[n + 2], offs[n + 1], rest, 0)
        for side, dst in ((0, keep), (1, send)):
            for q in range(wq):
                dst[q * h:(q + 1) * h, :] = dwo[side * h:(side + 1) * h, lane(q)].astype(dst.dtype)
            base = wq * h
            for q in range(h // LANES):
                dst[base + q * width:base + (q + 1) * width, :] = dwi[:, lane(side * (h // LANES) + q)].astype(dst.dtype)


def front(counts, groups, tok, cot, cw, cb, ns, nsh, gamma, bout, buf_a, buf_b, h):
    items, frames, width = tok.shape
    n = items // 2
    rows = n * frames + TILE
    packed = 2 * width * h // LANES
    wq, hq = width // LANES, h // LANES
    n_consts = -(-(cw.shape[0] + 2 + ns.shape[0]) // 8) * 8
    return pl.pallas_call(
        functools.partial(front_kernel, n),
        grid_spec=pl.GridSpec(
            grid=(n,),
            in_specs=[hbm()] * 4 + [whole(v.shape) for v in (cw, cb, ns, nsh, gamma, bout)] + [hbm()] * 2,
            out_specs=[vmem()] * 16 + [smem()],
            scratch_shapes=[pltpu.SMEM((n + 3,), jnp.int32), pltpu.SMEM((items,), jnp.int32), pltpu.SMEM((items,), jnp.int32),
                            pltpu.VMEM((wq, frames + 4 * PAD, LANES), F32),
                            pltpu.VMEM((frames, width), BF), pltpu.VMEM((frames, width), BF),
                            pltpu.VMEM((frames, width), BF), pltpu.VMEM((frames, LANES), F32),
                            pltpu.VMEM((2, 16, LANES), BF), pltpu.VMEM((1, 2 * h), F32),
                            pltpu.VMEM((2 * h, width), F32), pltpu.VMEM((width, 2 * h), F32),
                            pltpu.SemaphoreType.DMA((2, hq + wq + 1)), pltpu.SemaphoreType.DMA((2, n)),
                            pltpu.SemaphoreType.DMA((2,)), pltpu.SemaphoreType.DMA]),
        out_shape=[struct((rows, width), BF)] * 3 + [struct((rows, LANES), F32)]
        + [struct((rows, 2 * h), BF)] * 2 + [struct((width, 2 * h), BF), struct((2 * h, width), BF)]
        + [struct((packed, LANES), F32), struct((packed, LANES), BF), struct((8, width), F32), struct((8, 2 * h), F32)]
        + [struct((n, frames, width), BF)] * 2 + [struct((n_consts, width), F32), struct((rows, width), BF), struct((2 + 2 * items,), jnp.int32)],
        compiler_params=params(), cost_estimate=cost(0),
    )(counts, groups, tok, cot, cw, cb, ns, nsh, gamma, bout, buf_a, buf_b)


def combine_kernel(dp, meta, keep, recv, stay, leave):
    m = keep.shape[0] // dp
    for d in range(dp):
        src = pl.ds(pl.multiple_of((meta[1] ^ d) * m, m), m)
        total = keep[src, :] + recv[src, :].astype(F32)
        dst = leave if d % 2 else stay
        dst[d // 2 * m:(d // 2 + 1) * m, :] = total.astype(dst.dtype)


def combine(meta, keep, recv, dp):
    rows = keep.shape[0] // 2
    return pl.pallas_call(
        functools.partial(combine_kernel, dp),
        in_specs=[smem(), vmem(), vmem()], out_specs=[vmem(), vmem()],
        out_shape=[struct((rows, LANES), F32), struct((rows, LANES), BF)],
        compiler_params=params())(meta, keep, recv)


def mix_kernel(n, taps, meta, ad, low, act, pre, win1, wout1, consts, tokp, buf_c, buf_d, branch, ag, out,
               offs, win2, wout2, bias, bias_row, sems):
    copies = weight_copies(buf_c, 0, win2, wout2, bias, sems) + weight_copies(buf_d, 1, win2, wout2, bias, sems)
    for c in copies:
        c.start()
    place_items(n, meta, offs)

    def own(at):
        return dot(act[at, :], wout1[...]), dot_t(pre[at, :], win1[...])

    def rest(at, own_branch, own_ag):
        a, b = ad[at, :], low[at, :]
        activation, slope = gelu_parts(dot(a, win2[...]) + bias_row[...])
        grad = dot_t(b, wout2[...]) * slope
        value = (own_branch + dot(activation.astype(BF), wout2[...])) + consts[taps + 1:taps + 2, :]
        branch[at, :] = value
        out[at, :] = (tokp[at, :].astype(F32) + consts[taps:taps + 1, :] * value).astype(BF)
        ag[at, :] = own_ag + dot_t(grad.astype(BF), win2[...])

    first = pl.ds(0, TILE)
    branch[first, :], ag[first, :] = own(first)
    for c in copies:
        c.wait()
    spread_bias(bias, bias_row)
    rest(first, branch[first, :], ag[first, :])

    def tile(t, _):
        at = pl.ds(pl.multiple_of(t * TILE, TILE), TILE)
        rest(at, *own(at))
        return 0

    lax.fori_loop(1, offs[n + 1], tile, 0)


def mix(meta, ad, low, act, pre, win, wout, consts, tokp, buf_c, buf_d, n, taps):
    rows, width = ad.shape
    h = act.shape[1] // 2
    wq, hq = width // LANES, h // LANES
    return pl.pallas_call(
        functools.partial(mix_kernel, n, taps),
        in_specs=[smem()] + [vmem()] * 8 + [hbm()] * 2,
        out_specs=[vmem()] * 3,
        scratch_shapes=[pltpu.SMEM((n + 2,), jnp.int32),
                        pltpu.VMEM((width, 2 * h), BF), pltpu.VMEM((2 * h, width), BF),
                        pltpu.VMEM((2, 16, LANES), BF), pltpu.VMEM((1, 2 * h), F32),
                        pltpu.SemaphoreType.DMA((2, hq + wq + 1))],
        out_shape=[struct((rows, width), F32)] * 2 + [struct((rows, width), BF)],
        compiler_params=params(), cost_estimate=cost(0),
    )(meta, ad, low, act, pre, win, wout, consts, tokp, buf_c, buf_d)


def norm_grad_kernel(n, taps, rates, meta, tok, cot, branch, ag, nrm, inv, gbo, gbi, consts,
                     cgp, small_keep, small_send, offs, sums):
    s = pl.program_id(0)
    frames, width = tok.shape[1], tok.shape[2]
    half = taps // 2
    wq = width // LANES
    h = gbi.shape[1] // 2

    @pl.when(s == 0)
    def _():
        place_items(n, meta, offs)
        sums[...] = jnp.zeros_like(sums)

    item = meta[0] * n + s
    count = meta[2 + item]
    group = meta[2 + 2 * n + item]
    off = offs[s]
    scale = pick(consts.at[taps + 2:taps + 2 + rates], group)
    zero = jnp.zeros((8, LANES), F32)
    steps = pl.cdiv(count, CHUNK)
    wide = steps // 2

    def step(r0, size, accs):
        here = pl.ds(r0, size)
        live = (lax.broadcasted_iota(jnp.int32, (size, LANES), 0) + r0) < count
        src = pl.ds(pl.multiple_of(off + r0, 16), size)
        new = []
        ngs, nrs = [], []
        for q in range(wq):
            a_ls, a_sc, a_sh = accs[3 * q:3 * q + 3]
            br = jnp.where(live, branch[src, lane(q)], 0.0)
            g = jnp.where(live, ag[src, lane(q)], 0.0)
            nr = nrm[src, lane(q)].astype(F32)
            new += [a_ls + fold(cot[s, here, lane(q)].astype(F32) * br), a_sc + fold(g * nr), a_sh + fold(g)]
            ngs.append(g * scale[:, lane(q)])
            nrs.append(nr)
        cross = [a * b for a, b in zip(ngs, nrs)]
        m1 = jnp.sum(sum(ngs[1:], ngs[0]), axis=-1, keepdims=True) * (1.0 / width)
        m2 = jnp.sum(sum(cross[1:], cross[0]), axis=-1, keepdims=True) * (1.0 / width)
        istd = inv[src, :]
        for q in range(wq):
            cg = istd * (ngs[q] - m1 - nrs[q] * m2)
            cgp[s, q, pl.ds(pl.multiple_of(r0 + PAD, 8), size), :] = jnp.where(live, cg, 0.0)
        return tuple(new)

    def both_sizes(run, width_of_state, add):
        add(lax.fori_loop(0, wide, lambda i, accs: run(pl.multiple_of(i * 2 * CHUNK, 2 * CHUNK), 2 * CHUNK, accs),
                          (zero,) * width_of_state))

        @pl.when(steps > 2 * wide)
        def _():
            add(run(pl.multiple_of(wide * 2 * CHUNK, 2 * CHUNK), CHUNK, (zero,) * width_of_state))

    def add_norm(accs):
        for q in range(wq):
            sums[taps + 1, :, lane(q)] += accs[3 * q]
            sums[taps + 2 + group, :, lane(q)] += accs[3 * q + 1]
            sums[taps + 2 + rates + group, :, lane(q)] += accs[3 * q + 2]

    both_sizes(step, 3 * wq, add_norm)

    def clear(i, _):
        r0 = pl.multiple_of(i * CHUNK, CHUNK)
        for q in range(wq):
            cgp[s, q, pl.ds(pl.multiple_of(r0 + PAD, 8), CHUNK), :] = jnp.zeros((CHUNK, LANES), F32)
        return 0

    lax.fori_loop(steps, frames // CHUNK, clear, 0)
    for q in range(wq):
        cgp[s, q, :PAD, :] = jnp.zeros((PAD, LANES), F32)
        cgp[s, q, PAD + frames:, :] = jnp.zeros((cgp.shape[2] - PAD - frames, LANES), F32)

        def conv_step(r0, size, accs):
            here = pl.ds(r0, size)
            live = (lax.broadcasted_iota(jnp.int32, (size, LANES), 0) + r0) < count
            tk = jnp.where(live, tok[s, here, lane(q)].astype(F32), 0.0)
            new = []
            for k in range(taps):
                sh = cgp[s, q, pl.ds(r0 + (PAD + half - k), size), :]
                new.append(accs[k] + fold(tk * sh))
                if k == half:
                    new_bias = accs[taps] + fold(sh)
            return tuple(new) + (new_bias,)

        def add_conv(accs):
            for k in range(taps + 1):
                sums[k, :, lane(q)] += accs[k]

        both_sizes(conv_step, taps + 1, add_conv)

    @pl.when(s == n - 1)
    def _():
        last = taps + 2 + 2 * rates
        rows = [jnp.sum(sums[i], axis=0, keepdims=True) for i in range(last)]
        rows.append(jnp.sum(gbo[...], axis=0, keepdims=True))
        gb = jnp.sum(gbi[...], axis=0, keepdims=True)
        fill = jnp.zeros((1, width - h), F32)
        spare = [jnp.zeros((1, width), F32)] * (small_keep.shape[0] - last - 2)
        for side, dst in ((0, small_keep), (1, small_send)):
            tail = [jnp.concatenate([gb[:, side * h:(side + 1) * h], fill], axis=1)]
            dst[...] = jnp.concatenate(rows + tail + spare, axis=0)


def norm_grad(meta, tok, cot, branch, ag, nrm, inv, gbo, gbi, consts, taps, rates):
    n, frames, width = tok.shape
    wq = width // LANES
    n_small = -(-(taps + 4 + 2 * rates) // 8) * 8
    return pl.pallas_call(
        functools.partial(norm_grad_kernel, n, taps, rates), grid=(n,),
        in_specs=[smem()] + [vmem()] * 9, out_specs=[vmem()] * 3,
        scratch_shapes=[pltpu.SMEM((n + 2,), jnp.int32),
                        pltpu.VMEM((taps + 2 + 2 * rates, 8, width), F32)],
        out_shape=[struct((n, wq, frames + 4 * PAD, LANES), F32)] + [struct((n_small, width), F32)] * 2,
        compiler_params=params(), cost_estimate=cost(40000000),
    )(meta, tok, cot, branch, ag, nrm, inv, gbo, gbi, consts)


def place_out_kernel(n, meta, own, other, out, stage, sems):
    frames, width = stage.shape[1], stage.shape[2]
    copies = []
    for side, src in ((0, own), (1, other)):
        first = (meta[0] ^ side) * n
        off = jnp.int32(0)
        for j in range(n):
            count = meta[2 + first + j]
            for i in range(frames // CHUNK):
                live = (lax.broadcasted_iota(jnp.int32, (CHUNK, LANES), 0) + i * CHUNK) < count
                rows = pl.ds(pl.multiple_of(off + i * CHUNK, 16), CHUNK)
                for q in range(width // LANES):
                    value = jnp.where(live, src[rows, lane(q)].astype(F32), 0.0)
                    stage[side * n + j, i * CHUNK:(i + 1) * CHUNK, lane(q)] = value.astype(BF)
            copies.append(pltpu.make_async_copy(stage.at[side * n + j], out.at[first + j], sems.at[side * n + j]))
            copies[-1].start()
            off = off + ((count + 15) & -16)
    for c in copies:
        c.wait()


def place_out(meta, own, other, n, frames):
    width = own.shape[1]
    return pl.pallas_call(
        functools.partial(place_out_kernel, n),
        in_specs=[smem(), vmem(), vmem()], out_specs=hbm(), out_shape=struct((2 * n, frames, width), BF),
        scratch_shapes=[pltpu.VMEM((2 * n, frames, width), BF), pltpu.SemaphoreType.DMA((2 * n,))],
        compiler_params=params(), cost_estimate=cost(40000000),
    )(meta, own, other)


def token_grad_kernel(n, taps, meta, cot, cgp, consts, gtok, gtok_own, stage, sems):
    s = pl.program_id(0)
    frames, width = cot.shape[1], cot.shape[2]
    half = taps // 2
    wq = width // LANES
    count = meta[2 + meta[0] * n + s]
    w = consts[:taps, :]
    steps = pl.cdiv(count, CHUNK)

    def place(j):
        return pltpu.make_async_copy(stage.at[j], gtok.at[meta[0] * n + j], sems.at[j])

    def conv_step(i, _):
        r0 = pl.multiple_of(i * CHUNK, CHUNK)
        here = pl.ds(r0, CHUNK)
        live = (lax.broadcasted_iota(jnp.int32, (CHUNK, LANES), 0) + r0) < count
        for q in range(wq):
            total = cot[s, here, lane(q)].astype(F32)
            for k in range(taps):
                total = total + w[k:k + 1, lane(q)] * cgp[s, q, pl.ds(r0 + (PAD + half - k), CHUNK), :]
            total = jnp.where(live, total, 0.0).astype(BF)
            gtok_own[s, here, lane(q)] = total
            stage[s, here, lane(q)] = total.astype(F32)
        return 0

    lax.fori_loop(0, steps, conv_step, 0)

    def clear(i, _):
        here = pl.ds(pl.multiple_of(i * CHUNK, CHUNK), CHUNK)
        gtok_own[s, here, :] = jnp.zeros((CHUNK, width), BF)
        stage[s, here, :] = jnp.zeros((CHUNK, width), F32)
        return 0

    lax.fori_loop(steps, frames // CHUNK, clear, 0)
    place(s).start()

    @pl.when(s == n - 1)
    def _():
        for j in range(n):
            place(j).wait()


def token_grad(meta, cot, cgp, consts, taps):
    n, frames, width = cot.shape
    return pl.pallas_call(
        functools.partial(token_grad_kernel, n, taps), grid=(n,),
        in_specs=[smem()] + [vmem()] * 3, out_specs=[hbm(), vmem()],
        scratch_shapes=[pltpu.VMEM((n, frames, width), F32), pltpu.SemaphoreType.DMA((n,))],
        out_shape=[struct((2 * n, frames, width), F32), struct((n, frames, width), BF)],
        compiler_params=params(), cost_estimate=cost(40000000),
    )(meta, cot, cgp, consts)


def merge_gtok_kernel(n, meta, other, gtok_in, gtok, stage, sems):
    copies = [pltpu.make_async_copy(stage.at[j], gtok.at[(1 - meta[0]) * n + j], sems.at[j]) for j in range(n)]
    for j in range(n):
        stage[j] = other[j].astype(F32)
        copies[j].start()
    for c in copies:
        c.wait()


def merge_gtok(meta, other, gtok):
    n = other.shape[0]
    return pl.pallas_call(
        functools.partial(merge_gtok_kernel, n),
        in_specs=[smem(), vmem(), hbm()], out_specs=hbm(), out_shape=struct(gtok.shape, F32),
        scratch_shapes=[pltpu.VMEM(other.shape, F32), pltpu.SemaphoreType.DMA((n,))],
        input_output_aliases={2: 0},
        compiler_params=params(), cost_estimate=cost(20000000),
    )(meta, other, gtok)


def message_kernel(stay, keep, recv, *refs):
    pieces, (out, mine) = refs[:-2], refs[-2:]
    m = pieces[0].shape[0]
    total = stay[:m, :]
    for piece in pieces:
        total = total + piece[...].astype(F32)
    out[:m, :] = total.astype(BF)
    mine[...] = total.astype(BF)
    small = (keep[...] + recv[...]).astype(BF)
    rows = small.shape[0]
    for q in range(small.shape[1] // LANES):
        out[m + q * rows:m + (q + 1) * rows, :] = small[:, lane(q)]


def make_message(stay, keep, recv, pieces):
    rows = pieces[0].shape[0] + keep.size // LANES
    return pl.pallas_call(message_kernel, in_specs=[vmem()] * (3 + len(pieces)), out_specs=[vmem(), vmem()],
                          out_shape=[struct((rows, LANES), BF), struct(pieces[0].shape, BF)],
                          compiler_params=params())(stay, keep, recv, *pieces)


def relay_kernel(m, *refs):
    sources, out = refs[:-1], refs[-1]
    sums = []
    for d, src in enumerate(sources):
        if d > 1:
            out[(d - 2) * m:(d - 1) * m, :] = src[:m, :]
        sums.append(src[m:, :].astype(F32))
    while len(sums) > 1:
        sums = [a + b for a, b in zip(sums[::2], sums[1::2])]
    out[(len(sources) - 2) * m:, :] = sums[0].astype(BF)


def relay(m, sources):
    rows = (len(sources) - 2) * m + sources[0].shape[0] - m
    return pl.pallas_call(functools.partial(relay_kernel, m), in_specs=[vmem()] * len(sources), out_specs=vmem(),
                          out_shape=struct((rows, LANES), BF), compiler_params=params())(*sources)


def unpack_kernel(dp, taps, rates, meta, mine, theirs, near_1, far_1, near, far, gcw, gcb, gns, gnsh, gwi, gbi, gwo, gbo, gls, full):
    h, width = gwo.shape
    wq, hq = width // LANES, h // LANES
    m = full.shape[0] // dp
    for odd, early, others in ((0, (mine, near_1), near), (1, (theirs, far_1), far)):
        for d in range(dp // 2):
            piece = others[(d - 2) * m:(d - 1) * m, :] if d > 1 else early[d][:m, :]
            at = pl.multiple_of((meta[1] ^ (2 * d + odd)) * m, m)
            full[pl.ds(at, m), :] = piece.astype(F32)
    for q in range(wq):
        gwo[:, lane(q)] = full[q * h:(q + 1) * h, :]
    base = wq * h
    for q in range(hq):
        gwi[:, lane(q)] = full[base + q * width:base + (q + 1) * width, :]
    behind = (dp // 2 - 2) * m
    small = near[behind:, :].astype(F32) + far[behind:, :].astype(F32)
    rows = small.shape[0] // wq
    small = jnp.concatenate([small[q * rows:(q + 1) * rows] for q in range(wq)], axis=1)
    gcw[...] = small[:taps]
    gcb[...] = small[taps]
    gls[...] = small[taps + 1]
    gns[...] = small[taps + 2:taps + 2 + rates]
    gnsh[...] = small[taps + 2 + rates:taps + 2 + 2 * rates]
    at = taps + 2 + 2 * rates
    gbo[...] = small[at]
    gbi[...] = small[at + 1, :h]


def unpack(meta, mine, theirs, near_1, far_1, near, far, dp, taps, rates, width, h):
    shapes = [(taps, width), (width,), (rates, width), (rates, width), (width, h), (h,), (h, width), (width,), (width,)]
    return pl.pallas_call(
        functools.partial(unpack_kernel, dp, taps, rates), in_specs=[smem()] + [vmem()] * 6,
        out_shape=[struct(s, F32) for s in shapes],
        scratch_shapes=[pltpu.VMEM((2 * width * h // LANES, LANES), F32)],
        compiler_params=params())(meta, mine, theirs, near_1, far_1, near, far)


def swap(x, step):
    size = lax.axis_size("tp")
    return lax.ppermute(x, "tp", [(i, i ^ step) for i in range(size)])


def across(x, step):
    size = lax.axis_size("dp")
    return lax.ppermute(x, "dp", [(i, i ^ step) for i in range(size)])


def per_device(tokens, frame_counts, rate_groups, conv_weight, conv_bias, norm_scale, norm_shift,
               weight_in, bias_in, weight_out, bias_out, layer_scale, cotangent):
    width, h = weight_in.shape
    n = tokens.shape[0] // 2
    (tokens, cotangent, conv_weight, conv_bias, norm_scale, norm_shift, weight_in, bias_in, weight_out, bias_out,
     layer_scale, frame_counts, rate_groups) = [pltpu.with_memory_space_constraint(v, pltpu.HBM) for v in (
         tokens, cotangent, conv_weight, conv_bias, norm_scale, norm_shift, weight_in, bias_in, weight_out, bias_out,
         layer_scale, frame_counts, rate_groups)]
    taps, rates = conv_weight.shape[0], norm_scale.shape[0]
    dp = lax.axis_size("dp")
    buf_a = pack(weight_in, bias_in, weight_out)
    buf_b = swap(buf_a, 1)
    buf_c = swap(buf_a, 2)
    buf_d = swap(buf_c, 1)
    ad, nrm, low, inv, act, pre, win, wout, keep, send, gbo, gbi, tok, cot, consts, tokp, meta = front(
        frame_counts, rate_groups, tokens, cotangent, conv_weight, conv_bias, norm_scale, norm_shift, layer_scale, bias_out, buf_a, buf_b, h)
    stay, leave = combine(meta, keep, swap(send, 1), dp)
    arrived = across(leave, 1)
    branch, ag, out_own = mix(meta, ad, low, act, pre, win, wout, consts, tokp, buf_c, buf_d, n, taps)
    arrived, branch, out_own = lax.optimization_barrier((arrived, branch, out_own))
    out_b = swap(out_own, 1)
    stay = (stay + arrived.astype(F32)).reshape(dp // 2, -1, LANES)
    pieces = [across(stay[d].astype(BF), 2 * d) for d in range(1, dp // 2)]

    cgp, small_keep, small_send = norm_grad(meta, tok, cot, branch, ag, nrm, inv, gbo, gbi, consts, taps, rates)
    pieces, small_send, cgp, out_b = lax.optimization_barrier((pieces, small_send, cgp, out_b))
    small_got = swap(small_send, 1)
    message, mine = make_message(stay.reshape(-1, LANES), small_keep, small_got, pieces)
    message, mine, out_b = lax.optimization_barrier((message, mine, out_b))
    m = pieces[0].shape[0]
    near = [message] + [across(message, 2 * d) for d in range(1, dp // 2)]
    theirs = across(mine, 1)
    far_1 = across(message, 3)
    out = place_out(meta, out_own, out_b, n, tokens.shape[1])
    cgp, out = lax.optimization_barrier((cgp, out))
    gtok, gtok_own = token_grad(meta, cot, cgp, consts, taps)
    near, theirs, far_1, gtok_own = lax.optimization_barrier((near, theirs, far_1, gtok_own))
    late = relay(m, near)
    far = across(late, 1)
    gtok = merge_gtok(meta, swap(gtok_own, 1), gtok)
    far, gtok = lax.optimization_barrier((far, gtok))
    gcw, gcb, gns, gnsh, gwi, gbi, gwo, gbo, gls = unpack(meta, mine, theirs, near[1], far_1, late, far, dp, taps, rates,
                                                          width, h)
    return (out, gtok, gcw, gcb, gns, gnsh, gwi, gbi, gwo, gbo, gls)


def solution(mesh):
    items, copied = P("dp", None, None), P()
    in_specs = (items, P("dp"), P("dp"), copied, copied, copied, copied, P(None, "tp"), P("tp"), P("tp", None),
                copied, copied, items)
    out_specs = (items, items, copied, copied, copied, copied, P(None, "tp"), P("tp"), P("tp", None), copied, copied)
    return jax.shard_map(per_device, mesh=mesh, in_specs=in_specs, out_specs=out_specs, check_vma=False)
```

```python
import functools

import jax
import jax.numpy as jnp
from jax import lax
from jax.experimental import pallas as pl
from jax.experimental.pallas import tpu as pltpu
from jax.sharding import PartitionSpec as P

EPS = 1e-06
BF, F32 = jnp.bfloat16, jnp.float32
TILE = 256
LANES = 128
PAD = 8
CHUNK = 64
VMEM_LIMIT = 12 * 1024 * 1024


def params(**more):
    return pltpu.CompilerParams(vmem_limit_bytes=VMEM_LIMIT, **more)


def struct(shape, dtype):
    return jax.ShapeDtypeStruct(shape, dtype)


def whole(shape):
    return pl.BlockSpec(shape, lambda *_: (0,) * len(shape))


def hbm():
    return pl.BlockSpec(memory_space=pltpu.HBM)


def smem():
    return pl.BlockSpec(memory_space=pltpu.SMEM)


def cost(size):
    return pl.CostEstimate(flops=0, transcendentals=0, bytes_accessed=size)


def vmem():
    return pl.BlockSpec(memory_space=pltpu.VMEM)


def lane(q):
    return slice(q * LANES, (q + 1) * LANES)


def fold(x):
    return jnp.sum(x.reshape(x.shape[0] // 8, 8, x.shape[1]), axis=0)


def pick(table, group):
    rows = table[...].astype(F32)
    value = rows[0:1]
    for r in range(1, rows.shape[0]):
        value = jnp.where(group == r, rows[r:r + 1], value)
    return value


def as_row(ref):
    return ref[...].astype(F32).reshape(1, -1)


def gelu_parts(pre):
    cdf = 0.5 + 0.5 * lax.erf(pre * 0.7071067811865476)
    density = jnp.exp(-0.5 * pre * pre) * 0.3989422804014327
    return pre * cdf, cdf + pre * density


def dot(a, b):
    return jnp.dot(a, b, preferred_element_type=F32)


def dot_t(a, b):
    return lax.dot_general(a, b, (((1,), (1,)), ((), ())), preferred_element_type=F32)


def dot_rows(a, b):
    return lax.dot_general(a, b, (((0,), (0,)), ((), ())), preferred_element_type=F32)


def place_items(n, meta, offs):
    end = jnp.int32(0)
    for j in range(n):
        offs[j] = end
        end = end + ((meta[2 + meta[0] * n + j] + 15) & -16)
    offs[n] = end
    offs[n + 1] = (end + TILE - 1) // TILE


def pack_kernel(wi, bi, wo, out):
    width, h = wi.shape
    hq, wq = h // LANES, width // LANES
    for q in range(hq):
        out[q * width:(q + 1) * width, :] = wi[:, lane(q)]
    base = hq * width
    for q in range(wq):
        out[base + q * h:base + (q + 1) * h, :] = wo[:, lane(q)]
    base += wq * h
    bias = bi[...].astype(F32).reshape(1, h)
    rows = [bias[:, lane(q)] for q in range(hq)] + [jnp.zeros((1, LANES), F32)] * (16 - hq)
    out[base:base + 16, :] = jnp.concatenate(rows, axis=0).astype(BF)


def pack(wi, bi, wo):
    rows = 2 * wi.size // LANES + 16
    return pl.pallas_call(pack_kernel, out_shape=struct((rows, LANES), BF),
                          compiler_params=params())(wi, bi, wo)


def weight_copies(buf, side, win, wout, bias, sems):
    width, h = win.shape[0], win.shape[1] // 2
    hq, wq = h // LANES, width // LANES
    copies = []
    for q in range(hq):
        at = side * h + q * LANES
        copies.append((buf.at[pl.ds(q * width, width), :], win.at[:, pl.ds(at, LANES)]))
    base = hq * width
    for q in range(wq):
        copies.append((buf.at[pl.ds(base + q * h, h), :], wout.at[pl.ds(side * h, h), pl.ds(q * LANES, LANES)]))
    copies.append((buf.at[pl.ds(base + wq * h, 16), :], bias.at[side]))
    return [pltpu.make_async_copy(src, dst, sems.at[side, i]) for i, (src, dst) in enumerate(copies)]


def spread_bias(bias, row):
    hq = row.shape[1] // LANES // 2
    for side in range(2):
        for q in range(hq):
            at = side * hq + q
            row[:, lane(at)] = bias[side, q:q + 1, :].astype(F32)


def front_kernel(n, counts_hbm, groups_hbm, tok_hbm, cot_hbm, cw, cb, ns, nsh, gamma, bout, buf_a, buf_b,
                 ad, nrm, low, inv, act, pre, win, wout, keep, send, gbo, gbi, tok, cot, consts, tokp, meta,
                 offs, counts_s, groups_s, pad, ad_s, nrm_s, low_s, inv_s, bias, bias_row, dwo, dwi, sems, item_sems, meta_sems, packed_sem):
    s = pl.program_id(0)
    frames, width = tok.shape[1], tok.shape[2]
    taps, rates = cw.shape[0], ns.shape[0]
    half = taps // 2
    wq = width // LANES
    h = win.shape[1] // 2
    copies = weight_copies(buf_a, 0, win, wout, bias, sems) + weight_copies(buf_b, 1, win, wout, bias, sems)

    def fetch(j):
        at = (lax.axis_index("tp") & 1) * n + j
        return [pltpu.make_async_copy(src.at[at], dst.at[j], item_sems.at[i, j])
                for i, (src, dst) in enumerate(((tok_hbm, tok), (cot_hbm, cot)))]

    @pl.when(s == 0)
    def _():
        tables = [pltpu.make_async_copy(counts_hbm, counts_s, meta_sems.at[0]),
                  pltpu.make_async_copy(groups_hbm, groups_s, meta_sems.at[1])]
        for c in tables + fetch(0) + fetch(1):
            c.start()
        for c in copies:
            c.start()
        for j in range(2, n):
            for c in fetch(j):
                c.start()
        consts[...] = jnp.zeros_like(consts)
        consts[:taps, :] = cw[...].astype(F32)
        consts[taps:taps + 1, :] = as_row(gamma)
        consts[taps + 1:taps + 2, :] = as_row(bout)
        consts[taps + 2:taps + 2 + rates, :] = ns[...].astype(F32)
        offs[n + 2] = 0
        gbo[...] = jnp.zeros_like(gbo)
        pad[...] = jnp.zeros_like(pad)
        for stage in (ad_s, nrm_s, low_s, inv_s):
            stage[...] = jnp.zeros_like(stage)
        meta[0] = lax.axis_index("tp") & 1
        meta[1] = lax.axis_index("dp")
        for c in tables:
            c.wait()
        for j in range(2 * n):
            meta[2 + j] = counts_s[j]
            meta[2 + 2 * n + j] = groups_s[j]
        place_items(n, meta, offs)

    def flush(j):
        dst = pl.ds(pl.multiple_of(offs[j], 16), frames)
        for whole_ref, stage in ((ad, ad_s), (nrm, nrm_s), (low, low_s), (inv, inv_s)):
            whole_ref[dst, :] = stage[...]

    @pl.when(s > 0)
    def _():
        flush(s - 1)

    @pl.when(s == 1)
    def _():
        for c in copies:
            c.wait()
        spread_bias(bias, bias_row)
        dwo[...] = jnp.zeros_like(dwo)
        dwi[...] = jnp.zeros_like(dwi)
        gbi[...] = jnp.zeros_like(gbi)

    for c in fetch(s):
        c.wait()

    def fetch_packed(j):
        dst = pl.ds(pl.multiple_of(offs[j], 16), frames)
        return pltpu.make_async_copy(tok_hbm.at[(lax.axis_index("tp") & 1) * n + j], tokp.at[dst, :], packed_sem)

    @pl.when(s > 1)
    def _():
        fetch_packed(s - 2).wait()

    @pl.when(s > 0)
    def _():
        fetch_packed(s - 1).start()

    item = meta[0] * n + s
    count = meta[2 + item]
    group = meta[2 + 2 * n + item]

    def setup():
        rows = lax.broadcasted_iota(jnp.int32, (frames, LANES), 0)
        for q in range(wq):
            pad[q, PAD:PAD + frames, :] = jnp.where(rows < count, tok[s, :, lane(q)].astype(F32), 0.0)
        return pick(ns, group), pick(nsh, group), as_row(gamma), as_row(cb), cw[...].astype(F32)

    def conv_step(i, acc, consts):
        scale, shift, gam, conv_bias, w = consts
        r0 = i * CHUNK if isinstance(i, int) else pl.multiple_of(i * CHUNK, CHUNK)
        here = pl.ds(r0, CHUNK)
        live = (lax.broadcasted_iota(jnp.int32, (CHUNK, LANES), 0) + r0) < count
        convs = []
        for q in range(wq):
            conv = conv_bias[:, lane(q)]
            for k in range(taps):
                conv = conv + w[k:k + 1, lane(q)] * pad[q, pl.ds(r0 + (PAD - half + k), CHUNK), :]
            convs.append(conv)
        mean = jnp.sum(sum(convs[1:], convs[0]), axis=-1, keepdims=True) * (1.0 / width)
        cents = [c - mean for c in convs]
        sq = [c * c for c in cents]
        var = jnp.sum(sum(sq[1:], sq[0]), axis=-1, keepdims=True) * (1.0 / width)
        istd = lax.rsqrt(var + EPS)
        inv_s[here, :] = jnp.broadcast_to(istd, (CHUNK, LANES))
        new = []
        for q in range(wq):
            normed = cents[q] * istd
            ad_s[here, lane(q)] = (normed * scale[:, lane(q)] + shift[:, lane(q)]).astype(BF)
            nrm_s[here, lane(q)] = normed.astype(BF)
            back = jnp.where(live, cot[s, here, lane(q)].astype(F32), 0.0) * gam[:, lane(q)]
            low_s[here, lane(q)] = back.astype(BF)
            new.append(acc[q] + fold(back))
        return tuple(new)

    def add_gbo(accs):
        for q in range(wq):
            gbo[:, lane(q)] += accs[q]

    def tile(t, between=()):
        between = list(between)
        at = pl.ds(pl.multiple_of(t * TILE, TILE), TILE)
        a, b = ad[at, :], low[at, :]
        activation, slope = gelu_parts(dot(a, win[...]) + bias_row[...])
        if between:
            between.pop(0)()
        grad = dot_t(b, wout[...]) * slope
        lo = activation.astype(BF)
        act[at, :] = lo
        if between:
            between.pop(0)()
        dwo[...] += dot_rows(lo, b)
        gbi[...] += fold(grad)
        g = grad.astype(BF)
        pre[at, :] = g
        if between:
            between.pop(0)()
        dwi[...] += dot_rows(a, g)
        if between:
            between.pop(0)()

    done = offs[n + 2]
    ready = offs[s] >= (done + 1) * TILE
    none = (jnp.zeros((8, LANES), F32),) * wq

    def conv_with(chunks, with_tile):
        consts = setup()
        state = [none]

        def part(lo_i, hi_i):
            def run():
                for i in range(lo_i, hi_i):
                    state[0] = conv_step(i, state[0], consts)
            return run

        cuts = [chunks * k // 4 for k in range(5)]
        parts = [part(cuts[k], cuts[k + 1]) for k in range(4)]
        if with_tile:
            tile(done, parts)
        else:
            for run in parts:
                run()
        add_gbo(state[0])
        if with_tile:
            offs[n + 2] = done + 1

    all_chunks = frames // CHUNK
    short = count <= (all_chunks - 1) * CHUNK
    for with_tile in (True, False):
        for chunks in (all_chunks - 1, all_chunks):
            fits = short if chunks < all_chunks else jnp.logical_not(short)
            pl.when((ready == with_tile) & fits)(functools.partial(conv_with, chunks, with_tile))

    @pl.when(s == n - 1)
    def _():
        flush(s)
        end = pl.ds(pl.multiple_of(offs[n], 16), TILE)
        ad[end, :] = jnp.zeros((TILE, width), BF)
        low[end, :] = jnp.zeros((TILE, width), BF)

        fetch_packed(n - 2).wait()
        fetch_packed(n - 1).start()

        def rest(t, _):
            tile(t)
            return 0

        lax.fori_loop(offs[n + 2], offs[n + 1], rest, 0)
        fetch_packed(n - 1).wait()
        for side, dst in ((0, keep), (1, send)):
            for q in range(wq):
                dst[q * h:(q + 1) * h, :] = dwo[side * h:(side + 1) * h, lane(q)].astype(dst.dtype)
            base = wq * h
            for q in range(h // LANES):
                dst[base + q * width:base + (q + 1) * width, :] = dwi[:, lane(side * (h // LANES) + q)].astype(dst.dtype)


def front(counts, groups, tok, cot, cw, cb, ns, nsh, gamma, bout, buf_a, buf_b, h):
    items, frames, width = tok.shape
    n = items // 2
    rows = n * frames + TILE
    packed = 2 * width * h // LANES
    wq, hq = width // LANES, h // LANES
    n_consts = -(-(cw.shape[0] + 2 + ns.shape[0]) // 8) * 8
    return pl.pallas_call(
        functools.partial(front_kernel, n),
        grid_spec=pl.GridSpec(
            grid=(n,),
            in_specs=[hbm()] * 4 + [whole(v.shape) for v in (cw, cb, ns, nsh, gamma, bout)] + [hbm()] * 2,
            out_specs=[vmem()] * 16 + [smem()],
            scratch_shapes=[pltpu.SMEM((n + 3,), jnp.int32), pltpu.SMEM((items,), jnp.int32), pltpu.SMEM((items,), jnp.int32),
                            pltpu.VMEM((wq, frames + 4 * PAD, LANES), F32),
                            pltpu.VMEM((frames, width), BF), pltpu.VMEM((frames, width), BF),
                            pltpu.VMEM((frames, width), BF), pltpu.VMEM((frames, LANES), F32),
                            pltpu.VMEM((2, 16, LANES), BF), pltpu.VMEM((1, 2 * h), F32),
                            pltpu.VMEM((2 * h, width), F32), pltpu.VMEM((width, 2 * h), F32),
                            pltpu.SemaphoreType.DMA((2, hq + wq + 1)), pltpu.SemaphoreType.DMA((2, n)),
                            pltpu.SemaphoreType.DMA((2,)), pltpu.SemaphoreType.DMA]),
        out_shape=[struct((rows, width), BF)] * 3 + [struct((rows, LANES), F32)]
        + [struct((rows, 2 * h), BF)] * 2 + [struct((width, 2 * h), BF), struct((2 * h, width), BF)]
        + [struct((packed, LANES), F32), struct((packed, LANES), BF), struct((8, width), F32), struct((8, 2 * h), F32)]
        + [struct((n, frames, width), BF)] * 2 + [struct((n_consts, width), F32), struct((rows, width), BF), struct((2 + 2 * items,), jnp.int32)],
        compiler_params=params(), cost_estimate=cost(0),
    )(counts, groups, tok, cot, cw, cb, ns, nsh, gamma, bout, buf_a, buf_b)


def combine_kernel(dp, meta, keep, recv, stay, leave):
    m = keep.shape[0] // dp
    for d in range(dp):
        src = pl.ds(pl.multiple_of((meta[1] ^ d) * m, m), m)
        total = keep[src, :] + recv[src, :].astype(F32)
        dst = leave if d % 2 else stay
        dst[d // 2 * m:(d // 2 + 1) * m, :] = total.astype(dst.dtype)


def combine(meta, keep, recv, dp):
    rows = keep.shape[0] // 2
    return pl.pallas_call(
        functools.partial(combine_kernel, dp),
        in_specs=[smem(), vmem(), vmem()], out_specs=[vmem(), vmem()],
        out_shape=[struct((rows, LANES), F32), struct((rows, LANES), BF)],
        compiler_params=params())(meta, keep, recv)


def mix_kernel(n, taps, meta, ad, low, act, pre, win1, wout1, consts, tokp, buf_c, buf_d, branch, ag, out,
               offs, win2, wout2, bias, bias_row, sems):
    copies = weight_copies(buf_c, 0, win2, wout2, bias, sems) + weight_copies(buf_d, 1, win2, wout2, bias, sems)
    for c in copies:
        c.start()
    place_items(n, meta, offs)

    def own(at):
        return dot(act[at, :], wout1[...]), dot_t(pre[at, :], win1[...])

    def rest(at, own_branch, own_ag):
        a, b = ad[at, :], low[at, :]
        activation, slope = gelu_parts(dot(a, win2[...]) + bias_row[...])
        grad = dot_t(b, wout2[...]) * slope
        value = (own_branch + dot(activation.astype(BF), wout2[...])) + consts[taps + 1:taps + 2, :]
        branch[at, :] = value
        out[at, :] = (tokp[at, :].astype(F32) + consts[taps:taps + 1, :] * value).astype(BF)
        ag[at, :] = own_ag + dot_t(grad.astype(BF), win2[...])

    first = pl.ds(0, TILE)
    branch[first, :], ag[first, :] = own(first)
    for c in copies:
        c.wait()
    spread_bias(bias, bias_row)
    rest(first, branch[first, :], ag[first, :])

    def tile(t, _):
        at = pl.ds(pl.multiple_of(t * TILE, TILE), TILE)
        rest(at, *own(at))
        return 0

    lax.fori_loop(1, offs[n + 1], tile, 0)


def mix(meta, ad, low, act, pre, win, wout, consts, tokp, buf_c, buf_d, n, taps):
    rows, width = ad.shape
    h = act.shape[1] // 2
    wq, hq = width // LANES, h // LANES
    return pl.pallas_call(
        functools.partial(mix_kernel, n, taps),
        in_specs=[smem()] + [vmem()] * 8 + [hbm()] * 2,
        out_specs=[vmem()] * 3,
        scratch_shapes=[pltpu.SMEM((n + 2,), jnp.int32),
                        pltpu.VMEM((width, 2 * h), BF), pltpu.VMEM((2 * h, width), BF),
                        pltpu.VMEM((2, 16, LANES), BF), pltpu.VMEM((1, 2 * h), F32),
                        pltpu.SemaphoreType.DMA((2, hq + wq + 1))],
        out_shape=[struct((rows, width), F32)] * 2 + [struct((rows, width), BF)],
        compiler_params=params(), cost_estimate=cost(0),
    )(meta, ad, low, act, pre, win, wout, consts, tokp, buf_c, buf_d)


def norm_grad_kernel(n, taps, rates, meta, tok, cot, branch, ag, nrm, inv, gbo, gbi, consts,
                     cgp, small_keep, small_send, offs, sums):
    s = pl.program_id(0)
    frames, width = tok.shape[1], tok.shape[2]
    half = taps // 2
    wq = width // LANES
    h = gbi.shape[1] // 2

    @pl.when(s == 0)
    def _():
        place_items(n, meta, offs)
        sums[...] = jnp.zeros_like(sums)

    item = meta[0] * n + s
    count = meta[2 + item]
    group = meta[2 + 2 * n + item]
    off = offs[s]
    scale = pick(consts.at[taps + 2:taps + 2 + rates], group)
    zero = jnp.zeros((8, LANES), F32)
    steps = pl.cdiv(count, CHUNK)
    wide = steps // 2

    def step(r0, size, accs):
        here = pl.ds(r0, size)
        live = (lax.broadcasted_iota(jnp.int32, (size, LANES), 0) + r0) < count
        src = pl.ds(pl.multiple_of(off + r0, 16), size)
        new = []
        ngs, nrs = [], []
        for q in range(wq):
            a_ls, a_sc, a_sh = accs[3 * q:3 * q + 3]
            br = jnp.where(live, branch[src, lane(q)], 0.0)
            g = jnp.where(live, ag[src, lane(q)], 0.0)
            nr = nrm[src, lane(q)].astype(F32)
            new += [a_ls + fold(cot[s, here, lane(q)].astype(F32) * br), a_sc + fold(g * nr), a_sh + fold(g)]
            ngs.append(g * scale[:, lane(q)])
            nrs.append(nr)
        cross = [a * b for a, b in zip(ngs, nrs)]
        m1 = jnp.sum(sum(ngs[1:], ngs[0]), axis=-1, keepdims=True) * (1.0 / width)
        m2 = jnp.sum(sum(cross[1:], cross[0]), axis=-1, keepdims=True) * (1.0 / width)
        istd = inv[src, :]
        for q in range(wq):
            cg = istd * (ngs[q] - m1 - nrs[q] * m2)
            cgp[s, q, pl.ds(pl.multiple_of(r0 + PAD, 8), size), :] = jnp.where(live, cg, 0.0)
        return tuple(new)

    def both_sizes(run, width_of_state, add):
        add(lax.fori_loop(0, wide, lambda i, accs: run(pl.multiple_of(i * 2 * CHUNK, 2 * CHUNK), 2 * CHUNK, accs),
                          (zero,) * width_of_state))

        @pl.when(steps > 2 * wide)
        def _():
            add(run(pl.multiple_of(wide * 2 * CHUNK, 2 * CHUNK), CHUNK, (zero,) * width_of_state))

    def add_norm(accs):
        for q in range(wq):
            sums[taps + 1, :, lane(q)] += accs[3 * q]
            sums[taps + 2 + group, :, lane(q)] += accs[3 * q + 1]
            sums[taps + 2 + rates + group, :, lane(q)] += accs[3 * q + 2]

    both_sizes(step, 3 * wq, add_norm)

    def clear(i, _):
        r0 = pl.multiple_of(i * CHUNK, CHUNK)
        for q in range(wq):
            cgp[s, q, pl.ds(pl.multiple_of(r0 + PAD, 8), CHUNK), :] = jnp.zeros((CHUNK, LANES), F32)
        return 0

    lax.fori_loop(steps, frames // CHUNK, clear, 0)
    for q in range(wq):
        cgp[s, q, :PAD, :] = jnp.zeros((PAD, LANES), F32)
        cgp[s, q, PAD + frames:, :] = jnp.zeros((cgp.shape[2] - PAD - frames, LANES), F32)

        def conv_step(r0, size, accs):
            here = pl.ds(r0, size)
            live = (lax.broadcasted_iota(jnp.int32, (size, LANES), 0) + r0) < count
            tk = jnp.where(live, tok[s, here, lane(q)].astype(F32), 0.0)
            new = []
            for k in range(taps):
                sh = cgp[s, q, pl.ds(r0 + (PAD + half - k), size), :]
                new.append(accs[k] + fold(tk * sh))
                if k == half:
                    new_bias = accs[taps] + fold(sh)
            return tuple(new) + (new_bias,)

        def add_conv(accs):
            for k in range(taps + 1):
                sums[k, :, lane(q)] += accs[k]

        both_sizes(conv_step, taps + 1, add_conv)

    @pl.when(s == n - 1)
    def _():
        last = taps + 2 + 2 * rates
        rows = [jnp.sum(sums[i], axis=0, keepdims=True) for i in range(last)]
        rows.append(jnp.sum(gbo[...], axis=0, keepdims=True))
        gb = jnp.sum(gbi[...], axis=0, keepdims=True)
        fill = jnp.zeros((1, width - h), F32)
        spare = [jnp.zeros((1, width), F32)] * (small_keep.shape[0] - last - 2)
        for side, dst in ((0, small_keep), (1, small_send)):
            tail = [jnp.concatenate([gb[:, side * h:(side + 1) * h], fill], axis=1)]
            dst[...] = jnp.concatenate(rows + tail + spare, axis=0)


def norm_grad(meta, tok, cot, branch, ag, nrm, inv, gbo, gbi, consts, taps, rates):
    n, frames, width = tok.shape
    wq = width // LANES
    n_small = -(-(taps + 4 + 2 * rates) // 8) * 8
    return pl.pallas_call(
        functools.partial(norm_grad_kernel, n, taps, rates), grid=(n,),
        in_specs=[smem()] + [vmem()] * 9, out_specs=[vmem()] * 3,
        scratch_shapes=[pltpu.SMEM((n + 2,), jnp.int32),
                        pltpu.VMEM((taps + 2 + 2 * rates, 8, width), F32)],
        out_shape=[struct((n, wq, frames + 4 * PAD, LANES), F32)] + [struct((n_small, width), F32)] * 2,
        compiler_params=params(), cost_estimate=cost(40000000),
    )(meta, tok, cot, branch, ag, nrm, inv, gbo, gbi, consts)


def place_out_kernel(n, meta, own, other, out, stage, sems):
    frames, width = stage.shape[1], stage.shape[2]
    copies = []
    for side, src in ((0, own), (1, other)):
        first = (meta[0] ^ side) * n
        off = jnp.int32(0)
        for j in range(n):
            count = meta[2 + first + j]
            for i in range(frames // CHUNK):
                live = (lax.broadcasted_iota(jnp.int32, (CHUNK, LANES), 0) + i * CHUNK) < count
                rows = pl.ds(pl.multiple_of(off + i * CHUNK, 16), CHUNK)
                for q in range(width // LANES):
                    value = jnp.where(live, src[rows, lane(q)].astype(F32), 0.0)
                    stage[side * n + j, i * CHUNK:(i + 1) * CHUNK, lane(q)] = value.astype(BF)
            copies.append(pltpu.make_async_copy(stage.at[side * n + j], out.at[first + j], sems.at[side * n + j]))
            copies[-1].start()
            off = off + ((count + 15) & -16)
    for c in copies:
        c.wait()


def place_out(meta, own, other, n, frames):
    width = own.shape[1]
    return pl.pallas_call(
        functools.partial(place_out_kernel, n),
        in_specs=[smem(), vmem(), vmem()], out_specs=hbm(), out_shape=struct((2 * n, frames, width), BF),
        scratch_shapes=[pltpu.VMEM((2 * n, frames, width), BF), pltpu.SemaphoreType.DMA((2 * n,))],
        compiler_params=params(), cost_estimate=cost(40000000),
    )(meta, own, other)


def token_grad_kernel(n, taps, meta, cot, cgp, consts, gtok, gtok_own, stage, sems):
    s = pl.program_id(0)
    frames, width = cot.shape[1], cot.shape[2]
    half = taps // 2
    wq = width // LANES
    count = meta[2 + meta[0] * n + s]
    w = consts[:taps, :]
    steps = pl.cdiv(count, CHUNK)

    def place(j):
        return pltpu.make_async_copy(stage.at[j], gtok.at[meta[0] * n + j], sems.at[j])

    def conv_step(i, _):
        r0 = pl.multiple_of(i * CHUNK, CHUNK)
        here = pl.ds(r0, CHUNK)
        live = (lax.broadcasted_iota(jnp.int32, (CHUNK, LANES), 0) + r0) < count
        for q in range(wq):
            total = cot[s, here, lane(q)].astype(F32)
            for k in range(taps):
                total = total + w[k:k + 1, lane(q)] * cgp[s, q, pl.ds(r0 + (PAD + half - k), CHUNK), :]
            total = jnp.where(live, total, 0.0).astype(BF)
            gtok_own[s, here, lane(q)] = total
            stage[s, here, lane(q)] = total.astype(F32)
        return 0

    lax.fori_loop(0, steps, conv_step, 0)

    def clear(i, _):
        here = pl.ds(pl.multiple_of(i * CHUNK, CHUNK), CHUNK)
        gtok_own[s, here, :] = jnp.zeros((CHUNK, width), BF)
        stage[s, here, :] = jnp.zeros((CHUNK, width), F32)
        return 0

    lax.fori_loop(steps, frames // CHUNK, clear, 0)
    place(s).start()

    @pl.when(s == n - 1)
    def _():
        for j in range(n):
            place(j).wait()


def token_grad(meta, cot, cgp, consts, taps):
    n, frames, width = cot.shape
    return pl.pallas_call(
        functools.partial(token_grad_kernel, n, taps), grid=(n,),
        in_specs=[smem()] + [vmem()] * 3, out_specs=[hbm(), vmem()],
        scratch_shapes=[pltpu.VMEM((n, frames, width), F32), pltpu.SemaphoreType.DMA((n,))],
        out_shape=[struct((2 * n, frames, width), F32), struct((n, frames, width), BF)],
        compiler_params=params(), cost_estimate=cost(40000000),
    )(meta, cot, cgp, consts)


def merge_gtok_kernel(n, meta, other, gtok_in, gtok, stage, sems):
    copies = [pltpu.make_async_copy(stage.at[j], gtok.at[(1 - meta[0]) * n + j], sems.at[j]) for j in range(n)]
    for j in range(n):
        stage[j] = other[j].astype(F32)
        copies[j].start()
    for c in copies:
        c.wait()


def merge_gtok(meta, other, gtok):
    n = other.shape[0]
    return pl.pallas_call(
        functools.partial(merge_gtok_kernel, n),
        in_specs=[smem(), vmem(), hbm()], out_specs=hbm(), out_shape=struct(gtok.shape, F32),
        scratch_shapes=[pltpu.VMEM(other.shape, F32), pltpu.SemaphoreType.DMA((n,))],
        input_output_aliases={2: 0},
        compiler_params=params(), cost_estimate=cost(20000000),
    )(meta, other, gtok)


def message_kernel(stay, keep, recv, *refs):
    pieces, (out, mine) = refs[:-2], refs[-2:]
    m = pieces[0].shape[0]
    total = stay[:m, :]
    for piece in pieces:
        total = total + piece[...].astype(F32)
    out[:m, :] = total.astype(BF)
    mine[...] = total.astype(BF)
    small = (keep[...] + recv[...]).astype(BF)
    rows = small.shape[0]
    for q in range(small.shape[1] // LANES):
        out[m + q * rows:m + (q + 1) * rows, :] = small[:, lane(q)]


def make_message(stay, keep, recv, pieces):
    rows = pieces[0].shape[0] + keep.size // LANES
    return pl.pallas_call(message_kernel, in_specs=[vmem()] * (3 + len(pieces)), out_specs=[vmem(), vmem()],
                          out_shape=[struct((rows, LANES), BF), struct(pieces[0].shape, BF)],
                          compiler_params=params())(stay, keep, recv, *pieces)


def relay_kernel(m, *refs):
    sources, out = refs[:-1], refs[-1]
    sums = []
    for d, src in enumerate(sources):
        if d > 1:
            out[(d - 2) * m:(d - 1) * m, :] = src[:m, :]
        sums.append(src[m:, :].astype(F32))
    while len(sums) > 1:
        sums = [a + b for a, b in zip(sums[::2], sums[1::2])]
    out[(len(sources) - 2) * m:, :] = sums[0].astype(BF)


def relay(m, sources):
    rows = (len(sources) - 2) * m + sources[0].shape[0] - m
    return pl.pallas_call(functools.partial(relay_kernel, m), in_specs=[vmem()] * len(sources), out_specs=vmem(),
                          out_shape=struct((rows, LANES), BF), compiler_params=params())(*sources)


def unpack_kernel(dp, taps, rates, meta, mine, theirs, near_1, far_1, near, far, gcw, gcb, gns, gnsh, gwi, gbi, gwo, gbo, gls, full):
    h, width = gwo.shape
    wq, hq = width // LANES, h // LANES
    m = full.shape[0] // dp
    for odd, early, others in ((0, (mine, near_1), near), (1, (theirs, far_1), far)):
        for d in range(dp // 2):
            piece = others[(d - 2) * m:(d - 1) * m, :] if d > 1 else early[d][:m, :]
            at = pl.multiple_of((meta[1] ^ (2 * d + odd)) * m, m)
            full[pl.ds(at, m), :] = piece.astype(F32)
    for q in range(wq):
        gwo[:, lane(q)] = full[q * h:(q + 1) * h, :]
    base = wq * h
    for q in range(hq):
        gwi[:, lane(q)] = full[base + q * width:base + (q + 1) * width, :]
    behind = (dp // 2 - 2) * m
    small = near[behind:, :].astype(F32) + far[behind:, :].astype(F32)
    rows = small.shape[0] // wq
    small = jnp.concatenate([small[q * rows:(q + 1) * rows] for q in range(wq)], axis=1)
    gcw[...] = small[:taps]
    gcb[...] = small[taps]
    gls[...] = small[taps + 1]
    gns[...] = small[taps + 2:taps + 2 + rates]
    gnsh[...] = small[taps + 2 + rates:taps + 2 + 2 * rates]
    at = taps + 2 + 2 * rates
    gbo[...] = small[at]
    gbi[...] = small[at + 1, :h]


def unpack(meta, mine, theirs, near_1, far_1, near, far, dp, taps, rates, width, h):
    shapes = [(taps, width), (width,), (rates, width), (rates, width), (width, h), (h,), (h, width), (width,), (width,)]
    return pl.pallas_call(
        functools.partial(unpack_kernel, dp, taps, rates), in_specs=[smem()] + [vmem()] * 6,
        out_shape=[struct(s, F32) for s in shapes],
        scratch_shapes=[pltpu.VMEM((2 * width * h // LANES, LANES), F32)],
        compiler_params=params())(meta, mine, theirs, near_1, far_1, near, far)


def swap(x, step):
    size = lax.axis_size("tp")
    return lax.ppermute(x, "tp", [(i, i ^ step) for i in range(size)])


def across(x, step):
    size = lax.axis_size("dp")
    return lax.ppermute(x, "dp", [(i, i ^ step) for i in range(size)])


def per_device(tokens, frame_counts, rate_groups, conv_weight, conv_bias, norm_scale, norm_shift,
               weight_in, bias_in, weight_out, bias_out, layer_scale, cotangent):
    width, h = weight_in.shape
    n = tokens.shape[0] // 2
    (tokens, cotangent, conv_weight, conv_bias, norm_scale, norm_shift, weight_in, bias_in, weight_out, bias_out,
     layer_scale, frame_counts, rate_groups) = [pltpu.with_memory_space_constraint(v, pltpu.HBM) for v in (
         tokens, cotangent, conv_weight, conv_bias, norm_scale, norm_shift, weight_in, bias_in, weight_out, bias_out,
         layer_scale, frame_counts, rate_groups)]
    taps, rates = conv_weight.shape[0], norm_scale.shape[0]
    dp = lax.axis_size("dp")
    buf_a = pack(weight_in, bias_in, weight_out)
    buf_b = swap(buf_a, 1)
    buf_c = swap(buf_a, 2)
    buf_d = swap(buf_c, 1)
    ad, nrm, low, inv, act, pre, win, wout, keep, send, gbo, gbi, tok, cot, consts, tokp, meta = front(
        frame_counts, rate_groups, tokens, cotangent, conv_weight, conv_bias, norm_scale, norm_shift, layer_scale, bias_out, buf_a, buf_b, h)
    stay, leave = combine(meta, keep, swap(send, 1), dp)
    arrived = across(leave, 1)
    branch, ag, out_own = mix(meta, ad, low, act, pre, win, wout, consts, tokp, buf_c, buf_d, n, taps)
    arrived, branch, out_own = lax.optimization_barrier((arrived, branch, out_own))
    out_b = swap(out_own, 1)
    stay = (stay + arrived.astype(F32)).reshape(dp // 2, -1, LANES)
    pieces = [across(stay[d].astype(BF), 2 * d) for d in range(1, dp // 2)]

    cgp, small_keep, small_send = norm_grad(meta, tok, cot, branch, ag, nrm, inv, gbo, gbi, consts, taps, rates)
    pieces, small_send, cgp, out_b = lax.optimization_barrier((pieces, small_send, cgp, out_b))
    small_got = swap(small_send, 1)
    message, mine = make_message(stay.reshape(-1, LANES), small_keep, small_got, pieces)
    message, mine, out_b = lax.optimization_barrier((message, mine, out_b))
    m = pieces[0].shape[0]
    near = [message] + [across(message, 2 * d) for d in range(1, dp // 2)]
    theirs = across(mine, 1)
    far_1 = across(message, 3)
    out = place_out(meta, out_own, out_b, n, tokens.shape[1])
    cgp, out = lax.optimization_barrier((cgp, out))
    gtok, gtok_own = token_grad(meta, cot, cgp, consts, taps)
    near, theirs, far_1, gtok_own = lax.optimization_barrier((near, theirs, far_1, gtok_own))
    late = relay(m, near)
    far = across(late, 1)
    gtok = merge_gtok(meta, swap(gtok_own, 1), gtok)
    far, gtok = lax.optimization_barrier((far, gtok))
    gcw, gcb, gns, gnsh, gwi, gbi, gwo, gbo, gls = unpack(meta, mine, theirs, near[1], far_1, late, far, dp, taps, rates,
                                                          width, h)
    return (out, gtok, gcw, gcb, gns, gnsh, gwi, gbi, gwo, gbo, gls)


def solution(mesh):
    items, copied = P("dp", None, None), P()
    in_specs = (items, P("dp"), P("dp"), copied, copied, copied, copied, P(None, "tp"), P("tp"), P("tp", None),
                copied, copied, items)
    out_specs = (items, items, copied, copied, copied, copied, P(None, "tp"), P("tp"), P("tp", None), copied, copied)
    return jax.shard_map(per_device, mesh=mesh, in_specs=in_specs, out_specs=out_specs, check_vma=False)
```

```python
import functools

import jax
import jax.numpy as jnp
from jax import lax
from jax.experimental import pallas as pl
from jax.experimental.pallas import tpu as pltpu
from jax.sharding import PartitionSpec as P

EPS = 1e-06
BF, F32 = jnp.bfloat16, jnp.float32
TILE = 256
LANES = 128
PAD = 8
CHUNK = 64
VMEM_LIMIT = 12 * 1024 * 1024


def params(**more):
    return pltpu.CompilerParams(vmem_limit_bytes=VMEM_LIMIT, **more)


def struct(shape, dtype):
    return jax.ShapeDtypeStruct(shape, dtype)


def whole(shape):
    return pl.BlockSpec(shape, lambda *_: (0,) * len(shape))


def hbm():
    return pl.BlockSpec(memory_space=pltpu.HBM)


def smem():
    return pl.BlockSpec(memory_space=pltpu.SMEM)


def cost(size):
    return pl.CostEstimate(flops=0, transcendentals=0, bytes_accessed=size)


def vmem():
    return pl.BlockSpec(memory_space=pltpu.VMEM)


def lane(q):
    return slice(q * LANES, (q + 1) * LANES)


def fold(x):
    return jnp.sum(x.reshape(x.shape[0] // 8, 8, x.shape[1]), axis=0)


def pick(table, group):
    rows = table[...].astype(F32)
    value = rows[0:1]
    for r in range(1, rows.shape[0]):
        value = jnp.where(group == r, rows[r:r + 1], value)
    return value


def as_row(ref):
    return ref[...].astype(F32).reshape(1, -1)


def gelu_parts(pre):
    cdf = 0.5 + 0.5 * lax.erf(pre * 0.7071067811865476)
    density = jnp.exp(-0.5 * pre * pre) * 0.3989422804014327
    return pre * cdf, cdf + pre * density


def dot(a, b):
    return jnp.dot(a, b, preferred_element_type=F32)


def dot_t(a, b):
    return lax.dot_general(a, b, (((1,), (1,)), ((), ())), preferred_element_type=F32)


def dot_rows(a, b):
    return lax.dot_general(a, b, (((0,), (0,)), ((), ())), preferred_element_type=F32)


def place_items(n, meta, offs):
    end = jnp.int32(0)
    for j in range(n):
        offs[j] = end
        end = end + ((meta[2 + meta[0] * n + j] + 15) & -16)
    offs[n] = end
    offs[n + 1] = (end + TILE - 1) // TILE


def pack_kernel(wi, bi, wo, out):
    width, h = wi.shape
    hq, wq = h // LANES, width // LANES
    for q in range(hq):
        out[q * width:(q + 1) * width, :] = wi[:, lane(q)]
    base = hq * width
    for q in range(wq):
        out[base + q * h:base + (q + 1) * h, :] = wo[:, lane(q)]
    base += wq * h
    bias = bi[...].astype(F32).reshape(1, h)
    rows = [bias[:, lane(q)] for q in range(hq)] + [jnp.zeros((1, LANES), F32)] * (16 - hq)
    out[base:base + 16, :] = jnp.concatenate(rows, axis=0).astype(BF)


def pack(wi, bi, wo):
    rows = 2 * wi.size // LANES + 16
    return pl.pallas_call(pack_kernel, out_shape=struct((rows, LANES), BF),
                          compiler_params=params())(wi, bi, wo)


def weight_copies(buf, side, win, wout, bias, sems):
    width, h = win.shape[0], win.shape[1] // 2
    hq, wq = h // LANES, width // LANES
    copies = []
    for q in range(hq):
        at = side * h + q * LANES
        copies.append((buf.at[pl.ds(q * width, width), :], win.at[:, pl.ds(at, LANES)]))
    base = hq * width
    for q in range(wq):
        copies.append((buf.at[pl.ds(base + q * h, h), :], wout.at[pl.ds(side * h, h), pl.ds(q * LANES, LANES)]))
    copies.append((buf.at[pl.ds(base + wq * h, 16), :], bias.at[side]))
    return [pltpu.make_async_copy(src, dst, sems.at[side, i]) for i, (src, dst) in enumerate(copies)]


def spread_bias(bias, row):
    hq = row.shape[1] // LANES // 2
    for side in range(2):
        for q in range(hq):
            at = side * hq + q
            row[:, lane(at)] = bias[side, q:q + 1, :].astype(F32)


def front_kernel(n, counts_hbm, groups_hbm, tok_hbm, cot_hbm, cw, cb, ns, nsh, gamma, bout, buf_a, buf_b,
                 ad, nrm, low, inv, act, pre, win, wout, keep, send, gbo, gbi, tok, cot, consts, tokp, meta,
                 offs, counts_s, groups_s, pad, ad_s, nrm_s, low_s, inv_s, bias, bias_row, dwo, dwi, sems, item_sems, meta_sems, packed_sem):
    s = pl.program_id(0)
    frames, width = tok.shape[1], tok.shape[2]
    taps, rates = cw.shape[0], ns.shape[0]
    half = taps // 2
    wq = width // LANES
    h = win.shape[1] // 2
    copies = weight_copies(buf_a, 0, win, wout, bias, sems) + weight_copies(buf_b, 1, win, wout, bias, sems)

    def fetch(j):
        at = (lax.axis_index("tp") & 1) * n + j
        return [pltpu.make_async_copy(src.at[at], dst.at[j], item_sems.at[i, j])
                for i, (src, dst) in enumerate(((tok_hbm, tok), (cot_hbm, cot)))]

    @pl.when(s == 0)
    def _():
        tables = [pltpu.make_async_copy(counts_hbm, counts_s, meta_sems.at[0]),
                  pltpu.make_async_copy(groups_hbm, groups_s, meta_sems.at[1])]
        for c in tables + fetch(0) + fetch(1):
            c.start()
        for c in copies:
            c.start()
        for j in range(2, n):
            for c in fetch(j):
                c.start()
        consts[...] = jnp.zeros_like(consts)
        consts[:taps, :] = cw[...].astype(F32)
        consts[taps:taps + 1, :] = as_row(gamma)
        consts[taps + 1:taps + 2, :] = as_row(bout)
        consts[taps + 2:taps + 2 + rates, :] = ns[...].astype(F32)
        offs[n + 2] = 0
        gbo[...] = jnp.zeros_like(gbo)
        pad[...] = jnp.zeros_like(pad)
        for stage in (ad_s, nrm_s, low_s, inv_s):
            stage[...] = jnp.zeros_like(stage)
        meta[0] = lax.axis_index("tp") & 1
        meta[1] = lax.axis_index("dp")
        for c in tables:
            c.wait()
        for j in range(2 * n):
            meta[2 + j] = counts_s[j]
            meta[2 + 2 * n + j] = groups_s[j]
        place_items(n, meta, offs)

    def flush(j):
        dst = pl.ds(pl.multiple_of(offs[j], 16), frames)
        for whole_ref, stage in ((ad, ad_s), (nrm, nrm_s), (low, low_s), (inv, inv_s)):
            whole_ref[dst, :] = stage[...]

    @pl.when(s > 0)
    def _():
        flush(s - 1)

    @pl.when(s == 1)
    def _():
        for c in copies:
            c.wait()
        spread_bias(bias, bias_row)
        dwo[...] = jnp.zeros_like(dwo)
        dwi[...] = jnp.zeros_like(dwi)
        gbi[...] = jnp.zeros_like(gbi)

    for c in fetch(s):
        c.wait()

    def fetch_packed(j):
        dst = pl.ds(pl.multiple_of(offs[j], 16), frames)
        return pltpu.make_async_copy(tok.at[j], tokp.at[dst, :], packed_sem)

    @pl.when(s > 1)
    def _():
        fetch_packed(s - 2).wait()

    @pl.when(s > 0)
    def _():
        fetch_packed(s - 1).start()

    item = meta[0] * n + s
    count = meta[2 + item]
    group = meta[2 + 2 * n + item]

    def setup():
        rows = lax.broadcasted_iota(jnp.int32, (frames, LANES), 0)
        for q in range(wq):
            pad[q, PAD:PAD + frames, :] = jnp.where(rows < count, tok[s, :, lane(q)].astype(F32), 0.0)
        return pick(ns, group), pick(nsh, group), as_row(gamma), as_row(cb), cw[...].astype(F32)

    def conv_step(i, acc, consts):
        scale, shift, gam, conv_bias, w = consts
        r0 = i * CHUNK if isinstance(i, int) else pl.multiple_of(i * CHUNK, CHUNK)
        here = pl.ds(r0, CHUNK)
        live = (lax.broadcasted_iota(jnp.int32, (CHUNK, LANES), 0) + r0) < count
        convs = []
        for q in range(wq):
            conv = conv_bias[:, lane(q)]
            for k in range(taps):
                conv = conv + w[k:k + 1, lane(q)] * pad[q, pl.ds(r0 + (PAD - half + k), CHUNK), :]
            convs.append(conv)
        mean = jnp.sum(sum(convs[1:], convs[0]), axis=-1, keepdims=True) * (1.0 / width)
        cents = [c - mean for c in convs]
        sq = [c * c for c in cents]
        var = jnp.sum(sum(sq[1:], sq[0]), axis=-1, keepdims=True) * (1.0 / width)
        istd = lax.rsqrt(var + EPS)
        inv_s[here, :] = jnp.broadcast_to(istd, (CHUNK, LANES))
        new = []
        for q in range(wq):
            normed = cents[q] * istd
            ad_s[here, lane(q)] = (normed * scale[:, lane(q)] + shift[:, lane(q)]).astype(BF)
            nrm_s[here, lane(q)] = normed.astype(BF)
            back = jnp.where(live, cot[s, here, lane(q)].astype(F32), 0.0) * gam[:, lane(q)]
            low_s[here, lane(q)] = back.astype(BF)
            new.append(acc[q] + fold(back))
        return tuple(new)

    def add_gbo(accs):
        for q in range(wq):
            gbo[:, lane(q)] += accs[q]

    def tile(t, between=()):
        between = list(between)
        at = pl.ds(pl.multiple_of(t * TILE, TILE), TILE)
        a, b = ad[at, :], low[at, :]
        activation, slope = gelu_parts(dot(a, win[...]) + bias_row[...])
        if between:
            between.pop(0)()
        grad = dot_t(b, wout[...]) * slope
        lo = activation.astype(BF)
        act[at, :] = lo
        if between:
            between.pop(0)()
        dwo[...] += dot_rows(lo, b)
        gbi[...] += fold(grad)
        g = grad.astype(BF)
        pre[at, :] = g
        if between:
            between.pop(0)()
        dwi[...] += dot_rows(a, g)
        if between:
            between.pop(0)()

    done = offs[n + 2]
    ready = offs[s] >= (done + 1) * TILE
    none = (jnp.zeros((8, LANES), F32),) * wq

    def conv_with(chunks, with_tile):
        consts = setup()
        state = [none]

        def part(lo_i, hi_i):
            def run():
                for i in range(lo_i, hi_i):
                    state[0] = conv_step(i, state[0], consts)
            return run

        cuts = [chunks * k // 4 for k in range(5)]
        parts = [part(cuts[k], cuts[k + 1]) for k in range(4)]
        if with_tile:
            tile(done, parts)
        else:
            for run in parts:
                run()
        add_gbo(state[0])
        if with_tile:
            offs[n + 2] = done + 1

    all_chunks = frames // CHUNK
    short = count <= (all_chunks - 1) * CHUNK
    for with_tile in (True, False):
        for chunks in (all_chunks - 1, all_chunks):
            fits = short if chunks < all_chunks else jnp.logical_not(short)
            pl.when((ready == with_tile) & fits)(functools.partial(conv_with, chunks, with_tile))

    @pl.when(s == n - 1)
    def _():
        flush(s)
        end = pl.ds(pl.multiple_of(offs[n], 16), TILE)
        ad[end, :] = jnp.zeros((TILE, width), BF)
        low[end, :] = jnp.zeros((TILE, width), BF)

        fetch_packed(n - 2).wait()
        fetch_packed(n - 1).start()

        def rest(t, _):
            tile(t)
            return 0

        lax.fori_loop(offs[n + 2], offs[n + 1], rest, 0)
        fetch_packed(n - 1).wait()
        for side, dst in ((0, keep), (1, send)):
            for q in range(wq):
                dst[q * h:(q + 1) * h, :] = dwo[side * h:(side + 1) * h, lane(q)].astype(dst.dtype)
            base = wq * h
            for q in range(h // LANES):
                dst[base + q * width:base + (q + 1) * width, :] = dwi[:, lane(side * (h // LANES) + q)].astype(dst.dtype)


def front(counts, groups, tok, cot, cw, cb, ns, nsh, gamma, bout, buf_a, buf_b, h):
    items, frames, width = tok.shape
    n = items // 2
    rows = n * frames + TILE
    packed = 2 * width * h // LANES
    wq, hq = width // LANES, h // LANES
    n_consts = -(-(cw.shape[0] + 2 + ns.shape[0]) // 8) * 8
    return pl.pallas_call(
        functools.partial(front_kernel, n),
        grid_spec=pl.GridSpec(
            grid=(n,),
            in_specs=[hbm()] * 4 + [whole(v.shape) for v in (cw, cb, ns, nsh, gamma, bout)] + [hbm()] * 2,
            out_specs=[vmem()] * 16 + [smem()],
            scratch_shapes=[pltpu.SMEM((n + 3,), jnp.int32), pltpu.SMEM((items,), jnp.int32), pltpu.SMEM((items,), jnp.int32),
                            pltpu.VMEM((wq, frames + 4 * PAD, LANES), F32),
                            pltpu.VMEM((frames, width), BF), pltpu.VMEM((frames, width), BF),
                            pltpu.VMEM((frames, width), BF), pltpu.VMEM((frames, LANES), F32),
                            pltpu.VMEM((2, 16, LANES), BF), pltpu.VMEM((1, 2 * h), F32),
                            pltpu.VMEM((2 * h, width), F32), pltpu.VMEM((width, 2 * h), F32),
                            pltpu.SemaphoreType.DMA((2, hq + wq + 1)), pltpu.SemaphoreType.DMA((2, n)),
                            pltpu.SemaphoreType.DMA((2,)), pltpu.SemaphoreType.DMA]),
        out_shape=[struct((rows, width), BF)] * 3 + [struct((rows, LANES), F32)]
        + [struct((rows, 2 * h), BF)] * 2 + [struct((width, 2 * h), BF), struct((2 * h, width), BF)]
        + [struct((packed, LANES), F32), struct((packed, LANES), BF), struct((8, width), F32), struct((8, 2 * h), F32)]
        + [struct((n, frames, width), BF)] * 2 + [struct((n_consts, width), F32), struct((rows, width), BF), struct((2 + 2 * items,), jnp.int32)],
        compiler_params=params(), cost_estimate=cost(0),
    )(counts, groups, tok, cot, cw, cb, ns, nsh, gamma, bout, buf_a, buf_b)


def combine_kernel(dp, meta, keep, recv, stay, leave):
    m = keep.shape[0] // dp
    for d in range(dp):
        src = pl.ds(pl.multiple_of((meta[1] ^ d) * m, m), m)
        total = keep[src, :] + recv[src, :].astype(F32)
        dst = leave if d % 2 else stay
        dst[d // 2 * m:(d // 2 + 1) * m, :] = total.astype(dst.dtype)


def combine(meta, keep, recv, dp):
    rows = keep.shape[0] // 2
    return pl.pallas_call(
        functools.partial(combine_kernel, dp),
        in_specs=[smem(), vmem(), vmem()], out_specs=[vmem(), vmem()],
        out_shape=[struct((rows, LANES), F32), struct((rows, LANES), BF)],
        compiler_params=params())(meta, keep, recv)


def mix_kernel(n, taps, meta, ad, low, act, pre, win1, wout1, consts, tokp, buf_c, buf_d, branch, ag, out,
               offs, win2, wout2, bias, bias_row, sems):
    copies = weight_copies(buf_c, 0, win2, wout2, bias, sems) + weight_copies(buf_d, 1, win2, wout2, bias, sems)
    for c in copies:
        c.start()
    place_items(n, meta, offs)

    def own(at):
        return dot(act[at, :], wout1[...]), dot_t(pre[at, :], win1[...])

    def rest(at, own_branch, own_ag):
        a, b = ad[at, :], low[at, :]
        activation, slope = gelu_parts(dot(a, win2[...]) + bias_row[...])
        grad = dot_t(b, wout2[...]) * slope
        value = (own_branch + dot(activation.astype(BF), wout2[...])) + consts[taps + 1:taps + 2, :]
        branch[at, :] = value
        out[at, :] = (tokp[at, :].astype(F32) + consts[taps:taps + 1, :] * value).astype(BF)
        ag[at, :] = own_ag + dot_t(grad.astype(BF), win2[...])

    first = pl.ds(0, TILE)
    branch[first, :], ag[first, :] = own(first)
    for c in copies:
        c.wait()
    spread_bias(bias, bias_row)
    rest(first, branch[first, :], ag[first, :])

    def pair(t, _):
        at = pl.ds(pl.multiple_of((2 * t + 1) * TILE, TILE), 2 * TILE)
        rest(at, *own(at))
        return 0

    left = offs[n + 1] - 1
    pairs = lax.shift_right_arithmetic(left, 1)
    lax.fori_loop(0, pairs, pair, 0)

    @pl.when(left > 2 * pairs)
    def _():
        at = pl.ds(pl.multiple_of(left * TILE, TILE), TILE)
        rest(at, *own(at))


def mix(meta, ad, low, act, pre, win, wout, consts, tokp, buf_c, buf_d, n, taps):
    rows, width = ad.shape
    h = act.shape[1] // 2
    wq, hq = width // LANES, h // LANES
    return pl.pallas_call(
        functools.partial(mix_kernel, n, taps),
        in_specs=[smem()] + [vmem()] * 8 + [hbm()] * 2,
        out_specs=[vmem()] * 3,
        scratch_shapes=[pltpu.SMEM((n + 2,), jnp.int32),
                        pltpu.VMEM((width, 2 * h), BF), pltpu.VMEM((2 * h, width), BF),
                        pltpu.VMEM((2, 16, LANES), BF), pltpu.VMEM((1, 2 * h), F32),
                        pltpu.SemaphoreType.DMA((2, hq + wq + 1))],
        out_shape=[struct((rows, width), F32)] * 2 + [struct((rows, width), BF)],
        compiler_params=params(), cost_estimate=cost(0),
    )(meta, ad, low, act, pre, win, wout, consts, tokp, buf_c, buf_d)


def norm_grad_kernel(n, taps, rates, meta, tok, cot, branch, ag, nrm, inv, gbo, gbi, consts,
                     cgp, small_keep, small_send, offs, sums):
    s = pl.program_id(0)
    frames, width = tok.shape[1], tok.shape[2]
    half = taps // 2
    wq = width // LANES
    h = gbi.shape[1] // 2

    @pl.when(s == 0)
    def _():
        place_items(n, meta, offs)
        sums[...] = jnp.zeros_like(sums)

    item = meta[0] * n + s
    count = meta[2 + item]
    group = meta[2 + 2 * n + item]
    off = offs[s]
    scale = pick(consts.at[taps + 2:taps + 2 + rates], group)
    zero = jnp.zeros((8, LANES), F32)
    steps = pl.cdiv(count, CHUNK)
    wide = steps // 2

    def step(r0, size, accs):
        here = pl.ds(r0, size)
        live = (lax.broadcasted_iota(jnp.int32, (size, LANES), 0) + r0) < count
        src = pl.ds(pl.multiple_of(off + r0, 16), size)
        new = []
        ngs, nrs = [], []
        for q in range(wq):
            a_ls, a_sc, a_sh = accs[3 * q:3 * q + 3]
            br = jnp.where(live, branch[src, lane(q)], 0.0)
            g = jnp.where(live, ag[src, lane(q)], 0.0)
            nr = nrm[src, lane(q)].astype(F32)
            new += [a_ls + fold(cot[s, here, lane(q)].astype(F32) * br), a_sc + fold(g * nr), a_sh + fold(g)]
            ngs.append(g * scale[:, lane(q)])
            nrs.append(nr)
        cross = [a * b for a, b in zip(ngs, nrs)]
        m1 = jnp.sum(sum(ngs[1:], ngs[0]), axis=-1, keepdims=True) * (1.0 / width)
        m2 = jnp.sum(sum(cross[1:], cross[0]), axis=-1, keepdims=True) * (1.0 / width)
        istd = inv[src, :]
        for q in range(wq):
            cg = istd * (ngs[q] - m1 - nrs[q] * m2)
            cgp[s, q, pl.ds(pl.multiple_of(r0 + PAD, 8), size), :] = jnp.where(live, cg, 0.0)
        return tuple(new)

    def both_sizes(run, width_of_state, add):
        add(lax.fori_loop(0, wide, lambda i, accs: run(pl.multiple_of(i * 2 * CHUNK, 2 * CHUNK), 2 * CHUNK, accs),
                          (zero,) * width_of_state))

        @pl.when(steps > 2 * wide)
        def _():
            add(run(pl.multiple_of(wide * 2 * CHUNK, 2 * CHUNK), CHUNK, (zero,) * width_of_state))

    def add_norm(accs):
        for q in range(wq):
            sums[taps + 1, :, lane(q)] += accs[3 * q]
            sums[taps + 2 + group, :, lane(q)] += accs[3 * q + 1]
            sums[taps + 2 + rates + group, :, lane(q)] += accs[3 * q + 2]

    both_sizes(step, 3 * wq, add_norm)

    def clear(i, _):
        r0 = pl.multiple_of(i * CHUNK, CHUNK)
        for q in range(wq):
            cgp[s, q, pl.ds(pl.multiple_of(r0 + PAD, 8), CHUNK), :] = jnp.zeros((CHUNK, LANES), F32)
        return 0

    lax.fori_loop(steps, frames // CHUNK, clear, 0)
    for q in range(wq):
        cgp[s, q, :PAD, :] = jnp.zeros((PAD, LANES), F32)
        cgp[s, q, PAD + frames:, :] = jnp.zeros((cgp.shape[2] - PAD - frames, LANES), F32)

        def conv_step(r0, size, accs):
            here = pl.ds(r0, size)
            live = (lax.broadcasted_iota(jnp.int32, (size, LANES), 0) + r0) < count
            tk = jnp.where(live, tok[s, here, lane(q)].astype(F32), 0.0)
            new = []
            for k in range(taps):
                sh = cgp[s, q, pl.ds(r0 + (PAD + half - k), size), :]
                new.append(accs[k] + fold(tk * sh))
                if k == half:
                    new_bias = accs[taps] + fold(sh)
            return tuple(new) + (new_bias,)

        def add_conv(accs):
            for k in range(taps + 1):
                sums[k, :, lane(q)] += accs[k]

        both_sizes(conv_step, taps + 1, add_conv)

    @pl.when(s == n - 1)
    def _():
        last = taps + 2 + 2 * rates
        rows = [jnp.sum(sums[i], axis=0, keepdims=True) for i in range(last)]
        rows.append(jnp.sum(gbo[...], axis=0, keepdims=True))
        gb = jnp.sum(gbi[...], axis=0, keepdims=True)
        fill = jnp.zeros((1, width - h), F32)
        spare = [jnp.zeros((1, width), F32)] * (small_keep.shape[0] - last - 2)
        for side, dst in ((0, small_keep), (1, small_send)):
            tail = [jnp.concatenate([gb[:, side * h:(side + 1) * h], fill], axis=1)]
            dst[...] = jnp.concatenate(rows + tail + spare, axis=0)


def norm_grad(meta, tok, cot, branch, ag, nrm, inv, gbo, gbi, consts, taps, rates):
    n, frames, width = tok.shape
    wq = width // LANES
    n_small = -(-(taps + 4 + 2 * rates) // 8) * 8
    return pl.pallas_call(
        functools.partial(norm_grad_kernel, n, taps, rates), grid=(n,),
        in_specs=[smem()] + [vmem()] * 9, out_specs=[vmem()] * 3,
        scratch_shapes=[pltpu.SMEM((n + 2,), jnp.int32),
                        pltpu.VMEM((taps + 2 + 2 * rates, 8, width), F32)],
        out_shape=[struct((n, wq, frames + 4 * PAD, LANES), F32)] + [struct((n_small, width), F32)] * 2,
        compiler_params=params(), cost_estimate=cost(40000000),
    )(meta, tok, cot, branch, ag, nrm, inv, gbo, gbi, consts)


def place_out_kernel(n, meta, own, other, out, stage, sems):
    frames, width = stage.shape[1], stage.shape[2]
    copies = []
    for side, src in ((0, own), (1, other)):
        first = (meta[0] ^ side) * n
        off = jnp.int32(0)
        for j in range(n):
            count = meta[2 + first + j]
            for i in range(frames // CHUNK):
                live = (lax.broadcasted_iota(jnp.int32, (CHUNK, LANES), 0) + i * CHUNK) < count
                rows = pl.ds(pl.multiple_of(off + i * CHUNK, 16), CHUNK)
                for q in range(width // LANES):
                    value = jnp.where(live, src[rows, lane(q)].astype(F32), 0.0)
                    stage[side * n + j, i * CHUNK:(i + 1) * CHUNK, lane(q)] = value.astype(BF)
            copies.append(pltpu.make_async_copy(stage.at[side * n + j], out.at[first + j], sems.at[side * n + j]))
            copies[-1].start()
            off = off + ((count + 15) & -16)
    for c in copies:
        c.wait()


def place_out(meta, own, other, n, frames):
    width = own.shape[1]
    return pl.pallas_call(
        functools.partial(place_out_kernel, n),
        in_specs=[smem(), vmem(), vmem()], out_specs=hbm(), out_shape=struct((2 * n, frames, width), BF),
        scratch_shapes=[pltpu.VMEM((2 * n, frames, width), BF), pltpu.SemaphoreType.DMA((2 * n,))],
        compiler_params=params(), cost_estimate=cost(40000000),
    )(meta, own, other)


def token_grad_kernel(n, taps, meta, cot, cgp, consts, gtok, gtok_own, stage, sems):
    s = pl.program_id(0)
    frames, width = cot.shape[1], cot.shape[2]
    half = taps // 2
    wq = width // LANES
    count = meta[2 + meta[0] * n + s]
    w = consts[:taps, :]
    steps = pl.cdiv(count, CHUNK)

    def place(j):
        return pltpu.make_async_copy(stage.at[j], gtok.at[meta[0] * n + j], sems.at[j])

    def conv_step(i, _):
        r0 = pl.multiple_of(i * CHUNK, CHUNK)
        here = pl.ds(r0, CHUNK)
        live = (lax.broadcasted_iota(jnp.int32, (CHUNK, LANES), 0) + r0) < count
        for q in range(wq):
            total = cot[s, here, lane(q)].astype(F32)
            for k in range(taps):
                total = total + w[k:k + 1, lane(q)] * cgp[s, q, pl.ds(r0 + (PAD + half - k), CHUNK), :]
            total = jnp.where(live, total, 0.0).astype(BF)
            gtok_own[s, here, lane(q)] = total
            stage[s, here, lane(q)] = total.astype(F32)
        return 0

    lax.fori_loop(0, steps, conv_step, 0)

    def clear(i, _):
        here = pl.ds(pl.multiple_of(i * CHUNK, CHUNK), CHUNK)
        gtok_own[s, here, :] = jnp.zeros((CHUNK, width), BF)
        stage[s, here, :] = jnp.zeros((CHUNK, width), F32)
        return 0

    lax.fori_loop(steps, frames // CHUNK, clear, 0)
    place(s).start()

    @pl.when(s == n - 1)
    def _():
        for j in range(n):
            place(j).wait()


def token_grad(meta, cot, cgp, consts, taps):
    n, frames, width = cot.shape
    return pl.pallas_call(
        functools.partial(token_grad_kernel, n, taps), grid=(n,),
        in_specs=[smem()] + [vmem()] * 3, out_specs=[hbm(), vmem()],
        scratch_shapes=[pltpu.VMEM((n, frames, width), F32), pltpu.SemaphoreType.DMA((n,))],
        out_shape=[struct((2 * n, frames, width), F32), struct((n, frames, width), BF)],
        compiler_params=params(), cost_estimate=cost(40000000),
    )(meta, cot, cgp, consts)


def merge_gtok_kernel(n, meta, other, gtok_in, gtok, stage, sems):
    copies = [pltpu.make_async_copy(stage.at[j], gtok.at[(1 - meta[0]) * n + j], sems.at[j]) for j in range(n)]
    for j in range(n):
        stage[j] = other[j].astype(F32)
        copies[j].start()
    for c in copies:
        c.wait()


def merge_gtok(meta, other, gtok):
    n = other.shape[0]
    return pl.pallas_call(
        functools.partial(merge_gtok_kernel, n),
        in_specs=[smem(), vmem(), hbm()], out_specs=hbm(), out_shape=struct(gtok.shape, F32),
        scratch_shapes=[pltpu.VMEM(other.shape, F32), pltpu.SemaphoreType.DMA((n,))],
        input_output_aliases={2: 0},
        compiler_params=params(), cost_estimate=cost(20000000),
    )(meta, other, gtok)


def message_kernel(stay, keep, recv, *refs):
    pieces, (out, mine) = refs[:-2], refs[-2:]
    m = pieces[0].shape[0]
    total = stay[:m, :]
    for piece in pieces:
        total = total + piece[...].astype(F32)
    out[:m, :] = total.astype(BF)
    mine[...] = total.astype(BF)
    small = (keep[...] + recv[...]).astype(BF)
    rows = small.shape[0]
    for q in range(small.shape[1] // LANES):
        out[m + q * rows:m + (q + 1) * rows, :] = small[:, lane(q)]


def make_message(stay, keep, recv, pieces):
    rows = pieces[0].shape[0] + keep.size // LANES
    return pl.pallas_call(message_kernel, in_specs=[vmem()] * (3 + len(pieces)), out_specs=[vmem(), vmem()],
                          out_shape=[struct((rows, LANES), BF), struct(pieces[0].shape, BF)],
                          compiler_params=params())(stay, keep, recv, *pieces)


def relay_kernel(m, *refs):
    sources, out = refs[:-1], refs[-1]
    sums = []
    for d, src in enumerate(sources):
        if d > 1:
            out[(d - 2) * m:(d - 1) * m, :] = src[:m, :]
        sums.append(src[m:, :].astype(F32))
    while len(sums) > 1:
        sums = [a + b for a, b in zip(sums[::2], sums[1::2])]
    out[(len(sources) - 2) * m:, :] = sums[0].astype(BF)


def relay(m, sources):
    rows = (len(sources) - 2) * m + sources[0].shape[0] - m
    return pl.pallas_call(functools.partial(relay_kernel, m), in_specs=[vmem()] * len(sources), out_specs=vmem(),
                          out_shape=struct((rows, LANES), BF), compiler_params=params())(*sources)


def unpack_kernel(dp, taps, rates, meta, mine, theirs, near_1, far_1, near, far, gcw, gcb, gns, gnsh, gwi, gbi, gwo, gbo, gls, full):
    h, width = gwo.shape
    wq, hq = width // LANES, h // LANES
    m = full.shape[0] // dp
    for odd, early, others in ((0, (mine, near_1), near), (1, (theirs, far_1), far)):
        for d in range(dp // 2):
            piece = others[(d - 2) * m:(d - 1) * m, :] if d > 1 else early[d][:m, :]
            at = pl.multiple_of((meta[1] ^ (2 * d + odd)) * m, m)
            full[pl.ds(at, m), :] = piece.astype(F32)
    for q in range(wq):
        gwo[:, lane(q)] = full[q * h:(q + 1) * h, :]
    base = wq * h
    for q in range(hq):
        gwi[:, lane(q)] = full[base + q * width:base + (q + 1) * width, :]
    behind = (dp // 2 - 2) * m
    small = near[behind:, :].astype(F32) + far[behind:, :].astype(F32)
    rows = small.shape[0] // wq
    small = jnp.concatenate([small[q * rows:(q + 1) * rows] for q in range(wq)], axis=1)
    gcw[...] = small[:taps]
    gcb[...] = small[taps]
    gls[...] = small[taps + 1]
    gns[...] = small[taps + 2:taps + 2 + rates]
    gnsh[...] = small[taps + 2 + rates:taps + 2 + 2 * rates]
    at = taps + 2 + 2 * rates
    gbo[...] = small[at]
    gbi[...] = small[at + 1, :h]


def unpack(meta, mine, theirs, near_1, far_1, near, far, dp, taps, rates, width, h):
    shapes = [(taps, width), (width,), (rates, width), (rates, width), (width, h), (h,), (h, width), (width,), (width,)]
    return pl.pallas_call(
        functools.partial(unpack_kernel, dp, taps, rates), in_specs=[smem()] + [vmem()] * 6,
        out_shape=[struct(s, F32) for s in shapes],
        scratch_shapes=[pltpu.VMEM((2 * width * h // LANES, LANES), F32)],
        compiler_params=params())(meta, mine, theirs, near_1, far_1, near, far)


def swap(x, step):
    size = lax.axis_size("tp")
    return lax.ppermute(x, "tp", [(i, i ^ step) for i in range(size)])


def across(x, step):
    size = lax.axis_size("dp")
    return lax.ppermute(x, "dp", [(i, i ^ step) for i in range(size)])


def per_device(tokens, frame_counts, rate_groups, conv_weight, conv_bias, norm_scale, norm_shift,
               weight_in, bias_in, weight_out, bias_out, layer_scale, cotangent):
    width, h = weight_in.shape
    n = tokens.shape[0] // 2
    (tokens, cotangent, conv_weight, conv_bias, norm_scale, norm_shift, weight_in, bias_in, weight_out, bias_out,
     layer_scale, frame_counts, rate_groups) = [pltpu.with_memory_space_constraint(v, pltpu.HBM) for v in (
         tokens, cotangent, conv_weight, conv_bias, norm_scale, norm_shift, weight_in, bias_in, weight_out, bias_out,
         layer_scale, frame_counts, rate_groups)]
    taps, rates = conv_weight.shape[0], norm_scale.shape[0]
    dp = lax.axis_size("dp")
    buf_a = pack(weight_in, bias_in, weight_out)
    buf_b = swap(buf_a, 1)
    buf_c = swap(buf_a, 2)
    buf_d = swap(buf_c, 1)
    ad, nrm, low, inv, act, pre, win, wout, keep, send, gbo, gbi, tok, cot, consts, tokp, meta = front(
        frame_counts, rate_groups, tokens, cotangent, conv_weight, conv_bias, norm_scale, norm_shift, layer_scale, bias_out, buf_a, buf_b, h)
    stay, leave = combine(meta, keep, swap(send, 1), dp)
    arrived = across(leave, 1)
    branch, ag, out_own = mix(meta, ad, low, act, pre, win, wout, consts, tokp, buf_c, buf_d, n, taps)
    arrived, branch, out_own = lax.optimization_barrier((arrived, branch, out_own))
    out_b = swap(out_own, 1)
    stay = (stay + arrived.astype(F32)).reshape(dp // 2, -1, LANES)
    pieces = [across(stay[d].astype(BF), 2 * d) for d in range(1, dp // 2)]

    cgp, small_keep, small_send = norm_grad(meta, tok, cot, branch, ag, nrm, inv, gbo, gbi, consts, taps, rates)
    pieces, small_send, cgp, out_b = lax.optimization_barrier((pieces, small_send, cgp, out_b))
    small_got = swap(small_send, 1)
    message, mine = make_message(stay.reshape(-1, LANES), small_keep, small_got, pieces)
    message, mine, out_b = lax.optimization_barrier((message, mine, out_b))
    m = pieces[0].shape[0]
    near = [message] + [across(message, 2 * d) for d in range(1, dp // 2)]
    theirs = across(mine, 1)
    far_1 = across(message, 3)
    out = place_out(meta, out_own, out_b, n, tokens.shape[1])
    cgp, out = lax.optimization_barrier((cgp, out))
    gtok, gtok_own = token_grad(meta, cot, cgp, consts, taps)
    near, theirs, far_1, gtok_own = lax.optimization_barrier((near, theirs, far_1, gtok_own))
    late = relay(m, near)
    far = across(late, 1)
    gtok = merge_gtok(meta, swap(gtok_own, 1), gtok)
    far, gtok = lax.optimization_barrier((far, gtok))
    gcw, gcb, gns, gnsh, gwi, gbi, gwo, gbo, gls = unpack(meta, mine, theirs, near[1], far_1, late, far, dp, taps, rates,
                                                          width, h)
    return (out, gtok, gcw, gcb, gns, gnsh, gwi, gbi, gwo, gbo, gls)


def solution(mesh):
    items, copied = P("dp", None, None), P()
    in_specs = (items, P("dp"), P("dp"), copied, copied, copied, copied, P(None, "tp"), P("tp"), P("tp", None),
                copied, copied, items)
    out_specs = (items, items, copied, copied, copied, copied, P(None, "tp"), P("tp"), P("tp", None), copied, copied)
    return jax.shard_map(per_device, mesh=mesh, in_specs=in_specs, out_specs=out_specs, check_vma=False)
```

```python
import functools

import jax
import jax.numpy as jnp
from jax import lax
from jax.experimental import pallas as pl
from jax.experimental.pallas import tpu as pltpu
from jax.sharding import PartitionSpec as P

EPS = 1e-06
BF, F32 = jnp.bfloat16, jnp.float32
TILE = 256
LANES = 128
PAD = 8
CHUNK = 64
VMEM_LIMIT = 12 * 1024 * 1024


def params(**more):
    return pltpu.CompilerParams(vmem_limit_bytes=VMEM_LIMIT, **more)


def struct(shape, dtype):
    return jax.ShapeDtypeStruct(shape, dtype)


def whole(shape):
    return pl.BlockSpec(shape, lambda *_: (0,) * len(shape))


def hbm():
    return pl.BlockSpec(memory_space=pltpu.HBM)


def smem():
    return pl.BlockSpec(memory_space=pltpu.SMEM)


def cost(size):
    return pl.CostEstimate(flops=0, transcendentals=0, bytes_accessed=size)


def vmem():
    return pl.BlockSpec(memory_space=pltpu.VMEM)


def lane(q):
    return slice(q * LANES, (q + 1) * LANES)


def fold(x):
    return jnp.sum(x.reshape(x.shape[0] // 8, 8, x.shape[1]), axis=0)


def pick(table, group):
    rows = table[...].astype(F32)
    value = rows[0:1]
    for r in range(1, rows.shape[0]):
        value = jnp.where(group == r, rows[r:r + 1], value)
    return value


def as_row(ref):
    return ref[...].astype(F32).reshape(1, -1)


def gelu_parts(pre):
    cdf = 0.5 + 0.5 * lax.erf(pre * 0.7071067811865476)
    density = jnp.exp(-0.5 * pre * pre) * 0.3989422804014327
    return pre * cdf, cdf + pre * density


def dot(a, b):
    return jnp.dot(a, b, preferred_element_type=F32)


def dot_t(a, b):
    return lax.dot_general(a, b, (((1,), (1,)), ((), ())), preferred_element_type=F32)


def dot_rows(a, b):
    return lax.dot_general(a, b, (((0,), (0,)), ((), ())), preferred_element_type=F32)


def place_items(n, meta, offs):
    end = jnp.int32(0)
    for j in range(n):
        offs[j] = end
        end = end + ((meta[2 + meta[0] * n + j] + 15) & -16)
    offs[n] = end
    offs[n + 1] = (end + TILE - 1) // TILE


def pack_kernel(wi, bi, wo, out):
    width, h = wi.shape
    hq, wq = h // LANES, width // LANES
    for q in range(hq):
        out[q * width:(q + 1) * width, :] = wi[:, lane(q)]
    base = hq * width
    for q in range(wq):
        out[base + q * h:base + (q + 1) * h, :] = wo[:, lane(q)]
    base += wq * h
    bias = bi[...].astype(F32).reshape(1, h)
    rows = [bias[:, lane(q)] for q in range(hq)] + [jnp.zeros((1, LANES), F32)] * (16 - hq)
    out[base:base + 16, :] = jnp.concatenate(rows, axis=0).astype(BF)


def pack(wi, bi, wo):
    rows = 2 * wi.size // LANES + 16
    return pl.pallas_call(pack_kernel, out_shape=struct((rows, LANES), BF),
                          compiler_params=params())(wi, bi, wo)


def weight_copies(buf, side, win, wout, bias, sems):
    width, h = win.shape[0], win.shape[1] // 2
    hq, wq = h // LANES, width // LANES
    copies = []
    for q in range(hq):
        at = side * h + q * LANES
        copies.append((buf.at[pl.ds(q * width, width), :], win.at[:, pl.ds(at, LANES)]))
    base = hq * width
    for q in range(wq):
        copies.append((buf.at[pl.ds(base + q * h, h), :], wout.at[pl.ds(side * h, h), pl.ds(q * LANES, LANES)]))
    copies.append((buf.at[pl.ds(base + wq * h, 16), :], bias.at[side]))
    return [pltpu.make_async_copy(src, dst, sems.at[side, i]) for i, (src, dst) in enumerate(copies)]


def spread_bias(bias, row):
    hq = row.shape[1] // LANES // 2
    for side in range(2):
        for q in range(hq):
            at = side * hq + q
            row[:, lane(at)] = bias[side, q:q + 1, :].astype(F32)


def front_kernel(n, counts_hbm, groups_hbm, tok_hbm, cot_hbm, cw, cb, ns, nsh, gamma, bout, buf_a, buf_b,
                 ad, nrm, low, inv, act, pre, win, wout, keep, send, gbo, gbi, tok, cot, consts, tokp, meta,
                 offs, counts_s, groups_s, pad, ad_s, nrm_s, low_s, inv_s, bias, bias_row, dwo, dwi, sems, item_sems, meta_sems, packed_sem):
    s = pl.program_id(0)
    frames, width = tok.shape[1], tok.shape[2]
    taps, rates = cw.shape[0], ns.shape[0]
    half = taps // 2
    wq = width // LANES
    h = win.shape[1] // 2
    copies = weight_copies(buf_a, 0, win, wout, bias, sems) + weight_copies(buf_b, 1, win, wout, bias, sems)

    def fetch(j):
        at = (lax.axis_index("tp") & 1) * n + j
        return [pltpu.make_async_copy(src.at[at], dst.at[j], item_sems.at[i, j])
                for i, (src, dst) in enumerate(((tok_hbm, tok), (cot_hbm, cot)))]

    @pl.when(s == 0)
    def _():
        tables = [pltpu.make_async_copy(counts_hbm, counts_s, meta_sems.at[0]),
                  pltpu.make_async_copy(groups_hbm, groups_s, meta_sems.at[1])]
        for c in tables + fetch(0) + fetch(1):
            c.start()
        for c in copies:
            c.start()
        for j in range(2, n):
            for c in fetch(j):
                c.start()
        consts[...] = jnp.zeros_like(consts)
        consts[:taps, :] = cw[...].astype(F32)
        consts[taps:taps + 1, :] = as_row(gamma)
        consts[taps + 1:taps + 2, :] = as_row(bout)
        consts[taps + 2:taps + 2 + rates, :] = ns[...].astype(F32)
        offs[n + 2] = 0
        gbo[...] = jnp.zeros_like(gbo)
        pad[...] = jnp.zeros_like(pad)
        for stage in (ad_s, nrm_s, low_s, inv_s):
            stage[...] = jnp.zeros_like(stage)
        meta[0] = lax.axis_index("tp") & 1
        meta[1] = lax.axis_index("dp")
        for c in tables:
            c.wait()
        for j in range(2 * n):
            meta[2 + j] = counts_s[j]
            meta[2 + 2 * n + j] = groups_s[j]
        place_items(n, meta, offs)

    def flush(j):
        dst = pl.ds(pl.multiple_of(offs[j], 16), frames)
        for whole_ref, stage in ((ad, ad_s), (nrm, nrm_s), (low, low_s), (inv, inv_s)):
            whole_ref[dst, :] = stage[...]

    @pl.when(s > 0)
    def _():
        flush(s - 1)

    @pl.when(s == 1)
    def _():
        for c in copies:
            c.wait()
        spread_bias(bias, bias_row)
        dwo[...] = jnp.zeros_like(dwo)
        dwi[...] = jnp.zeros_like(dwi)
        gbi[...] = jnp.zeros_like(gbi)

    for c in fetch(s):
        c.wait()

    def fetch_packed(j):
        dst = pl.ds(pl.multiple_of(offs[j], 16), frames)
        return pltpu.make_async_copy(tok.at[j], tokp.at[dst, :], packed_sem)

    @pl.when(s > 1)
    def _():
        fetch_packed(s - 2).wait()

    @pl.when(s > 0)
    def _():
        fetch_packed(s - 1).start()

    item = meta[0] * n + s
    count = meta[2 + item]
    group = meta[2 + 2 * n + item]

    def setup():
        rows = lax.broadcasted_iota(jnp.int32, (frames, LANES), 0)
        for q in range(wq):
            pad[q, PAD:PAD + frames, :] = jnp.where(rows < count, tok[s, :, lane(q)].astype(F32), 0.0)
        return pick(ns, group), pick(nsh, group), as_row(gamma), as_row(cb), cw[...].astype(F32)

    def conv_step(i, acc, consts):
        scale, shift, gam, conv_bias, w = consts
        r0 = i * CHUNK if isinstance(i, int) else pl.multiple_of(i * CHUNK, CHUNK)
        here = pl.ds(r0, CHUNK)
        live = (lax.broadcasted_iota(jnp.int32, (CHUNK, LANES), 0) + r0) < count
        convs = []
        for q in range(wq):
            conv = conv_bias[:, lane(q)]
            for k in range(taps):
                conv = conv + w[k:k + 1, lane(q)] * pad[q, pl.ds(r0 + (PAD - half + k), CHUNK), :]
            convs.append(conv)
        mean = jnp.sum(sum(convs[1:], convs[0]), axis=-1, keepdims=True) * (1.0 / width)
        cents = [c - mean for c in convs]
        sq = [c * c for c in cents]
        var = jnp.sum(sum(sq[1:], sq[0]), axis=-1, keepdims=True) * (1.0 / width)
        istd = lax.rsqrt(var + EPS)
        inv_s[here, :] = jnp.broadcast_to(istd, (CHUNK, LANES))
        new = []
        for q in range(wq):
            normed = cents[q] * istd
            ad_s[here, lane(q)] = (normed * scale[:, lane(q)] + shift[:, lane(q)]).astype(BF)
            nrm_s[here, lane(q)] = normed.astype(BF)
            back = jnp.where(live, cot[s, here, lane(q)].astype(F32), 0.0) * gam[:, lane(q)]
            low_s[here, lane(q)] = back.astype(BF)
            new.append(acc[q] + fold(back))
        return tuple(new)

    def add_gbo(accs):
        for q in range(wq):
            gbo[:, lane(q)] += accs[q]

    def tile(t, size, between=()):
        between = list(between)
        at = pl.ds(pl.multiple_of(t * TILE, TILE), size)
        a, b = ad[at, :], low[at, :]
        activation, slope = gelu_parts(dot(a, win[...]) + bias_row[...])
        if between:
            between.pop(0)()
        grad = dot_t(b, wout[...]) * slope
        lo = activation.astype(BF)
        act[at, :] = lo
        if between:
            between.pop(0)()
        dwo[...] += dot_rows(lo, b)
        gbi[...] += fold(grad)
        g = grad.astype(BF)
        pre[at, :] = g
        if between:
            between.pop(0)()
        dwi[...] += dot_rows(a, g)
        if between:
            between.pop(0)()

    done = offs[n + 2]
    ready = offs[s] >= (done + 2) * TILE
    none = (jnp.zeros((8, LANES), F32),) * wq

    def conv_with(chunks, with_tile):
        consts = setup()
        state = [none]

        def part(lo_i, hi_i):
            def run():
                for i in range(lo_i, hi_i):
                    state[0] = conv_step(i, state[0], consts)
            return run

        cuts = [chunks * k // 4 for k in range(5)]
        parts = [part(cuts[k], cuts[k + 1]) for k in range(4)]
        if with_tile:
            tile(done, 2 * TILE, parts)
        else:
            for run in parts:
                run()
        add_gbo(state[0])
        if with_tile:
            offs[n + 2] = done + 2

    all_chunks = frames // CHUNK
    short = count <= (all_chunks - 1) * CHUNK
    for with_tile in (True, False):
        for chunks in (all_chunks - 1, all_chunks):
            fits = short if chunks < all_chunks else jnp.logical_not(short)
            pl.when((ready == with_tile) & fits)(functools.partial(conv_with, chunks, with_tile))

    @pl.when(s == n - 1)
    def _():
        flush(s)
        end = pl.ds(pl.multiple_of(offs[n], 16), TILE)
        ad[end, :] = jnp.zeros((TILE, width), BF)
        low[end, :] = jnp.zeros((TILE, width), BF)

        fetch_packed(n - 2).wait()
        fetch_packed(n - 1).start()

        start = offs[n + 2]
        left = offs[n + 1] - start
        pairs = lax.shift_right_arithmetic(left, 1)

        def rest(t, _):
            tile(start + 2 * t, 2 * TILE)
            return 0

        lax.fori_loop(0, pairs, rest, 0)

        @pl.when(left > 2 * pairs)
        def _():
            tile(offs[n + 1] - 1, TILE)

        fetch_packed(n - 1).wait()
        for side, dst in ((0, keep), (1, send)):
            for q in range(wq):
                dst[q * h:(q + 1) * h, :] = dwo[side * h:(side + 1) * h, lane(q)].astype(dst.dtype)
            base = wq * h
            for q in range(h // LANES):
                dst[base + q * width:base + (q + 1) * width, :] = dwi[:, lane(side * (h // LANES) + q)].astype(dst.dtype)


def front(counts, groups, tok, cot, cw, cb, ns, nsh, gamma, bout, buf_a, buf_b, h):
    items, frames, width = tok.shape
    n = items // 2
    rows = n * frames + TILE
    packed = 2 * width * h // LANES
    wq, hq = width // LANES, h // LANES
    n_consts = -(-(cw.shape[0] + 2 + ns.shape[0]) // 8) * 8
    return pl.pallas_call(
        functools.partial(front_kernel, n),
        grid_spec=pl.GridSpec(
            grid=(n,),
            in_specs=[hbm()] * 4 + [whole(v.shape) for v in (cw, cb, ns, nsh, gamma, bout)] + [hbm()] * 2,
            out_specs=[vmem()] * 16 + [smem()],
            scratch_shapes=[pltpu.SMEM((n + 3,), jnp.int32), pltpu.SMEM((items,), jnp.int32), pltpu.SMEM((items,), jnp.int32),
                            pltpu.VMEM((wq, frames + 4 * PAD, LANES), F32),
                            pltpu.VMEM((frames, width), BF), pltpu.VMEM((frames, width), BF),
                            pltpu.VMEM((frames, width), BF), pltpu.VMEM((frames, LANES), F32),
                            pltpu.VMEM((2, 16, LANES), BF), pltpu.VMEM((1, 2 * h), F32),
                            pltpu.VMEM((2 * h, width), F32), pltpu.VMEM((width, 2 * h), F32),
                            pltpu.SemaphoreType.DMA((2, hq + wq + 1)), pltpu.SemaphoreType.DMA((2, n)),
                            pltpu.SemaphoreType.DMA((2,)), pltpu.SemaphoreType.DMA]),
        out_shape=[struct((rows, width), BF)] * 3 + [struct((rows, LANES), F32)]
        + [struct((rows, 2 * h), BF)] * 2 + [struct((width, 2 * h), BF), struct((2 * h, width), BF)]
        + [struct((packed, LANES), F32), struct((packed, LANES), BF), struct((8, width), F32), struct((8, 2 * h), F32)]
        + [struct((n, frames, width), BF)] * 2 + [struct((n_consts, width), F32), struct((rows, width), BF), struct((2 + 2 * items,), jnp.int32)],
        compiler_params=params(), cost_estimate=cost(0),
    )(counts, groups, tok, cot, cw, cb, ns, nsh, gamma, bout, buf_a, buf_b)


def combine_kernel(dp, meta, keep, recv, stay, leave):
    m = keep.shape[0] // dp
    for d in range(dp):
        src = pl.ds(pl.multiple_of((meta[1] ^ d) * m, m), m)
        total = keep[src, :] + recv[src, :].astype(F32)
        dst = leave if d % 2 else stay
        dst[d // 2 * m:(d // 2 + 1) * m, :] = total.astype(dst.dtype)


def combine(meta, keep, recv, dp):
    rows = keep.shape[0] // 2
    return pl.pallas_call(
        functools.partial(combine_kernel, dp),
        in_specs=[smem(), vmem(), vmem()], out_specs=[vmem(), vmem()],
        out_shape=[struct((rows, LANES), F32), struct((rows, LANES), BF)],
        compiler_params=params())(meta, keep, recv)


def mix_kernel(n, taps, meta, ad, low, act, pre, win1, wout1, consts, tokp, buf_c, buf_d, branch, ag, out,
               offs, win2, wout2, bias, bias_row, sems):
    copies = weight_copies(buf_c, 0, win2, wout2, bias, sems) + weight_copies(buf_d, 1, win2, wout2, bias, sems)
    for c in copies:
        c.start()
    place_items(n, meta, offs)

    def own(at):
        return dot(act[at, :], wout1[...]), dot_t(pre[at, :], win1[...])

    def rest(at, own_branch, own_ag):
        a, b = ad[at, :], low[at, :]
        activation, slope = gelu_parts(dot(a, win2[...]) + bias_row[...])
        grad = dot_t(b, wout2[...]) * slope
        value = (own_branch + dot(activation.astype(BF), wout2[...])) + consts[taps + 1:taps + 2, :]
        branch[at, :] = value
        out[at, :] = (tokp[at, :].astype(F32) + consts[taps:taps + 1, :] * value).astype(BF)
        ag[at, :] = own_ag + dot_t(grad.astype(BF), win2[...])

    first = pl.ds(0, TILE)
    branch[first, :], ag[first, :] = own(first)
    for c in copies:
        c.wait()
    spread_bias(bias, bias_row)
    rest(first, branch[first, :], ag[first, :])

    def pair(t, _):
        at = pl.ds(pl.multiple_of((2 * t + 1) * TILE, TILE), 2 * TILE)
        rest(at, *own(at))
        return 0

    left = offs[n + 1] - 1
    pairs = lax.shift_right_arithmetic(left, 1)
    lax.fori_loop(0, pairs, pair, 0)

    @pl.when(left > 2 * pairs)
    def _():
        at = pl.ds(pl.multiple_of(left * TILE, TILE), TILE)
        rest(at, *own(at))


def mix(meta, ad, low, act, pre, win, wout, consts, tokp, buf_c, buf_d, n, taps):
    rows, width = ad.shape
    h = act.shape[1] // 2
    wq, hq = width // LANES, h // LANES
    return pl.pallas_call(
        functools.partial(mix_kernel, n, taps),
        in_specs=[smem()] + [vmem()] * 8 + [hbm()] * 2,
        out_specs=[vmem()] * 3,
        scratch_shapes=[pltpu.SMEM((n + 2,), jnp.int32),
                        pltpu.VMEM((width, 2 * h), BF), pltpu.VMEM((2 * h, width), BF),
                        pltpu.VMEM((2, 16, LANES), BF), pltpu.VMEM((1, 2 * h), F32),
                        pltpu.SemaphoreType.DMA((2, hq + wq + 1))],
        out_shape=[struct((rows, width), F32)] * 2 + [struct((rows, width), BF)],
        compiler_params=params(), cost_estimate=cost(0),
    )(meta, ad, low, act, pre, win, wout, consts, tokp, buf_c, buf_d)


def norm_grad_kernel(n, taps, rates, meta, tok, cot, branch, ag, nrm, inv, gbo, gbi, consts,
                     cgp, small_keep, small_send, offs, sums):
    s = pl.program_id(0)
    frames, width = tok.shape[1], tok.shape[2]
    half = taps // 2
    wq = width // LANES
    h = gbi.shape[1] // 2

    @pl.when(s == 0)
    def _():
        place_items(n, meta, offs)
        sums[...] = jnp.zeros_like(sums)

    item = meta[0] * n + s
    count = meta[2 + item]
    group = meta[2 + 2 * n + item]
    off = offs[s]
    scale = pick(consts.at[taps + 2:taps + 2 + rates], group)
    zero = jnp.zeros((8, LANES), F32)
    steps = pl.cdiv(count, CHUNK)
    wide = steps // 2

    def step(r0, size, accs):
        here = pl.ds(r0, size)
        live = (lax.broadcasted_iota(jnp.int32, (size, LANES), 0) + r0) < count
        src = pl.ds(pl.multiple_of(off + r0, 16), size)
        new = []
        ngs, nrs = [], []
        for q in range(wq):
            a_ls, a_sc, a_sh = accs[3 * q:3 * q + 3]
            br = jnp.where(live, branch[src, lane(q)], 0.0)
            g = jnp.where(live, ag[src, lane(q)], 0.0)
            nr = nrm[src, lane(q)].astype(F32)
            new += [a_ls + fold(cot[s, here, lane(q)].astype(F32) * br), a_sc + fold(g * nr), a_sh + fold(g)]
            ngs.append(g * scale[:, lane(q)])
            nrs.append(nr)
        cross = [a * b for a, b in zip(ngs, nrs)]
        m1 = jnp.sum(sum(ngs[1:], ngs[0]), axis=-1, keepdims=True) * (1.0 / width)
        m2 = jnp.sum(sum(cross[1:], cross[0]), axis=-1, keepdims=True) * (1.0 / width)
        istd = inv[src, :]
        for q in range(wq):
            cg = istd * (ngs[q] - m1 - nrs[q] * m2)
            cgp[s, q, pl.ds(pl.multiple_of(r0 + PAD, 8), size), :] = jnp.where(live, cg, 0.0)
        return tuple(new)

    def both_sizes(run, width_of_state, add):
        add(lax.fori_loop(0, wide, lambda i, accs: run(pl.multiple_of(i * 2 * CHUNK, 2 * CHUNK), 2 * CHUNK, accs),
                          (zero,) * width_of_state))

        @pl.when(steps > 2 * wide)
        def _():
            add(run(pl.multiple_of(wide * 2 * CHUNK, 2 * CHUNK), CHUNK, (zero,) * width_of_state))

    def add_norm(accs):
        for q in range(wq):
            sums[taps + 1, :, lane(q)] += accs[3 * q]
            sums[taps + 2 + group, :, lane(q)] += accs[3 * q + 1]
            sums[taps + 2 + rates + group, :, lane(q)] += accs[3 * q + 2]

    both_sizes(step, 3 * wq, add_norm)

    def clear(i, _):
        r0 = pl.multiple_of(i * CHUNK, CHUNK)
        for q in range(wq):
            cgp[s, q, pl.ds(pl.multiple_of(r0 + PAD, 8), CHUNK), :] = jnp.zeros((CHUNK, LANES), F32)
        return 0

    lax.fori_loop(steps, frames // CHUNK, clear, 0)
    for q in range(wq):
        cgp[s, q, :PAD, :] = jnp.zeros((PAD, LANES), F32)
        cgp[s, q, PAD + frames:, :] = jnp.zeros((cgp.shape[2] - PAD - frames, LANES), F32)

        def conv_step(r0, size, accs):
            here = pl.ds(r0, size)
            live = (lax.broadcasted_iota(jnp.int32, (size, LANES), 0) + r0) < count
            tk = jnp.where(live, tok[s, here, lane(q)].astype(F32), 0.0)
            new = []
            for k in range(taps):
                sh = cgp[s, q, pl.ds(r0 + (PAD + half - k), size), :]
                new.append(accs[k] + fold(tk * sh))
                if k == half:
                    new_bias = accs[taps] + fold(sh)
            return tuple(new) + (new_bias,)

        def add_conv(accs):
            for k in range(taps + 1):
                sums[k, :, lane(q)] += accs[k]

        both_sizes(conv_step, taps + 1, add_conv)

    @pl.when(s == n - 1)
    def _():
        last = taps + 2 + 2 * rates
        rows = [jnp.sum(sums[i], axis=0, keepdims=True) for i in range(last)]
        rows.append(jnp.sum(gbo[...], axis=0, keepdims=True))
        gb = jnp.sum(gbi[...], axis=0, keepdims=True)
        fill = jnp.zeros((1, width - h), F32)
        spare = [jnp.zeros((1, width), F32)] * (small_keep.shape[0] - last - 2)
        for side, dst in ((0, small_keep), (1, small_send)):
            tail = [jnp.concatenate([gb[:, side * h:(side + 1) * h], fill], axis=1)]
            dst[...] = jnp.concatenate(rows + tail + spare, axis=0)


def norm_grad(meta, tok, cot, branch, ag, nrm, inv, gbo, gbi, consts, taps, rates):
    n, frames, width = tok.shape
    wq = width // LANES
    n_small = -(-(taps + 4 + 2 * rates) // 8) * 8
    return pl.pallas_call(
        functools.partial(norm_grad_kernel, n, taps, rates), grid=(n,),
        in_specs=[smem()] + [vmem()] * 9, out_specs=[vmem()] * 3,
        scratch_shapes=[pltpu.SMEM((n + 2,), jnp.int32),
                        pltpu.VMEM((taps + 2 + 2 * rates, 8, width), F32)],
        out_shape=[struct((n, wq, frames + 4 * PAD, LANES), F32)] + [struct((n_small, width), F32)] * 2,
        compiler_params=params(), cost_estimate=cost(40000000),
    )(meta, tok, cot, branch, ag, nrm, inv, gbo, gbi, consts)


def place_out_kernel(n, meta, own, other, out, stage, sems):
    frames, width = stage.shape[1], stage.shape[2]
    copies = []
    for side, src in ((0, own), (1, other)):
        first = (meta[0] ^ side) * n
        off = jnp.int32(0)
        for j in range(n):
            count = meta[2 + first + j]
            for i in range(frames // CHUNK):
                live = (lax.broadcasted_iota(jnp.int32, (CHUNK, LANES), 0) + i * CHUNK) < count
                rows = pl.ds(pl.multiple_of(off + i * CHUNK, 16), CHUNK)
                for q in range(width // LANES):
                    value = jnp.where(live, src[rows, lane(q)].astype(F32), 0.0)
                    stage[side * n + j, i * CHUNK:(i + 1) * CHUNK, lane(q)] = value.astype(BF)
            copies.append(pltpu.make_async_copy(stage.at[side * n + j], out.at[first + j], sems.at[side * n + j]))
            copies[-1].start()
            off = off + ((count + 15) & -16)
    for c in copies:
        c.wait()


def place_out(meta, own, other, n, frames):
    width = own.shape[1]
    return pl.pallas_call(
        functools.partial(place_out_kernel, n),
        in_specs=[smem(), vmem(), vmem()], out_specs=hbm(), out_shape=struct((2 * n, frames, width), BF),
        scratch_shapes=[pltpu.VMEM((2 * n, frames, width), BF), pltpu.SemaphoreType.DMA((2 * n,))],
        compiler_params=params(), cost_estimate=cost(40000000),
    )(meta, own, other)


def token_grad_kernel(n, taps, meta, cot, cgp, consts, gtok, gtok_own, stage, sems):
    s = pl.program_id(0)
    frames, width = cot.shape[1], cot.shape[2]
    half = taps // 2
    wq = width // LANES
    count = meta[2 + meta[0] * n + s]
    w = consts[:taps, :]
    steps = pl.cdiv(count, CHUNK)

    def place(j):
        return pltpu.make_async_copy(stage.at[j], gtok.at[meta[0] * n + j], sems.at[j])

    def conv_step(i, _):
        r0 = pl.multiple_of(i * CHUNK, CHUNK)
        here = pl.ds(r0, CHUNK)
        live = (lax.broadcasted_iota(jnp.int32, (CHUNK, LANES), 0) + r0) < count
        for q in range(wq):
            total = cot[s, here, lane(q)].astype(F32)
            for k in range(taps):
                total = total + w[k:k + 1, lane(q)] * cgp[s, q, pl.ds(r0 + (PAD + half - k), CHUNK), :]
            total = jnp.where(live, total, 0.0).astype(BF)
            gtok_own[s, here, lane(q)] = total
            stage[s, here, lane(q)] = total.astype(F32)
        return 0

    lax.fori_loop(0, steps, conv_step, 0)

    def clear(i, _):
        here = pl.ds(pl.multiple_of(i * CHUNK, CHUNK), CHUNK)
        gtok_own[s, here, :] = jnp.zeros((CHUNK, width), BF)
        stage[s, here, :] = jnp.zeros((CHUNK, width), F32)
        return 0

    lax.fori_loop(steps, frames // CHUNK, clear, 0)
    place(s).start()

    @pl.when(s == n - 1)
    def _():
        for j in range(n):
            place(j).wait()


def token_grad(meta, cot, cgp, consts, taps):
    n, frames, width = cot.shape
    return pl.pallas_call(
        functools.partial(token_grad_kernel, n, taps), grid=(n,),
        in_specs=[smem()] + [vmem()] * 3, out_specs=[hbm(), vmem()],
        scratch_shapes=[pltpu.VMEM((n, frames, width), F32), pltpu.SemaphoreType.DMA((n,))],
        out_shape=[struct((2 * n, frames, width), F32), struct((n, frames, width), BF)],
        compiler_params=params(), cost_estimate=cost(40000000),
    )(meta, cot, cgp, consts)


def merge_gtok_kernel(n, meta, other, gtok_in, gtok, stage, sems):
    copies = [pltpu.make_async_copy(stage.at[j], gtok.at[(1 - meta[0]) * n + j], sems.at[j]) for j in range(n)]
    for j in range(n):
        stage[j] = other[j].astype(F32)
        copies[j].start()
    for c in copies:
        c.wait()


def merge_gtok(meta, other, gtok):
    n = other.shape[0]
    return pl.pallas_call(
        functools.partial(merge_gtok_kernel, n),
        in_specs=[smem(), vmem(), hbm()], out_specs=hbm(), out_shape=struct(gtok.shape, F32),
        scratch_shapes=[pltpu.VMEM(other.shape, F32), pltpu.SemaphoreType.DMA((n,))],
        input_output_aliases={2: 0},
        compiler_params=params(), cost_estimate=cost(20000000),
    )(meta, other, gtok)


def message_kernel(stay, keep, recv, *refs):
    pieces, (out, mine) = refs[:-2], refs[-2:]
    m = pieces[0].shape[0]
    total = stay[:m, :]
    for piece in pieces:
        total = total + piece[...].astype(F32)
    out[:m, :] = total.astype(BF)
    mine[...] = total.astype(BF)
    small = (keep[...] + recv[...]).astype(BF)
    rows = small.shape[0]
    for q in range(small.shape[1] // LANES):
        out[m + q * rows:m + (q + 1) * rows, :] = small[:, lane(q)]


def make_message(stay, keep, recv, pieces):
    rows = pieces[0].shape[0] + keep.size // LANES
    return pl.pallas_call(message_kernel, in_specs=[vmem()] * (3 + len(pieces)), out_specs=[vmem(), vmem()],
                          out_shape=[struct((rows, LANES), BF), struct(pieces[0].shape, BF)],
                          compiler_params=params())(stay, keep, recv, *pieces)


def relay_kernel(m, *refs):
    sources, out = refs[:-1], refs[-1]
    sums = []
    for d, src in enumerate(sources):
        if d > 1:
            out[(d - 2) * m:(d - 1) * m, :] = src[:m, :]
        sums.append(src[m:, :].astype(F32))
    while len(sums) > 1:
        sums = [a + b for a, b in zip(sums[::2], sums[1::2])]
    out[(len(sources) - 2) * m:, :] = sums[0].astype(BF)


def relay(m, sources):
    rows = (len(sources) - 2) * m + sources[0].shape[0] - m
    return pl.pallas_call(functools.partial(relay_kernel, m), in_specs=[vmem()] * len(sources), out_specs=vmem(),
                          out_shape=struct((rows, LANES), BF), compiler_params=params())(*sources)


def unpack_kernel(dp, taps, rates, meta, mine, theirs, near_1, far_1, near, far, gcw, gcb, gns, gnsh, gwi, gbi, gwo, gbo, gls, full):
    h, width = gwo.shape
    wq, hq = width // LANES, h // LANES
    m = full.shape[0] // dp
    for odd, early, others in ((0, (mine, near_1), near), (1, (theirs, far_1), far)):
        for d in range(dp // 2):
            piece = others[(d - 2) * m:(d - 1) * m, :] if d > 1 else early[d][:m, :]
            at = pl.multiple_of((meta[1] ^ (2 * d + odd)) * m, m)
            full[pl.ds(at, m), :] = piece.astype(F32)
    for q in range(wq):
        gwo[:, lane(q)] = full[q * h:(q + 1) * h, :]
    base = wq * h
    for q in range(hq):
        gwi[:, lane(q)] = full[base + q * width:base + (q + 1) * width, :]
    behind = (dp // 2 - 2) * m
    small = near[behind:, :].astype(F32) + far[behind:, :].astype(F32)
    rows = small.shape[0] // wq
    small = jnp.concatenate([small[q * rows:(q + 1) * rows] for q in range(wq)], axis=1)
    gcw[...] = small[:taps]
    gcb[...] = small[taps]
    gls[...] = small[taps + 1]
    gns[...] = small[taps + 2:taps + 2 + rates]
    gnsh[...] = small[taps + 2 + rates:taps + 2 + 2 * rates]
    at = taps + 2 + 2 * rates
    gbo[...] = small[at]
    gbi[...] = small[at + 1, :h]


def unpack(meta, mine, theirs, near_1, far_1, near, far, dp, taps, rates, width, h):
    shapes = [(taps, width), (width,), (rates, width), (rates, width), (width, h), (h,), (h, width), (width,), (width,)]
    return pl.pallas_call(
        functools.partial(unpack_kernel, dp, taps, rates), in_specs=[smem()] + [vmem()] * 6,
        out_shape=[struct(s, F32) for s in shapes],
        scratch_shapes=[pltpu.VMEM((2 * width * h // LANES, LANES), F32)],
        compiler_params=params())(meta, mine, theirs, near_1, far_1, near, far)


def swap(x, step):
    size = lax.axis_size("tp")
    return lax.ppermute(x, "tp", [(i, i ^ step) for i in range(size)])


def across(x, step):
    size = lax.axis_size("dp")
    return lax.ppermute(x, "dp", [(i, i ^ step) for i in range(size)])


def per_device(tokens, frame_counts, rate_groups, conv_weight, conv_bias, norm_scale, norm_shift,
               weight_in, bias_in, weight_out, bias_out, layer_scale, cotangent):
    width, h = weight_in.shape
    n = tokens.shape[0] // 2
    (tokens, cotangent, conv_weight, conv_bias, norm_scale, norm_shift, weight_in, bias_in, weight_out, bias_out,
     layer_scale, frame_counts, rate_groups) = [pltpu.with_memory_space_constraint(v, pltpu.HBM) for v in (
         tokens, cotangent, conv_weight, conv_bias, norm_scale, norm_shift, weight_in, bias_in, weight_out, bias_out,
         layer_scale, frame_counts, rate_groups)]
    taps, rates = conv_weight.shape[0], norm_scale.shape[0]
    dp = lax.axis_size("dp")
    buf_a = pack(weight_in, bias_in, weight_out)
    buf_b = swap(buf_a, 1)
    buf_c = swap(buf_a, 2)
    buf_d = swap(buf_c, 1)
    ad, nrm, low, inv, act, pre, win, wout, keep, send, gbo, gbi, tok, cot, consts, tokp, meta = front(
        frame_counts, rate_groups, tokens, cotangent, conv_weight, conv_bias, norm_scale, norm_shift, layer_scale, bias_out, buf_a, buf_b, h)
    stay, leave = combine(meta, keep, swap(send, 1), dp)
    arrived = across(leave, 1)
    branch, ag, out_own = mix(meta, ad, low, act, pre, win, wout, consts, tokp, buf_c, buf_d, n, taps)
    arrived, branch, out_own = lax.optimization_barrier((arrived, branch, out_own))
    out_b = swap(out_own, 1)
    stay = (stay + arrived.astype(F32)).reshape(dp // 2, -1, LANES)
    pieces = [across(stay[d].astype(BF), 2 * d) for d in range(1, dp // 2)]

    cgp, small_keep, small_send = norm_grad(meta, tok, cot, branch, ag, nrm, inv, gbo, gbi, consts, taps, rates)
    pieces, small_send, cgp, out_b = lax.optimization_barrier((pieces, small_send, cgp, out_b))
    small_got = swap(small_send, 1)
    message, mine = make_message(stay.reshape(-1, LANES), small_keep, small_got, pieces)
    message, mine, out_b = lax.optimization_barrier((message, mine, out_b))
    m = pieces[0].shape[0]
    near = [message] + [across(message, 2 * d) for d in range(1, dp // 2)]
    theirs = across(mine, 1)
    far_1 = across(message, 3)
    out = place_out(meta, out_own, out_b, n, tokens.shape[1])
    cgp, out = lax.optimization_barrier((cgp, out))
    gtok, gtok_own = token_grad(meta, cot, cgp, consts, taps)
    near, theirs, far_1, gtok_own = lax.optimization_barrier((near, theirs, far_1, gtok_own))
    late = relay(m, near)
    far = across(late, 1)
    gtok = merge_gtok(meta, swap(gtok_own, 1), gtok)
    far, gtok = lax.optimization_barrier((far, gtok))
    gcw, gcb, gns, gnsh, gwi, gbi, gwo, gbo, gls = unpack(meta, mine, theirs, near[1], far_1, late, far, dp, taps, rates,
                                                          width, h)
    return (out, gtok, gcw, gcb, gns, gnsh, gwi, gbi, gwo, gbo, gls)


def solution(mesh):
    items, copied = P("dp", None, None), P()
    in_specs = (items, P("dp"), P("dp"), copied, copied, copied, copied, P(None, "tp"), P("tp"), P("tp", None),
                copied, copied, items)
    out_specs = (items, items, copied, copied, copied, copied, P(None, "tp"), P("tp"), P("tp", None), copied, copied)
    return jax.shard_map(per_device, mesh=mesh, in_specs=in_specs, out_specs=out_specs, check_vma=False)
```

```python
import functools

import jax
import jax.numpy as jnp
from jax import lax
from jax.experimental import pallas as pl
from jax.experimental.pallas import tpu as pltpu
from jax.sharding import PartitionSpec as P

EPS = 1e-06
BF, F32 = jnp.bfloat16, jnp.float32
TILE = 256
LANES = 128
PAD = 8
CHUNK = 64
VMEM_LIMIT = 12 * 1024 * 1024


def params(**more):
    return pltpu.CompilerParams(vmem_limit_bytes=VMEM_LIMIT, **more)


def struct(shape, dtype):
    return jax.ShapeDtypeStruct(shape, dtype)


def whole(shape):
    return pl.BlockSpec(shape, lambda *_: (0,) * len(shape))


def hbm():
    return pl.BlockSpec(memory_space=pltpu.HBM)


def smem():
    return pl.BlockSpec(memory_space=pltpu.SMEM)


def cost(size):
    return pl.CostEstimate(flops=0, transcendentals=0, bytes_accessed=size)


def vmem():
    return pl.BlockSpec(memory_space=pltpu.VMEM)


def lane(q):
    return slice(q * LANES, (q + 1) * LANES)


def fold(x):
    return jnp.sum(x.reshape(x.shape[0] // 8, 8, x.shape[1]), axis=0)


def pick(table, group):
    rows = table[...].astype(F32)
    value = rows[0:1]
    for r in range(1, rows.shape[0]):
        value = jnp.where(group == r, rows[r:r + 1], value)
    return value


def as_row(ref):
    return ref[...].astype(F32).reshape(1, -1)


def gelu_parts(pre):
    scaled = pre * 0.7071067811865476
    cdf = 0.5 + 0.5 * lax.erf(scaled)
    density = jnp.exp(-(scaled * scaled)) * 0.3989422804014327
    return pre * cdf, cdf + pre * density


def dot(a, b):
    return jnp.dot(a, b, preferred_element_type=F32)


def dot_t(a, b):
    return lax.dot_general(a, b, (((1,), (1,)), ((), ())), preferred_element_type=F32)


def dot_rows(a, b):
    return lax.dot_general(a, b, (((0,), (0,)), ((), ())), preferred_element_type=F32)


def place_items(n, meta, offs):
    end = jnp.int32(0)
    for j in range(n):
        offs[j] = end
        end = end + ((meta[2 + meta[0] * n + j] + 15) & -16)
    offs[n] = end
    offs[n + 1] = (end + TILE - 1) // TILE


def pack_kernel(wi, bi, wo, out):
    width, h = wi.shape
    hq, wq = h // LANES, width // LANES
    for q in range(hq):
        out[q * width:(q + 1) * width, :] = wi[:, lane(q)]
    base = hq * width
    for q in range(wq):
        out[base + q * h:base + (q + 1) * h, :] = wo[:, lane(q)]
    base += wq * h
    bias = bi[...].astype(F32).reshape(1, h)
    rows = [bias[:, lane(q)] for q in range(hq)] + [jnp.zeros((1, LANES), F32)] * (16 - hq)
    out[base:base + 16, :] = jnp.concatenate(rows, axis=0).astype(BF)


def pack(wi, bi, wo):
    rows = 2 * wi.size // LANES + 16
    return pl.pallas_call(pack_kernel, out_shape=struct((rows, LANES), BF),
                          compiler_params=params())(wi, bi, wo)


def weight_copies(buf, side, win, wout, bias, sems):
    width, h = win.shape[0], win.shape[1] // 2
    hq, wq = h // LANES, width // LANES
    copies = []
    for q in range(hq):
        at = side * h + q * LANES
        copies.append((buf.at[pl.ds(q * width, width), :], win.at[:, pl.ds(at, LANES)]))
    base = hq * width
    for q in range(wq):
        copies.append((buf.at[pl.ds(base + q * h, h), :], wout.at[pl.ds(side * h, h), pl.ds(q * LANES, LANES)]))
    copies.append((buf.at[pl.ds(base + wq * h, 16), :], bias.at[side]))
    return [pltpu.make_async_copy(src, dst, sems.at[side, i]) for i, (src, dst) in enumerate(copies)]


def spread_bias(bias, row):
    hq = row.shape[1] // LANES // 2
    for side in range(2):
        for q in range(hq):
            at = side * hq + q
            row[:, lane(at)] = bias[side, q:q + 1, :].astype(F32)


def front_kernel(n, counts_hbm, groups_hbm, tok_hbm, cot_hbm, cw, cb, ns, nsh, gamma, bout, buf_a, buf_b,
                 ad, nrm, low, inv, act, pre, win, wout, keep, send, gbo, gbi, tok, cot, consts, tokp, meta,
                 offs, counts_s, groups_s, pad, ad_s, nrm_s, low_s, inv_s, bias, bias_row, dwo, dwi, sems, item_sems, meta_sems, packed_sem):
    s = pl.program_id(0)
    frames, width = tok.shape[1], tok.shape[2]
    taps, rates = cw.shape[0], ns.shape[0]
    half = taps // 2
    wq = width // LANES
    h = win.shape[1] // 2
    copies = weight_copies(buf_a, 0, win, wout, bias, sems) + weight_copies(buf_b, 1, win, wout, bias, sems)

    def fetch(j):
        at = (lax.axis_index("tp") & 1) * n + j
        return [pltpu.make_async_copy(src.at[at], dst.at[j], item_sems.at[i, j])
                for i, (src, dst) in enumerate(((tok_hbm, tok), (cot_hbm, cot)))]

    @pl.when(s == 0)
    def _():
        tables = [pltpu.make_async_copy(counts_hbm, counts_s, meta_sems.at[0]),
                  pltpu.make_async_copy(groups_hbm, groups_s, meta_sems.at[1])]
        for c in tables + fetch(0) + fetch(1):
            c.start()
        for c in copies:
            c.start()
        for j in range(2, n):
            for c in fetch(j):
                c.start()
        consts[...] = jnp.zeros_like(consts)
        consts[:taps, :] = cw[...].astype(F32)
        consts[taps:taps + 1, :] = as_row(gamma)
        consts[taps + 1:taps + 2, :] = as_row(bout)
        consts[taps + 2:taps + 2 + rates, :] = ns[...].astype(F32)
        offs[n + 2] = 0
        gbo[...] = jnp.zeros_like(gbo)
        pad[...] = jnp.zeros_like(pad)
        for stage in (ad_s, nrm_s, low_s, inv_s):
            stage[...] = jnp.zeros_like(stage)
        meta[0] = lax.axis_index("tp") & 1
        meta[1] = lax.axis_index("dp")
        for c in tables:
            c.wait()
        for j in range(2 * n):
            meta[2 + j] = counts_s[j]
            meta[2 + 2 * n + j] = groups_s[j]
        place_items(n, meta, offs)

    def flush(j):
        dst = pl.ds(pl.multiple_of(offs[j], 16), frames)
        for whole_ref, stage in ((ad, ad_s), (nrm, nrm_s), (low, low_s), (inv, inv_s)):
            whole_ref[dst, :] = stage[...]

    @pl.when(s > 0)
    def _():
        flush(s - 1)

    @pl.when(s == 1)
    def _():
        for c in copies:
            c.wait()
        spread_bias(bias, bias_row)
        dwo[...] = jnp.zeros_like(dwo)
        dwi[...] = jnp.zeros_like(dwi)
        gbi[...] = jnp.zeros_like(gbi)

    for c in fetch(s):
        c.wait()

    def fetch_packed(j):
        dst = pl.ds(pl.multiple_of(offs[j], 16), frames)
        return pltpu.make_async_copy(tok.at[j], tokp.at[dst, :], packed_sem)

    @pl.when(s > 1)
    def _():
        fetch_packed(s - 2).wait()

    @pl.when(s > 0)
    def _():
        fetch_packed(s - 1).start()

    item = meta[0] * n + s
    count = meta[2 + item]
    group = meta[2 + 2 * n + item]

    def setup():
        rows = lax.broadcasted_iota(jnp.int32, (frames, LANES), 0)
        for q in range(wq):
            pad[q, PAD:PAD + frames, :] = jnp.where(rows < count, tok[s, :, lane(q)].astype(F32), 0.0)
        return pick(ns, group), pick(nsh, group), as_row(gamma), as_row(cb), cw[...].astype(F32)

    def conv_step(i, acc, consts):
        scale, shift, gam, conv_bias, w = consts
        r0 = i * CHUNK if isinstance(i, int) else pl.multiple_of(i * CHUNK, CHUNK)
        here = pl.ds(r0, CHUNK)
        live = (lax.broadcasted_iota(jnp.int32, (CHUNK, LANES), 0) + r0) < count
        convs = []
        for q in range(wq):
            conv = conv_bias[:, lane(q)]
            for k in range(taps):
                conv = conv + w[k:k + 1, lane(q)] * pad[q, pl.ds(r0 + (PAD - half + k), CHUNK), :]
            convs.append(conv)
        mean = jnp.sum(sum(convs[1:], convs[0]), axis=-1, keepdims=True) * (1.0 / width)
        cents = [c - mean for c in convs]
        sq = [c * c for c in cents]
        var = jnp.sum(sum(sq[1:], sq[0]), axis=-1, keepdims=True) * (1.0 / width)
        istd = lax.rsqrt(var + EPS)
        inv_s[here, :] = jnp.broadcast_to(istd, (CHUNK, LANES))
        new = []
        for q in range(wq):
            normed = cents[q] * istd
            ad_s[here, lane(q)] = (normed * scale[:, lane(q)] + shift[:, lane(q)]).astype(BF)
            nrm_s[here, lane(q)] = normed.astype(BF)
            back = jnp.where(live, cot[s, here, lane(q)].astype(F32), 0.0) * gam[:, lane(q)]
            low_s[here, lane(q)] = back.astype(BF)
            new.append(acc[q] + fold(back))
        return tuple(new)

    def add_gbo(accs):
        for q in range(wq):
            gbo[:, lane(q)] += accs[q]

    def tile(t, size, between=()):
        between = list(between)
        at = pl.ds(pl.multiple_of(t * TILE, TILE), size)
        a, b = ad[at, :], low[at, :]
        activation, slope = gelu_parts(dot(a, win[...]) + bias_row[...])
        if between:
            between.pop(0)()
        grad = dot_t(b, wout[...]) * slope
        lo = activation.astype(BF)
        act[at, :] = lo
        if between:
            between.pop(0)()
        dwo[...] += dot_rows(lo, b)
        gbi[...] += fold(grad)
        g = grad.astype(BF)
        pre[at, :] = g
        if between:
            between.pop(0)()
        dwi[...] += dot_rows(a, g)
        if between:
            between.pop(0)()

    done = offs[n + 2]
    ready = offs[s] >= (done + 2) * TILE
    none = (jnp.zeros((8, LANES), F32),) * wq

    def conv_with(chunks, with_tile):
        consts = setup()
        state = [none]

        def part(lo_i, hi_i):
            def run():
                for i in range(lo_i, hi_i):
                    state[0] = conv_step(i, state[0], consts)
            return run

        cuts = [chunks * k // 4 for k in range(5)]
        parts = [part(cuts[k], cuts[k + 1]) for k in range(4)]
        if with_tile:
            tile(done, 2 * TILE, parts)
        else:
            for run in parts:
                run()
        add_gbo(state[0])
        if with_tile:
            offs[n + 2] = done + 2

    all_chunks = frames // CHUNK
    short = count <= (all_chunks - 1) * CHUNK
    for with_tile in (True, False):
        for chunks in (all_chunks - 1, all_chunks):
            fits = short if chunks < all_chunks else jnp.logical_not(short)
            pl.when((ready == with_tile) & fits)(functools.partial(conv_with, chunks, with_tile))

    @pl.when(s == n - 1)
    def _():
        flush(s)
        end = pl.ds(pl.multiple_of(offs[n], 16), TILE)
        ad[end, :] = jnp.zeros((TILE, width), BF)
        low[end, :] = jnp.zeros((TILE, width), BF)

        fetch_packed(n - 2).wait()
        fetch_packed(n - 1).start()

        start = offs[n + 2]
        left = offs[n + 1] - start
        pairs = lax.shift_right_arithmetic(left, 1)

        def rest(t, _):
            tile(start + 2 * t, 2 * TILE)
            return 0

        lax.fori_loop(0, pairs, rest, 0)

        @pl.when(left > 2 * pairs)
        def _():
            tile(offs[n + 1] - 1, TILE)

        fetch_packed(n - 1).wait()
        for side, dst in ((0, keep), (1, send)):
            for q in range(wq):
                dst[q * h:(q + 1) * h, :] = dwo[side * h:(side + 1) * h, lane(q)].astype(dst.dtype)
            base = wq * h
            for q in range(h // LANES):
                dst[base + q * width:base + (q + 1) * width, :] = dwi[:, lane(side * (h // LANES) + q)].astype(dst.dtype)


def front(counts, groups, tok, cot, cw, cb, ns, nsh, gamma, bout, buf_a, buf_b, h):
    items, frames, width = tok.shape
    n = items // 2
    rows = n * frames + TILE
    packed = 2 * width * h // LANES
    wq, hq = width // LANES, h // LANES
    n_consts = -(-(cw.shape[0] + 2 + ns.shape[0]) // 8) * 8
    return pl.pallas_call(
        functools.partial(front_kernel, n),
        grid_spec=pl.GridSpec(
            grid=(n,),
            in_specs=[hbm()] * 4 + [whole(v.shape) for v in (cw, cb, ns, nsh, gamma, bout)] + [hbm()] * 2,
            out_specs=[vmem()] * 16 + [smem()],
            scratch_shapes=[pltpu.SMEM((n + 3,), jnp.int32), pltpu.SMEM((items,), jnp.int32), pltpu.SMEM((items,), jnp.int32),
                            pltpu.VMEM((wq, frames + 4 * PAD, LANES), F32),
                            pltpu.VMEM((frames, width), BF), pltpu.VMEM((frames, width), BF),
                            pltpu.VMEM((frames, width), BF), pltpu.VMEM((frames, LANES), F32),
                            pltpu.VMEM((2, 16, LANES), BF), pltpu.VMEM((1, 2 * h), F32),
                            pltpu.VMEM((2 * h, width), F32), pltpu.VMEM((width, 2 * h), F32),
                            pltpu.SemaphoreType.DMA((2, hq + wq + 1)), pltpu.SemaphoreType.DMA((2, n)),
                            pltpu.SemaphoreType.DMA((2,)), pltpu.SemaphoreType.DMA]),
        out_shape=[struct((rows, width), BF)] * 3 + [struct((rows, LANES), F32)]
        + [struct((rows, 2 * h), BF)] * 2 + [struct((width, 2 * h), BF), struct((2 * h, width), BF)]
        + [struct((packed, LANES), F32), struct((packed, LANES), BF), struct((8, width), F32), struct((8, 2 * h), F32)]
        + [struct((n, frames, width), BF)] * 2 + [struct((n_consts, width), F32), struct((rows, width), BF), struct((2 + 2 * items,), jnp.int32)],
        compiler_params=params(), cost_estimate=cost(0),
    )(counts, groups, tok, cot, cw, cb, ns, nsh, gamma, bout, buf_a, buf_b)


def combine_kernel(dp, meta, keep, recv, stay, leave):
    m = keep.shape[0] // dp
    for d in range(dp):
        src = pl.ds(pl.multiple_of((meta[1] ^ d) * m, m), m)
        total = keep[src, :] + recv[src, :].astype(F32)
        dst = leave if d % 2 else stay
        dst[d // 2 * m:(d // 2 + 1) * m, :] = total.astype(dst.dtype)


def combine(meta, keep, recv, dp):
    rows = keep.shape[0] // 2
    return pl.pallas_call(
        functools.partial(combine_kernel, dp),
        in_specs=[smem(), vmem(), vmem()], out_specs=[vmem(), vmem()],
        out_shape=[struct((rows, LANES), F32), struct((rows, LANES), BF)],
        compiler_params=params())(meta, keep, recv)


def mix_kernel(n, taps, meta, ad, low, act, pre, win1, wout1, consts, tokp, buf_c, buf_d, branch, ag, out,
               offs, win2, wout2, bias, bias_row, sems):
    copies = weight_copies(buf_c, 0, win2, wout2, bias, sems) + weight_copies(buf_d, 1, win2, wout2, bias, sems)
    for c in copies:
        c.start()
    place_items(n, meta, offs)

    def own(at):
        return dot(act[at, :], wout1[...]), dot_t(pre[at, :], win1[...])

    def rest(at, own_branch, own_ag):
        a, b = ad[at, :], low[at, :]
        activation, slope = gelu_parts(dot(a, win2[...]) + bias_row[...])
        grad = dot_t(b, wout2[...]) * slope
        value = (own_branch + dot(activation.astype(BF), wout2[...])) + consts[taps + 1:taps + 2, :]
        branch[at, :] = value
        out[at, :] = (tokp[at, :].astype(F32) + consts[taps:taps + 1, :] * value).astype(BF)
        ag[at, :] = own_ag + dot_t(grad.astype(BF), win2[...])

    first = pl.ds(0, 2 * TILE)
    branch[first, :], ag[first, :] = own(first)
    for c in copies:
        c.wait()
    spread_bias(bias, bias_row)
    rest(first, branch[first, :], ag[first, :])

    def pair(t, _):
        at = pl.ds(pl.multiple_of((2 * t + 2) * TILE, TILE), 2 * TILE)
        rest(at, *own(at))
        return 0

    left = jnp.maximum(offs[n + 1] - 2, 0)
    pairs = lax.shift_right_arithmetic(left, 1)
    lax.fori_loop(0, pairs, pair, 0)

    @pl.when(left > 2 * pairs)
    def _():
        at = pl.ds(pl.multiple_of((left + 1) * TILE, TILE), TILE)
        rest(at, *own(at))


def mix(meta, ad, low, act, pre, win, wout, consts, tokp, buf_c, buf_d, n, taps):
    rows, width = ad.shape
    h = act.shape[1] // 2
    wq, hq = width // LANES, h // LANES
    return pl.pallas_call(
        functools.partial(mix_kernel, n, taps),
        in_specs=[smem()] + [vmem()] * 8 + [hbm()] * 2,
        out_specs=[vmem()] * 3,
        scratch_shapes=[pltpu.SMEM((n + 2,), jnp.int32),
                        pltpu.VMEM((width, 2 * h), BF), pltpu.VMEM((2 * h, width), BF),
                        pltpu.VMEM((2, 16, LANES), BF), pltpu.VMEM((1, 2 * h), F32),
                        pltpu.SemaphoreType.DMA((2, hq + wq + 1))],
        out_shape=[struct((rows, width), F32)] * 2 + [struct((rows, width), BF)],
        compiler_params=params(), cost_estimate=cost(0),
    )(meta, ad, low, act, pre, win, wout, consts, tokp, buf_c, buf_d)


def norm_grad_kernel(n, taps, rates, meta, tok, cot, branch, ag, nrm, inv, gbo, gbi, consts,
                     cgp, small_keep, small_send, offs, sums):
    s = pl.program_id(0)
    frames, width = tok.shape[1], tok.shape[2]
    half = taps // 2
    wq = width // LANES
    h = gbi.shape[1] // 2

    @pl.when(s == 0)
    def _():
        place_items(n, meta, offs)
        sums[...] = jnp.zeros_like(sums)

    item = meta[0] * n + s
    count = meta[2 + item]
    group = meta[2 + 2 * n + item]
    off = offs[s]
    scale = pick(consts.at[taps + 2:taps + 2 + rates], group)
    zero = jnp.zeros((8, LANES), F32)
    steps = pl.cdiv(count, CHUNK)
    wide = steps // 2

    def step(r0, size, accs):
        here = pl.ds(r0, size)
        live = (lax.broadcasted_iota(jnp.int32, (size, LANES), 0) + r0) < count
        src = pl.ds(pl.multiple_of(off + r0, 16), size)
        new = []
        ngs, nrs = [], []
        for q in range(wq):
            a_ls, a_sc, a_sh = accs[3 * q:3 * q + 3]
            br = jnp.where(live, branch[src, lane(q)], 0.0)
            g = jnp.where(live, ag[src, lane(q)], 0.0)
            nr = nrm[src, lane(q)].astype(F32)
            new += [a_ls + fold(cot[s, here, lane(q)].astype(F32) * br), a_sc + fold(g * nr), a_sh + fold(g)]
            ngs.append(g * scale[:, lane(q)])
            nrs.append(nr)
        cross = [a * b for a, b in zip(ngs, nrs)]
        m1 = jnp.sum(sum(ngs[1:], ngs[0]), axis=-1, keepdims=True) * (1.0 / width)
        m2 = jnp.sum(sum(cross[1:], cross[0]), axis=-1, keepdims=True) * (1.0 / width)
        istd = inv[src, :]
        for q in range(wq):
            cg = istd * (ngs[q] - m1 - nrs[q] * m2)
            cgp[s, q, pl.ds(pl.multiple_of(r0 + PAD, 8), size), :] = cg
        return tuple(new)

    def both_sizes(run, width_of_state, add):
        add(lax.fori_loop(0, wide, lambda i, accs: run(pl.multiple_of(i * 2 * CHUNK, 2 * CHUNK), 2 * CHUNK, accs),
                          (zero,) * width_of_state))

        @pl.when(steps > 2 * wide)
        def _():
            add(run(pl.multiple_of(wide * 2 * CHUNK, 2 * CHUNK), CHUNK, (zero,) * width_of_state))

    def add_norm(accs):
        for q in range(wq):
            sums[taps + 1, :, lane(q)] += accs[3 * q]
            sums[taps + 2 + group, :, lane(q)] += accs[3 * q + 1]
            sums[taps + 2 + rates + group, :, lane(q)] += accs[3 * q + 2]

    both_sizes(step, 3 * wq, add_norm)

    def clear(i, _):
        r0 = pl.multiple_of(i * CHUNK, CHUNK)
        for q in range(wq):
            cgp[s, q, pl.ds(pl.multiple_of(r0 + PAD, 8), CHUNK), :] = jnp.zeros((CHUNK, LANES), F32)
        return 0

    lax.fori_loop(steps, frames // CHUNK, clear, 0)
    for q in range(wq):
        cgp[s, q, :PAD, :] = jnp.zeros((PAD, LANES), F32)
        cgp[s, q, PAD + frames:, :] = jnp.zeros((cgp.shape[2] - PAD - frames, LANES), F32)

        def conv_step(r0, size, accs):
            here = pl.ds(r0, size)
            live = (lax.broadcasted_iota(jnp.int32, (size, LANES), 0) + r0) < count
            tk = jnp.where(live, tok[s, here, lane(q)].astype(F32), 0.0)
            new = []
            for k in range(taps):
                sh = cgp[s, q, pl.ds(r0 + (PAD + half - k), size), :]
                new.append(accs[k] + fold(tk * sh))
                if k == half:
                    new_bias = accs[taps] + fold(sh)
            return tuple(new) + (new_bias,)

        def add_conv(accs):
            for k in range(taps + 1):
                sums[k, :, lane(q)] += accs[k]

        both_sizes(conv_step, taps + 1, add_conv)

    @pl.when(s == n - 1)
    def _():
        last = taps + 2 + 2 * rates
        rows = [jnp.sum(sums[i], axis=0, keepdims=True) for i in range(last)]
        rows.append(jnp.sum(gbo[...], axis=0, keepdims=True))
        gb = jnp.sum(gbi[...], axis=0, keepdims=True)
        fill = jnp.zeros((1, width - h), F32)
        spare = [jnp.zeros((1, width), F32)] * (small_keep.shape[0] - last - 2)
        for side, dst in ((0, small_keep), (1, small_send)):
            tail = [jnp.concatenate([gb[:, side * h:(side + 1) * h], fill], axis=1)]
            dst[...] = jnp.concatenate(rows + tail + spare, axis=0)


def norm_grad(meta, tok, cot, branch, ag, nrm, inv, gbo, gbi, consts, taps, rates):
    n, frames, width = tok.shape
    wq = width // LANES
    n_small = -(-(taps + 4 + 2 * rates) // 8) * 8
    return pl.pallas_call(
        functools.partial(norm_grad_kernel, n, taps, rates), grid=(n,),
        in_specs=[smem()] + [vmem()] * 9, out_specs=[vmem()] * 3,
        scratch_shapes=[pltpu.SMEM((n + 2,), jnp.int32),
                        pltpu.VMEM((taps + 2 + 2 * rates, 8, width), F32)],
        out_shape=[struct((n, wq, frames + 4 * PAD, LANES), F32)] + [struct((n_small, width), F32)] * 2,
        compiler_params=params(), cost_estimate=cost(40000000),
    )(meta, tok, cot, branch, ag, nrm, inv, gbo, gbi, consts)


def place_out_kernel(n, meta, own, other, out, stage, sems):
    frames, width = stage.shape[1], stage.shape[2]
    copies = []
    for side, src in ((0, own), (1, other)):
        first = (meta[0] ^ side) * n
        off = jnp.int32(0)
        for j in range(n):
            count = meta[2 + first + j]
            for i in range(frames // CHUNK):
                live = (lax.broadcasted_iota(jnp.int32, (CHUNK, LANES), 0) + i * CHUNK) < count
                rows = pl.ds(pl.multiple_of(off + i * CHUNK, 16), CHUNK)
                for q in range(width // LANES):
                    value = jnp.where(live, src[rows, lane(q)].astype(F32), 0.0)
                    stage[side * n + j, i * CHUNK:(i + 1) * CHUNK, lane(q)] = value.astype(BF)
            copies.append(pltpu.make_async_copy(stage.at[side * n + j], out.at[first + j], sems.at[side * n + j]))
            copies[-1].start()
            off = off + ((count + 15) & -16)
    for c in copies:
        c.wait()


def place_out(meta, own, other, n, frames):
    width = own.shape[1]
    return pl.pallas_call(
        functools.partial(place_out_kernel, n),
        in_specs=[smem(), vmem(), vmem()], out_specs=hbm(), out_shape=struct((2 * n, frames, width), BF),
        scratch_shapes=[pltpu.VMEM((2 * n, frames, width), BF), pltpu.SemaphoreType.DMA((2 * n,))],
        compiler_params=params(), cost_estimate=cost(40000000),
    )(meta, own, other)


def token_grad_kernel(n, taps, meta, cot, cgp, consts, gtok, gtok_own, stage, sems):
    s = pl.program_id(0)
    frames, width = cot.shape[1], cot.shape[2]
    half = taps // 2
    wq = width // LANES
    count = meta[2 + meta[0] * n + s]
    w = consts[:taps, :]
    steps = pl.cdiv(count, CHUNK)

    def place(j):
        return pltpu.make_async_copy(stage.at[j], gtok.at[meta[0] * n + j], sems.at[j])

    def conv_step(i, _):
        r0 = pl.multiple_of(i * CHUNK, CHUNK)
        here = pl.ds(r0, CHUNK)
        live = (lax.broadcasted_iota(jnp.int32, (CHUNK, LANES), 0) + r0) < count
        for q in range(wq):
            total = cot[s, here, lane(q)].astype(F32)
            for k in range(taps):
                total = total + w[k:k + 1, lane(q)] * cgp[s, q, pl.ds(r0 + (PAD + half - k), CHUNK), :]
            total = jnp.where(live, total, 0.0).astype(BF)
            gtok_own[s, here, lane(q)] = total
            stage[s, here, lane(q)] = total.astype(F32)
        return 0

    lax.fori_loop(0, steps, conv_step, 0)

    def clear(i, _):
        here = pl.ds(pl.multiple_of(i * CHUNK, CHUNK), CHUNK)
        gtok_own[s, here, :] = jnp.zeros((CHUNK, width), BF)
        stage[s, here, :] = jnp.zeros((CHUNK, width), F32)
        return 0

    lax.fori_loop(steps, frames // CHUNK, clear, 0)
    place(s).start()

    @pl.when(s == n - 1)
    def _():
        for j in range(n):
            place(j).wait()


def token_grad(meta, cot, cgp, consts, taps):
    n, frames, width = cot.shape
    return pl.pallas_call(
        functools.partial(token_grad_kernel, n, taps), grid=(n,),
        in_specs=[smem()] + [vmem()] * 3, out_specs=[hbm(), vmem()],
        scratch_shapes=[pltpu.VMEM((n, frames, width), F32), pltpu.SemaphoreType.DMA((n,))],
        out_shape=[struct((2 * n, frames, width), F32), struct((n, frames, width), BF)],
        compiler_params=params(), cost_estimate=cost(40000000),
    )(meta, cot, cgp, consts)


def merge_gtok_kernel(n, meta, other, gtok_in, gtok, stage, sems):
    copies = [pltpu.make_async_copy(stage.at[j], gtok.at[(1 - meta[0]) * n + j], sems.at[j]) for j in range(n)]
    for j in range(n):
        stage[j] = other[j].astype(F32)
        copies[j].start()
    for c in copies:
        c.wait()


def merge_gtok(meta, other, gtok):
    n = other.shape[0]
    return pl.pallas_call(
        functools.partial(merge_gtok_kernel, n),
        in_specs=[smem(), vmem(), hbm()], out_specs=hbm(), out_shape=struct(gtok.shape, F32),
        scratch_shapes=[pltpu.VMEM(other.shape, F32), pltpu.SemaphoreType.DMA((n,))],
        input_output_aliases={2: 0},
        compiler_params=params(), cost_estimate=cost(20000000),
    )(meta, other, gtok)


def message_kernel(stay, keep, recv, *refs):
    pieces, (out, mine) = refs[:-2], refs[-2:]
    m = pieces[0].shape[0]
    total = stay[:m, :]
    for piece in pieces:
        total = total + piece[...].astype(F32)
    out[:m, :] = total.astype(BF)
    mine[...] = total.astype(BF)
    small = (keep[...] + recv[...]).astype(BF)
    rows = small.shape[0]
    for q in range(small.shape[1] // LANES):
        out[m + q * rows:m + (q + 1) * rows, :] = small[:, lane(q)]


def make_message(stay, keep, recv, pieces):
    rows = pieces[0].shape[0] + keep.size // LANES
    return pl.pallas_call(message_kernel, in_specs=[vmem()] * (3 + len(pieces)), out_specs=[vmem(), vmem()],
                          out_shape=[struct((rows, LANES), BF), struct(pieces[0].shape, BF)],
                          compiler_params=params())(stay, keep, recv, *pieces)


def relay_kernel(m, *refs):
    sources, out = refs[:-1], refs[-1]
    sums = []
    for d, src in enumerate(sources):
        if d > 1:
            out[(d - 2) * m:(d - 1) * m, :] = src[:m, :]
        sums.append(src[m:, :].astype(F32))
    while len(sums) > 1:
        sums = [a + b for a, b in zip(sums[::2], sums[1::2])]
    out[(len(sources) - 2) * m:, :] = sums[0].astype(BF)


def relay(m, sources):
    rows = (len(sources) - 2) * m + sources[0].shape[0] - m
    return pl.pallas_call(functools.partial(relay_kernel, m), in_specs=[vmem()] * len(sources), out_specs=vmem(),
                          out_shape=struct((rows, LANES), BF), compiler_params=params())(*sources)


def unpack_kernel(dp, taps, rates, meta, mine, theirs, near_1, far_1, near, far, gcw, gcb, gns, gnsh, gwi, gbi, gwo, gbo, gls, full):
    h, width = gwo.shape
    wq, hq = width // LANES, h // LANES
    m = full.shape[0] // dp
    for odd, early, others in ((0, (mine, near_1), near), (1, (theirs, far_1), far)):
        for d in range(dp // 2):
            piece = others[(d - 2) * m:(d - 1) * m, :] if d > 1 else early[d][:m, :]
            at = pl.multiple_of((meta[1] ^ (2 * d + odd)) * m, m)
            full[pl.ds(at, m), :] = piece.astype(F32)
    for q in range(wq):
        gwo[:, lane(q)] = full[q * h:(q + 1) * h, :]
    base = wq * h
    for q in range(hq):
        gwi[:, lane(q)] = full[base + q * width:base + (q + 1) * width, :]
    behind = (dp // 2 - 2) * m
    small = near[behind:, :].astype(F32) + far[behind:, :].astype(F32)
    rows = small.shape[0] // wq
    small = jnp.concatenate([small[q * rows:(q + 1) * rows] for q in range(wq)], axis=1)
    gcw[...] = small[:taps]
    gcb[...] = small[taps]
    gls[...] = small[taps + 1]
    gns[...] = small[taps + 2:taps + 2 + rates]
    gnsh[...] = small[taps + 2 + rates:taps + 2 + 2 * rates]
    at = taps + 2 + 2 * rates
    gbo[...] = small[at]
    gbi[...] = small[at + 1, :h]


def unpack(meta, mine, theirs, near_1, far_1, near, far, dp, taps, rates, width, h):
    shapes = [(taps, width), (width,), (rates, width), (rates, width), (width, h), (h,), (h, width), (width,), (width,)]
    return pl.pallas_call(
        functools.partial(unpack_kernel, dp, taps, rates), in_specs=[smem()] + [vmem()] * 6,
        out_shape=[struct(s, F32) for s in shapes],
        scratch_shapes=[pltpu.VMEM((2 * width * h // LANES, LANES), F32)],
        compiler_params=params())(meta, mine, theirs, near_1, far_1, near, far)


def swap(x, step):
    size = lax.axis_size("tp")
    return lax.ppermute(x, "tp", [(i, i ^ step) for i in range(size)])


def across(x, step):
    size = lax.axis_size("dp")
    return lax.ppermute(x, "dp", [(i, i ^ step) for i in range(size)])


def per_device(tokens, frame_counts, rate_groups, conv_weight, conv_bias, norm_scale, norm_shift,
               weight_in, bias_in, weight_out, bias_out, layer_scale, cotangent):
    width, h = weight_in.shape
    n = tokens.shape[0] // 2
    (tokens, cotangent, conv_weight, conv_bias, norm_scale, norm_shift, weight_in, bias_in, weight_out, bias_out,
     layer_scale, frame_counts, rate_groups) = [pltpu.with_memory_space_constraint(v, pltpu.HBM) for v in (
         tokens, cotangent, conv_weight, conv_bias, norm_scale, norm_shift, weight_in, bias_in, weight_out, bias_out,
         layer_scale, frame_counts, rate_groups)]
    taps, rates = conv_weight.shape[0], norm_scale.shape[0]
    dp = lax.axis_size("dp")
    buf_a = pack(weight_in, bias_in, weight_out)
    buf_b = swap(buf_a, 1)
    buf_c = swap(buf_a, 2)
    buf_d = swap(buf_c, 1)
    ad, nrm, low, inv, act, pre, win, wout, keep, send, gbo, gbi, tok, cot, consts, tokp, meta = front(
        frame_counts, rate_groups, tokens, cotangent, conv_weight, conv_bias, norm_scale, norm_shift, layer_scale, bias_out, buf_a, buf_b, h)
    stay, leave = combine(meta, keep, swap(send, 1), dp)
    arrived = across(leave, 1)
    branch, ag, out_own = mix(meta, ad, low, act, pre, win, wout, consts, tokp, buf_c, buf_d, n, taps)
    arrived, branch, out_own = lax.optimization_barrier((arrived, branch, out_own))
    out_b = swap(out_own, 1)
    stay = (stay + arrived.astype(F32)).reshape(dp // 2, -1, LANES)
    pieces = [across(stay[d].astype(BF), 2 * d) for d in range(1, dp // 2)]

    cgp, small_keep, small_send = norm_grad(meta, tok, cot, branch, ag, nrm, inv, gbo, gbi, consts, taps, rates)
    pieces, small_send, cgp, out_b = lax.optimization_barrier((pieces, small_send, cgp, out_b))
    small_got = swap(small_send, 1)
    message, mine = make_message(stay.reshape(-1, LANES), small_keep, small_got, pieces)
    message, mine, out_b = lax.optimization_barrier((message, mine, out_b))
    m = pieces[0].shape[0]
    near = [message] + [across(message, 2 * d) for d in range(1, dp // 2)]
    theirs = across(mine, 1)
    far_1 = across(message, 3)
    out = place_out(meta, out_own, out_b, n, tokens.shape[1])
    cgp, out = lax.optimization_barrier((cgp, out))
    gtok, gtok_own = token_grad(meta, cot, cgp, consts, taps)
    near, theirs, far_1, gtok_own = lax.optimization_barrier((near, theirs, far_1, gtok_own))
    late = relay(m, near)
    far = across(late, 1)
    gtok = merge_gtok(meta, swap(gtok_own, 1), gtok)
    far, gtok = lax.optimization_barrier((far, gtok))
    gcw, gcb, gns, gnsh, gwi, gbi, gwo, gbo, gls = unpack(meta, mine, theirs, near[1], far_1, late, far, dp, taps, rates,
                                                          width, h)
    return (out, gtok, gcw, gcb, gns, gnsh, gwi, gbi, gwo, gbo, gls)


def solution(mesh):
    items, copied = P("dp", None, None), P()
    in_specs = (items, P("dp"), P("dp"), copied, copied, copied, copied, P(None, "tp"), P("tp"), P("tp", None),
                copied, copied, items)
    out_specs = (items, items, copied, copied, copied, copied, P(None, "tp"), P("tp"), P("tp", None), copied, copied)
    return jax.shard_map(per_device, mesh=mesh, in_specs=in_specs, out_specs=out_specs, check_vma=False)
```

```python
import functools

import jax
import jax.numpy as jnp
from jax import lax
from jax.experimental import pallas as pl
from jax.experimental.pallas import tpu as pltpu
from jax.sharding import PartitionSpec as P

EPS = 1e-06
BF, F32 = jnp.bfloat16, jnp.float32
TILE = 256
LANES = 128
PAD = 8
CHUNK = 64
FRONT_CHUNK = 32
VMEM_LIMIT = 12 * 1024 * 1024


def params(**more):
    return pltpu.CompilerParams(vmem_limit_bytes=VMEM_LIMIT, **more)


def struct(shape, dtype):
    return jax.ShapeDtypeStruct(shape, dtype)


def whole(shape):
    return pl.BlockSpec(shape, lambda *_: (0,) * len(shape))


def hbm():
    return pl.BlockSpec(memory_space=pltpu.HBM)


def smem():
    return pl.BlockSpec(memory_space=pltpu.SMEM)


def cost(size):
    return pl.CostEstimate(flops=0, transcendentals=0, bytes_accessed=size)


def vmem():
    return pl.BlockSpec(memory_space=pltpu.VMEM)


def lane(q):
    return slice(q * LANES, (q + 1) * LANES)


def fold(x):
    return jnp.sum(x.reshape(x.shape[0] // 8, 8, x.shape[1]), axis=0)


def pick(table, group):
    rows = table[...].astype(F32)
    value = rows[0:1]
    for r in range(1, rows.shape[0]):
        value = jnp.where(group == r, rows[r:r + 1], value)
    return value


def as_row(ref):
    return ref[...].astype(F32).reshape(1, -1)


def gelu_parts(pre):
    cdf = 0.5 + 0.5 * lax.erf(pre * 0.7071067811865476)
    density = jnp.exp(-0.5 * pre * pre) * 0.3989422804014327
    return pre * cdf, cdf + pre * density


def dot(a, b):
    return jnp.dot(a, b, preferred_element_type=F32)


def dot_t(a, b):
    return lax.dot_general(a, b, (((1,), (1,)), ((), ())), preferred_element_type=F32)


def dot_rows(a, b):
    return lax.dot_general(a, b, (((0,), (0,)), ((), ())), preferred_element_type=F32)


def place_items(n, meta, offs):
    end = jnp.int32(0)
    for j in range(n):
        offs[j] = end
        end = end + ((meta[2 + meta[0] * n + j] + 15) & -16)
    offs[n] = end
    offs[n + 1] = (end + TILE - 1) // TILE


def pack_kernel(wi, bi, wo, out):
    width, h = wi.shape
    hq, wq = h // LANES, width // LANES
    for q in range(hq):
        out[q * width:(q + 1) * width, :] = wi[:, lane(q)]
    base = hq * width
    for q in range(wq):
        out[base + q * h:base + (q + 1) * h, :] = wo[:, lane(q)]
    base += wq * h
    bias = bi[...].astype(F32).reshape(1, h)
    rows = [bias[:, lane(q)] for q in range(hq)] + [jnp.zeros((1, LANES), F32)] * (16 - hq)
    out[base:base + 16, :] = jnp.concatenate(rows, axis=0).astype(BF)


def pack(wi, bi, wo):
    rows = 2 * wi.size // LANES + 16
    return pl.pallas_call(pack_kernel, out_shape=struct((rows, LANES), BF),
                          compiler_params=params())(wi, bi, wo)


def weight_copies(buf, side, win, wout, bias, sems):
    width, h = win.shape[0], win.shape[1] // 2
    hq, wq = h // LANES, width // LANES
    copies = []
    for q in range(hq):
        at = side * h + q * LANES
        copies.append((buf.at[pl.ds(q * width, width), :], win.at[:, pl.ds(at, LANES)]))
    base = hq * width
    for q in range(wq):
        copies.append((buf.at[pl.ds(base + q * h, h), :], wout.at[pl.ds(side * h, h), pl.ds(q * LANES, LANES)]))
    copies.append((buf.at[pl.ds(base + wq * h, 16), :], bias.at[side]))
    return [pltpu.make_async_copy(src, dst, sems.at[side, i]) for i, (src, dst) in enumerate(copies)]


def spread_bias(bias, row):
    hq = row.shape[1] // LANES // 2
    for side in range(2):
        for q in range(hq):
            at = side * hq + q
            row[:, lane(at)] = bias[side, q:q + 1, :].astype(F32)


def front_kernel(n, counts_hbm, groups_hbm, tok_hbm, cot_hbm, cw, cb, ns, nsh, gamma, bout, buf_a, buf_b,
                 ad, nrm, low, inv, act, pre, win, wout, keep, send, gbo, gbi, tok, cot, consts, tokp, meta,
                 offs, counts_s, groups_s, pad, ad_s, nrm_s, low_s, inv_s, bias, bias_row, dwo, dwi, sems, item_sems, meta_sems, packed_sem):
    s = pl.program_id(0)
    frames, width = tok.shape[1], tok.shape[2]
    taps, rates = cw.shape[0], ns.shape[0]
    half = taps // 2
    wq = width // LANES
    h = win.shape[1] // 2
    copies = weight_copies(buf_a, 0, win, wout, bias, sems) + weight_copies(buf_b, 1, win, wout, bias, sems)

    def fetch(j):
        at = (lax.axis_index("tp") & 1) * n + j
        return [pltpu.make_async_copy(src.at[at], dst.at[j], item_sems.at[i, j])
                for i, (src, dst) in enumerate(((tok_hbm, tok), (cot_hbm, cot)))]

    @pl.when(s == 0)
    def _():
        tables = [pltpu.make_async_copy(counts_hbm, counts_s, meta_sems.at[0]),
                  pltpu.make_async_copy(groups_hbm, groups_s, meta_sems.at[1])]
        for c in tables + fetch(0) + fetch(1):
            c.start()
        for c in copies:
            c.start()
        for j in range(2, n):
            for c in fetch(j):
                c.start()
        consts[...] = jnp.zeros_like(consts)
        consts[:taps, :] = cw[...].astype(F32)
        consts[taps:taps + 1, :] = as_row(gamma)
        consts[taps + 1:taps + 2, :] = as_row(bout)
        consts[taps + 2:taps + 2 + rates, :] = ns[...].astype(F32)
        offs[n + 2] = 0
        gbo[...] = jnp.zeros_like(gbo)
        pad[...] = jnp.zeros_like(pad)
        for stage in (ad_s, nrm_s, low_s, inv_s):
            stage[...] = jnp.zeros_like(stage)
        meta[0] = lax.axis_index("tp") & 1
        meta[1] = lax.axis_index("dp")
        for c in tables:
            c.wait()
        for j in range(2 * n):
            meta[2 + j] = counts_s[j]
            meta[2 + 2 * n + j] = groups_s[j]
        place_items(n, meta, offs)

    def flush(j):
        dst = pl.ds(pl.multiple_of(offs[j], 16), frames)
        for whole_ref, stage in ((ad, ad_s), (nrm, nrm_s), (low, low_s), (inv, inv_s)):
            whole_ref[dst, :] = stage[...]

    @pl.when(s > 0)
    def _():
        flush(s - 1)

    @pl.when(s == 1)
    def _():
        for c in copies:
            c.wait()
        spread_bias(bias, bias_row)
        dwo[...] = jnp.zeros_like(dwo)
        dwi[...] = jnp.zeros_like(dwi)
        gbi[...] = jnp.zeros_like(gbi)

    for c in fetch(s):
        c.wait()

    def fetch_packed(j):
        dst = pl.ds(pl.multiple_of(offs[j], 16), frames)
        return pltpu.make_async_copy(tok.at[j], tokp.at[dst, :], packed_sem)

    @pl.when(s > 1)
    def _():
        fetch_packed(s - 2).wait()

    @pl.when(s > 0)
    def _():
        fetch_packed(s - 1).start()

    item = meta[0] * n + s
    count = meta[2 + item]
    group = meta[2 + 2 * n + item]

    def setup():
        rows = lax.broadcasted_iota(jnp.int32, (frames, LANES), 0)
        for q in range(wq):
            pad[q, PAD:PAD + frames, :] = jnp.where(rows < count, tok[s, :, lane(q)].astype(F32), 0.0)
        return pick(ns, group), pick(nsh, group), as_row(gamma), as_row(cb), cw[...].astype(F32)

    def conv_step(i, acc, consts):
        scale, shift, gam, conv_bias, w = consts
        r0 = i * FRONT_CHUNK if isinstance(i, int) else pl.multiple_of(i * FRONT_CHUNK, FRONT_CHUNK)
        here = pl.ds(r0, FRONT_CHUNK)
        live = (lax.broadcasted_iota(jnp.int32, (FRONT_CHUNK, LANES), 0) + r0) < count
        convs = []
        for q in range(wq):
            conv = conv_bias[:, lane(q)]
            for k in range(taps):
                conv = conv + w[k:k + 1, lane(q)] * pad[q, pl.ds(r0 + (PAD - half + k), FRONT_CHUNK), :]
            convs.append(conv)
        mean = jnp.sum(sum(convs[1:], convs[0]), axis=-1, keepdims=True) * (1.0 / width)
        cents = [c - mean for c in convs]
        sq = [c * c for c in cents]
        var = jnp.sum(sum(sq[1:], sq[0]), axis=-1, keepdims=True) * (1.0 / width)
        istd = lax.rsqrt(var + EPS)
        inv_s[here, :] = jnp.broadcast_to(istd, (FRONT_CHUNK, LANES))
        new = []
        for q in range(wq):
            normed = cents[q] * istd
            ad_s[here, lane(q)] = (normed * scale[:, lane(q)] + shift[:, lane(q)]).astype(BF)
            nrm_s[here, lane(q)] = normed.astype(BF)
            back = jnp.where(live, cot[s, here, lane(q)].astype(F32), 0.0) * gam[:, lane(q)]
            low_s[here, lane(q)] = back.astype(BF)
            new.append(acc[q] + fold(back))
        return tuple(new)

    def add_gbo(accs):
        for q in range(wq):
            gbo[:, lane(q)] += accs[q]

    def tile(t, size, between=()):
        between = list(between)
        at = pl.ds(pl.multiple_of(t * TILE, TILE), size)
        a, b = ad[at, :], low[at, :]
        activation, slope = gelu_parts(dot(a, win[...]) + bias_row[...])
        if between:
            between.pop(0)()
        grad = dot_t(b, wout[...]) * slope
        lo = activation.astype(BF)
        act[at, :] = lo
        if between:
            between.pop(0)()
        dwo[...] += dot_rows(lo, b)
        gbi[...] += fold(grad)
        g = grad.astype(BF)
        pre[at, :] = g
        if between:
            between.pop(0)()
        dwi[...] += dot_rows(a, g)
        if between:
            between.pop(0)()

    done = offs[n + 2]
    ready = offs[s] >= (done + 2) * TILE
    none = (jnp.zeros((8, LANES), F32),) * wq

    def conv_with(chunks, with_tile):
        consts = setup()
        state = [none]

        def part(lo_i, hi_i):
            def run():
                for i in range(lo_i, hi_i):
                    state[0] = conv_step(i, state[0], consts)
            return run

        cuts = [chunks * k // 4 for k in range(5)]
        parts = [part(cuts[k], cuts[k + 1]) for k in range(4)]
        if with_tile:
            tile(done, 2 * TILE, parts)
        else:
            for run in parts:
                run()
        add_gbo(state[0])
        if with_tile:
            offs[n + 2] = done + 2

    all_chunks = frames // FRONT_CHUNK
    short = count <= (all_chunks * 3 // 4) * FRONT_CHUNK
    for with_tile in (True, False):
        for chunks in (all_chunks * 3 // 4, all_chunks):
            fits = short if chunks < all_chunks else jnp.logical_not(short)
            pl.when((ready == with_tile) & fits)(functools.partial(conv_with, chunks, with_tile))

    @pl.when(s == n - 1)
    def _():
        flush(s)
        end = pl.ds(pl.multiple_of(offs[n], 16), TILE)
        ad[end, :] = jnp.zeros((TILE, width), BF)
        low[end, :] = jnp.zeros((TILE, width), BF)

        fetch_packed(n - 2).wait()
        fetch_packed(n - 1).start()

        start = offs[n + 2]
        left = offs[n + 1] - start
        pairs = lax.shift_right_arithmetic(left, 1)

        def rest(t, _):
            tile(start + 2 * t, 2 * TILE)
            return 0

        lax.fori_loop(0, pairs, rest, 0)

        @pl.when(left > 2 * pairs)
        def _():
            tile(offs[n + 1] - 1, TILE)

        fetch_packed(n - 1).wait()
        for side, dst in ((0, keep), (1, send)):
            for q in range(wq):
                dst[q * h:(q + 1) * h, :] = dwo[side * h:(side + 1) * h, lane(q)].astype(dst.dtype)
            base = wq * h
            for q in range(h // LANES):
                dst[base + q * width:base + (q + 1) * width, :] = dwi[:, lane(side * (h // LANES) + q)].astype(dst.dtype)


def front(counts, groups, tok, cot, cw, cb, ns, nsh, gamma, bout, buf_a, buf_b, h):
    items, frames, width = tok.shape
    n = items // 2
    rows = n * frames + TILE
    packed = 2 * width * h // LANES
    wq, hq = width // LANES, h // LANES
    n_consts = -(-(cw.shape[0] + 2 + ns.shape[0]) // 8) * 8
    return pl.pallas_call(
        functools.partial(front_kernel, n),
        grid_spec=pl.GridSpec(
            grid=(n,),
            in_specs=[hbm()] * 4 + [whole(v.shape) for v in (cw, cb, ns, nsh, gamma, bout)] + [hbm()] * 2,
            out_specs=[vmem()] * 16 + [smem()],
            scratch_shapes=[pltpu.SMEM((n + 3,), jnp.int32), pltpu.SMEM((items,), jnp.int32), pltpu.SMEM((items,), jnp.int32),
                            pltpu.VMEM((wq, frames + 4 * PAD, LANES), F32),
                            pltpu.VMEM((frames, width), BF), pltpu.VMEM((frames, width), BF),
                            pltpu.VMEM((frames, width), BF), pltpu.VMEM((frames, LANES), F32),
                            pltpu.VMEM((2, 16, LANES), BF), pltpu.VMEM((1, 2 * h), F32),
                            pltpu.VMEM((2 * h, width), F32), pltpu.VMEM((width, 2 * h), F32),
                            pltpu.SemaphoreType.DMA((2, hq + wq + 1)), pltpu.SemaphoreType.DMA((2, n)),
                            pltpu.SemaphoreType.DMA((2,)), pltpu.SemaphoreType.DMA]),
        out_shape=[struct((rows, width), BF)] * 3 + [struct((rows, LANES), F32)]
        + [struct((rows, 2 * h), BF)] * 2 + [struct((width, 2 * h), BF), struct((2 * h, width), BF)]
        + [struct((packed, LANES), F32), struct((packed, LANES), BF), struct((8, width), F32), struct((8, 2 * h), F32)]
        + [struct((n, frames, width), BF)] * 2 + [struct((n_consts, width), F32), struct((rows, width), BF), struct((2 + 2 * items,), jnp.int32)],
        compiler_params=params(), cost_estimate=cost(0),
    )(counts, groups, tok, cot, cw, cb, ns, nsh, gamma, bout, buf_a, buf_b)


def combine_kernel(dp, meta, keep, recv, stay, leave):
    m = keep.shape[0] // dp
    for d in range(dp):
        src = pl.ds(pl.multiple_of((meta[1] ^ d) * m, m), m)
        total = keep[src, :] + recv[src, :].astype(F32)
        dst = leave if d % 2 else stay
        dst[d // 2 * m:(d // 2 + 1) * m, :] = total.astype(dst.dtype)


def combine(meta, keep, recv, dp):
    rows = keep.shape[0] // 2
    return pl.pallas_call(
        functools.partial(combine_kernel, dp),
        in_specs=[smem(), vmem(), vmem()], out_specs=[vmem(), vmem()],
        out_shape=[struct((rows, LANES), F32), struct((rows, LANES), BF)],
        compiler_params=params())(meta, keep, recv)


def mix_kernel(n, taps, meta, ad, low, act, pre, win1, wout1, consts, tokp, buf_c, buf_d, branch, ag, out,
               offs, win2, wout2, bias, bias_row, sems):
    copies = weight_copies(buf_c, 0, win2, wout2, bias, sems) + weight_copies(buf_d, 1, win2, wout2, bias, sems)
    for c in copies:
        c.start()
    place_items(n, meta, offs)

    def own(at):
        return dot(act[at, :], wout1[...]), dot_t(pre[at, :], win1[...])

    def rest(at, own_branch, own_ag):
        a, b = ad[at, :], low[at, :]
        activation, slope = gelu_parts(dot(a, win2[...]) + bias_row[...])
        grad = dot_t(b, wout2[...]) * slope
        value = (own_branch + dot(activation.astype(BF), wout2[...])) + consts[taps + 1:taps + 2, :]
        branch[at, :] = value
        out[at, :] = (tokp[at, :].astype(F32) + consts[taps:taps + 1, :] * value).astype(BF)
        ag[at, :] = own_ag + dot_t(grad.astype(BF), win2[...])

    first = pl.ds(0, TILE)
    branch[first, :], ag[first, :] = own(first)
    for c in copies:
        c.wait()
    spread_bias(bias, bias_row)
    rest(first, branch[first, :], ag[first, :])

    def pair(t, _):
        at = pl.ds(pl.multiple_of((2 * t + 1) * TILE, TILE), 2 * TILE)
        rest(at, *own(at))
        return 0

    left = offs[n + 1] - 1
    pairs = lax.shift_right_arithmetic(left, 1)
    lax.fori_loop(0, pairs, pair, 0)

    @pl.when(left > 2 * pairs)
    def _():
        at = pl.ds(pl.multiple_of(left * TILE, TILE), TILE)
        rest(at, *own(at))


def mix(meta, ad, low, act, pre, win, wout, consts, tokp, buf_c, buf_d, n, taps):
    rows, width = ad.shape
    h = act.shape[1] // 2
    wq, hq = width // LANES, h // LANES
    return pl.pallas_call(
        functools.partial(mix_kernel, n, taps),
        in_specs=[smem()] + [vmem()] * 8 + [hbm()] * 2,
        out_specs=[vmem()] * 3,
        scratch_shapes=[pltpu.SMEM((n + 2,), jnp.int32),
                        pltpu.VMEM((width, 2 * h), BF), pltpu.VMEM((2 * h, width), BF),
                        pltpu.VMEM((2, 16, LANES), BF), pltpu.VMEM((1, 2 * h), F32),
                        pltpu.SemaphoreType.DMA((2, hq + wq + 1))],
        out_shape=[struct((rows, width), F32)] * 2 + [struct((rows, width), BF)],
        compiler_params=params(), cost_estimate=cost(0),
    )(meta, ad, low, act, pre, win, wout, consts, tokp, buf_c, buf_d)


def norm_grad_kernel(n, taps, rates, meta, tok, cot, branch, ag, nrm, inv, gbo, gbi, consts,
                     cgp, small_keep, small_send, offs, sums):
    s = pl.program_id(0)
    frames, width = tok.shape[1], tok.shape[2]
    half = taps // 2
    wq = width // LANES
    h = gbi.shape[1] // 2

    @pl.when(s == 0)
    def _():
        place_items(n, meta, offs)
        sums[...] = jnp.zeros_like(sums)

    item = meta[0] * n + s
    count = meta[2 + item]
    group = meta[2 + 2 * n + item]
    off = offs[s]
    scale = pick(consts.at[taps + 2:taps + 2 + rates], group)
    zero = jnp.zeros((8, LANES), F32)
    steps = pl.cdiv(count, CHUNK)
    wide = steps // 2

    def step(r0, size, accs):
        here = pl.ds(r0, size)
        live = (lax.broadcasted_iota(jnp.int32, (size, LANES), 0) + r0) < count
        src = pl.ds(pl.multiple_of(off + r0, 16), size)
        new = []
        ngs, nrs = [], []
        for q in range(wq):
            a_ls, a_sc, a_sh = accs[3 * q:3 * q + 3]
            br = jnp.where(live, branch[src, lane(q)], 0.0)
            g = jnp.where(live, ag[src, lane(q)], 0.0)
            nr = nrm[src, lane(q)].astype(F32)
            new += [a_ls + fold(cot[s, here, lane(q)].astype(F32) * br), a_sc + fold(g * nr), a_sh + fold(g)]
            ngs.append(g * scale[:, lane(q)])
            nrs.append(nr)
        cross = [a * b for a, b in zip(ngs, nrs)]
        m1 = jnp.sum(sum(ngs[1:], ngs[0]), axis=-1, keepdims=True) * (1.0 / width)
        m2 = jnp.sum(sum(cross[1:], cross[0]), axis=-1, keepdims=True) * (1.0 / width)
        istd = inv[src, :]
        for q in range(wq):
            cg = istd * (ngs[q] - m1 - nrs[q] * m2)
            cgp[s, q, pl.ds(pl.multiple_of(r0 + PAD, 8), size), :] = cg
        return tuple(new)

    def both_sizes(run, width_of_state, add):
        add(lax.fori_loop(0, wide, lambda i, accs: run(pl.multiple_of(i * 2 * CHUNK, 2 * CHUNK), 2 * CHUNK, accs),
                          (zero,) * width_of_state))

        @pl.when(steps > 2 * wide)
        def _():
            add(run(pl.multiple_of(wide * 2 * CHUNK, 2 * CHUNK), CHUNK, (zero,) * width_of_state))

    def add_norm(accs):
        for q in range(wq):
            sums[taps + 1, :, lane(q)] += accs[3 * q]
            sums[taps + 2 + group, :, lane(q)] += accs[3 * q + 1]
            sums[taps + 2 + rates + group, :, lane(q)] += accs[3 * q + 2]

    both_sizes(step, 3 * wq, add_norm)

    def clear(i, _):
        r0 = pl.multiple_of(i * CHUNK, CHUNK)
        for q in range(wq):
            cgp[s, q, pl.ds(pl.multiple_of(r0 + PAD, 8), CHUNK), :] = jnp.zeros((CHUNK, LANES), F32)
        return 0

    lax.fori_loop(steps, frames // CHUNK, clear, 0)
    for q in range(wq):
        cgp[s, q, :PAD, :] = jnp.zeros((PAD, LANES), F32)
        cgp[s, q, PAD + frames:, :] = jnp.zeros((cgp.shape[2] - PAD - frames, LANES), F32)

        def conv_step(r0, size, accs):
            here = pl.ds(r0, size)
            live = (lax.broadcasted_iota(jnp.int32, (size, LANES), 0) + r0) < count
            tk = jnp.where(live, tok[s, here, lane(q)].astype(F32), 0.0)
            new = []
            for k in range(taps):
                sh = cgp[s, q, pl.ds(r0 + (PAD + half - k), size), :]
                new.append(accs[k] + fold(tk * sh))
                if k == half:
                    new_bias = accs[taps] + fold(sh)
            return tuple(new) + (new_bias,)

        def add_conv(accs):
            for k in range(taps + 1):
                sums[k, :, lane(q)] += accs[k]

        both_sizes(conv_step, taps + 1, add_conv)

    @pl.when(s == n - 1)
    def _():
        last = taps + 2 + 2 * rates
        rows = [jnp.sum(sums[i], axis=0, keepdims=True) for i in range(last)]
        rows.append(jnp.sum(gbo[...], axis=0, keepdims=True))
        gb = jnp.sum(gbi[...], axis=0, keepdims=True)
        fill = jnp.zeros((1, width - h), F32)
        spare = [jnp.zeros((1, width), F32)] * (small_keep.shape[0] - last - 2)
        for side, dst in ((0, small_keep), (1, small_send)):
            tail = [jnp.concatenate([gb[:, side * h:(side + 1) * h], fill], axis=1)]
            dst[...] = jnp.concatenate(rows + tail + spare, axis=0)


def norm_grad(meta, tok, cot, branch, ag, nrm, inv, gbo, gbi, consts, taps, rates):
    n, frames, width = tok.shape
    wq = width // LANES
    n_small = -(-(taps + 4 + 2 * rates) // 8) * 8
    return pl.pallas_call(
        functools.partial(norm_grad_kernel, n, taps, rates), grid=(n,),
        in_specs=[smem()] + [vmem()] * 9, out_specs=[vmem()] * 3,
        scratch_shapes=[pltpu.SMEM((n + 2,), jnp.int32),
                        pltpu.VMEM((taps + 2 + 2 * rates, 8, width), F32)],
        out_shape=[struct((n, wq, frames + 4 * PAD, LANES), F32)] + [struct((n_small, width), F32)] * 2,
        compiler_params=params(), cost_estimate=cost(40000000),
    )(meta, tok, cot, branch, ag, nrm, inv, gbo, gbi, consts)


def place_out_kernel(n, meta, own, other, out, stage, sems):
    frames, width = stage.shape[1], stage.shape[2]
    copies = []
    for side, src in ((0, own), (1, other)):
        first = (meta[0] ^ side) * n
        off = jnp.int32(0)
        for j in range(n):
            count = meta[2 + first + j]
            for i in range(frames // CHUNK):
                live = (lax.broadcasted_iota(jnp.int32, (CHUNK, LANES), 0) + i * CHUNK) < count
                rows = pl.ds(pl.multiple_of(off + i * CHUNK, 16), CHUNK)
                for q in range(width // LANES):
                    value = jnp.where(live, src[rows, lane(q)].astype(F32), 0.0)
                    stage[side * n + j, i * CHUNK:(i + 1) * CHUNK, lane(q)] = value.astype(BF)
            copies.append(pltpu.make_async_copy(stage.at[side * n + j], out.at[first + j], sems.at[side * n + j]))
            copies[-1].start()
            off = off + ((count + 15) & -16)
    for c in copies:
        c.wait()


def place_out(meta, own, other, n, frames):
    width = own.shape[1]
    return pl.pallas_call(
        functools.partial(place_out_kernel, n),
        in_specs=[smem(), vmem(), vmem()], out_specs=hbm(), out_shape=struct((2 * n, frames, width), BF),
        scratch_shapes=[pltpu.VMEM((2 * n, frames, width), BF), pltpu.SemaphoreType.DMA((2 * n,))],
        compiler_params=params(), cost_estimate=cost(40000000),
    )(meta, own, other)


def token_grad_kernel(n, taps, meta, cot, cgp, consts, gtok, gtok_own, stage, sems):
    s = pl.program_id(0)
    frames, width = cot.shape[1], cot.shape[2]
    half = taps // 2
    wq = width // LANES
    count = meta[2 + meta[0] * n + s]
    w = consts[:taps, :]
    steps = pl.cdiv(count, CHUNK)

    def place(j):
        return pltpu.make_async_copy(stage.at[j], gtok.at[meta[0] * n + j], sems.at[j])

    def conv_step(i, _):
        r0 = pl.multiple_of(i * CHUNK, CHUNK)
        here = pl.ds(r0, CHUNK)
        live = (lax.broadcasted_iota(jnp.int32, (CHUNK, LANES), 0) + r0) < count
        for q in range(wq):
            total = cot[s, here, lane(q)].astype(F32)
            for k in range(taps):
                total = total + w[k:k + 1, lane(q)] * cgp[s, q, pl.ds(r0 + (PAD + half - k), CHUNK), :]
            total = jnp.where(live, total, 0.0).astype(BF)
            gtok_own[s, here, lane(q)] = total
            stage[s, here, lane(q)] = total.astype(F32)
        return 0

    lax.fori_loop(0, steps, conv_step, 0)

    def clear(i, _):
        here = pl.ds(pl.multiple_of(i * CHUNK, CHUNK), CHUNK)
        gtok_own[s, here, :] = jnp.zeros((CHUNK, width), BF)
        stage[s, here, :] = jnp.zeros((CHUNK, width), F32)
        return 0

    lax.fori_loop(steps, frames // CHUNK, clear, 0)
    place(s).start()

    @pl.when(s == n - 1)
    def _():
        for j in range(n):
            place(j).wait()


def token_grad(meta, cot, cgp, consts, taps):
    n, frames, width = cot.shape
    return pl.pallas_call(
        functools.partial(token_grad_kernel, n, taps), grid=(n,),
        in_specs=[smem()] + [vmem()] * 3, out_specs=[hbm(), vmem()],
        scratch_shapes=[pltpu.VMEM((n, frames, width), F32), pltpu.SemaphoreType.DMA((n,))],
        out_shape=[struct((2 * n, frames, width), F32), struct((n, frames, width), BF)],
        compiler_params=params(), cost_estimate=cost(40000000),
    )(meta, cot, cgp, consts)


def merge_gtok_kernel(n, meta, other, gtok_in, gtok, stage, sems):
    copies = [pltpu.make_async_copy(stage.at[j], gtok.at[(1 - meta[0]) * n + j], sems.at[j]) for j in range(n)]
    for j in range(n):
        stage[j] = other[j].astype(F32)
        copies[j].start()
    for c in copies:
        c.wait()


def merge_gtok(meta, other, gtok):
    n = other.shape[0]
    return pl.pallas_call(
        functools.partial(merge_gtok_kernel, n),
        in_specs=[smem(), vmem(), hbm()], out_specs=hbm(), out_shape=struct(gtok.shape, F32),
        scratch_shapes=[pltpu.VMEM(other.shape, F32), pltpu.SemaphoreType.DMA((n,))],
        input_output_aliases={2: 0},
        compiler_params=params(), cost_estimate=cost(20000000),
    )(meta, other, gtok)


def message_kernel(stay, keep, recv, *refs):
    pieces, (out, mine) = refs[:-2], refs[-2:]
    m = pieces[0].shape[0]
    total = stay[:m, :]
    for piece in pieces:
        total = total + piece[...].astype(F32)
    out[:m, :] = total.astype(BF)
    mine[...] = total.astype(BF)
    small = (keep[...] + recv[...]).astype(BF)
    rows = small.shape[0]
    for q in range(small.shape[1] // LANES):
        out[m + q * rows:m + (q + 1) * rows, :] = small[:, lane(q)]


def make_message(stay, keep, recv, pieces):
    rows = pieces[0].shape[0] + keep.size // LANES
    return pl.pallas_call(message_kernel, in_specs=[vmem()] * (3 + len(pieces)), out_specs=[vmem(), vmem()],
                          out_shape=[struct((rows, LANES), BF), struct(pieces[0].shape, BF)],
                          compiler_params=params())(stay, keep, recv, *pieces)


def relay_kernel(m, *refs):
    sources, out = refs[:-1], refs[-1]
    sums = []
    for d, src in enumerate(sources):
        if d > 1:
            out[(d - 2) * m:(d - 1) * m, :] = src[:m, :]
        sums.append(src[m:, :].astype(F32))
    while len(sums) > 1:
        sums = [a + b for a, b in zip(sums[::2], sums[1::2])]
    out[(len(sources) - 2) * m:, :] = sums[0].astype(BF)


def relay(m, sources):
    rows = (len(sources) - 2) * m + sources[0].shape[0] - m
    return pl.pallas_call(functools.partial(relay_kernel, m), in_specs=[vmem()] * len(sources), out_specs=vmem(),
                          out_shape=struct((rows, LANES), BF), compiler_params=params())(*sources)


def unpack_kernel(dp, taps, rates, meta, mine, theirs, near_1, far_1, near, far, gcw, gcb, gns, gnsh, gwi, gbi, gwo, gbo, gls, full):
    h, width = gwo.shape
    wq, hq = width // LANES, h // LANES
    m = full.shape[0] // dp
    for odd, early, others in ((0, (mine, near_1), near), (1, (theirs, far_1), far)):
        for d in range(dp // 2):
            piece = others[(d - 2) * m:(d - 1) * m, :] if d > 1 else early[d][:m, :]
            at = pl.multiple_of((meta[1] ^ (2 * d + odd)) * m, m)
            full[pl.ds(at, m), :] = piece.astype(F32)
    for q in range(wq):
        gwo[:, lane(q)] = full[q * h:(q + 1) * h, :]
    base = wq * h
    for q in range(hq):
        gwi[:, lane(q)] = full[base + q * width:base + (q + 1) * width, :]
    behind = (dp // 2 - 2) * m
    small = near[behind:, :].astype(F32) + far[behind:, :].astype(F32)
    rows = small.shape[0] // wq
    small = jnp.concatenate([small[q * rows:(q + 1) * rows] for q in range(wq)], axis=1)
    gcw[...] = small[:taps]
    gcb[...] = small[taps]
    gls[...] = small[taps + 1]
    gns[...] = small[taps + 2:taps + 2 + rates]
    gnsh[...] = small[taps + 2 + rates:taps + 2 + 2 * rates]
    at = taps + 2 + 2 * rates
    gbo[...] = small[at]
    gbi[...] = small[at + 1, :h]


def unpack(meta, mine, theirs, near_1, far_1, near, far, dp, taps, rates, width, h):
    shapes = [(taps, width), (width,), (rates, width), (rates, width), (width, h), (h,), (h, width), (width,), (width,)]
    return pl.pallas_call(
        functools.partial(unpack_kernel, dp, taps, rates), in_specs=[smem()] + [vmem()] * 6,
        out_shape=[struct(s, F32) for s in shapes],
        scratch_shapes=[pltpu.VMEM((2 * width * h // LANES, LANES), F32)],
        compiler_params=params())(meta, mine, theirs, near_1, far_1, near, far)


def swap(x, step):
    size = lax.axis_size("tp")
    return lax.ppermute(x, "tp", [(i, i ^ step) for i in range(size)])


def across(x, step):
    size = lax.axis_size("dp")
    return lax.ppermute(x, "dp", [(i, i ^ step) for i in range(size)])


def per_device(tokens, frame_counts, rate_groups, conv_weight, conv_bias, norm_scale, norm_shift,
               weight_in, bias_in, weight_out, bias_out, layer_scale, cotangent):
    width, h = weight_in.shape
    n = tokens.shape[0] // 2
    (tokens, cotangent, conv_weight, conv_bias, norm_scale, norm_shift, weight_in, bias_in, weight_out, bias_out,
     layer_scale, frame_counts, rate_groups) = [pltpu.with_memory_space_constraint(v, pltpu.HBM) for v in (
         tokens, cotangent, conv_weight, conv_bias, norm_scale, norm_shift, weight_in, bias_in, weight_out, bias_out,
         layer_scale, frame_counts, rate_groups)]
    taps, rates = conv_weight.shape[0], norm_scale.shape[0]
    dp = lax.axis_size("dp")
    buf_a = pack(weight_in, bias_in, weight_out)
    buf_b = swap(buf_a, 1)
    buf_c = swap(buf_a, 2)
    buf_d = swap(buf_c, 1)
    ad, nrm, low, inv, act, pre, win, wout, keep, send, gbo, gbi, tok, cot, consts, tokp, meta = front(
        frame_counts, rate_groups, tokens, cotangent, conv_weight, conv_bias, norm_scale, norm_shift, layer_scale, bias_out, buf_a, buf_b, h)
    stay, leave = combine(meta, keep, swap(send, 1), dp)
    arrived = across(leave, 1)
    branch, ag, out_own = mix(meta, ad, low, act, pre, win, wout, consts, tokp, buf_c, buf_d, n, taps)
    arrived, branch, out_own = lax.optimization_barrier((arrived, branch, out_own))
    out_b = swap(out_own, 1)
    stay = (stay + arrived.astype(F32)).reshape(dp // 2, -1, LANES)
    pieces = [across(stay[d].astype(BF), 2 * d) for d in range(1, dp // 2)]

    cgp, small_keep, small_send = norm_grad(meta, tok, cot, branch, ag, nrm, inv, gbo, gbi, consts, taps, rates)
    pieces, small_send, cgp, out_b = lax.optimization_barrier((pieces, small_send, cgp, out_b))
    small_got = swap(small_send, 1)
    message, mine = make_message(stay.reshape(-1, LANES), small_keep, small_got, pieces)
    message, mine, out_b = lax.optimization_barrier((message, mine, out_b))
    m = pieces[0].shape[0]
    near = [message] + [across(message, 2 * d) for d in range(1, dp // 2)]
    theirs = across(mine, 1)
    far_1 = across(message, 3)
    out = place_out(meta, out_own, out_b, n, tokens.shape[1])
    cgp, out = lax.optimization_barrier((cgp, out))
    gtok, gtok_own = token_grad(meta, cot, cgp, consts, taps)
    near, theirs, far_1, gtok_own = lax.optimization_barrier((near, theirs, far_1, gtok_own))
    late = relay(m, near)
    far = across(late, 1)
    gtok = merge_gtok(meta, swap(gtok_own, 1), gtok)
    far, gtok = lax.optimization_barrier((far, gtok))
    gcw, gcb, gns, gnsh, gwi, gbi, gwo, gbo, gls = unpack(meta, mine, theirs, near[1], far_1, late, far, dp, taps, rates,
                                                          width, h)
    return (out, gtok, gcw, gcb, gns, gnsh, gwi, gbi, gwo, gbo, gls)


def solution(mesh):
    items, copied = P("dp", None, None), P()
    in_specs = (items, P("dp"), P("dp"), copied, copied, copied, copied, P(None, "tp"), P("tp"), P("tp", None),
                copied, copied, items)
    out_specs = (items, items, copied, copied, copied, copied, P(None, "tp"), P("tp"), P("tp", None), copied, copied)
    return jax.shard_map(per_device, mesh=mesh, in_specs=in_specs, out_specs=out_specs, check_vma=False)
```

```python
import functools

import jax
import jax.numpy as jnp
from jax import lax
from jax.experimental import pallas as pl
from jax.experimental.pallas import tpu as pltpu
from jax.sharding import PartitionSpec as P

EPS = 1e-06
BF, F32 = jnp.bfloat16, jnp.float32
TILE = 256
LANES = 128
PAD = 8
CHUNK = 64
FRONT_CHUNK = 32
VMEM_LIMIT = 12 * 1024 * 1024


def params(**more):
    return pltpu.CompilerParams(vmem_limit_bytes=VMEM_LIMIT, **more)


def struct(shape, dtype):
    return jax.ShapeDtypeStruct(shape, dtype)


def whole(shape):
    return pl.BlockSpec(shape, lambda *_: (0,) * len(shape))


def hbm():
    return pl.BlockSpec(memory_space=pltpu.HBM)


def smem():
    return pl.BlockSpec(memory_space=pltpu.SMEM)


def cost(size):
    return pl.CostEstimate(flops=0, transcendentals=0, bytes_accessed=size)


def vmem():
    return pl.BlockSpec(memory_space=pltpu.VMEM)


def lane(q):
    return slice(q * LANES, (q + 1) * LANES)


def fold(x):
    return jnp.sum(x.reshape(x.shape[0] // 8, 8, x.shape[1]), axis=0)


def pick(table, group):
    rows = table[...].astype(F32)
    value = rows[0:1]
    for r in range(1, rows.shape[0]):
        value = jnp.where(group == r, rows[r:r + 1], value)
    return value


def as_row(ref):
    return ref[...].astype(F32).reshape(1, -1)


def gelu_parts(pre):
    cdf = 0.5 + 0.5 * lax.erf(pre * 0.7071067811865476)
    density = jnp.exp(-0.5 * pre * pre) * 0.3989422804014327
    return pre * cdf, cdf + pre * density


def dot(a, b):
    return jnp.dot(a, b, preferred_element_type=F32)


def dot_t(a, b):
    return lax.dot_general(a, b, (((1,), (1,)), ((), ())), preferred_element_type=F32)


def dot_rows(a, b):
    return lax.dot_general(a, b, (((0,), (0,)), ((), ())), preferred_element_type=F32)


def place_items(n, meta, offs):
    end = jnp.int32(0)
    for j in range(n):
        offs[j] = end
        end = end + ((meta[2 + meta[0] * n + j] + 15) & -16)
    offs[n] = end
    offs[n + 1] = (end + TILE - 1) // TILE


def pack_kernel(wi, bi, wo, out):
    width, h = wi.shape
    hq, wq = h // LANES, width // LANES
    for q in range(hq):
        out[q * width:(q + 1) * width, :] = wi[:, lane(q)]
    base = hq * width
    for q in range(wq):
        out[base + q * h:base + (q + 1) * h, :] = wo[:, lane(q)]
    base += wq * h
    bias = bi[...].astype(F32).reshape(1, h)
    rows = [bias[:, lane(q)] for q in range(hq)] + [jnp.zeros((1, LANES), F32)] * (16 - hq)
    out[base:base + 16, :] = jnp.concatenate(rows, axis=0).astype(BF)


def pack(wi, bi, wo):
    rows = 2 * wi.size // LANES + 16
    return pl.pallas_call(pack_kernel, out_shape=struct((rows, LANES), BF),
                          compiler_params=params())(wi, bi, wo)


def weight_copies(buf, side, win, wout, bias, sems):
    width, h = win.shape[0], win.shape[1] // 2
    hq, wq = h // LANES, width // LANES
    copies = []
    for q in range(hq):
        at = side * h + q * LANES
        copies.append((buf.at[pl.ds(q * width, width), :], win.at[:, pl.ds(at, LANES)]))
    base = hq * width
    for q in range(wq):
        copies.append((buf.at[pl.ds(base + q * h, h), :], wout.at[pl.ds(side * h, h), pl.ds(q * LANES, LANES)]))
    copies.append((buf.at[pl.ds(base + wq * h, 16), :], bias.at[side]))
    return [pltpu.make_async_copy(src, dst, sems.at[side, i]) for i, (src, dst) in enumerate(copies)]


def spread_bias(bias, row):
    hq = row.shape[1] // LANES // 2
    for side in range(2):
        for q in range(hq):
            at = side * hq + q
            row[:, lane(at)] = bias[side, q:q + 1, :].astype(F32)


def front_kernel(n, counts_hbm, groups_hbm, tok_hbm, cot_hbm, cw, cb, ns, nsh, gamma, bout, buf_a, buf_b,
                 ad, nrm, low, inv, act, pre, win, wout, keep, send, gbo, gbi, tok, cot, consts, tokp, meta,
                 offs, counts_s, groups_s, pad, ad_s, nrm_s, low_s, inv_s, bias, bias_row, dwo, dwi, sems, item_sems, meta_sems, packed_sem):
    s = pl.program_id(0)
    frames, width = tok.shape[1], tok.shape[2]
    taps, rates = cw.shape[0], ns.shape[0]
    half = taps // 2
    wq = width // LANES
    h = win.shape[1] // 2
    copies = weight_copies(buf_a, 0, win, wout, bias, sems) + weight_copies(buf_b, 1, win, wout, bias, sems)

    def fetch(j):
        at = (lax.axis_index("tp") & 1) * n + j
        return [pltpu.make_async_copy(src.at[at], dst.at[j], item_sems.at[i, j])
                for i, (src, dst) in enumerate(((tok_hbm, tok), (cot_hbm, cot)))]

    @pl.when(s == 0)
    def _():
        tables = [pltpu.make_async_copy(counts_hbm, counts_s, meta_sems.at[0]),
                  pltpu.make_async_copy(groups_hbm, groups_s, meta_sems.at[1])]
        for c in tables + fetch(0) + fetch(1):
            c.start()
        for c in copies:
            c.start()
        for j in range(2, n):
            for c in fetch(j):
                c.start()
        consts[...] = jnp.zeros_like(consts)
        consts[:taps, :] = cw[...].astype(F32)
        consts[taps:taps + 1, :] = as_row(gamma)
        consts[taps + 1:taps + 2, :] = as_row(bout)
        consts[taps + 2:taps + 2 + rates, :] = ns[...].astype(F32)
        offs[n + 2] = 0
        gbo[...] = jnp.zeros_like(gbo)
        pad[...] = jnp.zeros_like(pad)
        for stage in (ad_s, nrm_s, low_s, inv_s):
            stage[...] = jnp.zeros_like(stage)
        meta[0] = lax.axis_index("tp") & 1
        meta[1] = lax.axis_index("dp")
        for c in tables:
            c.wait()
        for j in range(2 * n):
            meta[2 + j] = counts_s[j]
            meta[2 + 2 * n + j] = groups_s[j]
        place_items(n, meta, offs)

    def flush(j):
        dst = pl.ds(pl.multiple_of(offs[j], 16), frames)
        for whole_ref, stage in ((ad, ad_s), (nrm, nrm_s), (low, low_s), (inv, inv_s)):
            whole_ref[dst, :] = stage[...]

    @pl.when(s > 0)
    def _():
        flush(s - 1)

    @pl.when(s == 1)
    def _():
        for c in copies:
            c.wait()
        spread_bias(bias, bias_row)
        dwo[...] = jnp.zeros_like(dwo)
        dwi[...] = jnp.zeros_like(dwi)
        gbi[...] = jnp.zeros_like(gbi)

    for c in fetch(s):
        c.wait()

    def fetch_packed(j):
        dst = pl.ds(pl.multiple_of(offs[j], 16), frames)
        return pltpu.make_async_copy(tok.at[j], tokp.at[dst, :], packed_sem)

    @pl.when(s > 1)
    def _():
        fetch_packed(s - 2).wait()

    @pl.when(s > 0)
    def _():
        fetch_packed(s - 1).start()

    item = meta[0] * n + s
    count = meta[2 + item]
    group = meta[2 + 2 * n + item]

    def setup():
        rows = lax.broadcasted_iota(jnp.int32, (frames, LANES), 0)
        for q in range(wq):
            pad[q, PAD:PAD + frames, :] = jnp.where(rows < count, tok[s, :, lane(q)].astype(F32), 0.0)
        return pick(ns, group), pick(nsh, group), as_row(gamma), as_row(cb), cw[...].astype(F32)

    def conv_step(i, acc, consts):
        scale, shift, gam, conv_bias, w = consts
        r0 = i * FRONT_CHUNK if isinstance(i, int) else pl.multiple_of(i * FRONT_CHUNK, FRONT_CHUNK)
        here = pl.ds(r0, FRONT_CHUNK)
        live = (lax.broadcasted_iota(jnp.int32, (FRONT_CHUNK, LANES), 0) + r0) < count
        convs = []
        for q in range(wq):
            conv = conv_bias[:, lane(q)]
            for k in range(taps):
                conv = conv + w[k:k + 1, lane(q)] * pad[q, pl.ds(r0 + (PAD - half + k), FRONT_CHUNK), :]
            convs.append(conv)
        mean = jnp.sum(sum(convs[1:], convs[0]), axis=-1, keepdims=True) * (1.0 / width)
        cents = [c - mean for c in convs]
        sq = [c * c for c in cents]
        var = jnp.sum(sum(sq[1:], sq[0]), axis=-1, keepdims=True) * (1.0 / width)
        istd = lax.rsqrt(var + EPS)
        inv_s[here, :] = jnp.broadcast_to(istd, (FRONT_CHUNK, LANES))
        new = []
        for q in range(wq):
            normed = cents[q] * istd
            ad_s[here, lane(q)] = (normed * scale[:, lane(q)] + shift[:, lane(q)]).astype(BF)
            nrm_s[here, lane(q)] = normed.astype(BF)
            back = jnp.where(live, cot[s, here, lane(q)].astype(F32), 0.0) * gam[:, lane(q)]
            low_s[here, lane(q)] = back.astype(BF)
            new.append(acc[q] + fold(back))
        return tuple(new)

    def add_gbo(accs):
        for q in range(wq):
            gbo[:, lane(q)] += accs[q]

    def tile(t, size, between=()):
        between = list(between)
        at = pl.ds(pl.multiple_of(t * TILE, TILE), size)
        a, b = ad[at, :], low[at, :]
        activation, slope = gelu_parts(dot(a, win[...]) + bias_row[...])
        if between:
            between.pop(0)()
        grad = dot_t(b, wout[...]) * slope
        lo = activation.astype(BF)
        act[at, :] = lo
        if between:
            between.pop(0)()
        dwo[...] += dot_rows(lo, b)
        gbi[...] += fold(grad)
        g = grad.astype(BF)
        pre[at, :] = g
        if between:
            between.pop(0)()
        dwi[...] += dot_rows(a, g)
        if between:
            between.pop(0)()

    done = offs[n + 2]
    ready = offs[s] >= (done + 2) * TILE
    none = (jnp.zeros((8, LANES), F32),) * wq

    def conv_with(chunks, with_tile):
        consts = setup()
        state = [none]

        def part(lo_i, hi_i):
            def run():
                for i in range(lo_i, hi_i):
                    state[0] = conv_step(i, state[0], consts)
            return run

        cuts = [chunks * k // 4 for k in range(5)]
        parts = [part(cuts[k], cuts[k + 1]) for k in range(4)]
        if with_tile:
            tile(done, 2 * TILE, parts)
        else:
            for run in parts:
                run()
        add_gbo(state[0])
        if with_tile:
            offs[n + 2] = done + 2

    all_chunks = frames // FRONT_CHUNK
    short = count <= (all_chunks * 3 // 4) * FRONT_CHUNK
    for with_tile in (True, False):
        for chunks in (all_chunks * 3 // 4, all_chunks):
            fits = short if chunks < all_chunks else jnp.logical_not(short)
            pl.when((ready == with_tile) & fits)(functools.partial(conv_with, chunks, with_tile))

    @pl.when(s == n - 1)
    def _():
        flush(s)
        end = pl.ds(pl.multiple_of(offs[n], 16), TILE)
        ad[end, :] = jnp.zeros((TILE, width), BF)
        low[end, :] = jnp.zeros((TILE, width), BF)

        fetch_packed(n - 2).wait()
        fetch_packed(n - 1).start()

        start = offs[n + 2]
        left = offs[n + 1] - start
        pairs = lax.shift_right_arithmetic(left, 1)

        def rest(t, _):
            tile(start + 2 * t, 2 * TILE)
            return 0

        lax.fori_loop(0, pairs, rest, 0)

        @pl.when(left > 2 * pairs)
        def _():
            tile(offs[n + 1] - 1, TILE)

        fetch_packed(n - 1).wait()
        for side, dst in ((0, keep), (1, send)):
            for q in range(wq):
                dst[q * h:(q + 1) * h, :] = dwo[side * h:(side + 1) * h, lane(q)].astype(dst.dtype)
            base = wq * h
            for q in range(h // LANES):
                dst[base + q * width:base + (q + 1) * width, :] = dwi[:, lane(side * (h // LANES) + q)].astype(dst.dtype)


def front(counts, groups, tok, cot, cw, cb, ns, nsh, gamma, bout, buf_a, buf_b, h):
    items, frames, width = tok.shape
    n = items // 2
    rows = n * frames + TILE
    packed = 2 * width * h // LANES
    wq, hq = width // LANES, h // LANES
    n_consts = -(-(cw.shape[0] + 2 + ns.shape[0]) // 8) * 8
    return pl.pallas_call(
        functools.partial(front_kernel, n),
        grid_spec=pl.GridSpec(
            grid=(n,),
            in_specs=[hbm()] * 4 + [whole(v.shape) for v in (cw, cb, ns, nsh, gamma, bout)] + [hbm()] * 2,
            out_specs=[vmem()] * 16 + [smem()],
            scratch_shapes=[pltpu.SMEM((n + 3,), jnp.int32), pltpu.SMEM((items,), jnp.int32), pltpu.SMEM((items,), jnp.int32),
                            pltpu.VMEM((wq, frames + 4 * PAD, LANES), F32),
                            pltpu.VMEM((frames, width), BF), pltpu.VMEM((frames, width), BF),
                            pltpu.VMEM((frames, width), BF), pltpu.VMEM((frames, LANES), F32),
                            pltpu.VMEM((2, 16, LANES), BF), pltpu.VMEM((1, 2 * h), F32),
                            pltpu.VMEM((2 * h, width), F32), pltpu.VMEM((width, 2 * h), F32),
                            pltpu.SemaphoreType.DMA((2, hq + wq + 1)), pltpu.SemaphoreType.DMA((2, n)),
                            pltpu.SemaphoreType.DMA((2,)), pltpu.SemaphoreType.DMA]),
        out_shape=[struct((rows, width), BF)] * 3 + [struct((rows, LANES), F32)]
        + [struct((rows, 2 * h), BF)] * 2 + [struct((width, 2 * h), BF), struct((2 * h, width), BF)]
        + [struct((packed, LANES), F32), struct((packed, LANES), BF), struct((8, width), F32), struct((8, 2 * h), F32)]
        + [struct((n, frames, width), BF)] * 2 + [struct((n_consts, width), F32), struct((rows, width), BF), struct((2 + 2 * items,), jnp.int32)],
        compiler_params=params(), cost_estimate=cost(0),
    )(counts, groups, tok, cot, cw, cb, ns, nsh, gamma, bout, buf_a, buf_b)


def combine_kernel(dp, meta, keep, recv, stay, leave):
    m = keep.shape[0] // dp
    for d in range(dp):
        src = pl.ds(pl.multiple_of((meta[1] ^ d) * m, m), m)
        total = keep[src, :] + recv[src, :].astype(F32)
        dst = leave if d % 2 else stay
        dst[d // 2 * m:(d // 2 + 1) * m, :] = total.astype(dst.dtype)


def combine(meta, keep, recv, dp):
    rows = keep.shape[0] // 2
    return pl.pallas_call(
        functools.partial(combine_kernel, dp),
        in_specs=[smem(), vmem(), vmem()], out_specs=[vmem(), vmem()],
        out_shape=[struct((rows, LANES), F32), struct((rows, LANES), BF)],
        compiler_params=params())(meta, keep, recv)


def mix_kernel(n, taps, meta, ad, low, act, pre, win1, wout1, consts, tokp, buf_c, buf_d, branch, ag, out,
               offs, win2, wout2, bias, bias_row, sems):
    copies = weight_copies(buf_c, 0, win2, wout2, bias, sems) + weight_copies(buf_d, 1, win2, wout2, bias, sems)
    for c in copies:
        c.start()
    place_items(n, meta, offs)

    def own(at):
        return dot(act[at, :], wout1[...]), dot_t(pre[at, :], win1[...])

    def rest(at, own_branch, own_ag):
        a, b = ad[at, :], low[at, :]
        activation, slope = gelu_parts(dot(a, win2[...]) + bias_row[...])
        grad = dot_t(b, wout2[...]) * slope
        value = (own_branch + dot(activation.astype(BF), wout2[...])) + consts[taps + 1:taps + 2, :]
        branch[at, :] = value
        out[at, :] = (tokp[at, :].astype(F32) + consts[taps:taps + 1, :] * value).astype(BF)
        ag[at, :] = own_ag + dot_t(grad.astype(BF), win2[...])

    first = pl.ds(0, TILE)
    branch[first, :], ag[first, :] = own(first)
    for c in copies:
        c.wait()
    spread_bias(bias, bias_row)
    rest(first, branch[first, :], ag[first, :])

    def pair(t, _):
        at = pl.ds(pl.multiple_of((2 * t + 1) * TILE, TILE), 2 * TILE)
        rest(at, *own(at))
        return 0

    left = offs[n + 1] - 1
    pairs = lax.shift_right_arithmetic(left, 1)
    lax.fori_loop(0, pairs, pair, 0)

    @pl.when(left > 2 * pairs)
    def _():
        at = pl.ds(pl.multiple_of(left * TILE, TILE), TILE)
        rest(at, *own(at))


def mix(meta, ad, low, act, pre, win, wout, consts, tokp, buf_c, buf_d, n, taps):
    rows, width = ad.shape
    h = act.shape[1] // 2
    wq, hq = width // LANES, h // LANES
    return pl.pallas_call(
        functools.partial(mix_kernel, n, taps),
        in_specs=[smem()] + [vmem()] * 8 + [hbm()] * 2,
        out_specs=[vmem()] * 3,
        scratch_shapes=[pltpu.SMEM((n + 2,), jnp.int32),
                        pltpu.VMEM((width, 2 * h), BF), pltpu.VMEM((2 * h, width), BF),
                        pltpu.VMEM((2, 16, LANES), BF), pltpu.VMEM((1, 2 * h), F32),
                        pltpu.SemaphoreType.DMA((2, hq + wq + 1))],
        out_shape=[struct((rows, width), F32)] * 2 + [struct((rows, width), BF)],
        compiler_params=params(), cost_estimate=cost(0),
    )(meta, ad, low, act, pre, win, wout, consts, tokp, buf_c, buf_d)


def norm_grad_kernel(n, taps, rates, meta, tok, cot, branch, ag, nrm, inv, gbo, gbi, consts,
                     cgp, small_keep, small_send, offs, sums):
    s = pl.program_id(0)
    frames, width = tok.shape[1], tok.shape[2]
    half = taps // 2
    wq = width // LANES
    h = gbi.shape[1] // 2

    @pl.when(s == 0)
    def _():
        place_items(n, meta, offs)
        sums[...] = jnp.zeros_like(sums)

    item = meta[0] * n + s
    count = meta[2 + item]
    group = meta[2 + 2 * n + item]
    off = offs[s]
    scale = pick(consts.at[taps + 2:taps + 2 + rates], group)
    zero = jnp.zeros((8, LANES), F32)
    steps = pl.cdiv(count, CHUNK)
    wide = steps // 2

    def step(r0, size, accs):
        here = pl.ds(r0, size)
        live = (lax.broadcasted_iota(jnp.int32, (size, LANES), 0) + r0) < count
        src = pl.ds(pl.multiple_of(off + r0, 16), size)
        new = []
        ngs, nrs = [], []
        for q in range(wq):
            a_ls, a_sc, a_sh = accs[3 * q:3 * q + 3]
            br = jnp.where(live, branch[src, lane(q)], 0.0)
            g = jnp.where(live, ag[src, lane(q)], 0.0)
            nr = nrm[src, lane(q)].astype(F32)
            new += [a_ls + fold(cot[s, here, lane(q)].astype(F32) * br), a_sc + fold(g * nr), a_sh + fold(g)]
            ngs.append(g * scale[:, lane(q)])
            nrs.append(nr)
        cross = [a * b for a, b in zip(ngs, nrs)]
        m1 = jnp.sum(sum(ngs[1:], ngs[0]), axis=-1, keepdims=True) * (1.0 / width)
        m2 = jnp.sum(sum(cross[1:], cross[0]), axis=-1, keepdims=True) * (1.0 / width)
        istd = inv[src, :]
        for q in range(wq):
            cg = istd * (ngs[q] - m1 - nrs[q] * m2)
            cgp[s, q, pl.ds(pl.multiple_of(r0 + PAD, 8), size), :] = cg
        return tuple(new)

    def both_sizes(run, width_of_state, add):
        add(lax.fori_loop(0, wide, lambda i, accs: run(pl.multiple_of(i * 2 * CHUNK, 2 * CHUNK), 2 * CHUNK, accs),
                          (zero,) * width_of_state))

        @pl.when(steps > 2 * wide)
        def _():
            add(run(pl.multiple_of(wide * 2 * CHUNK, 2 * CHUNK), CHUNK, (zero,) * width_of_state))

    def add_norm(accs):
        for q in range(wq):
            sums[taps + 1, :, lane(q)] += accs[3 * q]
            sums[taps + 2 + group, :, lane(q)] += accs[3 * q + 1]
            sums[taps + 2 + rates + group, :, lane(q)] += accs[3 * q + 2]

    both_sizes(step, 3 * wq, add_norm)

    def clear(i, _):
        r0 = pl.multiple_of(i * CHUNK, CHUNK)
        for q in range(wq):
            cgp[s, q, pl.ds(pl.multiple_of(r0 + PAD, 8), CHUNK), :] = jnp.zeros((CHUNK, LANES), F32)
        return 0

    lax.fori_loop(steps, frames // CHUNK, clear, 0)
    for q in range(wq):
        cgp[s, q, :PAD, :] = jnp.zeros((PAD, LANES), F32)
        cgp[s, q, PAD + frames:, :] = jnp.zeros((cgp.shape[2] - PAD - frames, LANES), F32)

        def conv_step(r0, size, accs):
            here = pl.ds(r0, size)
            live = (lax.broadcasted_iota(jnp.int32, (size, LANES), 0) + r0) < count
            tk = jnp.where(live, tok[s, here, lane(q)].astype(F32), 0.0)
            new = []
            for k in range(taps):
                sh = cgp[s, q, pl.ds(r0 + (PAD + half - k), size), :]
                new.append(accs[k] + fold(tk * sh))
                if k == half:
                    new_bias = accs[taps] + fold(sh)
            return tuple(new) + (new_bias,)

        def add_conv(accs):
            for k in range(taps + 1):
                sums[k, :, lane(q)] += accs[k]

        both_sizes(conv_step, taps + 1, add_conv)

    @pl.when(s == n - 1)
    def _():
        last = taps + 2 + 2 * rates
        rows = [jnp.sum(sums[i], axis=0, keepdims=True) for i in range(last)]
        rows.append(jnp.sum(gbo[...], axis=0, keepdims=True))
        gb = jnp.sum(gbi[...], axis=0, keepdims=True)
        fill = jnp.zeros((1, width - h), F32)
        spare = [jnp.zeros((1, width), F32)] * (small_keep.shape[0] - last - 2)
        for side, dst in ((0, small_keep), (1, small_send)):
            tail = [jnp.concatenate([gb[:, side * h:(side + 1) * h], fill], axis=1)]
            dst[...] = jnp.concatenate(rows + tail + spare, axis=0)


def norm_grad(meta, tok, cot, branch, ag, nrm, inv, gbo, gbi, consts, taps, rates):
    n, frames, width = tok.shape
    wq = width // LANES
    n_small = -(-(taps + 4 + 2 * rates) // 8) * 8
    return pl.pallas_call(
        functools.partial(norm_grad_kernel, n, taps, rates), grid=(n,),
        in_specs=[smem()] + [vmem()] * 9, out_specs=[vmem()] * 3,
        scratch_shapes=[pltpu.SMEM((n + 2,), jnp.int32),
                        pltpu.VMEM((taps + 2 + 2 * rates, 8, width), F32)],
        out_shape=[struct((n, wq, frames + 4 * PAD, LANES), F32)] + [struct((n_small, width), F32)] * 2,
        compiler_params=params(), cost_estimate=cost(40000000),
    )(meta, tok, cot, branch, ag, nrm, inv, gbo, gbi, consts)


def place_out_kernel(n, meta, own, other, out, stage, sems):
    frames, width = stage.shape[1], stage.shape[2]
    copies = []
    for side, src in ((0, own), (1, other)):
        first = (meta[0] ^ side) * n
        off = jnp.int32(0)
        for j in range(n):
            count = meta[2 + first + j]
            for i in range(frames // CHUNK):
                live = (lax.broadcasted_iota(jnp.int32, (CHUNK, LANES), 0) + i * CHUNK) < count
                rows = pl.ds(pl.multiple_of(off + i * CHUNK, 16), CHUNK)
                for q in range(width // LANES):
                    value = jnp.where(live, src[rows, lane(q)].astype(F32), 0.0)
                    stage[side * n + j, i * CHUNK:(i + 1) * CHUNK, lane(q)] = value.astype(BF)
            copies.append(pltpu.make_async_copy(stage.at[side * n + j], out.at[first + j], sems.at[side * n + j]))
            copies[-1].start()
            off = off + ((count + 15) & -16)
    for c in copies:
        c.wait()


def place_out(meta, own, other, n, frames):
    width = own.shape[1]
    return pl.pallas_call(
        functools.partial(place_out_kernel, n),
        in_specs=[smem(), vmem(), vmem()], out_specs=hbm(), out_shape=struct((2 * n, frames, width), BF),
        scratch_shapes=[pltpu.VMEM((2 * n, frames, width), BF), pltpu.SemaphoreType.DMA((2 * n,))],
        compiler_params=params(), cost_estimate=cost(40000000),
    )(meta, own, other)


def token_grad_kernel(n, taps, meta, cot, cgp, consts, gtok, gtok_own, stage, sems):
    s = pl.program_id(0)
    frames, width = cot.shape[1], cot.shape[2]
    half = taps // 2
    wq = width // LANES
    count = meta[2 + meta[0] * n + s]
    w = consts[:taps, :]
    steps = pl.cdiv(count, CHUNK)

    def place(j):
        return pltpu.make_async_copy(stage.at[j], gtok.at[meta[0] * n + j], sems.at[j])

    def conv_step(i, _):
        r0 = pl.multiple_of(i * CHUNK, CHUNK)
        here = pl.ds(r0, CHUNK)
        live = (lax.broadcasted_iota(jnp.int32, (CHUNK, LANES), 0) + r0) < count
        for q in range(wq):
            total = cot[s, here, lane(q)].astype(F32)
            for k in range(taps):
                total = total + w[k:k + 1, lane(q)] * cgp[s, q, pl.ds(r0 + (PAD + half - k), CHUNK), :]
            total = jnp.where(live, total, 0.0).astype(BF)
            gtok_own[s, here, lane(q)] = total
            stage[s, here, lane(q)] = total.astype(F32)
        return 0

    lax.fori_loop(0, steps, conv_step, 0)

    def clear(i, _):
        here = pl.ds(pl.multiple_of(i * CHUNK, CHUNK), CHUNK)
        gtok_own[s, here, :] = jnp.zeros((CHUNK, width), BF)
        stage[s, here, :] = jnp.zeros((CHUNK, width), F32)
        return 0

    lax.fori_loop(steps, frames // CHUNK, clear, 0)
    place(s).start()

    @pl.when(s == n - 1)
    def _():
        for j in range(n):
            place(j).wait()


def token_grad(meta, cot, cgp, consts, taps):
    n, frames, width = cot.shape
    return pl.pallas_call(
        functools.partial(token_grad_kernel, n, taps), grid=(n,),
        in_specs=[smem()] + [vmem()] * 3, out_specs=[hbm(), vmem()],
        scratch_shapes=[pltpu.VMEM((n, frames, width), F32), pltpu.SemaphoreType.DMA((n,))],
        out_shape=[struct((2 * n, frames, width), F32), struct((n, frames, width), BF)],
        compiler_params=params(), cost_estimate=cost(40000000),
    )(meta, cot, cgp, consts)


def merge_gtok_kernel(n, meta, other, gtok_in, gtok, stage, sems):
    copies = [pltpu.make_async_copy(stage.at[j], gtok.at[(1 - meta[0]) * n + j], sems.at[j]) for j in range(n)]
    for j in range(n):
        stage[j] = other[j].astype(F32)
        copies[j].start()
    for c in copies:
        c.wait()


def merge_gtok(meta, other, gtok):
    n = other.shape[0]
    return pl.pallas_call(
        functools.partial(merge_gtok_kernel, n),
        in_specs=[smem(), vmem(), hbm()], out_specs=hbm(), out_shape=struct(gtok.shape, F32),
        scratch_shapes=[pltpu.VMEM(other.shape, F32), pltpu.SemaphoreType.DMA((n,))],
        input_output_aliases={2: 0},
        compiler_params=params(), cost_estimate=cost(20000000),
    )(meta, other, gtok)


def message_kernel(stay, keep, recv, *refs):
    pieces, (out, mine) = refs[:-2], refs[-2:]
    m = pieces[0].shape[0]
    total = stay[:m, :]
    for piece in pieces:
        total = total + piece[...].astype(F32)
    out[:m, :] = total.astype(BF)
    mine[...] = total.astype(BF)
    small = (keep[...] + recv[...]).astype(BF)
    rows = small.shape[0]
    for q in range(small.shape[1] // LANES):
        out[m + q * rows:m + (q + 1) * rows, :] = small[:, lane(q)]


def make_message(stay, keep, recv, pieces):
    rows = pieces[0].shape[0] + keep.size // LANES
    return pl.pallas_call(message_kernel, in_specs=[vmem()] * (3 + len(pieces)), out_specs=[vmem(), vmem()],
                          out_shape=[struct((rows, LANES), BF), struct(pieces[0].shape, BF)],
                          compiler_params=params())(stay, keep, recv, *pieces)


def relay_kernel(m, *refs):
    sources, out = refs[:-1], refs[-1]
    sums = []
    for d, src in enumerate(sources):
        if d > 1:
            out[(d - 2) * m:(d - 1) * m, :] = src[:m, :]
        sums.append(src[m:, :].astype(F32))
    while len(sums) > 1:
        sums = [a + b for a, b in zip(sums[::2], sums[1::2])]
    out[(len(sources) - 2) * m:, :] = sums[0].astype(BF)


def relay(m, sources):
    rows = (len(sources) - 2) * m + sources[0].shape[0] - m
    return pl.pallas_call(functools.partial(relay_kernel, m), in_specs=[vmem()] * len(sources), out_specs=vmem(),
                          out_shape=struct((rows, LANES), BF), compiler_params=params())(*sources)


def unpack_kernel(dp, taps, rates, meta, mine, theirs, near_1, far_1, near, far, gcw, gcb, gns, gnsh, gwi, gbi, gwo, gbo, gls, full):
    h, width = gwo.shape
    wq, hq = width // LANES, h // LANES
    m = full.shape[0] // dp
    for odd, early, others in ((0, (mine, near_1), near), (1, (theirs, far_1), far)):
        for d in range(dp // 2):
            piece = others[(d - 2) * m:(d - 1) * m, :] if d > 1 else early[d][:m, :]
            at = pl.multiple_of((meta[1] ^ (2 * d + odd)) * m, m)
            full[pl.ds(at, m), :] = piece.astype(F32)
    for q in range(wq):
        gwo[:, lane(q)] = full[q * h:(q + 1) * h, :]
    base = wq * h
    for q in range(hq):
        gwi[:, lane(q)] = full[base + q * width:base + (q + 1) * width, :]
    behind = (dp // 2 - 2) * m
    small = near[behind:, :].astype(F32) + far[behind:, :].astype(F32)
    rows = small.shape[0] // wq
    small = jnp.concatenate([small[q * rows:(q + 1) * rows] for q in range(wq)], axis=1)
    gcw[...] = small[:taps]
    gcb[...] = small[taps]
    gls[...] = small[taps + 1]
    gns[...] = small[taps + 2:taps + 2 + rates]
    gnsh[...] = small[taps + 2 + rates:taps + 2 + 2 * rates]
    at = taps + 2 + 2 * rates
    gbo[...] = small[at]
    gbi[...] = small[at + 1, :h]


def unpack(meta, mine, theirs, near_1, far_1, near, far, dp, taps, rates, width, h):
    shapes = [(taps, width), (width,), (rates, width), (rates, width), (width, h), (h,), (h, width), (width,), (width,)]
    return pl.pallas_call(
        functools.partial(unpack_kernel, dp, taps, rates), in_specs=[smem()] + [vmem()] * 6,
        out_shape=[struct(s, F32) for s in shapes],
        scratch_shapes=[pltpu.VMEM((2 * width * h // LANES, LANES), F32)],
        compiler_params=params())(meta, mine, theirs, near_1, far_1, near, far)


def swap(x, step):
    size = lax.axis_size("tp")
    return lax.ppermute(x, "tp", [(i, i ^ step) for i in range(size)])


def across(x, step):
    size = lax.axis_size("dp")
    return lax.ppermute(x, "dp", [(i, i ^ step) for i in range(size)])


def per_device(tokens, frame_counts, rate_groups, conv_weight, conv_bias, norm_scale, norm_shift,
               weight_in, bias_in, weight_out, bias_out, layer_scale, cotangent):
    width, h = weight_in.shape
    n = tokens.shape[0] // 2
    (tokens, cotangent, conv_weight, conv_bias, norm_scale, norm_shift, weight_in, bias_in, weight_out, bias_out,
     layer_scale, frame_counts, rate_groups) = [pltpu.with_memory_space_constraint(v, pltpu.HBM) for v in (
         tokens, cotangent, conv_weight, conv_bias, norm_scale, norm_shift, weight_in, bias_in, weight_out, bias_out,
         layer_scale, frame_counts, rate_groups)]
    taps, rates = conv_weight.shape[0], norm_scale.shape[0]
    dp = lax.axis_size("dp")
    buf_a = pack(weight_in, bias_in, weight_out)
    buf_b = swap(buf_a, 1)
    buf_c = swap(buf_a, 2)
    buf_d = swap(buf_c, 1)
    ad, nrm, low, inv, act, pre, win, wout, keep, send, gbo, gbi, tok, cot, consts, tokp, meta = front(
        frame_counts, rate_groups, tokens, cotangent, conv_weight, conv_bias, norm_scale, norm_shift, layer_scale, bias_out, buf_a, buf_b, h)
    stay, leave = combine(meta, keep, swap(send, 1), dp)
    arrived = across(leave, 1)
    branch, ag, out_own = mix(meta, ad, low, act, pre, win, wout, consts, tokp, buf_c, buf_d, n, taps)
    arrived, branch, out_own = lax.optimization_barrier((arrived, branch, out_own))
    out_b = swap(out_own, 1)
    stay = (stay + arrived.astype(F32)).reshape(dp // 2, -1, LANES)
    pieces = [across(stay[d].astype(BF), 2 * d) for d in range(1, dp // 2)]

    cgp, small_keep, small_send = norm_grad(meta, tok, cot, branch, ag, nrm, inv, gbo, gbi, consts, taps, rates)
    pieces, small_send, cgp, out_b = lax.optimization_barrier((pieces, small_send, cgp, out_b))
    small_got = swap(small_send, 1)
    message, mine = make_message(stay.reshape(-1, LANES), small_keep, small_got, pieces)
    message, mine, out_b = lax.optimization_barrier((message, mine, out_b))
    m = pieces[0].shape[0]
    near = [message] + [across(message, 2 * d) for d in range(1, dp // 2)]
    theirs = across(mine, 1)
    far_1 = across(mine, 3)
    out = place_out(meta, out_own, out_b, n, tokens.shape[1])
    cgp, out = lax.optimization_barrier((cgp, out))
    gtok, gtok_own = token_grad(meta, cot, cgp, consts, taps)
    near, theirs, far_1, gtok_own = lax.optimization_barrier((near, theirs, far_1, gtok_own))
    late = relay(m, near)
    far = across(late, 1)
    gtok = merge_gtok(meta, swap(gtok_own, 1), gtok)
    far, gtok = lax.optimization_barrier((far, gtok))
    gcw, gcb, gns, gnsh, gwi, gbi, gwo, gbo, gls = unpack(meta, mine, theirs, near[1], far_1, late, far, dp, taps, rates,
                                                          width, h)
    return (out, gtok, gcw, gcb, gns, gnsh, gwi, gbi, gwo, gbo, gls)


def solution(mesh):
    items, copied = P("dp", None, None), P()
    in_specs = (items, P("dp"), P("dp"), copied, copied, copied, copied, P(None, "tp"), P("tp"), P("tp", None),
                copied, copied, items)
    out_specs = (items, items, copied, copied, copied, copied, P(None, "tp"), P("tp"), P("tp", None), copied, copied)
    return jax.shard_map(per_device, mesh=mesh, in_specs=in_specs, out_specs=out_specs, check_vma=False)
```

```python
import functools

import jax
import jax.numpy as jnp
from jax import lax
from jax.experimental import pallas as pl
from jax.experimental.pallas import tpu as pltpu
from jax.sharding import PartitionSpec as P

EPS = 1e-06
BF, F32 = jnp.bfloat16, jnp.float32
TILE = 256
LANES = 128
PAD = 8
CHUNK = 64
FRONT_CHUNK = 32
VMEM_LIMIT = 12 * 1024 * 1024


def params(**more):
    return pltpu.CompilerParams(vmem_limit_bytes=VMEM_LIMIT, **more)


def struct(shape, dtype):
    return jax.ShapeDtypeStruct(shape, dtype)


def whole(shape):
    return pl.BlockSpec(shape, lambda *_: (0,) * len(shape))


def hbm():
    return pl.BlockSpec(memory_space=pltpu.HBM)


def smem():
    return pl.BlockSpec(memory_space=pltpu.SMEM)


def cost(size):
    return pl.CostEstimate(flops=0, transcendentals=0, bytes_accessed=size)


def vmem():
    return pl.BlockSpec(memory_space=pltpu.VMEM)


def lane(q):
    return slice(q * LANES, (q + 1) * LANES)


def fold(x):
    return jnp.sum(x.reshape(x.shape[0] // 8, 8, x.shape[1]), axis=0)


def pick(table, group):
    rows = table[...].astype(F32)
    value = rows[0:1]
    for r in range(1, rows.shape[0]):
        value = jnp.where(group == r, rows[r:r + 1], value)
    return value


def as_row(ref):
    return ref[...].astype(F32).reshape(1, -1)


def gelu_parts(pre):
    cdf = 0.5 + 0.5 * lax.erf(pre * 0.7071067811865476)
    density = jnp.exp(-0.5 * pre * pre) * 0.3989422804014327
    return pre * cdf, cdf + pre * density


def dot(a, b):
    return jnp.dot(a, b, preferred_element_type=F32)


def dot_t(a, b):
    return lax.dot_general(a, b, (((1,), (1,)), ((), ())), preferred_element_type=F32)


def dot_rows(a, b):
    return lax.dot_general(a, b, (((0,), (0,)), ((), ())), preferred_element_type=F32)


def place_items(n, meta, offs):
    end = jnp.int32(0)
    for j in range(n):
        offs[j] = end
        end = end + ((meta[2 + meta[0] * n + j] + 15) & -16)
    offs[n] = end
    offs[n + 1] = (end + TILE - 1) // TILE


def pack_kernel(wi, bi, wo, out):
    width, h = wi.shape
    hq, wq = h // LANES, width // LANES
    for q in range(hq):
        out[q * width:(q + 1) * width, :] = wi[:, lane(q)]
    base = hq * width
    for q in range(wq):
        out[base + q * h:base + (q + 1) * h, :] = wo[:, lane(q)]
    base += wq * h
    bias = bi[...].astype(F32).reshape(1, h)
    rows = [bias[:, lane(q)] for q in range(hq)] + [jnp.zeros((1, LANES), F32)] * (16 - hq)
    out[base:base + 16, :] = jnp.concatenate(rows, axis=0).astype(BF)


def pack(wi, bi, wo):
    rows = 2 * wi.size // LANES + 16
    return pl.pallas_call(pack_kernel, out_shape=struct((rows, LANES), BF),
                          compiler_params=params())(wi, bi, wo)


def weight_copies(buf, side, win, wout, bias, sems):
    width, h = win.shape[0], win.shape[1] // 2
    hq, wq = h // LANES, width // LANES
    copies = []
    for q in range(hq):
        at = side * h + q * LANES
        copies.append((buf.at[pl.ds(q * width, width), :], win.at[:, pl.ds(at, LANES)]))
    base = hq * width
    for q in range(wq):
        copies.append((buf.at[pl.ds(base + q * h, h), :], wout.at[pl.ds(side * h, h), pl.ds(q * LANES, LANES)]))
    copies.append((buf.at[pl.ds(base + wq * h, 16), :], bias.at[side]))
    return [pltpu.make_async_copy(src, dst, sems.at[side, i]) for i, (src, dst) in enumerate(copies)]


def spread_bias(bias, row):
    hq = row.shape[1] // LANES // 2
    for side in range(2):
        for q in range(hq):
            at = side * hq + q
            row[:, lane(at)] = bias[side, q:q + 1, :].astype(F32)


def front_kernel(n, counts_hbm, groups_hbm, tok_hbm, cot_hbm, cw, cb, ns, nsh, gamma, bout, buf_a, buf_b,
                 ad, nrm, low, inv, act, pre, win, wout, keep, send, gbo, gbi, tok, cot, consts, tokp, meta,
                 offs, counts_s, groups_s, pad, ad_s, nrm_s, low_s, inv_s, bias, bias_row, dwo, dwi, sems, item_sems, meta_sems, packed_sem):
    s = pl.program_id(0)
    frames, width = tok.shape[1], tok.shape[2]
    taps, rates = cw.shape[0], ns.shape[0]
    half = taps // 2
    wq = width // LANES
    h = win.shape[1] // 2
    copies = weight_copies(buf_a, 0, win, wout, bias, sems) + weight_copies(buf_b, 1, win, wout, bias, sems)

    def fetch(j):
        at = (lax.axis_index("tp") & 1) * n + j
        return [pltpu.make_async_copy(src.at[at], dst.at[j], item_sems.at[i, j])
                for i, (src, dst) in enumerate(((tok_hbm, tok), (cot_hbm, cot)))]

    @pl.when(s == 0)
    def _():
        tables = [pltpu.make_async_copy(counts_hbm, counts_s, meta_sems.at[0]),
                  pltpu.make_async_copy(groups_hbm, groups_s, meta_sems.at[1])]
        for c in tables + fetch(0) + fetch(1):
            c.start()
        for c in copies:
            c.start()
        for j in range(2, n):
            for c in fetch(j):
                c.start()
        consts[...] = jnp.zeros_like(consts)
        consts[:taps, :] = cw[...].astype(F32)
        consts[taps:taps + 1, :] = as_row(gamma)
        consts[taps + 1:taps + 2, :] = as_row(bout)
        consts[taps + 2:taps + 2 + rates, :] = ns[...].astype(F32)
        offs[n + 2] = 0
        gbo[...] = jnp.zeros_like(gbo)
        pad[...] = jnp.zeros_like(pad)
        for stage in (ad_s, nrm_s, low_s, inv_s):
            stage[...] = jnp.zeros_like(stage)
        meta[0] = lax.axis_index("tp") & 1
        meta[1] = lax.axis_index("dp")
        for c in tables:
            c.wait()
        for j in range(2 * n):
            meta[2 + j] = counts_s[j]
            meta[2 + 2 * n + j] = groups_s[j]
        place_items(n, meta, offs)

    def flush(j):
        dst = pl.ds(pl.multiple_of(offs[j], 16), frames)
        for whole_ref, stage in ((ad, ad_s), (nrm, nrm_s), (low, low_s), (inv, inv_s)):
            whole_ref[dst, :] = stage[...]

    @pl.when(s > 0)
    def _():
        flush(s - 1)

    @pl.when(s == 1)
    def _():
        for c in copies:
            c.wait()
        spread_bias(bias, bias_row)
        dwo[...] = jnp.zeros_like(dwo)
        dwi[...] = jnp.zeros_like(dwi)
        gbi[...] = jnp.zeros_like(gbi)

    for c in fetch(s):
        c.wait()

    def fetch_packed(j):
        dst = pl.ds(pl.multiple_of(offs[j], 16), frames)
        return pltpu.make_async_copy(tok.at[j], tokp.at[dst, :], packed_sem)

    @pl.when(s > 1)
    def _():
        fetch_packed(s - 2).wait()

    @pl.when(s > 0)
    def _():
        fetch_packed(s - 1).start()

    item = meta[0] * n + s
    count = meta[2 + item]
    group = meta[2 + 2 * n + item]

    def setup():
        rows = lax.broadcasted_iota(jnp.int32, (frames, LANES), 0)
        for q in range(wq):
            pad[q, PAD:PAD + frames, :] = jnp.where(rows < count, tok[s, :, lane(q)].astype(F32), 0.0)
        return pick(ns, group), pick(nsh, group), as_row(gamma), as_row(cb), cw[...].astype(F32)

    def conv_step(i, acc, consts):
        scale, shift, gam, conv_bias, w = consts
        r0 = i * FRONT_CHUNK if isinstance(i, int) else pl.multiple_of(i * FRONT_CHUNK, FRONT_CHUNK)
        here = pl.ds(r0, FRONT_CHUNK)
        live = (lax.broadcasted_iota(jnp.int32, (FRONT_CHUNK, LANES), 0) + r0) < count
        convs = []
        for q in range(wq):
            conv = conv_bias[:, lane(q)]
            for k in range(taps):
                conv = conv + w[k:k + 1, lane(q)] * pad[q, pl.ds(r0 + (PAD - half + k), FRONT_CHUNK), :]
            convs.append(conv)
        mean = jnp.sum(sum(convs[1:], convs[0]), axis=-1, keepdims=True) * (1.0 / width)
        cents = [c - mean for c in convs]
        sq = [c * c for c in cents]
        var = jnp.sum(sum(sq[1:], sq[0]), axis=-1, keepdims=True) * (1.0 / width)
        istd = lax.rsqrt(var + EPS)
        inv_s[here, :] = jnp.broadcast_to(istd, (FRONT_CHUNK, LANES))
        new = []
        for q in range(wq):
            normed = cents[q] * istd
            ad_s[here, lane(q)] = (normed * scale[:, lane(q)] + shift[:, lane(q)]).astype(BF)
            nrm_s[here, lane(q)] = normed.astype(BF)
            back = jnp.where(live, cot[s, here, lane(q)].astype(F32), 0.0) * gam[:, lane(q)]
            low_s[here, lane(q)] = back.astype(BF)
            new.append(acc[q] + fold(back))
        return tuple(new)

    def add_gbo(accs):
        for q in range(wq):
            gbo[:, lane(q)] += accs[q]

    def tile(t, size, between=()):
        between = list(between)
        at = pl.ds(pl.multiple_of(t * TILE, TILE), size)
        a, b = ad[at, :], low[at, :]
        activation, slope = gelu_parts(dot(a, win[...]) + bias_row[...])
        if between:
            between.pop(0)()
        grad = dot_t(b, wout[...]) * slope
        lo = activation.astype(BF)
        act[at, :] = lo
        if between:
            between.pop(0)()
        dwo[...] += dot_rows(lo, b)
        gbi[...] += fold(grad)
        g = grad.astype(BF)
        pre[at, :] = g
        if between:
            between.pop(0)()
        dwi[...] += dot_rows(a, g)
        if between:
            between.pop(0)()

    done = offs[n + 2]
    ready = offs[s] >= (done + 2) * TILE
    none = (jnp.zeros((8, LANES), F32),) * wq

    def conv_with(chunks, with_tile):
        consts = setup()
        state = [none]

        def part(lo_i, hi_i):
            def run():
                for i in range(lo_i, hi_i):
                    state[0] = conv_step(i, state[0], consts)
            return run

        cuts = [chunks * k // 4 for k in range(5)]
        parts = [part(cuts[k], cuts[k + 1]) for k in range(4)]
        if with_tile:
            tile(done, 2 * TILE, parts)
        else:
            for run in parts:
                run()
        add_gbo(state[0])
        if with_tile:
            offs[n + 2] = done + 2

    all_chunks = frames // FRONT_CHUNK
    short = count <= (all_chunks * 3 // 4) * FRONT_CHUNK
    for with_tile in (True, False):
        for chunks in (all_chunks * 3 // 4, all_chunks):
            fits = short if chunks < all_chunks else jnp.logical_not(short)
            pl.when((ready == with_tile) & fits)(functools.partial(conv_with, chunks, with_tile))

    @pl.when(s == n - 1)
    def _():
        flush(s)
        end = pl.ds(pl.multiple_of(offs[n], 16), TILE)
        ad[end, :] = jnp.zeros((TILE, width), BF)
        low[end, :] = jnp.zeros((TILE, width), BF)

        fetch_packed(n - 2).wait()
        fetch_packed(n - 1).start()

        start = offs[n + 2]
        left = offs[n + 1] - start
        pairs = lax.shift_right_arithmetic(left, 1)

        def rest(t, _):
            tile(start + 2 * t, 2 * TILE)
            return 0

        lax.fori_loop(0, pairs, rest, 0)

        @pl.when(left > 2 * pairs)
        def _():
            tile(offs[n + 1] - 1, TILE)

        fetch_packed(n - 1).wait()
        for side, dst in ((0, keep), (1, send)):
            for q in range(wq):
                dst[q * h:(q + 1) * h, :] = dwo[side * h:(side + 1) * h, lane(q)].astype(dst.dtype)
            base = wq * h
            for q in range(h // LANES):
                dst[base + q * width:base + (q + 1) * width, :] = dwi[:, lane(side * (h // LANES) + q)].astype(dst.dtype)


def front(counts, groups, tok, cot, cw, cb, ns, nsh, gamma, bout, buf_a, buf_b, h):
    items, frames, width = tok.shape
    n = items // 2
    rows = n * frames + TILE
    packed = 2 * width * h // LANES
    wq, hq = width // LANES, h // LANES
    n_consts = -(-(cw.shape[0] + 2 + ns.shape[0]) // 8) * 8
    return pl.pallas_call(
        functools.partial(front_kernel, n),
        grid_spec=pl.GridSpec(
            grid=(n,),
            in_specs=[hbm()] * 4 + [whole(v.shape) for v in (cw, cb, ns, nsh, gamma, bout)] + [hbm()] * 2,
            out_specs=[vmem()] * 16 + [smem()],
            scratch_shapes=[pltpu.SMEM((n + 3,), jnp.int32), pltpu.SMEM((items,), jnp.int32), pltpu.SMEM((items,), jnp.int32),
                            pltpu.VMEM((wq, frames + 4 * PAD, LANES), F32),
                            pltpu.VMEM((frames, width), BF), pltpu.VMEM((frames, width), BF),
                            pltpu.VMEM((frames, width), BF), pltpu.VMEM((frames, LANES), F32),
                            pltpu.VMEM((2, 16, LANES), BF), pltpu.VMEM((1, 2 * h), F32),
                            pltpu.VMEM((2 * h, width), F32), pltpu.VMEM((width, 2 * h), F32),
                            pltpu.SemaphoreType.DMA((2, hq + wq + 1)), pltpu.SemaphoreType.DMA((2, n)),
                            pltpu.SemaphoreType.DMA((2,)), pltpu.SemaphoreType.DMA]),
        out_shape=[struct((rows, width), BF)] * 3 + [struct((rows, LANES), F32)]
        + [struct((rows, 2 * h), BF)] * 2 + [struct((width, 2 * h), BF), struct((2 * h, width), BF)]
        + [struct((packed, LANES), F32), struct((packed, LANES), BF), struct((8, width), F32), struct((8, 2 * h), F32)]
        + [struct((n, frames, width), BF)] * 2 + [struct((n_consts, width), F32), struct((rows, width), BF), struct((2 + 2 * items,), jnp.int32)],
        compiler_params=params(), cost_estimate=cost(0),
    )(counts, groups, tok, cot, cw, cb, ns, nsh, gamma, bout, buf_a, buf_b)


def combine_kernel(dp, meta, keep, recv, stay, leave):
    m = keep.shape[0] // dp
    for d in range(dp):
        src = pl.ds(pl.multiple_of((meta[1] ^ d) * m, m), m)
        total = keep[src, :] + recv[src, :].astype(F32)
        dst = leave if d % 2 else stay
        dst[d // 2 * m:(d // 2 + 1) * m, :] = total.astype(dst.dtype)


def combine(meta, keep, recv, dp):
    rows = keep.shape[0] // 2
    return pl.pallas_call(
        functools.partial(combine_kernel, dp),
        in_specs=[smem(), vmem(), vmem()], out_specs=[vmem(), vmem()],
        out_shape=[struct((rows, LANES), F32), struct((rows, LANES), BF)],
        compiler_params=params())(meta, keep, recv)


def mix_kernel(n, taps, meta, ad, low, act, pre, win1, wout1, consts, tokp, buf_c, buf_d, branch, ag, out,
               offs, win2, wout2, bias, bias_row, sems):
    copies = weight_copies(buf_c, 0, win2, wout2, bias, sems) + weight_copies(buf_d, 1, win2, wout2, bias, sems)
    for c in copies:
        c.start()
    place_items(n, meta, offs)

    def own(at):
        return dot(act[at, :], wout1[...]), dot_t(pre[at, :], win1[...])

    def rest(at, own_branch, own_ag):
        a, b = ad[at, :], low[at, :]
        activation, slope = gelu_parts(dot(a, win2[...]) + bias_row[...])
        grad = dot_t(b, wout2[...]) * slope
        value = (own_branch + dot(activation.astype(BF), wout2[...])) + consts[taps + 1:taps + 2, :]
        branch[at, :] = value
        out[at, :] = (tokp[at, :].astype(F32) + consts[taps:taps + 1, :] * value).astype(BF)
        ag[at, :] = own_ag + dot_t(grad.astype(BF), win2[...])

    first = pl.ds(0, TILE)
    branch[first, :], ag[first, :] = own(first)
    for c in copies:
        c.wait()
    spread_bias(bias, bias_row)
    rest(first, branch[first, :], ag[first, :])

    def block(start, tiles):
        at = pl.ds(pl.multiple_of(start * TILE, TILE), tiles * TILE)
        rest(at, *own(at))

    def triple(t, _):
        block(3 * t + 1, 3)
        return 0

    left = offs[n + 1] - 1
    triples = lax.div(left, 3)
    lax.fori_loop(0, triples, triple, 0)
    for tiles in (1, 2):
        pl.when(left - 3 * triples == tiles)(functools.partial(block, 3 * triples + 1, tiles))


def mix(meta, ad, low, act, pre, win, wout, consts, tokp, buf_c, buf_d, n, taps):
    rows, width = ad.shape
    h = act.shape[1] // 2
    wq, hq = width // LANES, h // LANES
    return pl.pallas_call(
        functools.partial(mix_kernel, n, taps),
        in_specs=[smem()] + [vmem()] * 8 + [hbm()] * 2,
        out_specs=[vmem()] * 3,
        scratch_shapes=[pltpu.SMEM((n + 2,), jnp.int32),
                        pltpu.VMEM((width, 2 * h), BF), pltpu.VMEM((2 * h, width), BF),
                        pltpu.VMEM((2, 16, LANES), BF), pltpu.VMEM((1, 2 * h), F32),
                        pltpu.SemaphoreType.DMA((2, hq + wq + 1))],
        out_shape=[struct((rows, width), F32)] * 2 + [struct((rows, width), BF)],
        compiler_params=params(), cost_estimate=cost(0),
    )(meta, ad, low, act, pre, win, wout, consts, tokp, buf_c, buf_d)


def norm_grad_kernel(n, taps, rates, meta, tok, cot, branch, ag, nrm, inv, gbo, gbi, consts,
                     cgp, small_keep, small_send, offs, sums):
    s = pl.program_id(0)
    frames, width = tok.shape[1], tok.shape[2]
    half = taps // 2
    wq = width // LANES
    h = gbi.shape[1] // 2

    @pl.when(s == 0)
    def _():
        place_items(n, meta, offs)
        sums[...] = jnp.zeros_like(sums)

    item = meta[0] * n + s
    count = meta[2 + item]
    group = meta[2 + 2 * n + item]
    off = offs[s]
    scale = pick(consts.at[taps + 2:taps + 2 + rates], group)
    zero = jnp.zeros((8, LANES), F32)
    steps = pl.cdiv(count, CHUNK)
    wide = steps // 2

    def step(r0, size, accs):
        here = pl.ds(r0, size)
        live = (lax.broadcasted_iota(jnp.int32, (size, LANES), 0) + r0) < count
        src = pl.ds(pl.multiple_of(off + r0, 16), size)
        new = []
        ngs, nrs = [], []
        for q in range(wq):
            a_ls, a_sc, a_sh = accs[3 * q:3 * q + 3]
            br = jnp.where(live, branch[src, lane(q)], 0.0)
            g = jnp.where(live, ag[src, lane(q)], 0.0)
            nr = nrm[src, lane(q)].astype(F32)
            new += [a_ls + fold(cot[s, here, lane(q)].astype(F32) * br), a_sc + fold(g * nr), a_sh + fold(g)]
            ngs.append(g * scale[:, lane(q)])
            nrs.append(nr)
        cross = [a * b for a, b in zip(ngs, nrs)]
        m1 = jnp.sum(sum(ngs[1:], ngs[0]), axis=-1, keepdims=True) * (1.0 / width)
        m2 = jnp.sum(sum(cross[1:], cross[0]), axis=-1, keepdims=True) * (1.0 / width)
        istd = inv[src, :]
        for q in range(wq):
            cg = istd * (ngs[q] - m1 - nrs[q] * m2)
            cgp[s, q, pl.ds(pl.multiple_of(r0 + PAD, 8), size), :] = cg
        return tuple(new)

    def both_sizes(run, width_of_state, add):
        add(lax.fori_loop(0, wide, lambda i, accs: run(pl.multiple_of(i * 2 * CHUNK, 2 * CHUNK), 2 * CHUNK, accs),
                          (zero,) * width_of_state))

        @pl.when(steps > 2 * wide)
        def _():
            add(run(pl.multiple_of(wide * 2 * CHUNK, 2 * CHUNK), CHUNK, (zero,) * width_of_state))

    def add_norm(accs):
        for q in range(wq):
            sums[taps + 1, :, lane(q)] += accs[3 * q]
            sums[taps + 2 + group, :, lane(q)] += accs[3 * q + 1]
            sums[taps + 2 + rates + group, :, lane(q)] += accs[3 * q + 2]

    both_sizes(step, 3 * wq, add_norm)

    def clear(i, _):
        r0 = pl.multiple_of(i * CHUNK, CHUNK)
        for q in range(wq):
            cgp[s, q, pl.ds(pl.multiple_of(r0 + PAD, 8), CHUNK), :] = jnp.zeros((CHUNK, LANES), F32)
        return 0

    lax.fori_loop(steps, frames // CHUNK, clear, 0)
    for q in range(wq):
        cgp[s, q, :PAD, :] = jnp.zeros((PAD, LANES), F32)
        cgp[s, q, PAD + frames:, :] = jnp.zeros((cgp.shape[2] - PAD - frames, LANES), F32)

        def conv_step(r0, size, accs):
            here = pl.ds(r0, size)
            live = (lax.broadcasted_iota(jnp.int32, (size, LANES), 0) + r0) < count
            tk = jnp.where(live, tok[s, here, lane(q)].astype(F32), 0.0)
            new = []
            for k in range(taps):
                sh = cgp[s, q, pl.ds(r0 + (PAD + half - k), size), :]
                new.append(accs[k] + fold(tk * sh))
                if k == half:
                    new_bias = accs[taps] + fold(sh)
            return tuple(new) + (new_bias,)

        def add_conv(accs):
            for k in range(taps + 1):
                sums[k, :, lane(q)] += accs[k]

        both_sizes(conv_step, taps + 1, add_conv)

    @pl.when(s == n - 1)
    def _():
        last = taps + 2 + 2 * rates
        rows = [jnp.sum(sums[i], axis=0, keepdims=True) for i in range(last)]
        rows.append(jnp.sum(gbo[...], axis=0, keepdims=True))
        gb = jnp.sum(gbi[...], axis=0, keepdims=True)
        fill = jnp.zeros((1, width - h), F32)
        spare = [jnp.zeros((1, width), F32)] * (small_keep.shape[0] - last - 2)
        for side, dst in ((0, small_keep), (1, small_send)):
            tail = [jnp.concatenate([gb[:, side * h:(side + 1) * h], fill], axis=1)]
            dst[...] = jnp.concatenate(rows + tail + spare, axis=0)


def norm_grad(meta, tok, cot, branch, ag, nrm, inv, gbo, gbi, consts, taps, rates):
    n, frames, width = tok.shape
    wq = width // LANES
    n_small = -(-(taps + 4 + 2 * rates) // 8) * 8
    return pl.pallas_call(
        functools.partial(norm_grad_kernel, n, taps, rates), grid=(n,),
        in_specs=[smem()] + [vmem()] * 9, out_specs=[vmem()] * 3,
        scratch_shapes=[pltpu.SMEM((n + 2,), jnp.int32),
                        pltpu.VMEM((taps + 2 + 2 * rates, 8, width), F32)],
        out_shape=[struct((n, wq, frames + 4 * PAD, LANES), F32)] + [struct((n_small, width), F32)] * 2,
        compiler_params=params(), cost_estimate=cost(40000000),
    )(meta, tok, cot, branch, ag, nrm, inv, gbo, gbi, consts)


def place_out_kernel(n, meta, own, other, out, stage, sems):
    frames, width = stage.shape[1], stage.shape[2]
    copies = []
    for side, src in ((0, own), (1, other)):
        first = (meta[0] ^ side) * n
        off = jnp.int32(0)
        for j in range(n):
            count = meta[2 + first + j]
            for i in range(frames // CHUNK):
                live = (lax.broadcasted_iota(jnp.int32, (CHUNK, LANES), 0) + i * CHUNK) < count
                rows = pl.ds(pl.multiple_of(off + i * CHUNK, 16), CHUNK)
                for q in range(width // LANES):
                    value = jnp.where(live, src[rows, lane(q)].astype(F32), 0.0)
                    stage[side * n + j, i * CHUNK:(i + 1) * CHUNK, lane(q)] = value.astype(BF)
            copies.append(pltpu.make_async_copy(stage.at[side * n + j], out.at[first + j], sems.at[side * n + j]))
            copies[-1].start()
            off = off + ((count + 15) & -16)
    for c in copies:
        c.wait()


def place_out(meta, own, other, n, frames):
    width = own.shape[1]
    return pl.pallas_call(
        functools.partial(place_out_kernel, n),
        in_specs=[smem(), vmem(), vmem()], out_specs=hbm(), out_shape=struct((2 * n, frames, width), BF),
        scratch_shapes=[pltpu.VMEM((2 * n, frames, width), BF), pltpu.SemaphoreType.DMA((2 * n,))],
        compiler_params=params(), cost_estimate=cost(40000000),
    )(meta, own, other)


def token_grad_kernel(n, taps, meta, cot, cgp, consts, gtok, gtok_own, stage, sems):
    s = pl.program_id(0)
    frames, width = cot.shape[1], cot.shape[2]
    half = taps // 2
    wq = width // LANES
    count = meta[2 + meta[0] * n + s]
    w = consts[:taps, :]
    steps = pl.cdiv(count, CHUNK)

    def place(j):
        return pltpu.make_async_copy(stage.at[j], gtok.at[meta[0] * n + j], sems.at[j])

    def conv_step(i, _):
        r0 = pl.multiple_of(i * CHUNK, CHUNK)
        here = pl.ds(r0, CHUNK)
        live = (lax.broadcasted_iota(jnp.int32, (CHUNK, LANES), 0) + r0) < count
        for q in range(wq):
            total = cot[s, here, lane(q)].astype(F32)
            for k in range(taps):
                total = total + w[k:k + 1, lane(q)] * cgp[s, q, pl.ds(r0 + (PAD + half - k), CHUNK), :]
            total = jnp.where(live, total, 0.0).astype(BF)
            gtok_own[s, here, lane(q)] = total
            stage[s, here, lane(q)] = total.astype(F32)
        return 0

    lax.fori_loop(0, steps, conv_step, 0)

    def clear(i, _):
        here = pl.ds(pl.multiple_of(i * CHUNK, CHUNK), CHUNK)
        gtok_own[s, here, :] = jnp.zeros((CHUNK, width), BF)
        stage[s, here, :] = jnp.zeros((CHUNK, width), F32)
        return 0

    lax.fori_loop(steps, frames // CHUNK, clear, 0)
    place(s).start()

    @pl.when(s == n - 1)
    def _():
        for j in range(n):
            place(j).wait()


def token_grad(meta, cot, cgp, consts, taps):
    n, frames, width = cot.shape
    return pl.pallas_call(
        functools.partial(token_grad_kernel, n, taps), grid=(n,),
        in_specs=[smem()] + [vmem()] * 3, out_specs=[hbm(), vmem()],
        scratch_shapes=[pltpu.VMEM((n, frames, width), F32), pltpu.SemaphoreType.DMA((n,))],
        out_shape=[struct((2 * n, frames, width), F32), struct((n, frames, width), BF)],
        compiler_params=params(), cost_estimate=cost(40000000),
    )(meta, cot, cgp, consts)


def merge_gtok_kernel(n, meta, other, gtok_in, gtok, stage, sems):
    copies = [pltpu.make_async_copy(stage.at[j], gtok.at[(1 - meta[0]) * n + j], sems.at[j]) for j in range(n)]
    for j in range(n):
        stage[j] = other[j].astype(F32)
        copies[j].start()
    for c in copies:
        c.wait()


def merge_gtok(meta, other, gtok):
    n = other.shape[0]
    return pl.pallas_call(
        functools.partial(merge_gtok_kernel, n),
        in_specs=[smem(), vmem(), hbm()], out_specs=hbm(), out_shape=struct(gtok.shape, F32),
        scratch_shapes=[pltpu.VMEM(other.shape, F32), pltpu.SemaphoreType.DMA((n,))],
        input_output_aliases={2: 0},
        compiler_params=params(), cost_estimate=cost(20000000),
    )(meta, other, gtok)


def message_kernel(stay, keep, recv, *refs):
    pieces, (out, mine) = refs[:-2], refs[-2:]
    m = pieces[0].shape[0]
    total = stay[:m, :]
    for piece in pieces:
        total = total + piece[...].astype(F32)
    out[:m, :] = total.astype(BF)
    mine[...] = total.astype(BF)
    small = (keep[...] + recv[...]).astype(BF)
    rows = small.shape[0]
    for q in range(small.shape[1] // LANES):
        out[m + q * rows:m + (q + 1) * rows, :] = small[:, lane(q)]


def make_message(stay, keep, recv, pieces):
    rows = pieces[0].shape[0] + keep.size // LANES
    return pl.pallas_call(message_kernel, in_specs=[vmem()] * (3 + len(pieces)), out_specs=[vmem(), vmem()],
                          out_shape=[struct((rows, LANES), BF), struct(pieces[0].shape, BF)],
                          compiler_params=params())(stay, keep, recv, *pieces)


def relay_kernel(m, *refs):
    sources, out = refs[:-1], refs[-1]
    sums = []
    for d, src in enumerate(sources):
        if d > 1:
            out[(d - 2) * m:(d - 1) * m, :] = src[:m, :]
        sums.append(src[m:, :].astype(F32))
    while len(sums) > 1:
        sums = [a + b for a, b in zip(sums[::2], sums[1::2])]
    out[(len(sources) - 2) * m:, :] = sums[0].astype(BF)


def relay(m, sources):
    rows = (len(sources) - 2) * m + sources[0].shape[0] - m
    return pl.pallas_call(functools.partial(relay_kernel, m), in_specs=[vmem()] * len(sources), out_specs=vmem(),
                          out_shape=struct((rows, LANES), BF), compiler_params=params())(*sources)


def unpack_kernel(dp, taps, rates, meta, mine, theirs, near_1, far_1, near, far, gcw, gcb, gns, gnsh, gwi, gbi, gwo, gbo, gls, full):
    h, width = gwo.shape
    wq, hq = width // LANES, h // LANES
    m = full.shape[0] // dp
    for odd, early, others in ((0, (mine, near_1), near), (1, (theirs, far_1), far)):
        for d in range(dp // 2):
            piece = others[(d - 2) * m:(d - 1) * m, :] if d > 1 else early[d][:m, :]
            at = pl.multiple_of((meta[1] ^ (2 * d + odd)) * m, m)
            full[pl.ds(at, m), :] = piece.astype(F32)
    for q in range(wq):
        gwo[:, lane(q)] = full[q * h:(q + 1) * h, :]
    base = wq * h
    for q in range(hq):
        gwi[:, lane(q)] = full[base + q * width:base + (q + 1) * width, :]
    behind = (dp // 2 - 2) * m
    small = near[behind:, :].astype(F32) + far[behind:, :].astype(F32)
    rows = small.shape[0] // wq
    small = jnp.concatenate([small[q * rows:(q + 1) * rows] for q in range(wq)], axis=1)
    gcw[...] = small[:taps]
    gcb[...] = small[taps]
    gls[...] = small[taps + 1]
    gns[...] = small[taps + 2:taps + 2 + rates]
    gnsh[...] = small[taps + 2 + rates:taps + 2 + 2 * rates]
    at = taps + 2 + 2 * rates
    gbo[...] = small[at]
    gbi[...] = small[at + 1, :h]


def unpack(meta, mine, theirs, near_1, far_1, near, far, dp, taps, rates, width, h):
    shapes = [(taps, width), (width,), (rates, width), (rates, width), (width, h), (h,), (h, width), (width,), (width,)]
    return pl.pallas_call(
        functools.partial(unpack_kernel, dp, taps, rates), in_specs=[smem()] + [vmem()] * 6,
        out_shape=[struct(s, F32) for s in shapes],
        scratch_shapes=[pltpu.VMEM((2 * width * h // LANES, LANES), F32)],
        compiler_params=params())(meta, mine, theirs, near_1, far_1, near, far)


def swap(x, step):
    size = lax.axis_size("tp")
    return lax.ppermute(x, "tp", [(i, i ^ step) for i in range(size)])


def across(x, step):
    size = lax.axis_size("dp")
    return lax.ppermute(x, "dp", [(i, i ^ step) for i in range(size)])


def per_device(tokens, frame_counts, rate_groups, conv_weight, conv_bias, norm_scale, norm_shift,
               weight_in, bias_in, weight_out, bias_out, layer_scale, cotangent):
    width, h = weight_in.shape
    n = tokens.shape[0] // 2
    (tokens, cotangent, conv_weight, conv_bias, norm_scale, norm_shift, weight_in, bias_in, weight_out, bias_out,
     layer_scale, frame_counts, rate_groups) = [pltpu.with_memory_space_constraint(v, pltpu.HBM) for v in (
         tokens, cotangent, conv_weight, conv_bias, norm_scale, norm_shift, weight_in, bias_in, weight_out, bias_out,
         layer_scale, frame_counts, rate_groups)]
    taps, rates = conv_weight.shape[0], norm_scale.shape[0]
    dp = lax.axis_size("dp")
    buf_a = pack(weight_in, bias_in, weight_out)
    buf_b = swap(buf_a, 1)
    buf_c = swap(buf_a, 2)
    buf_d = swap(buf_c, 1)
    ad, nrm, low, inv, act, pre, win, wout, keep, send, gbo, gbi, tok, cot, consts, tokp, meta = front(
        frame_counts, rate_groups, tokens, cotangent, conv_weight, conv_bias, norm_scale, norm_shift, layer_scale, bias_out, buf_a, buf_b, h)
    stay, leave = combine(meta, keep, swap(send, 1), dp)
    arrived = across(leave, 1)
    branch, ag, out_own = mix(meta, ad, low, act, pre, win, wout, consts, tokp, buf_c, buf_d, n, taps)
    arrived, branch, out_own = lax.optimization_barrier((arrived, branch, out_own))
    out_b = swap(out_own, 1)
    stay = (stay + arrived.astype(F32)).reshape(dp // 2, -1, LANES)
    pieces = [across(stay[d].astype(BF), 2 * d) for d in range(1, dp // 2)]

    cgp, small_keep, small_send = norm_grad(meta, tok, cot, branch, ag, nrm, inv, gbo, gbi, consts, taps, rates)
    pieces, small_send, cgp, out_b = lax.optimization_barrier((pieces, small_send, cgp, out_b))
    small_got = swap(small_send, 1)
    message, mine = make_message(stay.reshape(-1, LANES), small_keep, small_got, pieces)
    message, mine, out_b = lax.optimization_barrier((message, mine, out_b))
    m = pieces[0].shape[0]
    near = [message] + [across(message, 2 * d) for d in range(1, dp // 2)]
    theirs = across(mine, 1)
    far_1 = across(mine, 3)
    out = place_out(meta, out_own, out_b, n, tokens.shape[1])
    cgp, out = lax.optimization_barrier((cgp, out))
    gtok, gtok_own = token_grad(meta, cot, cgp, consts, taps)
    near, theirs, far_1, gtok_own = lax.optimization_barrier((near, theirs, far_1, gtok_own))
    late = relay(m, near)
    far = across(late, 1)
    gtok = merge_gtok(meta, swap(gtok_own, 1), gtok)
    far, gtok = lax.optimization_barrier((far, gtok))
    gcw, gcb, gns, gnsh, gwi, gbi, gwo, gbo, gls = unpack(meta, mine, theirs, near[1], far_1, late, far, dp, taps, rates,
                                                          width, h)
    return (out, gtok, gcw, gcb, gns, gnsh, gwi, gbi, gwo, gbo, gls)


def solution(mesh):
    items, copied = P("dp", None, None), P()
    in_specs = (items, P("dp"), P("dp"), copied, copied, copied, copied, P(None, "tp"), P("tp"), P("tp", None),
                copied, copied, items)
    out_specs = (items, items, copied, copied, copied, copied, P(None, "tp"), P("tp"), P("tp", None), copied, copied)
    return jax.shard_map(per_device, mesh=mesh, in_specs=in_specs, out_specs=out_specs, check_vma=False)
```

```python
import functools

import jax
import jax.numpy as jnp
from jax import lax
from jax.experimental import pallas as pl
from jax.experimental.pallas import tpu as pltpu
from jax.sharding import PartitionSpec as P

EPS = 1e-06
BF, F32 = jnp.bfloat16, jnp.float32
TILE = 256
LANES = 128
PAD = 8
CHUNK = 64
FRONT_CHUNK = 32
VMEM_LIMIT = 12 * 1024 * 1024


def params(**more):
    return pltpu.CompilerParams(vmem_limit_bytes=VMEM_LIMIT, **more)


def struct(shape, dtype):
    return jax.ShapeDtypeStruct(shape, dtype)


def whole(shape):
    return pl.BlockSpec(shape, lambda *_: (0,) * len(shape))


def hbm():
    return pl.BlockSpec(memory_space=pltpu.HBM)


def smem():
    return pl.BlockSpec(memory_space=pltpu.SMEM)


def cost(size):
    return pl.CostEstimate(flops=0, transcendentals=0, bytes_accessed=size)


def vmem():
    return pl.BlockSpec(memory_space=pltpu.VMEM)


def lane(q):
    return slice(q * LANES, (q + 1) * LANES)


def fold(x):
    return jnp.sum(x.reshape(x.shape[0] // 8, 8, x.shape[1]), axis=0)


def pick(table, group):
    rows = table[...].astype(F32)
    value = rows[0:1]
    for r in range(1, rows.shape[0]):
        value = jnp.where(group == r, rows[r:r + 1], value)
    return value


def as_row(ref):
    return ref[...].astype(F32).reshape(1, -1)


def gelu_parts(pre):
    cdf = 0.5 + 0.5 * lax.erf(pre * 0.7071067811865476)
    density = jnp.exp(-0.5 * pre * pre) * 0.3989422804014327
    return pre * cdf, cdf + pre * density


def dot(a, b):
    return jnp.dot(a, b, preferred_element_type=F32)


def dot_t(a, b):
    return lax.dot_general(a, b, (((1,), (1,)), ((), ())), preferred_element_type=F32)


def dot_rows(a, b):
    return lax.dot_general(a, b, (((0,), (0,)), ((), ())), preferred_element_type=F32)


def place_items(n, meta, offs):
    end = jnp.int32(0)
    for j in range(n):
        offs[j] = end
        end = end + ((meta[2 + meta[0] * n + j] + 15) & -16)
    offs[n] = end
    offs[n + 1] = (end + TILE - 1) // TILE


def pack_kernel(wi, bi, wo, out):
    width, h = wi.shape
    hq, wq = h // LANES, width // LANES
    for q in range(hq):
        out[q * width:(q + 1) * width, :] = wi[:, lane(q)]
    base = hq * width
    for q in range(wq):
        out[base + q * h:base + (q + 1) * h, :] = wo[:, lane(q)]
    base += wq * h
    bias = bi[...].astype(F32).reshape(1, h)
    rows = [bias[:, lane(q)] for q in range(hq)] + [jnp.zeros((1, LANES), F32)] * (16 - hq)
    out[base:base + 16, :] = jnp.concatenate(rows, axis=0).astype(BF)


def pack(wi, bi, wo):
    rows = 2 * wi.size // LANES + 16
    return pl.pallas_call(pack_kernel, out_shape=struct((rows, LANES), BF),
                          compiler_params=params())(wi, bi, wo)


def weight_copies(buf, side, win, wout, bias, sems):
    width, h = win.shape[0], win.shape[1] // 2
    hq, wq = h // LANES, width // LANES
    copies = []
    for q in range(hq):
        at = side * h + q * LANES
        copies.append((buf.at[pl.ds(q * width, width), :], win.at[:, pl.ds(at, LANES)]))
    base = hq * width
    for q in range(wq):
        copies.append((buf.at[pl.ds(base + q * h, h), :], wout.at[pl.ds(side * h, h), pl.ds(q * LANES, LANES)]))
    copies.append((buf.at[pl.ds(base + wq * h, 16), :], bias.at[side]))
    return [pltpu.make_async_copy(src, dst, sems.at[side, i]) for i, (src, dst) in enumerate(copies)]


def spread_bias(bias, row):
    hq = row.shape[1] // LANES // 2
    for side in range(2):
        for q in range(hq):
            at = side * hq + q
            row[:, lane(at)] = bias[side, q:q + 1, :].astype(F32)


def front_kernel(n, counts_hbm, groups_hbm, tok_hbm, cot_hbm, cw, cb, ns, nsh, gamma, bout, buf_a, buf_b,
                 ad, nrm, low, inv, act, pre, win, wout, keep, send, gbo, gbi, tok, cot, consts, tokp, meta,
                 offs, counts_s, groups_s, pad, ad_s, nrm_s, low_s, inv_s, bias, bias_row, dwo, dwi, sems, item_sems, meta_sems, packed_sem):
    s = pl.program_id(0)
    frames, width = tok.shape[1], tok.shape[2]
    taps, rates = cw.shape[0], ns.shape[0]
    half = taps // 2
    wq = width // LANES
    h = win.shape[1] // 2
    copies = weight_copies(buf_a, 0, win, wout, bias, sems) + weight_copies(buf_b, 1, win, wout, bias, sems)

    def fetch(j):
        at = (lax.axis_index("tp") & 1) * n + j
        return [pltpu.make_async_copy(src.at[at], dst.at[j], item_sems.at[i, j])
                for i, (src, dst) in enumerate(((tok_hbm, tok), (cot_hbm, cot)))]

    @pl.when(s == 0)
    def _():
        tables = [pltpu.make_async_copy(counts_hbm, counts_s, meta_sems.at[0]),
                  pltpu.make_async_copy(groups_hbm, groups_s, meta_sems.at[1])]
        for c in tables + fetch(0) + fetch(1):
            c.start()
        for c in copies:
            c.start()
        for j in range(2, n):
            for c in fetch(j):
                c.start()
        consts[...] = jnp.zeros_like(consts)
        consts[:taps, :] = cw[...].astype(F32)
        consts[taps:taps + 1, :] = as_row(gamma)
        consts[taps + 1:taps + 2, :] = as_row(bout)
        consts[taps + 2:taps + 2 + rates, :] = ns[...].astype(F32)
        offs[n + 2] = 0
        gbo[...] = jnp.zeros_like(gbo)
        pad[...] = jnp.zeros_like(pad)
        for stage in (ad_s, nrm_s, low_s, inv_s):
            stage[...] = jnp.zeros_like(stage)
        meta[0] = lax.axis_index("tp") & 1
        meta[1] = lax.axis_index("dp")
        for c in tables:
            c.wait()
        for j in range(2 * n):
            meta[2 + j] = counts_s[j]
            meta[2 + 2 * n + j] = groups_s[j]
        place_items(n, meta, offs)

    def flush(j):
        dst = pl.ds(pl.multiple_of(offs[j], 16), frames)
        for whole_ref, stage in ((ad, ad_s), (nrm, nrm_s), (low, low_s), (inv, inv_s)):
            whole_ref[dst, :] = stage[...]

    @pl.when(s > 0)
    def _():
        flush(s - 1)

    @pl.when(s == 1)
    def _():
        for c in copies:
            c.wait()
        spread_bias(bias, bias_row)
        dwo[...] = jnp.zeros_like(dwo)
        dwi[...] = jnp.zeros_like(dwi)
        gbi[...] = jnp.zeros_like(gbi)

    for c in fetch(s):
        c.wait()

    def fetch_packed(j):
        dst = pl.ds(pl.multiple_of(offs[j], 16), frames)
        return pltpu.make_async_copy(tok.at[j], tokp.at[dst, :], packed_sem)

    @pl.when(s > 1)
    def _():
        fetch_packed(s - 2).wait()

    @pl.when(s > 0)
    def _():
        fetch_packed(s - 1).start()

    item = meta[0] * n + s
    count = meta[2 + item]
    group = meta[2 + 2 * n + item]

    def setup():
        rows = lax.broadcasted_iota(jnp.int32, (frames, LANES), 0)
        for q in range(wq):
            pad[q, PAD:PAD + frames, :] = jnp.where(rows < count, tok[s, :, lane(q)].astype(F32), 0.0)
        return pick(ns, group), pick(nsh, group), as_row(gamma), as_row(cb), cw[...].astype(F32)

    def conv_step(i, acc, consts):
        scale, shift, gam, conv_bias, w = consts
        r0 = i * FRONT_CHUNK if isinstance(i, int) else pl.multiple_of(i * FRONT_CHUNK, FRONT_CHUNK)
        here = pl.ds(r0, FRONT_CHUNK)
        live = (lax.broadcasted_iota(jnp.int32, (FRONT_CHUNK, LANES), 0) + r0) < count
        convs = []
        for q in range(wq):
            conv = conv_bias[:, lane(q)]
            for k in range(taps):
                conv = conv + w[k:k + 1, lane(q)] * pad[q, pl.ds(r0 + (PAD - half + k), FRONT_CHUNK), :]
            convs.append(conv)
        mean = jnp.sum(sum(convs[1:], convs[0]), axis=-1, keepdims=True) * (1.0 / width)
        cents = [c - mean for c in convs]
        sq = [c * c for c in cents]
        var = jnp.sum(sum(sq[1:], sq[0]), axis=-1, keepdims=True) * (1.0 / width)
        istd = lax.rsqrt(var + EPS)
        inv_s[here, :] = jnp.broadcast_to(istd, (FRONT_CHUNK, LANES))
        new = []
        for q in range(wq):
            normed = cents[q] * istd
            ad_s[here, lane(q)] = (normed * scale[:, lane(q)] + shift[:, lane(q)]).astype(BF)
            nrm_s[here, lane(q)] = normed.astype(BF)
            back = jnp.where(live, cot[s, here, lane(q)].astype(F32), 0.0) * gam[:, lane(q)]
            low_s[here, lane(q)] = back.astype(BF)
            new.append(acc[q] + fold(back))
        return tuple(new)

    def add_gbo(accs):
        for q in range(wq):
            gbo[:, lane(q)] += accs[q]

    def tile(t, size, between=()):
        between = list(between)
        at = pl.ds(pl.multiple_of(t * TILE, TILE), size)
        a, b = ad[at, :], low[at, :]
        activation, slope = gelu_parts(dot(a, win[...]) + bias_row[...])
        if between:
            between.pop(0)()
        grad = dot_t(b, wout[...]) * slope
        lo = activation.astype(BF)
        act[at, :] = lo
        if between:
            between.pop(0)()
        dwo[...] += dot_rows(lo, b)
        gbi[...] += fold(grad)
        g = grad.astype(BF)
        pre[at, :] = g
        if between:
            between.pop(0)()
        dwi[...] += dot_rows(a, g)
        if between:
            between.pop(0)()

    done = offs[n + 2]
    ready = offs[s] >= (done + 2) * TILE
    none = (jnp.zeros((8, LANES), F32),) * wq

    def conv_with(chunks, with_tile):
        consts = setup()
        state = [none]

        def part(lo_i, hi_i):
            def run():
                for i in range(lo_i, hi_i):
                    state[0] = conv_step(i, state[0], consts)
            return run

        cuts = [chunks * k // 4 for k in range(5)]
        parts = [part(cuts[k], cuts[k + 1]) for k in range(4)]
        if with_tile:
            tile(done, 2 * TILE, parts)
        else:
            for run in parts:
                run()
        add_gbo(state[0])
        if with_tile:
            offs[n + 2] = done + 2

    all_chunks = frames // FRONT_CHUNK
    short = count <= (all_chunks * 3 // 4) * FRONT_CHUNK
    for with_tile in (True, False):
        for chunks in (all_chunks * 3 // 4, all_chunks):
            fits = short if chunks < all_chunks else jnp.logical_not(short)
            pl.when((ready == with_tile) & fits)(functools.partial(conv_with, chunks, with_tile))

    @pl.when(s == n - 1)
    def _():
        flush(s)
        end = pl.ds(pl.multiple_of(offs[n], 16), TILE)
        ad[end, :] = jnp.zeros((TILE, width), BF)
        low[end, :] = jnp.zeros((TILE, width), BF)

        fetch_packed(n - 2).wait()
        fetch_packed(n - 1).start()

        start = offs[n + 2]
        left = offs[n + 1] - start
        pairs = jnp.where(left == 3, 0, lax.shift_right_arithmetic(left, 1))

        def rest(t, _):
            tile(start + 2 * t, 2 * TILE)
            return 0

        lax.fori_loop(0, pairs, rest, 0)

        @pl.when(left == 3)
        def _():
            tile(start, 3 * TILE)

        @pl.when((left != 3) & (left > 2 * pairs))
        def _():
            tile(offs[n + 1] - 1, TILE)

        fetch_packed(n - 1).wait()
        for side, dst in ((0, keep), (1, send)):
            for q in range(wq):
                dst[q * h:(q + 1) * h, :] = dwo[side * h:(side + 1) * h, lane(q)].astype(dst.dtype)
            base = wq * h
            for q in range(h // LANES):
                dst[base + q * width:base + (q + 1) * width, :] = dwi[:, lane(side * (h // LANES) + q)].astype(dst.dtype)


def front(counts, groups, tok, cot, cw, cb, ns, nsh, gamma, bout, buf_a, buf_b, h):
    items, frames, width = tok.shape
    n = items // 2
    rows = n * frames + TILE
    packed = 2 * width * h // LANES
    wq, hq = width // LANES, h // LANES
    n_consts = -(-(cw.shape[0] + 2 + ns.shape[0]) // 8) * 8
    return pl.pallas_call(
        functools.partial(front_kernel, n),
        grid_spec=pl.GridSpec(
            grid=(n,),
            in_specs=[hbm()] * 4 + [whole(v.shape) for v in (cw, cb, ns, nsh, gamma, bout)] + [hbm()] * 2,
            out_specs=[vmem()] * 16 + [smem()],
            scratch_shapes=[pltpu.SMEM((n + 3,), jnp.int32), pltpu.SMEM((items,), jnp.int32), pltpu.SMEM((items,), jnp.int32),
                            pltpu.VMEM((wq, frames + 4 * PAD, LANES), F32),
                            pltpu.VMEM((frames, width), BF), pltpu.VMEM((frames, width), BF),
                            pltpu.VMEM((frames, width), BF), pltpu.VMEM((frames, LANES), F32),
                            pltpu.VMEM((2, 16, LANES), BF), pltpu.VMEM((1, 2 * h), F32),
                            pltpu.VMEM((2 * h, width), F32), pltpu.VMEM((width, 2 * h), F32),
                            pltpu.SemaphoreType.DMA((2, hq + wq + 1)), pltpu.SemaphoreType.DMA((2, n)),
                            pltpu.SemaphoreType.DMA((2,)), pltpu.SemaphoreType.DMA]),
        out_shape=[struct((rows, width), BF)] * 3 + [struct((rows, LANES), F32)]
        + [struct((rows, 2 * h), BF)] * 2 + [struct((width, 2 * h), BF), struct((2 * h, width), BF)]
        + [struct((packed, LANES), F32), struct((packed, LANES), BF), struct((8, width), F32), struct((8, 2 * h), F32)]
        + [struct((n, frames, width), BF)] * 2 + [struct((n_consts, width), F32), struct((rows, width), BF), struct((2 + 2 * items,), jnp.int32)],
        compiler_params=params(), cost_estimate=cost(0),
    )(counts, groups, tok, cot, cw, cb, ns, nsh, gamma, bout, buf_a, buf_b)


def combine_kernel(dp, meta, keep, recv, stay, leave):
    m = keep.shape[0] // dp
    for d in range(dp):
        src = pl.ds(pl.multiple_of((meta[1] ^ d) * m, m), m)
        total = keep[src, :] + recv[src, :].astype(F32)
        dst = leave if d % 2 else stay
        dst[d // 2 * m:(d // 2 + 1) * m, :] = total.astype(dst.dtype)


def combine(meta, keep, recv, dp):
    rows = keep.shape[0] // 2
    return pl.pallas_call(
        functools.partial(combine_kernel, dp),
        in_specs=[smem(), vmem(), vmem()], out_specs=[vmem(), vmem()],
        out_shape=[struct((rows, LANES), F32), struct((rows, LANES), BF)],
        compiler_params=params())(meta, keep, recv)


def mix_kernel(n, taps, meta, ad, low, act, pre, win1, wout1, consts, tokp, buf_c, buf_d, branch, ag, out,
               offs, win2, wout2, bias, bias_row, sems):
    copies = weight_copies(buf_c, 0, win2, wout2, bias, sems) + weight_copies(buf_d, 1, win2, wout2, bias, sems)
    for c in copies:
        c.start()
    place_items(n, meta, offs)

    def own(at):
        return dot(act[at, :], wout1[...]), dot_t(pre[at, :], win1[...])

    def rest(at, own_branch, own_ag):
        a, b = ad[at, :], low[at, :]
        activation, slope = gelu_parts(dot(a, win2[...]) + bias_row[...])
        grad = dot_t(b, wout2[...]) * slope
        value = (own_branch + dot(activation.astype(BF), wout2[...])) + consts[taps + 1:taps + 2, :]
        branch[at, :] = value
        out[at, :] = (tokp[at, :].astype(F32) + consts[taps:taps + 1, :] * value).astype(BF)
        ag[at, :] = own_ag + dot_t(grad.astype(BF), win2[...])

    first = pl.ds(0, TILE)
    branch[first, :], ag[first, :] = own(first)
    for c in copies:
        c.wait()
    spread_bias(bias, bias_row)
    rest(first, branch[first, :], ag[first, :])

    def block(start, tiles):
        at = pl.ds(pl.multiple_of(start * TILE, TILE), tiles * TILE)
        rest(at, *own(at))

    def triple(t, _):
        block(3 * t + 1, 3)
        return 0

    left = offs[n + 1] - 1
    triples = lax.div(left, 3)
    lax.fori_loop(0, triples, triple, 0)
    for tiles in (1, 2):
        pl.when(left - 3 * triples == tiles)(functools.partial(block, 3 * triples + 1, tiles))


def mix(meta, ad, low, act, pre, win, wout, consts, tokp, buf_c, buf_d, n, taps):
    rows, width = ad.shape
    h = act.shape[1] // 2
    wq, hq = width // LANES, h // LANES
    return pl.pallas_call(
        functools.partial(mix_kernel, n, taps),
        in_specs=[smem()] + [vmem()] * 8 + [hbm()] * 2,
        out_specs=[vmem()] * 3,
        scratch_shapes=[pltpu.SMEM((n + 2,), jnp.int32),
                        pltpu.VMEM((width, 2 * h), BF), pltpu.VMEM((2 * h, width), BF),
                        pltpu.VMEM((2, 16, LANES), BF), pltpu.VMEM((1, 2 * h), F32),
                        pltpu.SemaphoreType.DMA((2, hq + wq + 1))],
        out_shape=[struct((rows, width), F32)] * 2 + [struct((rows, width), BF)],
        compiler_params=params(), cost_estimate=cost(0),
    )(meta, ad, low, act, pre, win, wout, consts, tokp, buf_c, buf_d)


def norm_grad_kernel(n, taps, rates, meta, tok, cot, branch, ag, nrm, inv, gbo, gbi, consts,
                     cgp, small_keep, small_send, offs, sums):
    s = pl.program_id(0)
    frames, width = tok.shape[1], tok.shape[2]
    half = taps // 2
    wq = width // LANES
    h = gbi.shape[1] // 2

    @pl.when(s == 0)
    def _():
        place_items(n, meta, offs)
        sums[...] = jnp.zeros_like(sums)

    item = meta[0] * n + s
    count = meta[2 + item]
    group = meta[2 + 2 * n + item]
    off = offs[s]
    scale = pick(consts.at[taps + 2:taps + 2 + rates], group)
    zero = jnp.zeros((8, LANES), F32)
    steps = pl.cdiv(count, CHUNK)
    wide = steps // 2

    def step(r0, size, accs):
        here = pl.ds(r0, size)
        live = (lax.broadcasted_iota(jnp.int32, (size, LANES), 0) + r0) < count
        src = pl.ds(pl.multiple_of(off + r0, 16), size)
        new = []
        ngs, nrs = [], []
        for q in range(wq):
            a_ls, a_sc, a_sh = accs[3 * q:3 * q + 3]
            br = jnp.where(live, branch[src, lane(q)], 0.0)
            g = jnp.where(live, ag[src, lane(q)], 0.0)
            nr = nrm[src, lane(q)].astype(F32)
            new += [a_ls + fold(cot[s, here, lane(q)].astype(F32) * br), a_sc + fold(g * nr), a_sh + fold(g)]
            ngs.append(g * scale[:, lane(q)])
            nrs.append(nr)
        cross = [a * b for a, b in zip(ngs, nrs)]
        m1 = jnp.sum(sum(ngs[1:], ngs[0]), axis=-1, keepdims=True) * (1.0 / width)
        m2 = jnp.sum(sum(cross[1:], cross[0]), axis=-1, keepdims=True) * (1.0 / width)
        istd = inv[src, :]
        for q in range(wq):
            cg = istd * (ngs[q] - m1 - nrs[q] * m2)
            cgp[s, q, pl.ds(pl.multiple_of(r0 + PAD, 8), size), :] = cg
        return tuple(new)

    def both_sizes(run, width_of_state, add):
        add(lax.fori_loop(0, wide, lambda i, accs: run(pl.multiple_of(i * 2 * CHUNK, 2 * CHUNK), 2 * CHUNK, accs),
                          (zero,) * width_of_state))

        @pl.when(steps > 2 * wide)
        def _():
            add(run(pl.multiple_of(wide * 2 * CHUNK, 2 * CHUNK), CHUNK, (zero,) * width_of_state))

    def add_norm(accs):
        for q in range(wq):
            sums[taps + 1, :, lane(q)] += accs[3 * q]
            sums[taps + 2 + group, :, lane(q)] += accs[3 * q + 1]
            sums[taps + 2 + rates + group, :, lane(q)] += accs[3 * q + 2]

    both_sizes(step, 3 * wq, add_norm)

    def clear(i, _):
        r0 = pl.multiple_of(i * CHUNK, CHUNK)
        for q in range(wq):
            cgp[s, q, pl.ds(pl.multiple_of(r0 + PAD, 8), CHUNK), :] = jnp.zeros((CHUNK, LANES), F32)
        return 0

    lax.fori_loop(steps, frames // CHUNK, clear, 0)
    for q in range(wq):
        cgp[s, q, :PAD, :] = jnp.zeros((PAD, LANES), F32)
        cgp[s, q, PAD + frames:, :] = jnp.zeros((cgp.shape[2] - PAD - frames, LANES), F32)

        def conv_step(r0, size, accs):
            here = pl.ds(r0, size)
            live = (lax.broadcasted_iota(jnp.int32, (size, LANES), 0) + r0) < count
            tk = jnp.where(live, tok[s, here, lane(q)].astype(F32), 0.0)
            new = []
            for k in range(taps):
                sh = cgp[s, q, pl.ds(r0 + (PAD + half - k), size), :]
                new.append(accs[k] + fold(tk * sh))
                if k == half:
                    new_bias = accs[taps] + fold(sh)
            return tuple(new) + (new_bias,)

        def add_conv(accs):
            for k in range(taps + 1):
                sums[k, :, lane(q)] += accs[k]

        both_sizes(conv_step, taps + 1, add_conv)

    @pl.when(s == n - 1)
    def _():
        last = taps + 2 + 2 * rates
        rows = [jnp.sum(sums[i], axis=0, keepdims=True) for i in range(last)]
        rows.append(jnp.sum(gbo[...], axis=0, keepdims=True))
        gb = jnp.sum(gbi[...], axis=0, keepdims=True)
        fill = jnp.zeros((1, width - h), F32)
        spare = [jnp.zeros((1, width), F32)] * (small_keep.shape[0] - last - 2)
        for side, dst in ((0, small_keep), (1, small_send)):
            tail = [jnp.concatenate([gb[:, side * h:(side + 1) * h], fill], axis=1)]
            dst[...] = jnp.concatenate(rows + tail + spare, axis=0)


def norm_grad(meta, tok, cot, branch, ag, nrm, inv, gbo, gbi, consts, taps, rates):
    n, frames, width = tok.shape
    wq = width // LANES
    n_small = -(-(taps + 4 + 2 * rates) // 8) * 8
    return pl.pallas_call(
        functools.partial(norm_grad_kernel, n, taps, rates), grid=(n,),
        in_specs=[smem()] + [vmem()] * 9, out_specs=[vmem()] * 3,
        scratch_shapes=[pltpu.SMEM((n + 2,), jnp.int32),
                        pltpu.VMEM((taps + 2 + 2 * rates, 8, width), F32)],
        out_shape=[struct((n, wq, frames + 4 * PAD, LANES), F32)] + [struct((n_small, width), F32)] * 2,
        compiler_params=params(), cost_estimate=cost(40000000),
    )(meta, tok, cot, branch, ag, nrm, inv, gbo, gbi, consts)


def place_out_kernel(n, meta, own, other, out, stage, sems):
    frames, width = stage.shape[1], stage.shape[2]
    copies = []
    for side, src in ((0, own), (1, other)):
        first = (meta[0] ^ side) * n
        off = jnp.int32(0)
        for j in range(n):
            count = meta[2 + first + j]
            for i in range(frames // CHUNK):
                live = (lax.broadcasted_iota(jnp.int32, (CHUNK, LANES), 0) + i * CHUNK) < count
                rows = pl.ds(pl.multiple_of(off + i * CHUNK, 16), CHUNK)
                for q in range(width // LANES):
                    value = jnp.where(live, src[rows, lane(q)].astype(F32), 0.0)
                    stage[side * n + j, i * CHUNK:(i + 1) * CHUNK, lane(q)] = value.astype(BF)
            copies.append(pltpu.make_async_copy(stage.at[side * n + j], out.at[first + j], sems.at[side * n + j]))
            copies[-1].start()
            off = off + ((count + 15) & -16)
    for c in copies:
        c.wait()


def place_out(meta, own, other, n, frames):
    width = own.shape[1]
    return pl.pallas_call(
        functools.partial(place_out_kernel, n),
        in_specs=[smem(), vmem(), vmem()], out_specs=hbm(), out_shape=struct((2 * n, frames, width), BF),
        scratch_shapes=[pltpu.VMEM((2 * n, frames, width), BF), pltpu.SemaphoreType.DMA((2 * n,))],
        compiler_params=params(), cost_estimate=cost(40000000),
    )(meta, own, other)


def token_grad_kernel(n, taps, meta, cot, cgp, consts, gtok, gtok_own, stage, sems):
    s = pl.program_id(0)
    frames, width = cot.shape[1], cot.shape[2]
    half = taps // 2
    wq = width // LANES
    count = meta[2 + meta[0] * n + s]
    w = consts[:taps, :]
    steps = pl.cdiv(count, CHUNK)

    def place(j):
        return pltpu.make_async_copy(stage.at[j], gtok.at[meta[0] * n + j], sems.at[j])

    def conv_step(i, _):
        r0 = pl.multiple_of(i * CHUNK, CHUNK)
        here = pl.ds(r0, CHUNK)
        live = (lax.broadcasted_iota(jnp.int32, (CHUNK, LANES), 0) + r0) < count
        for q in range(wq):
            total = cot[s, here, lane(q)].astype(F32)
            for k in range(taps):
                total = total + w[k:k + 1, lane(q)] * cgp[s, q, pl.ds(r0 + (PAD + half - k), CHUNK), :]
            total = jnp.where(live, total, 0.0).astype(BF)
            gtok_own[s, here, lane(q)] = total
            stage[s, here, lane(q)] = total.astype(F32)
        return 0

    lax.fori_loop(0, steps, conv_step, 0)

    def clear(i, _):
        here = pl.ds(pl.multiple_of(i * CHUNK, CHUNK), CHUNK)
        gtok_own[s, here, :] = jnp.zeros((CHUNK, width), BF)
        stage[s, here, :] = jnp.zeros((CHUNK, width), F32)
        return 0

    lax.fori_loop(steps, frames // CHUNK, clear, 0)
    place(s).start()

    @pl.when(s == n - 1)
    def _():
        for j in range(n):
            place(j).wait()


def token_grad(meta, cot, cgp, consts, taps):
    n, frames, width = cot.shape
    return pl.pallas_call(
        functools.partial(token_grad_kernel, n, taps), grid=(n,),
        in_specs=[smem()] + [vmem()] * 3, out_specs=[hbm(), vmem()],
        scratch_shapes=[pltpu.VMEM((n, frames, width), F32), pltpu.SemaphoreType.DMA((n,))],
        out_shape=[struct((2 * n, frames, width), F32), struct((n, frames, width), BF)],
        compiler_params=params(), cost_estimate=cost(40000000),
    )(meta, cot, cgp, consts)


def merge_gtok_kernel(n, meta, other, gtok_in, gtok, stage, sems):
    copies = [pltpu.make_async_copy(stage.at[j], gtok.at[(1 - meta[0]) * n + j], sems.at[j]) for j in range(n)]
    for j in range(n):
        stage[j] = other[j].astype(F32)
        copies[j].start()
    for c in copies:
        c.wait()


def merge_gtok(meta, other, gtok):
    n = other.shape[0]
    return pl.pallas_call(
        functools.partial(merge_gtok_kernel, n),
        in_specs=[smem(), vmem(), hbm()], out_specs=hbm(), out_shape=struct(gtok.shape, F32),
        scratch_shapes=[pltpu.VMEM(other.shape, F32), pltpu.SemaphoreType.DMA((n,))],
        input_output_aliases={2: 0},
        compiler_params=params(), cost_estimate=cost(20000000),
    )(meta, other, gtok)


def message_kernel(stay, keep, recv, *refs):
    pieces, (out, mine) = refs[:-2], refs[-2:]
    m = pieces[0].shape[0]
    total = stay[:m, :]
    for piece in pieces:
        total = total + piece[...].astype(F32)
    out[:m, :] = total.astype(BF)
    mine[...] = total.astype(BF)
    small = (keep[...] + recv[...]).astype(BF)
    rows = small.shape[0]
    for q in range(small.shape[1] // LANES):
        out[m + q * rows:m + (q + 1) * rows, :] = small[:, lane(q)]


def make_message(stay, keep, recv, pieces):
    rows = pieces[0].shape[0] + keep.size // LANES
    return pl.pallas_call(message_kernel, in_specs=[vmem()] * (3 + len(pieces)), out_specs=[vmem(), vmem()],
                          out_shape=[struct((rows, LANES), BF), struct(pieces[0].shape, BF)],
                          compiler_params=params())(stay, keep, recv, *pieces)


def relay_kernel(m, *refs):
    sources, out = refs[:-1], refs[-1]
    sums = []
    for d, src in enumerate(sources):
        if d > 1:
            out[(d - 2) * m:(d - 1) * m, :] = src[:m, :]
        sums.append(src[m:, :].astype(F32))
    while len(sums) > 1:
        sums = [a + b for a, b in zip(sums[::2], sums[1::2])]
    out[(len(sources) - 2) * m:, :] = sums[0].astype(BF)


def relay(m, sources):
    rows = (len(sources) - 2) * m + sources[0].shape[0] - m
    return pl.pallas_call(functools.partial(relay_kernel, m), in_specs=[vmem()] * len(sources), out_specs=vmem(),
                          out_shape=struct((rows, LANES), BF), compiler_params=params())(*sources)


def unpack_kernel(dp, taps, rates, meta, mine, theirs, near_1, far_1, near, far, gcw, gcb, gns, gnsh, gwi, gbi, gwo, gbo, gls, full):
    h, width = gwo.shape
    wq, hq = width // LANES, h // LANES
    m = full.shape[0] // dp
    for odd, early, others in ((0, (mine, near_1), near), (1, (theirs, far_1), far)):
        for d in range(dp // 2):
            piece = others[(d - 2) * m:(d - 1) * m, :] if d > 1 else early[d][:m, :]
            at = pl.multiple_of((meta[1] ^ (2 * d + odd)) * m, m)
            full[pl.ds(at, m), :] = piece.astype(F32)
    for q in range(wq):
        gwo[:, lane(q)] = full[q * h:(q + 1) * h, :]
    base = wq * h
    for q in range(hq):
        gwi[:, lane(q)] = full[base + q * width:base + (q + 1) * width, :]
    behind = (dp // 2 - 2) * m
    small = near[behind:, :].astype(F32) + far[behind:, :].astype(F32)
    rows = small.shape[0] // wq
    small = jnp.concatenate([small[q * rows:(q + 1) * rows] for q in range(wq)], axis=1)
    gcw[...] = small[:taps]
    gcb[...] = small[taps]
    gls[...] = small[taps + 1]
    gns[...] = small[taps + 2:taps + 2 + rates]
    gnsh[...] = small[taps + 2 + rates:taps + 2 + 2 * rates]
    at = taps + 2 + 2 * rates
    gbo[...] = small[at]
    gbi[...] = small[at + 1, :h]


def unpack(meta, mine, theirs, near_1, far_1, near, far, dp, taps, rates, width, h):
    shapes = [(taps, width), (width,), (rates, width), (rates, width), (width, h), (h,), (h, width), (width,), (width,)]
    return pl.pallas_call(
        functools.partial(unpack_kernel, dp, taps, rates), in_specs=[smem()] + [vmem()] * 6,
        out_shape=[struct(s, F32) for s in shapes],
        scratch_shapes=[pltpu.VMEM((2 * width * h // LANES, LANES), F32)],
        compiler_params=params())(meta, mine, theirs, near_1, far_1, near, far)


def swap(x, step):
    size = lax.axis_size("tp")
    return lax.ppermute(x, "tp", [(i, i ^ step) for i in range(size)])


def across(x, step):
    size = lax.axis_size("dp")
    return lax.ppermute(x, "dp", [(i, i ^ step) for i in range(size)])


def per_device(tokens, frame_counts, rate_groups, conv_weight, conv_bias, norm_scale, norm_shift,
               weight_in, bias_in, weight_out, bias_out, layer_scale, cotangent):
    width, h = weight_in.shape
    n = tokens.shape[0] // 2
    (tokens, cotangent, conv_weight, conv_bias, norm_scale, norm_shift, weight_in, bias_in, weight_out, bias_out,
     layer_scale, frame_counts, rate_groups) = [pltpu.with_memory_space_constraint(v, pltpu.HBM) for v in (
         tokens, cotangent, conv_weight, conv_bias, norm_scale, norm_shift, weight_in, bias_in, weight_out, bias_out,
         layer_scale, frame_counts, rate_groups)]
    taps, rates = conv_weight.shape[0], norm_scale.shape[0]
    dp = lax.axis_size("dp")
    buf_a = pack(weight_in, bias_in, weight_out)
    buf_b = swap(buf_a, 1)
    buf_c = swap(buf_a, 2)
    buf_d = swap(buf_c, 1)
    ad, nrm, low, inv, act, pre, win, wout, keep, send, gbo, gbi, tok, cot, consts, tokp, meta = front(
        frame_counts, rate_groups, tokens, cotangent, conv_weight, conv_bias, norm_scale, norm_shift, layer_scale, bias_out, buf_a, buf_b, h)
    stay, leave = combine(meta, keep, swap(send, 1), dp)
    arrived = across(leave, 1)
    branch, ag, out_own = mix(meta, ad, low, act, pre, win, wout, consts, tokp, buf_c, buf_d, n, taps)
    arrived, branch, out_own = lax.optimization_barrier((arrived, branch, out_own))
    out_b = swap(out_own, 1)
    stay = (stay + arrived.astype(F32)).reshape(dp // 2, -1, LANES)
    pieces = [across(stay[d].astype(BF), 2 * d) for d in range(1, dp // 2)]

    cgp, small_keep, small_send = norm_grad(meta, tok, cot, branch, ag, nrm, inv, gbo, gbi, consts, taps, rates)
    pieces, small_send, cgp, out_b = lax.optimization_barrier((pieces, small_send, cgp, out_b))
    small_got = swap(small_send, 1)
    message, mine = make_message(stay.reshape(-1, LANES), small_keep, small_got, pieces)
    message, mine, out_b = lax.optimization_barrier((message, mine, out_b))
    m = pieces[0].shape[0]
    near = [message] + [across(message, 2 * d) for d in range(1, dp // 2)]
    theirs = across(mine, 1)
    far_1 = across(mine, 3)
    out = place_out(meta, out_own, out_b, n, tokens.shape[1])
    cgp, out = lax.optimization_barrier((cgp, out))
    gtok, gtok_own = token_grad(meta, cot, cgp, consts, taps)
    near, theirs, far_1, gtok_own = lax.optimization_barrier((near, theirs, far_1, gtok_own))
    late = relay(m, near)
    far = across(late, 1)
    gtok = merge_gtok(meta, swap(gtok_own, 1), gtok)
    far, gtok = lax.optimization_barrier((far, gtok))
    gcw, gcb, gns, gnsh, gwi, gbi, gwo, gbo, gls = unpack(meta, mine, theirs, near[1], far_1, late, far, dp, taps, rates,
                                                          width, h)
    return (out, gtok, gcw, gcb, gns, gnsh, gwi, gbi, gwo, gbo, gls)


def solution(mesh):
    items, copied = P("dp", None, None), P()
    in_specs = (items, P("dp"), P("dp"), copied, copied, copied, copied, P(None, "tp"), P("tp"), P("tp", None),
                copied, copied, items)
    out_specs = (items, items, copied, copied, copied, copied, P(None, "tp"), P("tp"), P("tp", None), copied, copied)
    return jax.shard_map(per_device, mesh=mesh, in_specs=in_specs, out_specs=out_specs, check_vma=False)
```
